32 devices in a mesh: wide: 8 (over z, x), narrow: 4 (over y, core).
Axes of the slice: x: 2, y: 2, z: 4, core: 2. Of those that a mesh axis runs over, the one named last changes fastest.
Arguments:
- tokens: bfloat16 [65536, 768], P(('wide', 'narrow')), may hold values from -6 to 6
- timestep: int32 [64], P(('wide', 'narrow')), may hold values from 0 to 999
- span_start: int32 [64], P(('wide', 'narrow')), may hold values from 0 to 511
- span_length: int32 [64], P(('wide', 'narrow')), may hold values from 1 to 512
- mask_embed: bfloat16 [768], P('narrow'), may hold values from -6 to 6
- ada_weight: bfloat16 [128, 4608], P(None, 'narrow'), may hold values from -0.5 to 0.5
- ada_bias: bfloat16 [4608], P('narrow'), may hold values from -3 to 3
- norm_first: bfloat16 [768], P('narrow'), may hold values from 0.099609375 to 1.8984375
- query_key_value_weight: bfloat16 [768, 2304], P('narrow'), may hold values from -0.21875 to 0.21875
- output_weight: bfloat16 [768, 768], P('narrow'), may hold values from -1.25 to 1.25
- norm_second: bfloat16 [768], P('narrow'), may hold values from 0.099609375 to 1.8984375
- up_projection_weight: bfloat16 [768, 3072], P('narrow'), may hold values from -0.21875 to 0.21875
- up_projection_bias: bfloat16 [3072], P('narrow'), may hold values from -3 to 3
- down_projection_weight: bfloat16 [3072, 768], P('narrow'), may hold values from -0.109375 to 0.109375
- down_projection_bias: bfloat16 [768], P('narrow'), may hold values from -3 to 3
- cotangent: bfloat16 [65536, 768], P(('wide', 'narrow')), may hold values from -6 to 6
Outputs:
- block_out: bfloat16 [65536, 768], P(('wide', 'narrow'))
- grad_tokens: float32 [65536, 768], P(('wide', 'narrow'))
- grad_mask_embed: float32 [768], P('narrow')
- grad_ada_weight: float32 [128, 4608], P(None, 'narrow')
- grad_ada_bias: float32 [4608], P('narrow')
- grad_norm_first: float32 [768], P('narrow')
- grad_qkv_weight: float32 [768, 2304], P('narrow')
- grad_out_weight: float32 [768, 768], P('narrow')
- grad_norm_second: float32 [768], P('narrow')
- grad_up_weight: float32 [768, 3072], P('narrow')
- grad_up_bias: float32 [3072], P('narrow')
- grad_down_weight: float32 [3072, 768], P('narrow')
- grad_down_bias: float32 [768], P('narrow')
The draws below stay inside these ranges and needn't reach their ends.
Inputs may be any that keep to these rules, and one draw needn't show every extreme that they name: `timestep`: one diffusion step index per sequence, below 1000. `span_start`: the masked span starts in the first half of its sequence. `span_length`: the masked span holds at least one position and ends inside its sequence.
All inputs are finite; a program needn't handle non-finite values.
Results may differ from the reference program's by a relative error of at most 0.012.
The reference program's roundings to bfloat16 on the way count: a program that leaves them out, or rounds other values in their place, can miss the bound.
Values may be sent and summed in bfloat16 or wider, within the bound.
A program may use at most 320 MiB of HBM per device.

```python
import math
import jax
import jax.numpy as jnp
from jax import lax

D = 768
HEAD = 64
FF = 3072
TDIM = 128
SEQ = 1024
STEPS = 1000
SEQS = 64
TOKENS = 65536


def with_ends(entries, own_key, least, top_value):
    shape = entries.shape
    spot = [jax.random.randint(jax.random.fold_in(own_key, axis), (), 0, shape[axis]) for axis in range(len(shape))]
    entries = entries.at[tuple(spot)].set(least)
    longest = shape.index(max(shape))
    spot[longest] = (spot[longest] + 1) % shape[longest]
    return entries.at[tuple(spot)].set(top_value)


def levels(own_key, shape, cuts, low, top_value):
    level, own = 1.0, jax.random.fold_in(own_key, 6)
    for position, shards_of in cuts:
        draws = jnp.exp(jax.random.uniform(jax.random.fold_in(own, position), (shards_of,), jnp.float32, low / len(cuts), top_value / len(cuts)))
        level = level * jnp.repeat(draws, shape[position] // shards_of).reshape([-1 if axis == position else 1 for axis in range(len(shape))])
    return level


def bell_draw(key, shape, scale, most, pieces=(), kind=jnp.bfloat16):
    entries = jax.random.normal(key, shape, jnp.float32) * scale
    if len(pieces) > 0:
        entries = levels(key, shape, pieces, -0.22, 0.18) * entries
    return jnp.clip(entries, min=-most, max=most).astype(kind)


def setup_inputs(seed: int = 0) -> dict:
    key_of = jax.random.split(jax.random.key(seed), 17)
    return {
        "tokens": bell_draw(key_of[0], (TOKENS, D), 1.0, 6.0, ((0, 32),)),
        "timestep": with_ends(jax.random.randint(key_of[1], (SEQS,), 0, STEPS), jax.random.fold_in(key_of[1], 1), 0, STEPS - 1).astype(jnp.int32),
        "span_start": with_ends(jax.random.randint(key_of[2], (SEQS,), 0, SEQ // 2), jax.random.fold_in(key_of[2], 1), 0, (SEQ // 2) - 1).astype(jnp.int32),
        "span_length": with_ends(jax.random.randint(key_of[3], (SEQS,), 1, SEQ // 2 + 1), jax.random.fold_in(key_of[3], 1), 1, (SEQ // 2 + 1) - 1).astype(jnp.int32),
        "mask_embed": bell_draw(key_of[4], (D,), 1.0, 6.0, ((0, 4),)),
        "ada_weight": bell_draw(key_of[5], (TDIM, 6 * D), TDIM ** -0.5, 0.5, ((1, 4),)),
        "ada_bias": bell_draw(key_of[6], (6 * D,), 0.5, 3.0, ((0, 4),)),
        "norm_first": jnp.clip(1.0 + 0.18 * jax.random.normal(key_of[7], (D,), jnp.float32), 0.099609375, 1.8984375).astype(jnp.bfloat16),
        "query_key_value_weight": bell_draw(key_of[8], (D, 3 * D), D ** -0.5, 0.21875, ((0, 4),)),
        "output_weight": bell_draw(key_of[9], (D, D), (D // 32) ** -0.5, 1.25, ((0, 4),)),
        "norm_second": jnp.clip(1.0 + 0.18 * jax.random.normal(key_of[10], (D,), jnp.float32), 0.099609375, 1.8984375).astype(jnp.bfloat16),
        "up_projection_weight": bell_draw(key_of[11], (D, FF), D ** -0.5, 0.21875, ((0, 4),)),
        "up_projection_bias": bell_draw(key_of[12], (FF,), 0.5, 3.0, ((0, 4),)),
        "down_projection_weight": bell_draw(key_of[13], (FF, D), FF ** -0.5, 0.109375, ((0, 4),)),
        "down_projection_bias": bell_draw(key_of[14], (D,), 0.5, 3.0, ((0, 4),)),
        "cotangent": bell_draw(key_of[15], (TOKENS, D), 1.0, 6.0, ((0, 32),)),
    }


EPSILON = 1e-05
FULL_PRECISION = lax.Precision.HIGHEST

@jax.custom_vjp
def low(v):
    return lax.optimization_barrier(v.astype(jnp.bfloat16)).astype(jnp.float32)

@jax.custom_vjp
def reduced_backward(v):
    return v

def low_keep(v):
    return (low(v), None)

def low_pass(kept, grad):
    return (grad,)

def back_keep(v):
    return (v, None)

def back_low(kept, grad):
    return (low(grad),)
low.defvjp(low_keep, low_pass)
reduced_backward.defvjp(back_keep, back_low)

def time_features(step_ids, feature_count):
    halfway = feature_count // 2
    spacing = jnp.exp(-math.log(10000.0) * jnp.arange(halfway, dtype=jnp.float32) / halfway)
    angles = step_ids.astype(jnp.float32)[:, None] * spacing[None, :]
    wave_rows = jnp.concatenate([jnp.cos(angles), jnp.sin(angles)], axis=-1)
    return jax.nn.silu(wave_rows)

def rotary_tables(seq_length, head_width):
    halfway = head_width // 2
    spacing = jnp.exp(-math.log(10000.0) * jnp.arange(halfway, dtype=jnp.float32) / halfway)
    angles = jnp.arange(seq_length, dtype=jnp.float32)[:, None] * spacing[None, :]
    cosine = jnp.concatenate([jnp.cos(angles), jnp.cos(angles)], axis=-1)[:, None, :]
    sine_table = jnp.concatenate([jnp.sin(angles), jnp.sin(angles)], axis=-1)[:, None, :]
    return (cosine, sine_table)

def rotate(vectors, cosine, sine_table):
    halfway = vectors.shape[-1] // 2
    turned = jnp.concatenate([-vectors[..., halfway:], vectors[..., :halfway]], axis=-1)
    return vectors * cosine + turned * sine_table

def modulate(hidden, norm_gain, shift_vec, scale_vec):
    centre = hidden - lax.optimization_barrier(jnp.mean(hidden, axis=-1, keepdims=True))
    spread = lax.optimization_barrier(jnp.mean(centre * centre, axis=-1, keepdims=True))
    return centre * lax.rsqrt(spread + EPSILON) * norm_gain * (1.0 + scale_vec) + shift_vec

def span_mask(starts, lengths, seq_length):
    positions = jnp.arange(seq_length, dtype=jnp.int32)[None, :]
    return (positions >= starts[:, None]) & (positions < starts[:, None] + lengths[:, None])

def forward_block(params, hidden_in, step_ids, starts, lengths):
    mask_embed, ada_weight, ada_bias, norm_first, query_key_value_weight, output_weight, norm_second, up_projection_weight, up_projection_bias, down_projection_weight, down_projection_bias = params
    seq_count, seq_length, model_width = hidden_in.shape
    head_count = model_width // HEAD
    features = time_features(step_ids, ada_weight.shape[0])
    modulation = (jnp.dot(features, ada_weight, precision=FULL_PRECISION) + ada_bias).reshape(seq_count, 6, 1, model_width)
    masked = span_mask(starts, lengths, seq_length)
    start_rows = jnp.where(masked[:, :, None], mask_embed, hidden_in)
    first_normed = low(modulate(start_rows, norm_first, modulation[:, 0], modulation[:, 1]))
    projected_rows = reduced_backward(jnp.einsum('pum,mr->pur', first_normed, query_key_value_weight, precision=FULL_PRECISION))
    projected_rows = projected_rows.reshape(seq_count, seq_length, 3, head_count, HEAD)
    cosine, sine_table = rotary_tables(seq_length, HEAD)
    queries = low(rotate(projected_rows[:, :, 0], cosine, sine_table))
    keys_all = low(rotate(projected_rows[:, :, 1], cosine, sine_table))
    values_all = low(projected_rows[:, :, 2])
    factor = 1.0 / math.sqrt(HEAD)
    scores = reduced_backward(jnp.einsum('sqhd,skhd->shqk', queries, keys_all, precision=FULL_PRECISION) * factor)
    probs_low = low(jax.nn.softmax(scores, axis=-1))
    mixed_values = jnp.einsum('shqk,skhd->sqhd', probs_low, values_all, precision=FULL_PRECISION)
    mixed_values = low(reduced_backward(mixed_values.reshape(seq_count, seq_length, model_width)))
    attended_rows = reduced_backward(jnp.einsum('pum,mr->pur', mixed_values, output_weight, precision=FULL_PRECISION))
    middle = start_rows + modulation[:, 2] * attended_rows
    second_normed = low(modulate(middle, norm_second, modulation[:, 3], modulation[:, 4]))
    upper_hidden = reduced_backward(jnp.einsum('nyx,xa->nya', second_normed, up_projection_weight, precision=FULL_PRECISION) + up_projection_bias)
    active_units = low(jax.nn.gelu(upper_hidden, approximate=True))
    branch_output = reduced_backward(jnp.einsum('xkc,co->xko', active_units, down_projection_weight, precision=FULL_PRECISION) + down_projection_bias)
    return middle + modulation[:, 5] * branch_output

def reference(tokens, timestep, span_start, span_length, mask_embed, ada_weight, ada_bias, norm_first, query_key_value_weight, output_weight, norm_second, up_projection_weight, up_projection_bias, down_projection_weight, down_projection_bias, cotangent):
    params = tuple((weight.astype(jnp.float32) for weight in (mask_embed, ada_weight, ada_bias, norm_first, query_key_value_weight, output_weight, norm_second, up_projection_weight, up_projection_bias, down_projection_weight, down_projection_bias)))
    seq_count = timestep.shape[0]
    model_width = tokens.shape[1]
    seq_length = tokens.shape[0] // seq_count
    rows_in = tokens.astype(jnp.float32).reshape(seq_count, seq_length, model_width)
    cot_rows = cotangent.astype(jnp.float32).reshape(seq_count, seq_length, model_width)

    def one_sequence(running, operands):
        hidden_seq, cot_seq, step_id, start_id, length_id = operands

        def local_forward(weights, hidden):
            return forward_block(weights, hidden[None], step_id[None], start_id[None], length_id[None])[0]
        result, pullback = jax.vjp(local_forward, params, hidden_seq)
        grad_params, grad_hidden = pullback(cot_seq)
        running = tuple((accrued + portion for accrued, portion in zip(running, grad_params)))
        return (running, (result.astype(jnp.bfloat16), grad_hidden))
    initial = tuple((jnp.zeros_like(weight) for weight in params))
    totals, (results, grad_rows) = lax.scan(one_sequence, initial, (rows_in, cot_rows, timestep, span_start, span_length))
    return (results.reshape(-1, model_width), grad_rows.reshape(-1, model_width), totals[0], totals[1], totals[2], totals[3], totals[4], totals[5], totals[6], totals[7], totals[8], totals[9], totals[10])
```

```python
import math

import jax
import jax.numpy as jnp
from jax import lax
from jax.experimental import pallas as pl
from jax.experimental.pallas import tpu as pltpu
from jax.sharding import PartitionSpec as P

HEAD = 64
PAIR = 2 * HEAD
GROUPS = 3
EPSILON = 1e-05
FULL_PRECISION = lax.Precision.HIGHEST
F32 = jnp.float32
BF16 = jnp.bfloat16
SCALE = 1.0 / math.sqrt(HEAD)
SCALE2 = SCALE * math.log2(math.e)
VMEM_BYTES = 60 << 20
PLAIN = (((1,), (0,)), ((), ()))
TRANSPOSED = (((1,), (1,)), ((), ()))


def mxu(left, right, dims=PLAIN):
    return lax.dot_general(left, right, dims, preferred_element_type=F32)


def call(kernel, name, grid, in_specs, out_specs, out_shape, scratch, flops, moved, exps=0):
    return pl.pallas_call(
        kernel,
        name=name,
        grid=grid,
        in_specs=in_specs,
        out_specs=out_specs,
        out_shape=out_shape,
        scratch_shapes=scratch,
        compiler_params=pltpu.CompilerParams(vmem_limit_bytes=VMEM_BYTES),
        cost_estimate=pl.CostEstimate(flops=flops, bytes_accessed=moved, transcendentals=exps),
    )


def whole(shape):
    return pl.BlockSpec(shape, lambda *_: (0,) * len(shape), pipeline_mode=pl.Buffered(1))


def smem():
    return pl.BlockSpec(memory_space=pltpu.SMEM)


def time_features(step_ids, feature_count):
    halfway = feature_count // 2
    spacing = jnp.exp(-math.log(10000.0) * jnp.arange(halfway, dtype=F32) / halfway)
    angles = step_ids.astype(F32)[:, None] * spacing[None, :]
    return jax.nn.silu(jnp.concatenate([jnp.cos(angles), jnp.sin(angles)], axis=-1))


def rotary_tables(seq_length):
    halfway = HEAD // 2
    spacing = jnp.exp(-math.log(10000.0) * jnp.arange(halfway, dtype=F32) / halfway)
    angles = jnp.arange(seq_length, dtype=F32)[:, None] * spacing[None, :]
    cosine, sine = jnp.cos(angles), jnp.sin(angles)
    nothing = jnp.zeros_like(sine)
    cosines = jnp.concatenate([cosine] * 4, axis=-1)
    upper = jnp.concatenate([-sine, nothing] * 2, axis=-1)
    lower = jnp.concatenate([nothing, sine] * 2, axis=-1)
    return cosines, upper, lower


def from_ahead(v):
    return pltpu.roll(v, PAIR - HEAD // 2, 1)


def from_behind(v):
    return pltpu.roll(v, HEAD // 2, 1)


def masked_rows(tokens, embed, start, length, first_row):
    rows = tokens.shape[0]
    position = lax.broadcasted_iota(jnp.int32, (rows, 1), 0) + first_row
    inside = (position >= start) & (position < start + length)
    return jnp.where(inside, embed, tokens.astype(F32)), inside


def normalized(rows):
    centre = rows - jnp.mean(rows, axis=-1, keepdims=True)
    spread = jnp.mean(centre * centre, axis=-1, keepdims=True)
    inverse = lax.rsqrt(spread + EPSILON)
    return centre * inverse, inverse


def norm_back(d_out, hat, inverse):
    return inverse * (
        d_out
        - jnp.mean(d_out, axis=-1, keepdims=True)
        - hat * jnp.mean(d_out * hat, axis=-1, keepdims=True)
    )


def column_sum(v):
    return jnp.sum(v, axis=0, keepdims=True)


def project(tokens, span, embed, gain, modulation, weight, tables, seqs, block=512):
    rows, width = tokens.shape
    seq_length = rows // seqs
    block = min(block, seq_length)
    per_seq = seq_length // block
    pairs = width // PAIR

    def kernel(span_ref, tok, emb, gn, mod, w, cos, upp, low, out, nt):
        step = pl.program_id(0)
        seq = step // per_seq
        first = (step - seq * per_seq) * block
        start, _ = masked_rows(tok[...], emb[...], span_ref[0, seq], span_ref[1, seq], first)
        hat, _ = normalized(start)
        shift = mod[pl.ds(seq, 1), 0:width]
        scale = mod[pl.ds(seq, 1), width : 2 * width]
        normed = (hat * (gn[...] * (1.0 + scale)) + shift).astype(BF16)
        nt[...] = jnp.transpose(normed)
        acc = mxu(normed, w[...])
        for part in range(2 * pairs):
            v = acc[:, part * PAIR : (part + 1) * PAIR]
            v = v * cos[...] + from_ahead(v) * upp[...] + from_behind(v) * low[...]
            out[:, part * PAIR : (part + 1) * PAIR] = v.astype(BF16)
        out[:, 2 * width :] = acc[:, 2 * width :].astype(BF16)

    table = pl.BlockSpec((block, PAIR), lambda i: (lax.rem(i, per_seq), 0))
    return call(
        kernel,
        "project",
        (rows // block,),
        [
            smem(),
            pl.BlockSpec((block, width), lambda i: (i, 0)),
            whole((1, width)),
            whole((1, width)),
            whole(modulation.shape),
            whole(weight.shape),
            table,
            table,
            table,
        ],
        (
            pl.BlockSpec((block, 3 * width), lambda i: (i, 0)),
            pl.BlockSpec((width, block), lambda i: (0, i)),
        ),
        (
            jax.ShapeDtypeStruct((rows, 3 * width), BF16),
            jax.ShapeDtypeStruct((width, rows), BF16),
        ),
        [],
        2 * rows * width * 3 * width,
        rows * width * 10 + 6 * width * width,
    )(span, tokens, embed, gain, modulation, weight, *tables)


def head_mask(v, half):
    lane = lax.broadcasted_iota(jnp.int32, (1, PAIR), 1)
    keep = (lane < HEAD) if half == 0 else (lane >= HEAD)
    return jnp.where(keep, v, jnp.zeros_like(v))


def attend(qkv, seqs, block=512, per=3):
    rows, width = qkv.shape[0], qkv.shape[1] // 3
    seq_length = rows // seqs
    block = min(block, seq_length)
    pairs = width // PAIR
    count = seq_length // block
    steps = pairs // per
    items = per * count
    wide = per * PAIR

    def kernel(q_ref, k_ref, v_ref, out, total, v_turned, out_turned, held):
        v_turned[...] = jnp.transpose(v_ref[...])

        def place(i):
            pair = i // count
            part = i - pair * count
            return (
                pair,
                pl.ds(pl.multiple_of(pair * PAIR, PAIR), PAIR),
                pl.ds(pl.multiple_of(part * block, block), block),
            )

        def score(i, half):
            _, cols, part = place(i)
            held[half] = mxu(k_ref[:, cols], head_mask(q_ref[part, cols], half), TRANSPOSED)

        def finish(i, half):
            pair, _, part = place(i)
            scores = held[half]
            top = jnp.max(scores, axis=0, keepdims=True)
            exponent = jnp.exp2(scores * SCALE2 - top * SCALE2).astype(BF16)
            head = pl.ds(pl.multiple_of(pair * PAIR + half * HEAD, HEAD), HEAD)
            left = jnp.concatenate([v_turned[head, :], jnp.ones((16, seq_length), BF16)], axis=0)
            mixed = mxu(left, exponent)
            denominator = mixed[HEAD : HEAD + 1]
            out_turned[head, part] = mixed[:HEAD] * (1.0 / denominator)
            total[0, pair, half : half + 1, part] = top * SCALE2 + jnp.log2(denominator)

        score(0, 0)

        def body(i, carry):
            score(i, 1)
            finish(i, 0)
            score(jnp.minimum(i + 1, items - 1), 0)
            finish(i, 1)
            return carry

        lax.fori_loop(0, items, body, 0)
        out[...] = jnp.transpose(out_turned[...]).astype(BF16)

    def part_of(which):
        return pl.BlockSpec((seq_length, wide), lambda s, p: (s, which * steps + p))

    return call(
        kernel,
        "attend",
        (seqs, steps),
        [part_of(0), part_of(1), part_of(2)],
        (part_of(0), pl.BlockSpec((1, per, 2, seq_length), lambda s, p: (s, p, 0, 0))),
        (
            jax.ShapeDtypeStruct((rows, width), BF16),
            jax.ShapeDtypeStruct((seqs, pairs, 2, seq_length), F32),
        ),
        [
            pltpu.VMEM((wide, seq_length), BF16),
            pltpu.VMEM((wide, seq_length), F32),
            pltpu.VMEM((2, seq_length, block), F32),
        ],
        16 * rows * seq_length * width,
        rows * width * 8,
        rows * seq_length * width // HEAD,
    )(qkv, qkv, qkv)


def attend_back(qkv, mixture, d_mixture, total, tables, seqs, block=512, per=3):
    rows, width = mixture.shape
    seq_length = rows // seqs
    block = min(block, seq_length)
    pairs = width // PAIR
    count = seq_length // block
    steps = pairs // per
    items = per * count
    wide = per * PAIR

    def kernel(
        q_ref, k_ref, v_ref, mix, grad, tot, cos, upp, low, dq, dk, dv,
        k_turned, dq_turned, dk_sum, dv_sum, inner, s_held, p_held,
    ):
        k_turned[...] = jnp.transpose(k_ref[...])
        product = jnp.transpose(mix[...].astype(F32) * grad[...].astype(F32))
        for pair in range(per):
            for half in range(2):
                lower = pair * PAIR + half * HEAD
                inner[pair, half : half + 1, :] = column_sum(product[lower : lower + HEAD, :])
        dk_sum[...] = jnp.zeros_like(dk_sum)
        dv_sum[...] = jnp.zeros_like(dv_sum)

        def body(i, carry):
            pair = i // count
            part = i - pair * count
            cols = pl.ds(pl.multiple_of(pair * PAIR, PAIR), PAIR)
            part = pl.ds(pl.multiple_of(part * block, block), block)
            for half in range(2):
                head = pl.ds(pl.multiple_of(pair * PAIR + half * HEAD, HEAD), HEAD)
                query = head_mask(q_ref[part, cols], half)
                cot = head_mask(grad[part, cols], half)
                s_held[half] = mxu(k_ref[:, cols], query, TRANSPOSED)
                p_held[half] = mxu(v_ref[:, cols], cot, TRANSPOSED)
                probs = jnp.exp2(s_held[half] * SCALE2 - tot[0, pair, half : half + 1, part])
                d_scores = (probs * (p_held[half] - inner[pair, half : half + 1, part])).astype(BF16)
                dv_sum[:, cols] += mxu(probs.astype(BF16), cot)
                dk_sum[:, cols] += mxu(d_scores, query)
                dq_turned[head, part] = mxu(k_turned[head, :], d_scores)
            return carry

        lax.fori_loop(0, items, body, 0)
        d_queries = jnp.transpose(dq_turned[...])
        for source, target in ((d_queries, dq), (dk_sum, dk)):
            for pair in range(per):
                v = source[:, pair * PAIR : (pair + 1) * PAIR] * SCALE
                v = v * cos[...] - from_ahead(v) * upp[...] - from_behind(v) * low[...]
                target[:, pair * PAIR : (pair + 1) * PAIR] = v.astype(BF16)
        dv[...] = dv_sum[...].astype(BF16)

    def part_of(which):
        return pl.BlockSpec((seq_length, wide), lambda s, p: (s, which * steps + p))

    table = whole((seq_length, PAIR))
    grads = jax.ShapeDtypeStruct((rows, width), BF16)
    return call(
        kernel,
        "attend_back",
        (seqs, steps),
        [part_of(0), part_of(1), part_of(2), part_of(0), part_of(0)]
        + [pl.BlockSpec((1, per, 2, seq_length), lambda s, p: (s, p, 0, 0))]
        + [table] * 3,
        (part_of(0), part_of(0), part_of(0)),
        (grads, grads, grads),
        [
            pltpu.VMEM((wide, seq_length), BF16),
            pltpu.VMEM((wide, seq_length), F32),
            pltpu.VMEM((seq_length, wide), F32),
            pltpu.VMEM((seq_length, wide), F32),
            pltpu.VMEM((per, 2, seq_length), F32),
            pltpu.VMEM((2, seq_length, block), F32),
            pltpu.VMEM((2, seq_length, block), F32),
        ],
        40 * rows * seq_length * width,
        rows * width * 16,
        rows * seq_length * width // HEAD,
    )(qkv, qkv, qkv, mixture, d_mixture, total, *tables)


def middle_norm(mixture, tokens, span, embed, gain, modulation, weight, seqs, block=512):
    rows, width = tokens.shape
    seq_length = rows // seqs
    block = min(block, seq_length)
    per_seq = seq_length // block

    def kernel(span_ref, mix, tok, emb, gn, mod, w, out):
        step = pl.program_id(0)
        seq = step // per_seq
        first = (step - seq * per_seq) * block
        start, _ = masked_rows(tok[...], emb[...], span_ref[0, seq], span_ref[1, seq], first)
        middle = start + mod[pl.ds(seq, 1), 2 * width : 3 * width] * mxu(mix[...], w[...])
        hat, _ = normalized(middle)
        shift = mod[pl.ds(seq, 1), 3 * width : 4 * width]
        scale = mod[pl.ds(seq, 1), 4 * width : 5 * width]
        out[...] = (hat * (gn[...] * (1.0 + scale)) + shift).astype(BF16)

    row = pl.BlockSpec((block, width), lambda i: (i, 0))
    return call(
        kernel,
        "middle_norm",
        (rows // block,),
        [smem(), row, row, whole((1, width)), whole((1, width)), whole(modulation.shape)]
        + [whole(weight.shape)],
        row,
        jax.ShapeDtypeStruct((rows, width), BF16),
        [],
        2 * rows * width * width,
        rows * width * 6,
    )(span, mixture, tokens, embed, gain, modulation, weight)


def gelu_pair(v):
    root = math.sqrt(2.0 / math.pi)
    square = v * v
    bent = jnp.tanh(v * (root + (root * 0.044715) * square))
    near = 0.5 + 0.5 * bent
    slope = near + (0.5 * v) * (1.0 - bent * bent) * (root + (3.0 * root * 0.044715) * square)
    return v * near, slope


def hidden_units(normed, cot, modulation, up, up_bias, down, seqs, block=512, tile=256):
    rows, width = normed.shape
    units = up.shape[1]
    seq_length = rows // seqs
    block = min(block, seq_length)
    per_seq = seq_length // block
    steps = rows // block
    tiles = width // tile

    def kernel(nrm, g, mod, w_up, b_up, w_down, act, d_up, g_up, g_down, g_bias, b_down,
               n_turned, d_turned, a_held, u_held):
        step = pl.program_id(0)

        @pl.when(step == 0)
        def _():
            g_bias[...] = jnp.zeros_like(g_bias)
            b_down[...] = jnp.zeros_like(b_down)

        @pl.when(step < steps)
        def _():
            seq = step // per_seq
            part = pl.ds(pl.multiple_of(step * block, block), block)
            d_branch = (mod[pl.ds(seq, 1), 5 * width : 6 * width] * g[...].astype(F32)).astype(BF16)
            upper = mxu(nrm[...], w_up[...]) + b_up[...]
            active, slope = gelu_pair(upper)
            active = active.astype(BF16)
            d_upper = (mxu(d_branch, w_down[...], TRANSPOSED) * slope).astype(BF16)
            act[...] = active
            a_held[part, :] = active
            d_up[...] = d_upper
            u_held[part, :] = d_upper
            n_turned[:, part] = jnp.transpose(nrm[...])
            d_turned[:, part] = jnp.transpose(d_branch)
            g_bias[...] += column_sum(d_upper.astype(F32))
            b_down[...] += column_sum(d_branch.astype(F32))

        @pl.when(step >= steps)
        def _():
            part = pl.ds(pl.multiple_of((step - steps) * tile, tile), tile)
            g_up[...] = mxu(n_turned[part, :], u_held[...]).astype(BF16)
            g_down[...] = jnp.transpose(mxu(d_turned[part, :], a_held[...])).astype(BF16)

    def early(i):
        return (jnp.minimum(i, steps - 1), 0)

    def late(i):
        return jnp.maximum(i - steps, 0)

    return call(
        kernel,
        "hidden_units",
        (steps + tiles,),
        [
            pl.BlockSpec((block, width), early),
            pl.BlockSpec((block, width), early),
            whole(modulation.shape),
            whole(up.shape),
            whole(up_bias.shape),
            whole(down.shape),
        ],
        (
            pl.BlockSpec((block, units), early),
            pl.BlockSpec((block, units), early),
            pl.BlockSpec((tile, units), lambda i: (late(i), 0)),
            pl.BlockSpec((units, tile), lambda i: (0, late(i))),
            pl.BlockSpec((1, units), lambda i: (0, 0)),
            pl.BlockSpec((1, width), lambda i: (0, 0)),
        ),
        (
            jax.ShapeDtypeStruct((rows, units), BF16),
            jax.ShapeDtypeStruct((rows, units), BF16),
            jax.ShapeDtypeStruct((width, units), BF16),
            jax.ShapeDtypeStruct((units, width), BF16),
            jax.ShapeDtypeStruct((1, units), F32),
            jax.ShapeDtypeStruct((1, width), F32),
        ),
        [
            pltpu.VMEM((width, rows), BF16),
            pltpu.VMEM((width, rows), BF16),
            pltpu.VMEM((rows, units), BF16),
            pltpu.VMEM((rows, units), BF16),
        ],
        8 * rows * width * units,
        rows * (width * 4 + units * 4) + 8 * width * units,
        rows * units,
    )(normed, cot, modulation, up, up_bias, down)


def finish_block(
    mixture, tokens, cot, span, embed, gain, modulation, out_weight, down_bias,
    actives, d_uppers, ups, downs, seqs, block=256,
):
    rows, width = tokens.shape
    seq_length = rows // seqs
    block = min(block, seq_length)
    per_seq = seq_length // block
    groups = len(actives)
    units = actives[0].shape[1]

    def kernel(*refs):
        span_ref, mix, tok, g, emb, gn, mod, w_out, b_down = refs[:9]
        acts, d_ups = refs[9 : 9 + groups], refs[9 + groups : 9 + 2 * groups]
        w_ups = refs[9 + 2 * groups : 9 + 3 * groups]
        w_downs = refs[9 + 3 * groups : 9 + 4 * groups]
        block_out, d_middle_out, d_mix, g_out, sums, g_sum = refs[9 + 4 * groups :]
        step = pl.program_id(0)
        seq = step // per_seq
        first = (step - seq * per_seq) * block

        @pl.when(step == 0)
        def _():
            g_sum[...] = jnp.zeros_like(g_sum)

        @pl.when(step == seq * per_seq)
        def _():
            sums[...] = jnp.zeros_like(sums)

        def vector(which):
            return mod[pl.ds(seq, 1), which * width : (which + 1) * width]

        cotangent = g[...].astype(F32)
        attended = mxu(mix[...], w_out[...])
        start, _ = masked_rows(tok[...], emb[...], span_ref[0, seq], span_ref[1, seq], first)
        middle = start + vector(2) * attended
        hat, inverse = normalized(middle)
        branch = mxu(acts[0][...], w_downs[0][...])
        for group in range(1, groups):
            branch += mxu(acts[group][...], w_downs[group][...])
        branch += b_down[...]
        block_out[...] = (middle + vector(5) * branch).astype(BF16)
        d_normed = mxu(d_ups[0][...], w_ups[0][...], TRANSPOSED)
        for group in range(1, groups):
            d_normed += mxu(d_ups[group][...], w_ups[group][...], TRANSPOSED)
        d_middle = cotangent + norm_back(d_normed * (gn[...] * (1.0 + vector(4))), hat, inverse)
        d_middle_out[...] = d_middle
        d_attended = (vector(2) * d_middle).astype(BF16)
        d_mix[...] = mxu(d_attended, w_out[...], TRANSPOSED).astype(BF16)
        g_sum[...] += mxu(jnp.transpose(mix[...]), d_attended)
        sums[0, 0:1, :] += column_sum(cotangent * branch)
        sums[0, 1:2, :] += column_sum(d_normed)
        sums[0, 2:3, :] += column_sum(d_normed * hat)
        sums[0, 3:4, :] += column_sum(d_middle * attended)

        @pl.when(step == seqs * per_seq - 1)
        def _():
            g_out[...] = g_sum[...].astype(BF16)

    row = pl.BlockSpec((block, width), lambda i: (i, 0))
    unit_row = pl.BlockSpec((block, units), lambda i: (i, 0))
    return call(
        kernel,
        "finish_block",
        (rows // block,),
        [smem(), row, row, row, whole((1, width)), whole((1, width)), whole(modulation.shape)]
        + [whole(out_weight.shape), whole((1, width))]
        + [unit_row] * (2 * groups)
        + [whole(ups[0].shape)] * groups
        + [whole(downs[0].shape)] * groups,
        (
            row,
            row,
            row,
            pl.BlockSpec((width, width), lambda i: (0, 0)),
            pl.BlockSpec((1, 8, width), lambda i: (i // per_seq, 0, 0)),
        ),
        (
            jax.ShapeDtypeStruct((rows, width), BF16),
            jax.ShapeDtypeStruct((rows, width), F32),
            jax.ShapeDtypeStruct((rows, width), BF16),
            jax.ShapeDtypeStruct((width, width), BF16),
            jax.ShapeDtypeStruct((seqs, 8, width), F32),
        ),
        [pltpu.VMEM((width, width), F32)],
        rows * width * (4 * units * groups + 6 * width),
        rows * (width * 14 + units * groups * 4) + 4 * width * units * groups,
    )(
        span, mixture, tokens, cot, embed, gain, modulation, out_weight, down_bias,
        *actives, *d_uppers, *ups, *downs,
    )


def weight_grad(turned, grads, tile=256):
    width, rows = turned.shape
    count = len(grads)
    tiles = grads[0].shape[1] // tile

    def kernel(left, *refs):
        out = refs[count]
        which = pl.program_id(0) // tiles
        for part in range(count):

            @pl.when(which == part)
            def _():
                out[...] = mxu(left[...], refs[part][...]).astype(BF16)

    def column(part):
        return pl.BlockSpec(
            (rows, tile), lambda i: (0, jnp.clip(i - part * tiles, 0, tiles - 1))
        )

    return call(
        kernel,
        "weight_grad",
        (count * tiles,),
        [whole(turned.shape)] + [column(part) for part in range(count)],
        pl.BlockSpec((width, tile), lambda i: (0, i)),
        jax.ShapeDtypeStruct((width, count * tiles * tile), BF16),
        [],
        2 * rows * width * count * tiles * tile,
        2 * (rows * width * (count + 1) + count * width * width),
    )(turned, *grads)


def finish_start(tokens, d_middle, d_parts, span, embed, gain, modulation, weight, seqs, block=512):
    rows, width = tokens.shape
    seq_length = rows // seqs
    block = min(block, seq_length)
    per_seq = seq_length // block

    def kernel(span_ref, tok, d_mid, dq, dk, dv, emb, gn, mod, w, g_tok, sums):
        step = pl.program_id(0)
        seq = step // per_seq
        first = (step - seq * per_seq) * block

        @pl.when(step == seq * per_seq)
        def _():
            sums[...] = jnp.zeros_like(sums)

        start, inside = masked_rows(tok[...], emb[...], span_ref[0, seq], span_ref[1, seq], first)
        hat, inverse = normalized(start)
        d_normed = mxu(dq[...], w[:, 0:width], TRANSPOSED)
        d_normed += mxu(dk[...], w[:, width : 2 * width], TRANSPOSED)
        d_normed += mxu(dv[...], w[:, 2 * width :], TRANSPOSED)
        scale = mod[pl.ds(seq, 1), width : 2 * width]
        d_start = d_mid[...] + norm_back(d_normed * (gn[...] * (1.0 + scale)), hat, inverse)
        g_tok[...] = jnp.where(inside, 0.0, d_start)
        sums[0, 0:1, :] += column_sum(d_normed)
        sums[0, 1:2, :] += column_sum(d_normed * hat)
        sums[0, 2:3, :] += column_sum(jnp.where(inside, d_start, 0.0))

    row = pl.BlockSpec((block, width), lambda i: (i, 0))
    return call(
        kernel,
        "finish_start",
        (rows // block,),
        [smem(), row, row, row, row, row, whole((1, width)), whole((1, width))]
        + [whole(modulation.shape), whole(weight.shape)],
        (row, pl.BlockSpec((1, 8, width), lambda i: (i // per_seq, 0, 0))),
        (
            jax.ShapeDtypeStruct((rows, width), F32),
            jax.ShapeDtypeStruct((seqs, 8, width), F32),
        ),
        [],
        2 * rows * width * 3 * width,
        rows * width * 16,
    )(span, tokens, d_middle, *d_parts, embed, gain, modulation, weight)


def gather(v, axis=0):
    return lax.all_gather(v, "narrow", axis=axis, tiled=True)


def reduce_share(v):
    return lax.psum(lax.psum_scatter(v, "narrow", scatter_dimension=0, tiled=True), "wide")


def per_device(
    tokens,
    timestep,
    span_start,
    span_length,
    mask_embed,
    ada_weight,
    ada_bias,
    norm_first,
    query_key_value_weight,
    output_weight,
    norm_second,
    up_projection_weight,
    up_projection_bias,
    down_projection_weight,
    down_projection_bias,
    cotangent,
):
    seqs = timestep.shape[0]
    rows, width = tokens.shape
    seq_length = rows // seqs
    ways = lax.axis_size("narrow")
    share = width // ways
    unit_share = down_projection_weight.shape[0]
    part = unit_share // GROUPS
    units = ways * part

    small = jnp.concatenate(
        [mask_embed, ada_bias, norm_first, norm_second, up_projection_bias, down_projection_bias]
    )
    ada_columns = ada_weight.shape[1]
    filler = -small.shape[0] % ada_columns
    small = jnp.pad(small, (0, filler)).reshape(-1, ada_columns)
    packed = gather(jnp.concatenate([ada_weight, small])[None])
    w_qkv = gather(query_key_value_weight)
    w_out = gather(output_weight)
    up_parts = up_projection_weight.reshape(share, ways, GROUPS, part)
    ups = [gather(up_parts[:, :, group].reshape(share, units)) for group in range(GROUPS)]
    downs = [
        gather(down_projection_weight[group * part : (group + 1) * part]) for group in range(GROUPS)
    ]

    time_width = ada_weight.shape[0]
    ada_full = jnp.moveaxis(packed[:, :time_width], 0, 1).reshape(time_width, -1)
    rest = packed[:, time_width:].reshape(ways, -1)

    def small_part(lower, size):
        return rest[:, lower : lower + size].reshape(1, ways * size)

    spot = 0
    smalls = []
    for size in (share, ada_columns, share, share, unit_share, share):
        smalls.append(small_part(spot, size))
        spot += size
    embed, bias_ada, gain_one, gain_two, bias_up, bias_down = [v.astype(F32) for v in smalls]
    features = time_features(timestep, time_width)
    modulation = jnp.dot(features, ada_full.astype(F32), precision=FULL_PRECISION) + bias_ada
    span = jnp.stack([span_start, span_length])
    tables = rotary_tables(seq_length)

    qkv, turned_one = project(tokens, span, embed, gain_one, modulation, w_qkv, tables, seqs)
    mixture, total = attend(qkv, seqs)
    normed_two = middle_norm(mixture, tokens, span, embed, gain_two, modulation, w_out, seqs)
    bias_parts = bias_up.reshape(ways, GROUPS, part)
    actives, d_uppers, g_ups, g_downs, g_biases = [], [], [], [], []
    for group in range(GROUPS):
        active, d_upper, g_up, g_down, g_bias, g_bias_down = hidden_units(
            normed_two,
            cotangent,
            modulation,
            ups[group],
            bias_parts[:, group].reshape(1, units),
            downs[group],
            seqs,
        )
        actives.append(active)
        d_uppers.append(d_upper)
        g_ups.append(reduce_share(g_up))
        g_downs.append(reduce_share(g_down))
        g_biases.append(g_bias)
    block_out, d_middle, d_mixture, g_out, sums_two = finish_block(
        mixture, tokens, cotangent, span, embed, gain_two, modulation, w_out, bias_down,
        actives, d_uppers, ups, downs, seqs,
    )
    g_out = reduce_share(g_out)
    d_parts = attend_back(qkv, mixture, d_mixture, total, tables, seqs)
    g_qkv = reduce_share(weight_grad(turned_one, d_parts))
    grad_tokens, sums_one = finish_start(
        tokens, d_middle, d_parts, span, embed, gain_one, modulation, w_qkv, seqs
    )

    scale_one = modulation[:, width : 2 * width]
    scale_two = modulation[:, 4 * width : 5 * width]
    d_modulation = jnp.concatenate(
        [
            sums_one[:, 0],
            sums_one[:, 1] * gain_one,
            sums_two[:, 3],
            sums_two[:, 1],
            sums_two[:, 2] * gain_two,
            sums_two[:, 0],
        ],
        axis=1,
    )
    d_modulation = lax.all_to_all(
        d_modulation.reshape(seqs, ways, -1), "narrow", split_axis=1, concat_axis=0, tiled=True
    )[:, 0]
    d_modulation = lax.all_gather(d_modulation, "wide", axis=0, tiled=True)
    steps = lax.all_gather(timestep, ("wide", "narrow"), axis=0, tiled=True)
    grad_ada_weight = lax.dot_general(
        time_features(steps, time_width),
        d_modulation,
        (((0,), (0,)), ((), ())),
        precision=FULL_PRECISION,
    )
    grad_ada_bias = jnp.sum(d_modulation, axis=0)

    g_bias_up = jnp.stack(
        [v.reshape(ways, part) for v in g_biases], axis=1
    ).reshape(ways, unit_share)
    vectors = jnp.concatenate(
        [
            jnp.sum(sums_one[:, 2], axis=0).reshape(ways, share),
            jnp.sum(sums_one[:, 1] * (1.0 + scale_one), axis=0).reshape(ways, share),
            jnp.sum(sums_two[:, 2] * (1.0 + scale_two), axis=0).reshape(ways, share),
            g_bias_up,
            g_bias_down.reshape(ways, share),
        ],
        axis=1,
    )
    vectors = lax.psum(vectors, ("wide", "narrow"))
    own = lax.dynamic_slice_in_dim(vectors, lax.axis_index("narrow"), 1, 0)[0]
    grad_mask_embed = own[:share]
    grad_norm_first = own[share : 2 * share]
    grad_norm_second = own[2 * share : 3 * share]
    grad_up_bias = own[3 * share : 3 * share + unit_share]
    grad_down_bias = own[3 * share + unit_share :]

    grad_up = jnp.stack(
        [v.reshape(share, ways, part) for v in g_ups], axis=2
    ).reshape(share, ways * unit_share)
    grad_down = jnp.concatenate(g_downs)
    return (
        block_out,
        grad_tokens,
        grad_mask_embed,
        grad_ada_weight,
        grad_ada_bias,
        grad_norm_first,
        g_qkv.astype(F32),
        g_out.astype(F32),
        grad_norm_second,
        grad_up.astype(F32),
        grad_up_bias,
        grad_down.astype(F32),
        grad_down_bias,
    )


def solution(mesh):
    rows = P(("wide", "narrow"), None)
    per_seq = P(("wide", "narrow"))
    vector, matrix, columns = P("narrow"), P("narrow", None), P(None, "narrow")
    return jax.shard_map(
        per_device,
        mesh=mesh,
        in_specs=(
            rows, per_seq, per_seq, per_seq, vector, columns, vector, vector,
            matrix, matrix, vector, matrix, vector, matrix, vector, rows,
        ),
        out_specs=(
            rows, rows, vector, columns, vector, vector, matrix, matrix, vector, matrix,
            vector, matrix, vector,
        ),
        check_vma=False,
    )
```

```python
import math

import jax
import jax.numpy as jnp
from jax import lax
from jax.experimental import pallas as pl
from jax.experimental.pallas import tpu as pltpu
from jax.sharding import PartitionSpec as P

HEAD = 64
PAIR = 2 * HEAD
GROUPS = 3
EPSILON = 1e-05
FULL_PRECISION = lax.Precision.HIGHEST
F32 = jnp.float32
BF16 = jnp.bfloat16
SCALE = 1.0 / math.sqrt(HEAD)
SCALE2 = SCALE * math.log2(math.e)
VMEM_BYTES = 60 << 20
PLAIN = (((1,), (0,)), ((), ()))
TRANSPOSED = (((1,), (1,)), ((), ()))


def mxu(left, right, dims=PLAIN):
    return lax.dot_general(left, right, dims, preferred_element_type=F32)


def call(
    kernel, name, grid, in_specs, out_specs, out_shape, scratch, flops, moved, exps=0, ident=None
):
    return pl.pallas_call(
        kernel,
        name=name,
        grid=grid,
        in_specs=in_specs,
        out_specs=out_specs,
        out_shape=out_shape,
        scratch_shapes=scratch,
        compiler_params=pltpu.CompilerParams(
            vmem_limit_bytes=VMEM_BYTES, collective_id=ident, has_side_effects=ident is not None
        ),
        cost_estimate=pl.CostEstimate(flops=flops, bytes_accessed=moved, transcendentals=exps),
    )


def whole(shape):
    return pl.BlockSpec(shape, lambda *_: (0,) * len(shape), pipeline_mode=pl.Buffered(1))


def smem():
    return pl.BlockSpec(memory_space=pltpu.SMEM)


def time_features(step_ids, feature_count):
    halfway = feature_count // 2
    spacing = jnp.exp(-math.log(10000.0) * jnp.arange(halfway, dtype=F32) / halfway)
    angles = step_ids.astype(F32)[:, None] * spacing[None, :]
    return jax.nn.silu(jnp.concatenate([jnp.cos(angles), jnp.sin(angles)], axis=-1))


def rotary_tables(seq_length):
    halfway = HEAD // 2
    spacing = jnp.exp(-math.log(10000.0) * jnp.arange(halfway, dtype=F32) / halfway)
    angles = jnp.arange(seq_length, dtype=F32)[:, None] * spacing[None, :]
    cosine, sine = jnp.cos(angles), jnp.sin(angles)
    nothing = jnp.zeros_like(sine)
    cosines = jnp.concatenate([cosine] * 4, axis=-1)
    upper = jnp.concatenate([-sine, nothing] * 2, axis=-1)
    lower = jnp.concatenate([nothing, sine] * 2, axis=-1)
    return cosines, upper, lower


def from_ahead(v):
    return pltpu.roll(v, PAIR - HEAD // 2, 1)


def from_behind(v):
    return pltpu.roll(v, HEAD // 2, 1)


def masked_rows(tokens, embed, start, length, first_row):
    rows = tokens.shape[0]
    position = lax.broadcasted_iota(jnp.int32, (rows, 1), 0) + first_row
    inside = (position >= start) & (position < start + length)
    return jnp.where(inside, embed, tokens.astype(F32)), inside


def normalized(rows):
    centre = rows - jnp.mean(rows, axis=-1, keepdims=True)
    spread = jnp.mean(centre * centre, axis=-1, keepdims=True)
    inverse = lax.rsqrt(spread + EPSILON)
    return centre * inverse, inverse


def norm_back(d_out, hat, inverse):
    return inverse * (
        d_out
        - jnp.mean(d_out, axis=-1, keepdims=True)
        - hat * jnp.mean(d_out * hat, axis=-1, keepdims=True)
    )


def column_sum(v):
    return jnp.sum(v, axis=0, keepdims=True)


def store_shares(target, value, order_ref, cols):
    count = order_ref.shape[1]
    share = value.shape[0] // count
    for index in range(count):
        spot = pl.ds(pl.multiple_of(order_ref[1, index] * share, share), share)
        target[spot, cols] = value[index * share : (index + 1) * share, :]


def project(tokens, span, order, embed, gain, modulation, weights, tables, seqs, block=512):
    rows, width = tokens.shape
    seq_length = rows // seqs
    block = min(block, seq_length)
    per_seq = seq_length // block
    pairs = width // PAIR

    def kernel(span_ref, order_ref, tok, emb, gn, mod, w_q, w_k, w_v, cos, upp, low, out, nt):
        step = pl.program_id(0)
        seq = step // per_seq
        first = (step - seq * per_seq) * block
        start, _ = masked_rows(tok[...], emb[...], span_ref[0, seq], span_ref[1, seq], first)
        hat, _ = normalized(start)
        shift = mod[pl.ds(seq, 1), 0:width]
        scale = mod[pl.ds(seq, 1), width : 2 * width]
        normed = (hat * (gn[...] * (1.0 + scale)) + shift).astype(BF16)
        store_shares(nt, jnp.transpose(normed), order_ref, slice(None))
        for which, w in enumerate((w_q, w_k)):
            turned = mxu(normed, w[...])
            for part in range(pairs):
                v = turned[:, part * PAIR : (part + 1) * PAIR]
                v = v * cos[...] + from_ahead(v) * upp[...] + from_behind(v) * low[...]
                lower = which * width + part * PAIR
                out[:, lower : lower + PAIR] = v.astype(BF16)
        out[:, 2 * width :] = mxu(normed, w_v[...]).astype(BF16)

    table = pl.BlockSpec((block, PAIR), lambda i: (lax.rem(i, per_seq), 0))
    return call(
        kernel,
        "project",
        (rows // block,),
        [
            smem(),
            smem(),
            pl.BlockSpec((block, width), lambda i: (i, 0)),
            whole((1, width)),
            whole((1, width)),
            whole(modulation.shape),
            whole((width, width)),
            whole((width, width)),
            whole((width, width)),
            table,
            table,
            table,
        ],
        (
            pl.BlockSpec((block, 3 * width), lambda i: (i, 0)),
            pl.BlockSpec((width, block), lambda i: (0, i)),
        ),
        (
            jax.ShapeDtypeStruct((rows, 3 * width), BF16),
            jax.ShapeDtypeStruct((width, rows), BF16),
        ),
        [],
        2 * rows * width * 3 * width,
        rows * width * 10 + 6 * width * width,
    )(span, order, tokens, embed, gain, modulation, *weights, *tables)


def flip(index, stride):
    return index + stride * (1 - 2 * lax.rem(index // stride, 2))


def exchange_stages():
    count = lax.axis_size("wide")
    strides = [1 << bit for bit in range(1, count.bit_length() - 1)]
    return [("pair", "narrow", 1), ("chip", "narrow", 2), ("split", "wide", 1)] + [
        ("full", "wide", stride) for stride in strides
    ] + [("join", "wide", 1)]


class Steps:
    def in_specs(self):
        return [pl.BlockSpec(memory_space=pl.ANY)] * self.count

    out_specs = in_specs

    def locate(self):
        self.at = {axis: lax.axis_index(axis) for axis in ("wide", "narrow")}
        self.odd = lax.rem(self.at["wide"], 2)

    def half_of(self, rows, which, lower=0):
        side = self.odd if which == 0 else 1 - self.odd
        return pl.ds(pl.multiple_of(lower + side * (rows // 2), rows // 2), rows // 2)

    def greet(self):
        barrier = pltpu.get_barrier_semaphore()
        for axis, stride in self.partners:
            pl.semaphore_signal(
                barrier,
                inc=1,
                device_id={axis: flip(self.at[axis], stride)},
                device_id_type=pl.DeviceIdType.MESH,
            )
        pl.semaphore_wait(barrier, len(self.partners))

    def push(self, source, target, sent, got, axis, stride):
        return pltpu.make_async_remote_copy(
            src_ref=source,
            dst_ref=target,
            send_sem=sent,
            recv_sem=got,
            device_id={axis: flip(self.at[axis], stride)},
            device_id_type=pl.DeviceIdType.MESH,
        )

    def tick(self, now, last):
        planned = sorted(self.plan(), key=lambda item: item[:3])
        for when in sorted({item[0] for item in planned if item[0] < last}):

            @pl.when(now == when)
            def _(when=when):
                if when == 0:
                    self.greet()
                for item in planned:
                    if item[0] == when:
                        item[3]()

    def rest(self, last):
        for item in sorted(self.plan(), key=lambda item: item[:3]):
            if item[0] >= last:
                item[3]()


class Gather(Steps):
    partners = (("narrow", 1), ("narrow", 2), ("wide", 1))

    def __init__(self, shapes, begins, waits):
        self.shapes, self.begins, self.waits = shapes, begins, waits
        self.count = len(shapes)

    def out_shape(self):
        return [jax.ShapeDtypeStruct((4 * rows, cols), BF16) for rows, cols in self.shapes]

    def scratch(self):
        dma = pltpu.SemaphoreType.DMA
        return [dma((5,)), dma((5,)), dma((1,))] * self.count

    def bind(self, ins, outs, held):
        self.refs = [(ins[k], outs[k]) + tuple(held[3 * k : 3 * k + 3]) for k in range(self.count)]
        self.locate()

    def block(self, k, index, which=None):
        rows = self.shapes[k][0]
        if which is None:
            return pl.ds(pl.multiple_of(index * rows, rows), rows)
        return self.half_of(rows, which, index * rows)

    def remote(self, k, step):
        source, out, sent, got, _ = self.refs[k]
        me, across = self.at["narrow"], flip(self.at["narrow"], 2)
        axis, stride = (("narrow", 1), ("narrow", 2), ("wide", 1), ("narrow", 1), ("narrow", 1))[step]
        if step == 0:
            ends = (source, out.at[self.block(k, me), :])
        elif step == 1:
            half = self.half_of(self.shapes[k][0], 0)
            ends = (source.at[half, :], out.at[self.block(k, me, 0), :])
        else:
            spot = self.block(k, across, 1 if step == 4 else 0)
            ends = (out.at[spot, :], out.at[spot, :])
        return self.push(*ends, sent.at[step], got.at[step], axis, stride)

    def local(self, k):
        source, out, _, _, near = self.refs[k]
        return pltpu.make_async_copy(
            source, out.at[self.block(k, self.at["narrow"]), :], near.at[0]
        )

    def begin(self, k):
        self.remote(k, 1).start()
        self.remote(k, 0).start()
        self.local(k).start()

    def relay(self, k):
        self.remote(k, 1).wait()
        self.remote(k, 2).start()
        self.remote(k, 3).start()

    def share(self, k):
        self.remote(k, 2).wait()
        self.remote(k, 4).start()

    def close(self, k):
        self.remote(k, 0).wait()
        self.remote(k, 3).wait()
        self.remote(k, 4).wait()
        self.local(k).wait()

    def plan(self):
        planned = []
        for k in range(self.count):
            when = self.begins[k]
            planned.append((when, 0, k, lambda k=k: self.begin(k)))
            for wait, act in zip(self.waits, (self.relay, self.share, self.close)):
                when += wait
                planned.append((when, 1, k, lambda k=k, act=act: act(k)))
        return planned


class Exchange(Steps):
    def __init__(self, shapes, times):
        self.stages = exchange_stages()
        self.shapes = [shape[1:] for shape in shapes]
        self.times = times
        self.count = len(shapes)
        self.partners = sorted({(axis, stride) for _, axis, stride in self.stages})

    def out_shape(self):
        return [jax.ShapeDtypeStruct(shape, BF16) for shape in self.shapes]

    def scratch(self):
        held = []
        for rows, cols in self.shapes:
            held += [
                pltpu.VMEM((2, rows, cols), BF16),
                pltpu.VMEM((2, rows, cols), BF16),
                pltpu.VMEM((rows, cols), BF16),
                pltpu.VMEM((len(self.stages) - 3, rows // 2, cols), BF16),
                pltpu.VMEM((rows // 2, cols), BF16),
                pltpu.SemaphoreType.DMA((len(self.stages),)),
                pltpu.SemaphoreType.DMA((len(self.stages),)),
                pltpu.SemaphoreType.DMA((2,)),
            ]
        return held

    def bind(self, ins, outs, held):
        self.refs = [
            (ins[k], outs[k]) + tuple(held[8 * k : 8 * k + 8]) for k in range(self.count)
        ]
        self.locate()

    def remote(self, k, step):
        source, out, pair, kept, chip, halves, mine, sent, got, _ = self.refs[k]
        kind, axis, stride = self.stages[step]
        rows = self.shapes[k][0]
        if kind == "pair":
            ends = (source.at[0:2], pair)
        elif kind == "chip":
            ends = (kept.at[0], chip)
        elif kind == "split":
            ends = (kept.at[1, self.half_of(rows, 1), :], halves.at[0])
        elif kind == "full":
            ends = (mine, halves.at[step - 2])
        else:
            ends = (mine, out.at[self.half_of(rows, 0), :])
        return self.push(*ends, sent.at[step], got.at[step], axis, stride)

    def local(self, k, which):
        source, out, _, kept, _, _, mine, _, _, near = self.refs[k]
        if which == 0:
            return pltpu.make_async_copy(source.at[2:4], kept, near.at[0])
        half = self.half_of(self.shapes[k][0], 0)
        return pltpu.make_async_copy(mine, out.at[half, :], near.at[1])

    def start(self, k, step):
        self.remote(k, step).start()
        if step == 0:
            self.local(k, 0).start()
        if step == len(self.stages) - 1:
            self.local(k, 1).start()

    def end(self, k, step):
        _, _, pair, kept, chip, halves, mine, _, _, _ = self.refs[k]
        kind = self.stages[step][0]
        self.remote(k, step).wait()
        if kind == "pair":
            self.local(k, 0).wait()
            kept[...] = (kept[...].astype(F32) + pair[...].astype(F32)).astype(BF16)
        elif kind == "chip":
            kept[1] = (kept[1].astype(F32) + chip[...].astype(F32)).astype(BF16)
        elif kind == "split":
            own = self.half_of(self.shapes[k][0], 0)
            mine[...] = (kept[1, own, :].astype(F32) + halves[0].astype(F32)).astype(BF16)
        elif kind == "full":
            mine[...] = (mine[...].astype(F32) + halves[step - 2].astype(F32)).astype(BF16)
        else:
            self.local(k, 1).wait()
        if step + 1 < len(self.stages):
            self.start(k, step + 1)

    def plan(self):
        planned = []
        last = len(self.stages) - 1
        for k, (begin, *ends) in enumerate(self.times):
            planned.append((begin, 0, k, lambda k=k: self.start(k, 0)))
            for step in range(last + 1):
                when = ends[-1] if step == last else ends[min(step, 4)]
                planned.append((when, 1, k, lambda k=k, step=step: self.end(k, step)))
        return planned


def paced(begins, waits):
    return [[begin + sum(waits[:count]) for count in range(len(waits) + 1)] for begin in begins]


def head_mask(v, half):
    lane = lax.broadcasted_iota(jnp.int32, (1, PAIR), 1)
    keep = (lane < HEAD) if half == 0 else (lane >= HEAD)
    return jnp.where(keep, v, jnp.zeros_like(v))


def attend(qkv, shares, begins, waits, ident, seqs, block=512, per=3):
    rows, width = qkv.shape[0], qkv.shape[1] // 3
    seq_length = rows // seqs
    block = min(block, seq_length)
    pairs = width // PAIR
    count = seq_length // block
    steps = pairs // per
    items = per * count
    wide = per * PAIR

    gathering = Gather([v.shape for v in shares], begins, waits)
    many = len(shares)
    ticks = seqs * steps * items

    def kernel(*refs):
        q_ref, k_ref, v_ref = refs[:3]
        out, total = refs[3 + many : 5 + many]
        v_turned, out_turned, held = refs[5 + 2 * many : 8 + 2 * many]
        gathering.bind(refs[3 : 3 + many], refs[5 + many : 5 + 2 * many], refs[8 + 2 * many :])
        spot = pl.program_id(0) * steps + pl.program_id(1)
        v_turned[...] = jnp.transpose(v_ref[...])

        def place(i):
            pair = i // count
            part = i - pair * count
            return (
                pair,
                pl.ds(pl.multiple_of(pair * PAIR, PAIR), PAIR),
                pl.ds(pl.multiple_of(part * block, block), block),
            )

        def score(i, half):
            _, cols, part = place(i)
            held[half] = mxu(k_ref[:, cols], head_mask(q_ref[part, cols], half), TRANSPOSED)

        def finish(i, half):
            pair, _, part = place(i)
            scores = held[half]
            top = jnp.max(scores, axis=0, keepdims=True)
            exponent = jnp.exp2(scores * SCALE2 - top * SCALE2).astype(BF16)
            head = pl.ds(pl.multiple_of(pair * PAIR + half * HEAD, HEAD), HEAD)
            left = jnp.concatenate([v_turned[head, :], jnp.ones((16, seq_length), BF16)], axis=0)
            mixed = mxu(left, exponent)
            denominator = mixed[HEAD : HEAD + 1]
            out_turned[head, part] = mixed[:HEAD] * (1.0 / denominator)
            total[0, pair, half : half + 1, part] = top * SCALE2 + jnp.log2(denominator)

        score(0, 0)

        def body(i, carry):
            gathering.tick(spot * items + i, ticks)
            score(i, 1)
            finish(i, 0)
            score(jnp.minimum(i + 1, items - 1), 0)
            finish(i, 1)
            return carry

        lax.fori_loop(0, items, body, 0)
        out[...] = jnp.transpose(out_turned[...]).astype(BF16)

        @pl.when(spot == seqs * steps - 1)
        def _():
            gathering.rest(ticks)

    def part_of(which):
        return pl.BlockSpec((seq_length, wide), lambda s, p: (s, which * steps + p))

    return call(
        kernel,
        "attend",
        (seqs, steps),
        [part_of(0), part_of(1), part_of(2)] + gathering.in_specs(),
        [part_of(0), pl.BlockSpec((1, per, 2, seq_length), lambda s, p: (s, p, 0, 0))]
        + gathering.out_specs(),
        [
            jax.ShapeDtypeStruct((rows, width), BF16),
            jax.ShapeDtypeStruct((seqs, pairs, 2, seq_length), F32),
        ]
        + gathering.out_shape(),
        [
            pltpu.VMEM((wide, seq_length), BF16),
            pltpu.VMEM((wide, seq_length), F32),
            pltpu.VMEM((2, seq_length, block), F32),
        ]
        + gathering.scratch(),
        16 * rows * seq_length * width,
        rows * width * 8,
        rows * seq_length * width // HEAD,
        ident,
    )(qkv, qkv, qkv, *shares)


def attend_back(
    qkv, mixture, d_mixture, total, tables, pieces, times, ident, seqs, block=512, per=3
):
    rows, width = mixture.shape
    seq_length = rows // seqs
    block = min(block, seq_length)
    pairs = width // PAIR
    count = seq_length // block
    steps = pairs // per
    items = per * count
    wide = per * PAIR
    exchange = Exchange([v.shape for v in pieces], times)
    many = len(pieces)
    ticks = seqs * steps * items

    def kernel(*refs):
        q_ref, k_ref, v_ref, mix, grad, tot, cos, upp, low = refs[:9]
        dq, dk, dv = refs[9 + many : 12 + many]
        k_turned, dq_turned, dk_sum, dv_sum, inner, s_held, p_held = refs[
            12 + 2 * many : 19 + 2 * many
        ]
        exchange.bind(refs[9 : 9 + many], refs[12 + many : 12 + 2 * many], refs[19 + 2 * many :])
        spot = pl.program_id(0) * steps + pl.program_id(1)
        k_turned[...] = jnp.transpose(k_ref[...])
        product = jnp.transpose(mix[...].astype(F32) * grad[...].astype(F32))
        for pair in range(per):
            for half in range(2):
                lower = pair * PAIR + half * HEAD
                inner[pair, half : half + 1, :] = column_sum(product[lower : lower + HEAD, :])
        dk_sum[...] = jnp.zeros_like(dk_sum)
        dv_sum[...] = jnp.zeros_like(dv_sum)

        def body(i, carry):
            exchange.tick(spot * items + i, ticks)
            pair = i // count
            part = i - pair * count
            cols = pl.ds(pl.multiple_of(pair * PAIR, PAIR), PAIR)
            part = pl.ds(pl.multiple_of(part * block, block), block)
            for half in range(2):
                head = pl.ds(pl.multiple_of(pair * PAIR + half * HEAD, HEAD), HEAD)
                query = head_mask(q_ref[part, cols], half)
                cot = head_mask(grad[part, cols], half)
                s_held[half] = mxu(k_ref[:, cols], query, TRANSPOSED)
                p_held[half] = mxu(v_ref[:, cols], cot, TRANSPOSED)
                probs = jnp.exp2(s_held[half] * SCALE2 - tot[0, pair, half : half + 1, part])
                d_scores = (probs * (p_held[half] - inner[pair, half : half + 1, part])).astype(BF16)
                dv_sum[:, cols] += mxu(probs.astype(BF16), cot)
                dk_sum[:, cols] += mxu(d_scores, query)
                dq_turned[head, part] = mxu(k_turned[head, :], d_scores)
            return carry

        lax.fori_loop(0, items, body, 0)
        d_queries = jnp.transpose(dq_turned[...])
        for source, target in ((d_queries, dq), (dk_sum, dk)):
            for pair in range(per):
                v = source[:, pair * PAIR : (pair + 1) * PAIR] * SCALE
                v = v * cos[...] - from_ahead(v) * upp[...] - from_behind(v) * low[...]
                target[:, pair * PAIR : (pair + 1) * PAIR] = v.astype(BF16)
        dv[...] = dv_sum[...].astype(BF16)

        @pl.when(spot == seqs * steps - 1)
        def _():
            exchange.rest(ticks)

    def part_of(which):
        return pl.BlockSpec((seq_length, wide), lambda s, p: (s, which * steps + p))

    table = whole((seq_length, PAIR))
    grads = jax.ShapeDtypeStruct((rows, width), BF16)
    return call(
        kernel,
        "attend_back",
        (seqs, steps),
        [part_of(0), part_of(1), part_of(2), part_of(0), part_of(0)]
        + [pl.BlockSpec((1, per, 2, seq_length), lambda s, p: (s, p, 0, 0))]
        + [table] * 3
        + exchange.in_specs(),
        [part_of(0), part_of(0), part_of(0)] + exchange.out_specs(),
        [grads, grads, grads] + exchange.out_shape(),
        [
            pltpu.VMEM((wide, seq_length), BF16),
            pltpu.VMEM((wide, seq_length), F32),
            pltpu.VMEM((seq_length, wide), F32),
            pltpu.VMEM((seq_length, wide), F32),
            pltpu.VMEM((per, 2, seq_length), F32),
            pltpu.VMEM((2, seq_length, block), F32),
            pltpu.VMEM((2, seq_length, block), F32),
        ]
        + exchange.scratch(),
        40 * rows * seq_length * width,
        rows * width * 16,
        rows * seq_length * width // HEAD,
        ident,
    )(qkv, qkv, qkv, mixture, d_mixture, total, *tables, *pieces)


def middle_norm(mixture, tokens, span, embed, gain, modulation, weight, seqs, block=512):
    rows, width = tokens.shape
    seq_length = rows // seqs
    block = min(block, seq_length)
    per_seq = seq_length // block

    def kernel(span_ref, mix, tok, emb, gn, mod, w, out):
        step = pl.program_id(0)
        seq = step // per_seq
        first = (step - seq * per_seq) * block
        start, _ = masked_rows(tok[...], emb[...], span_ref[0, seq], span_ref[1, seq], first)
        middle = start + mod[pl.ds(seq, 1), 2 * width : 3 * width] * mxu(mix[...], w[...])
        hat, _ = normalized(middle)
        shift = mod[pl.ds(seq, 1), 3 * width : 4 * width]
        scale = mod[pl.ds(seq, 1), 4 * width : 5 * width]
        out[...] = (hat * (gn[...] * (1.0 + scale)) + shift).astype(BF16)

    row = pl.BlockSpec((block, width), lambda i: (i, 0))
    return call(
        kernel,
        "middle_norm",
        (rows // block,),
        [smem(), row, row, whole((1, width)), whole((1, width)), whole(modulation.shape)]
        + [whole(weight.shape)],
        row,
        jax.ShapeDtypeStruct((rows, width), BF16),
        [],
        2 * rows * width * width,
        rows * width * 6,
    )(span, mixture, tokens, embed, gain, modulation, weight)


def gelu_pair(v):
    root = math.sqrt(2.0 / math.pi)
    square = v * v
    bent = jnp.tanh(v * (root + (root * 0.044715) * square))
    near = 0.5 + 0.5 * bent
    slope = near + (0.5 * v) * (1.0 - bent * bent) * (root + (3.0 * root * 0.044715) * square)
    return v * near, slope


def hidden_units(normed, cot, order, modulation, up, up_bias, down, seqs, block=512):
    rows, width = normed.shape
    units = up.shape[1]
    ways = order.shape[1]
    share, part_units = width // ways, units // ways
    seq_length = rows // seqs
    block = min(block, seq_length)
    per_seq = seq_length // block
    steps = rows // block

    def kernel(order_ref, nrm, g, mod, w_up, b_up, w_down, act, d_up, g_up, g_down, g_bias, d_gate,
               g_sum, n_turned, g_turned, a_held, u_held):
        step = pl.program_id(0)

        @pl.when(step == 0)
        def _():
            g_bias[...] = jnp.zeros_like(g_bias)
            d_gate[...] = jnp.zeros_like(d_gate)
            g_sum[...] = jnp.zeros_like(g_sum)

        @pl.when(step < steps)
        def _():
            seq = step // per_seq
            part = pl.ds(pl.multiple_of(step * block, block), block)
            cotangent = g[...].astype(F32)
            d_branch = (mod[pl.ds(seq, 1), 5 * width : 6 * width] * cotangent).astype(BF16)
            upper = mxu(nrm[...], w_up[...]) + b_up[...]
            active, slope = gelu_pair(upper)
            active = active.astype(BF16)
            d_upper = (mxu(d_branch, w_down[...], TRANSPOSED) * slope).astype(BF16)
            act[...] = active
            a_held[part, :] = active
            d_up[...] = d_upper
            u_held[part, :] = d_upper
            store_shares(n_turned, jnp.transpose(nrm[...]), order_ref, part)
            g_turned[:, part] = jnp.transpose(g[...])
            g_bias[...] += column_sum(d_upper.astype(F32))
            g_sum[pl.ds(seq, 1), :] += column_sum(cotangent)

        @pl.when(step >= steps)
        def _():
            spot = (step - steps) * part_units
            cols = pl.ds(pl.multiple_of(spot, part_units), part_units)
            g_up[...] = mxu(n_turned[...], u_held[:, cols]).astype(BF16).reshape(g_up.shape)
            own = w_down[cols, :].astype(F32)
            total = jnp.zeros((part_units, width), F32)
            for seq in range(seqs):
                lower, upper = seq * seq_length, (seq + 1) * seq_length
                product = mxu(g_turned[:, lower:upper], a_held[lower:upper, cols])
                product = jnp.transpose(product)
                total += product * mod[seq : seq + 1, 5 * width : 6 * width]
                d_gate[seq : seq + 1, :] += column_sum(product * own)
            g_down[0] = total.astype(BF16)

    def early(i, *_):
        return (jnp.minimum(i, steps - 1), 0)

    def late(i):
        return jnp.maximum(i - steps, 0)

    def fixed(shape):
        return pl.BlockSpec(shape, lambda *_: (0,) * len(shape))

    return pl.pallas_call(
        kernel,
        name="hidden_units",
        grid_spec=pltpu.PrefetchScalarGridSpec(
            num_scalar_prefetch=1,
            grid=(steps + ways,),
            in_specs=[
                pl.BlockSpec((block, width), early),
                pl.BlockSpec((block, width), early),
                whole(modulation.shape),
                whole(up.shape),
                whole(up_bias.shape),
                whole(down.shape),
            ],
            out_specs=(
                pl.BlockSpec((block, units), early),
                pl.BlockSpec((block, units), early),
                pl.BlockSpec((ways, share, part_units), lambda i, _: (0, 0, late(i))),
                pl.BlockSpec((1, part_units, width), lambda i, o: (o[1, late(i)], 0, 0)),
                fixed((1, units)),
                fixed((seqs, width)),
                fixed((seqs, width)),
            ),
            scratch_shapes=[
                pltpu.VMEM((width, rows), BF16),
                pltpu.VMEM((width, rows), BF16),
                pltpu.VMEM((rows, units), BF16),
                pltpu.VMEM((rows, units), BF16),
            ],
        ),
        out_shape=(
            jax.ShapeDtypeStruct((rows, units), BF16),
            jax.ShapeDtypeStruct((rows, units), BF16),
            jax.ShapeDtypeStruct((ways, share, units), BF16),
            jax.ShapeDtypeStruct((ways, part_units, width), BF16),
            jax.ShapeDtypeStruct((1, units), F32),
            jax.ShapeDtypeStruct((seqs, width), F32),
            jax.ShapeDtypeStruct((seqs, width), F32),
        ),
        compiler_params=pltpu.CompilerParams(vmem_limit_bytes=VMEM_BYTES),
        cost_estimate=pl.CostEstimate(
            flops=8 * rows * width * units,
            bytes_accessed=rows * (width * 4 + units * 4) + 8 * width * units,
            transcendentals=rows * units,
        ),
    )(order, normed, cot, modulation, up, up_bias, down)


def middle_back(
    mixture, tokens, cot, span, embed, gain, modulation, out_weight, d_uppers, ups, pieces, times,
    ident, seqs, ways, block=256,
):
    rows, width = tokens.shape
    seq_length = rows // seqs
    block = min(block, seq_length)
    per_seq = seq_length // block
    steps = rows // block
    groups = len(d_uppers)
    units = d_uppers[0].shape[1]
    share = width // ways
    exchange = Exchange([v.shape for v in pieces], times)
    many = len(pieces)

    def kernel(*refs):
        span_ref, mix, tok, g, emb, gn, mod, w_out = refs[:8]
        d_ups, w_ups = refs[8 : 8 + groups], refs[8 + groups : 8 + 2 * groups]
        spot = 8 + 2 * groups
        ins, spot = refs[spot : spot + many], spot + many
        d_middle_out, d_mix, g_out, sums = refs[spot : spot + 4]
        outs, spot = refs[spot + 4 : spot + 4 + many], spot + 4 + many
        g_sum = refs[spot]
        exchange.bind(ins, outs, refs[spot + 1 :])
        step = pl.program_id(0)
        seq = step // per_seq
        first = (step - seq * per_seq) * block
        exchange.tick(step, steps)

        @pl.when(step == 0)
        def _():
            g_sum[...] = jnp.zeros_like(g_sum)

        @pl.when(step == seq * per_seq)
        def _():
            sums[...] = jnp.zeros_like(sums)

        def vector(which):
            return mod[pl.ds(seq, 1), which * width : (which + 1) * width]

        attended = mxu(mix[...], w_out[...])
        start, _ = masked_rows(tok[...], emb[...], span_ref[0, seq], span_ref[1, seq], first)
        hat, inverse = normalized(start + vector(2) * attended)
        d_normed = mxu(d_ups[0][...], w_ups[0][...], TRANSPOSED)
        for group in range(1, groups):
            d_normed += mxu(d_ups[group][...], w_ups[group][...], TRANSPOSED)
        d_middle = g[...].astype(F32) + norm_back(
            d_normed * (gn[...] * (1.0 + vector(4))), hat, inverse
        )
        d_middle_out[...] = d_middle
        d_attended = (vector(2) * d_middle).astype(BF16)
        d_mix[...] = mxu(d_attended, w_out[...], TRANSPOSED).astype(BF16)
        g_sum[...] += mxu(jnp.transpose(mix[...]), d_attended)
        sums[0, 0:1, :] += column_sum(d_normed)
        sums[0, 1:2, :] += column_sum(d_normed * hat)
        sums[0, 2:3, :] += column_sum(d_middle * attended)

        @pl.when(step == steps - 1)
        def _():
            me = exchange.at["narrow"]
            for position, owner in enumerate((flip(flip(me, 1), 2), flip(me, 1), flip(me, 2), me)):
                spot = pl.ds(pl.multiple_of(owner * share, share), share)
                g_out[position] = g_sum[spot, :].astype(BF16)
            exchange.rest(steps)

    row = pl.BlockSpec((block, width), lambda i: (i, 0))
    unit_row = pl.BlockSpec((block, units), lambda i: (i, 0))
    return call(
        kernel,
        "middle_back",
        (steps,),
        [smem(), row, row, row, whole((1, width)), whole((1, width)), whole(modulation.shape)]
        + [whole(out_weight.shape)]
        + [unit_row] * groups
        + [whole(ups[0].shape)] * groups
        + exchange.in_specs(),
        [
            row,
            row,
            pl.BlockSpec((ways, share, width), lambda i: (0, 0, 0)),
            pl.BlockSpec((1, 8, width), lambda i: (i // per_seq, 0, 0)),
        ]
        + exchange.out_specs(),
        [
            jax.ShapeDtypeStruct((rows, width), F32),
            jax.ShapeDtypeStruct((rows, width), BF16),
            jax.ShapeDtypeStruct((ways, share, width), BF16),
            jax.ShapeDtypeStruct((seqs, 8, width), F32),
        ]
        + exchange.out_shape(),
        [pltpu.VMEM((width, width), F32)] + exchange.scratch(),
        rows * width * (2 * units * groups + 6 * width),
        rows * (width * 12 + units * groups * 2) + 2 * width * units * groups,
        0,
        ident,
    )(
        span, mixture, tokens, cot, embed, gain, modulation, out_weight, *d_uppers, *ups, *pieces
    )


class Finale(Steps):
    def __init__(self, ways):
        self.ways = ways
        self.wide = lax.axis_size("wide")

    def scratch(self, columns):
        dma = pltpu.SemaphoreType.DMA
        return [
            pltpu.VMEM((self.ways, 8, columns), F32),
            pltpu.VMEM((self.ways, 8, columns), F32),
            pltpu.VMEM((self.wide, 8, columns), F32),
            dma((self.ways,)),
            dma((self.ways,)),
            dma((self.wide,)),
            dma((self.wide,)),
        ]

    def bind(self, held):
        self.parts, self.narrow_got, self.wide_got, *self.sems = held
        self.locate()

    def others(self):
        targets = []
        for offset in range(1, self.ways):
            targets.append({"narrow": lax.rem(self.at["narrow"] + offset, self.ways)})
        for offset in range(1, self.wide):
            targets.append({"wide": lax.rem(self.at["wide"] + offset, self.wide)})
        return targets

    def greet(self):
        barrier = pltpu.get_barrier_semaphore()
        targets = self.others()
        for target in targets:
            pl.semaphore_signal(
                barrier, inc=1, device_id=target, device_id_type=pl.DeviceIdType.MESH
            )
        pl.semaphore_wait(barrier, len(targets))

    def along_narrow(self, offset):
        target = lax.rem(self.at["narrow"] + offset, self.ways)
        return pltpu.make_async_remote_copy(
            src_ref=self.parts.at[target],
            dst_ref=self.narrow_got.at[self.at["narrow"]],
            send_sem=self.sems[0].at[offset],
            recv_sem=self.sems[1].at[offset],
            device_id={"narrow": target},
            device_id_type=pl.DeviceIdType.MESH,
        )

    def along_wide(self, offset):
        me = self.at["wide"]
        return pltpu.make_async_remote_copy(
            src_ref=self.wide_got.at[me],
            dst_ref=self.wide_got.at[me],
            send_sem=self.sems[2].at[offset],
            recv_sem=self.sems[3].at[offset],
            device_id={"wide": lax.rem(me + offset, self.wide)},
            device_id_type=pl.DeviceIdType.MESH,
        )

    def begin(self):
        for offset in range(1, self.ways):
            self.along_narrow(offset).start()
        me = self.at["narrow"]
        self.narrow_got[pl.ds(me, 1)] = self.parts[pl.ds(me, 1)]

    def spread(self, seqs, row_lanes):
        for offset in range(1, self.ways):
            self.along_narrow(offset).wait()
        me = self.at["wide"]
        for way in range(self.ways):
            self.wide_got[pl.ds(me, 1), way * seqs : (way + 1) * seqs, 0:row_lanes] = (
                self.narrow_got[way : way + 1, 0:seqs, 0:row_lanes]
            )
        total = self.narrow_got[0:1, :, row_lanes:]
        for way in range(1, self.ways):
            total += self.narrow_got[way : way + 1, :, row_lanes:]
        self.wide_got[pl.ds(me, 1), :, row_lanes:] = total
        for offset in range(1, self.wide):
            self.along_wide(offset).start()

    def close(self):
        for offset in range(1, self.wide):
            self.along_wide(offset).wait()


def finish(
    turned, d_parts, tokens, cot, d_middle, mixture, span, embed, gain, modulation, weights,
    out_weight, down_bias, actives, downs, features, rows_two, vectors_two, times, ident, seqs,
    tile=256, block=512, late_block=256,
):
    rows, width = tokens.shape
    ways = lax.axis_size("narrow")
    share = width // ways
    seq_length = rows // seqs
    block, late_block = min(block, seq_length), min(late_block, seq_length)
    per_seq, late_per_seq = seq_length // block, seq_length // late_block
    tiles = width // tile
    columns, group_units = modulation.shape[1] // ways, actives[0].shape[1]
    groups = len(actives)
    time_width = features.shape[1]
    window = 2 * PAIR
    lanes = columns + time_width + window
    early, middle, late = 3 * tiles, rows // block, rows // late_block
    steps = early + middle + late
    exchange = Exchange([(ways, share, width)] * 3, times)
    finale = Finale(ways)

    def kernel(*refs):
        (
            span_ref, left, c_q, c_k, c_v, tok, d_mid, r_q, r_k, r_v, emb, gn, mod, w_q, w_k, w_v,
            tok_late, mix, w_out, b_down, feat, two, vec,
        ) = refs[:23]
        acts, w_downs = refs[23 : 23 + groups], refs[23 + groups : 23 + 2 * groups]
        spot = 23 + 2 * groups
        g_tok, block_out, g_ada, g_ada_bias, g_vec = refs[spot : spot + 5]
        outs = refs[spot + 5 : spot + 8]
        grads, sums = refs[spot + 8 : spot + 10]
        small = 7
        exchange.bind(
            [grads.at[part] for part in range(3)], outs, refs[spot + 10 + small :]
        )
        finale.bind(refs[spot + 10 : spot + 10 + small])
        step = pl.program_id(0)

        @pl.when(step == 0)
        def _():
            finale.greet()
            sums[...] = jnp.zeros_like(sums)

        exchange.tick(step, steps)

        for part, source in enumerate((c_q, c_k, c_v)):

            @pl.when((step >= part * tiles) & (step < (part + 1) * tiles))
            def _(part=part, source=source):
                cols = pl.ds(pl.multiple_of((step - part * tiles) * tile, tile), tile)
                product = mxu(left[...], source[...]).astype(BF16)
                grads[part, :, :, cols] = product.reshape(ways, share, tile)

        @pl.when((step >= early) & (step < early + middle))
        def _():
            at = step - early
            seq = at // per_seq
            first = (at - seq * per_seq) * block
            start, inside = masked_rows(
                tok[...], emb[...], span_ref[0, seq], span_ref[1, seq], first
            )
            hat, inverse = normalized(start)
            d_normed = mxu(r_q[...], w_q[...], TRANSPOSED)
            d_normed += mxu(r_k[...], w_k[...], TRANSPOSED)
            d_normed += mxu(r_v[...], w_v[...], TRANSPOSED)
            scale = mod[pl.ds(seq, 1), width : 2 * width]
            d_start = d_mid[...] + norm_back(d_normed * (gn[...] * (1.0 + scale)), hat, inverse)
            g_tok[...] = jnp.where(inside, 0.0, d_start)
            sums[seq, 0:1, :] += column_sum(d_normed)
            sums[seq, 1:2, :] += column_sum(d_normed * hat)
            sums[seq, 2:3, :] += column_sum(jnp.where(inside, d_start, 0.0))

        @pl.when(step == early + middle)
        def _():
            parts = finale.parts
            embed_sum = jnp.zeros((1, width), F32)
            gain_sum = jnp.zeros((1, width), F32)
            for seq in range(seqs):
                shift, scale = sums[seq, 0:1, :], sums[seq, 1:2, :]
                gain_sum += scale * (1.0 + mod[seq : seq + 1, width : 2 * width])
                embed_sum += sums[seq, 2:3, :]
                row = jnp.concatenate([shift, scale * gn[...], two[seq : seq + 1, :]], axis=1)
                for way in range(ways):
                    parts[way, seq : seq + 1, 0:columns] = row[
                        :, way * columns : (way + 1) * columns
                    ]
            for way in range(ways):
                parts[way, 0:seqs, columns : columns + time_width] = feat[...]
                lower = PAIR * (share * way // PAIR)
                parts[way, 0:1, columns + time_width :] = embed_sum[:, lower : lower + window]
                parts[way, 1:2, columns + time_width :] = gain_sum[:, lower : lower + window]
                parts[way, 2:8, columns + time_width :] = vec[way, 2:8, :]
            finale.begin()

        @pl.when(step == early + middle + 2)
        def _():
            finale.spread(seqs, columns + time_width)

        @pl.when(step >= early + middle)
        def _():
            at = step - early - middle
            seq = at // late_per_seq
            first = (at - seq * late_per_seq) * late_block
            start, _ = masked_rows(
                tok_late[...], emb[...], span_ref[0, seq], span_ref[1, seq], first
            )
            attended = mxu(mix[...], w_out[...])
            branch = mxu(acts[0][...], w_downs[0][...])
            for group in range(1, groups):
                branch += mxu(acts[group][...], w_downs[group][...])
            branch += b_down[...]
            hidden = start + mod[pl.ds(seq, 1), 2 * width : 3 * width] * attended
            block_out[...] = (
                hidden + mod[pl.ds(seq, 1), 5 * width : 6 * width] * branch
            ).astype(BF16)

        @pl.when(step == steps - 1)
        def _():
            finale.close()
            got = finale.wide_got
            every = got[...].reshape(finale.wide * 8, lanes)
            d_mods, feats = every[:, 0:columns], every[:, columns : columns + time_width]
            g_ada[...] = lax.dot_general(
                jnp.transpose(feats), d_mods, PLAIN, precision=FULL_PRECISION,
                preferred_element_type=F32,
            )
            g_ada_bias[...] = column_sum(d_mods)
            total = got[0, :, columns + time_width :]
            for index in range(1, finale.wide):
                total += got[index, :, columns + time_width :]
            g_vec[...] = total
            exchange.rest(steps)

    def column(part):
        return pl.BlockSpec((rows, tile), lambda i: (0, jnp.clip(i - part * tiles, 0, tiles - 1)))

    row = pl.BlockSpec((block, width), lambda i: (jnp.clip(i - early, 0, middle - 1), 0))

    def late_row(wide):
        return pl.BlockSpec(
            (late_block, wide), lambda i: (jnp.maximum(i - early - middle, 0), 0)
        )

    def fixed(shape):
        return pl.BlockSpec(shape, lambda i: (0,) * len(shape))

    return call(
        kernel,
        "finish",
        (steps,),
        [smem(), whole(turned.shape), column(0), column(1), column(2), row, row, row, row, row]
        + [whole((1, width)), whole((1, width)), whole(modulation.shape)]
        + [whole((width, width))] * 3
        + [late_row(width), late_row(width), whole((width, width)), whole((1, width))]
        + [whole(features.shape), whole(rows_two.shape), whole(vectors_two.shape)]
        + [late_row(group_units)] * groups
        + [whole((group_units, width))] * groups,
        [
            row,
            late_row(width),
            fixed((time_width, columns)),
            fixed((1, columns)),
            fixed((8, window)),
        ]
        + exchange.out_specs(),
        [
            jax.ShapeDtypeStruct((rows, width), F32),
            jax.ShapeDtypeStruct((rows, width), BF16),
            jax.ShapeDtypeStruct((time_width, columns), F32),
            jax.ShapeDtypeStruct((1, columns), F32),
            jax.ShapeDtypeStruct((8, window), F32),
        ]
        + exchange.out_shape(),
        [pltpu.VMEM((3, ways, share, width), BF16), pltpu.VMEM((seqs, 8, width), F32)]
        + finale.scratch(lanes)
        + exchange.scratch(),
        2 * rows * width * (7 * width + group_units * groups),
        rows * (width * 24 + 2 * group_units * groups),
        0,
        ident,
    )(
        span, turned, *d_parts, tokens, d_middle, *d_parts, embed, gain, modulation, *weights,
        tokens, mixture, out_weight, down_bias, features, rows_two, vectors_two, *actives, *downs,
    )


def gather_first(small, ada, weight, ident):
    share, wide = weight.shape
    width = wide // 3
    shapes = [small.shape, ada.shape] + [(share, width)] * 3
    gathering = Gather(shapes, [0] * 5, [0] * 3)

    def kernel(*refs):
        ins = [refs[0], refs[1]] + [refs[2].at[:, k * width : (k + 1) * width] for k in range(3)]
        gathering.bind(ins, refs[3:8], refs[8:])
        gathering.greet()
        gathering.begin(0)
        gathering.begin(1)
        gathering.begin(2)
        for k in range(5):
            gathering.relay(k)
            if k + 3 < 5:
                gathering.begin(k + 3)
            if k > 0:
                gathering.share(k - 1)
        gathering.share(4)
        for k in range(5):
            gathering.close(k)

    return call(
        kernel,
        "gather_first",
        (),
        [pl.BlockSpec(memory_space=pl.ANY)] * 3,
        gathering.out_specs(),
        gathering.out_shape(),
        gathering.scratch(),
        0,
        8 * share * wide,
        0,
        ident,
    )(small, ada, weight)


def per_device(
    tokens,
    timestep,
    span_start,
    span_length,
    mask_embed,
    ada_weight,
    ada_bias,
    norm_first,
    query_key_value_weight,
    output_weight,
    norm_second,
    up_projection_weight,
    up_projection_bias,
    down_projection_weight,
    down_projection_bias,
    cotangent,
):
    seqs = timestep.shape[0]
    rows, width = tokens.shape
    seq_length = rows // seqs
    ways = lax.axis_size("narrow")
    me = lax.axis_index("narrow")
    share = width // ways
    unit_share = down_projection_weight.shape[0]
    part = unit_share // GROUPS
    units = ways * part
    time_width, columns = ada_weight.shape

    vectors = (
        ada_bias, mask_embed, norm_first, norm_second, down_projection_bias, up_projection_bias,
    )
    small = jnp.stack([jnp.pad(v, (0, columns - v.shape[0])) for v in vectors])
    small = jnp.pad(small, ((0, 32 - len(vectors)), (0, 0)))
    small, ada, w_q, w_k, w_v = gather_first(small, ada_weight, query_key_value_weight, 0)
    up_parts = up_projection_weight.reshape(share, ways, GROUPS, part)
    shares = [output_weight]
    for group in range(GROUPS):
        shares.append(up_parts[:, :, group].reshape(share, units))
        shares.append(down_projection_weight[group * part : (group + 1) * part])

    small = small.reshape(ways, 32, columns)[:, : len(vectors)].astype(F32)
    bias_ada, embed, gain_one, gain_two, bias_down, bias_up = [
        small[:, index, : v.shape[0]].reshape(1, -1) for index, v in enumerate(vectors)
    ]
    ada = jnp.moveaxis(ada.reshape(ways, time_width, columns), 0, 1).reshape(time_width, -1)
    features = time_features(timestep, time_width)
    modulation = jnp.dot(features, ada.astype(F32), precision=FULL_PRECISION) + bias_ada
    span = jnp.stack([span_start, span_length])
    tables = rotary_tables(seq_length)
    places = jnp.arange(ways)
    order = jnp.stack(
        [
            me ^ (2 * (1 - places % 2) + (1 - places // 2)),
            2 * (1 - (me ^ places) % 2) + (1 - (me ^ places) // 2),
        ]
    ).astype(jnp.int32)

    qkv, turned_one = project(
        tokens, span, order, embed, gain_one, modulation, (w_q, w_k, w_v), tables, seqs
    )
    mixture, total, w_out, *rest = attend(
        qkv, shares, [0, 1, 4, 7, 10, 13, 16], [4, 4, 3], 1, seqs
    )
    ups, downs = rest[0::2], rest[1::2]
    normed_two = middle_norm(mixture, tokens, span, embed, gain_two, modulation, w_out, seqs)
    bias_parts = bias_up.reshape(ways, GROUPS, part)
    actives, d_uppers, pieces, g_biases, d_gate_two = [], [], [], [], 0.0
    for group in range(GROUPS):
        active, d_upper, g_up, g_down, g_bias, d_gate, g_sum = hidden_units(
            normed_two,
            cotangent,
            order,
            modulation,
            ups[group],
            bias_parts[:, group].reshape(1, units),
            downs[group],
            seqs,
        )
        actives.append(active)
        d_uppers.append(d_upper)
        pieces += [g_up, g_down]
        g_biases.append(g_bias)
        d_gate_two += d_gate
    d_gate_two += bias_down * g_sum
    d_middle, d_mixture, g_out, sums_two, *done_first = middle_back(
        mixture, tokens, cotangent, span, embed, gain_two, modulation, w_out, d_uppers, ups,
        pieces[:2], paced([0, 1], [1, 2, 1, 1, 2, 1]), 2, seqs, ways,
    )
    d_q, d_k, d_v, *done_second = attend_back(
        qkv, mixture, d_mixture, total, tables, pieces[2:] + [g_out],
        paced([0, 2, 4, 6, 8], [1, 5, 3, 3, 5, 3]), 3, seqs,
    )
    scale_two = modulation[:, 4 * width : 5 * width]
    rows_two = jnp.concatenate(
        [sums_two[:, 2], sums_two[:, 0], sums_two[:, 1] * gain_two, d_gate_two], axis=1
    )
    g_norm_two = jnp.sum(sums_two[:, 1] * (1.0 + scale_two), axis=0)
    g_bias_down = jnp.sum(modulation[:, 5 * width :] * g_sum, axis=0)
    lowers = [PAIR * (share * way // PAIR) for way in range(ways)]
    vectors_two = jnp.stack(
        [
            jnp.stack([v[lower : lower + 2 * PAIR] for lower in lowers])
            for v in (g_norm_two, g_norm_two, g_norm_two, g_bias_down)
        ]
        + [v.reshape(ways, part) for v in g_biases]
        + [jnp.zeros((ways, 2 * PAIR), F32)],
        axis=1,
    )
    grad_tokens, block_out, grad_ada_weight, grad_ada_bias, vectors, *g_qkv = finish(
        turned_one, (d_q, d_k, d_v), tokens, cotangent, d_middle, mixture, span, embed, gain_one,
        modulation, (w_q, w_k, w_v), w_out, bias_down, actives, downs, features, rows_two,
        vectors_two,
        [[3, 5, 11, 12, 13, 16, 18], [6, 8, 12, 13, 15, 18, 20], [9, 10, 14, 16, 18, 20, 21]],
        4, seqs,
    )
    skip = lax.rem(share * me, PAIR)
    own = lax.dynamic_slice_in_dim(vectors[:4], skip, share, 1)
    g_ups, g_downs = zip(*[done_first] + [done_second[2 * k : 2 * k + 2] for k in range(2)])
    grad_up = jnp.stack([v.reshape(share, ways, part) for v in g_ups], axis=2)
    return (
        block_out,
        grad_tokens,
        own[0],
        grad_ada_weight,
        grad_ada_bias[0],
        own[1],
        jnp.concatenate(g_qkv, axis=1).astype(F32),
        done_second[4].astype(F32),
        own[2],
        grad_up.reshape(share, ways * unit_share).astype(F32),
        vectors[4 : 4 + GROUPS].reshape(-1),
        jnp.concatenate(g_downs).astype(F32),
        own[3],
    )


def solution(mesh):
    rows = P(("wide", "narrow"), None)
    per_seq = P(("wide", "narrow"))
    vector, matrix, columns = P("narrow"), P("narrow", None), P(None, "narrow")
    return jax.shard_map(
        per_device,
        mesh=mesh,
        in_specs=(
            rows, per_seq, per_seq, per_seq, vector, columns, vector, vector,
            matrix, matrix, vector, matrix, vector, matrix, vector, rows,
        ),
        out_specs=(
            rows, rows, vector, columns, vector, vector, matrix, matrix, vector, matrix,
            vector, matrix, vector,
        ),
        check_vma=False,
    )
```

```python
import math

import jax
import jax.numpy as jnp
import numpy as np
from jax import lax
from jax.experimental import pallas as pl
from jax.experimental.pallas import tpu as pltpu
from jax.sharding import PartitionSpec as P

HEAD = 64
PAIR = 2 * HEAD
GROUPS = 3
EPSILON = 1e-05
FULL_PRECISION = lax.Precision.HIGHEST
F32 = jnp.float32
BF16 = jnp.bfloat16
SCALE = 1.0 / math.sqrt(HEAD)
SCALE2 = SCALE * math.log2(math.e)
VMEM_BYTES = 60 << 20
PLAIN = (((1,), (0,)), ((), ()))
TRANSPOSED = (((1,), (1,)), ((), ()))


def mxu(left, right, dims=PLAIN):
    return lax.dot_general(left, right, dims, preferred_element_type=F32)


def call(
    kernel, name, grid, in_specs, out_specs, out_shape, scratch, flops, moved, exps=0, ident=None
):
    return pl.pallas_call(
        kernel,
        name=name,
        grid=grid,
        in_specs=in_specs,
        out_specs=out_specs,
        out_shape=out_shape,
        scratch_shapes=scratch,
        compiler_params=pltpu.CompilerParams(
            vmem_limit_bytes=VMEM_BYTES, collective_id=ident, has_side_effects=ident is not None
        ),
        cost_estimate=pl.CostEstimate(flops=flops, bytes_accessed=moved, transcendentals=exps),
    )


def whole(shape):
    return pl.BlockSpec(shape, lambda *_: (0,) * len(shape), pipeline_mode=pl.Buffered(1))


def column_third(which, width):
    return pl.BlockSpec((width, width), lambda *_: (0, which), pipeline_mode=pl.Buffered(1))


def smem():
    return pl.BlockSpec(memory_space=pltpu.SMEM)


def time_features(step_ids, feature_count):
    halfway = feature_count // 2
    spacing = jnp.exp(-math.log(10000.0) * jnp.arange(halfway, dtype=F32) / halfway)
    angles = step_ids.astype(F32)[:, None] * spacing[None, :]
    return jax.nn.silu(jnp.concatenate([jnp.cos(angles), jnp.sin(angles)], axis=-1))


def rotary_tables(seq_length):
    halfway = HEAD // 2
    spacing = np.exp(-math.log(10000.0) * np.arange(halfway, dtype=np.float32) / halfway)
    angles = np.arange(seq_length, dtype=np.float32)[:, None] * spacing.astype(np.float32)
    cosine, sine = np.cos(angles), np.sin(angles)
    signed = np.concatenate([-sine, sine] * 2, axis=-1)
    return np.concatenate([cosine] * 4, axis=-1), signed


def partner_lanes(v):
    lane = lax.broadcasted_iota(jnp.int32, (1, PAIR), 1)
    return jnp.where(lax.rem(lane, HEAD) < HEAD // 2, from_ahead(v), from_behind(v))


def from_ahead(v):
    return pltpu.roll(v, PAIR - HEAD // 2, 1)


def from_behind(v):
    return pltpu.roll(v, HEAD // 2, 1)


def masked_rows(tokens, embed, start, length, first_row):
    rows = tokens.shape[0]
    position = lax.broadcasted_iota(jnp.int32, (rows, 1), 0) + first_row
    inside = (position >= start) & (position < start + length)
    return jnp.where(inside, embed, tokens.astype(F32)), inside


def normalized(rows):
    centre = rows - jnp.mean(rows, axis=-1, keepdims=True)
    spread = jnp.mean(centre * centre, axis=-1, keepdims=True)
    inverse = lax.rsqrt(spread + EPSILON)
    return centre * inverse, inverse


def norm_back(d_out, hat, inverse):
    return inverse * (
        d_out
        - jnp.mean(d_out, axis=-1, keepdims=True)
        - hat * jnp.mean(d_out * hat, axis=-1, keepdims=True)
    )


def column_sum(v):
    return jnp.sum(v, axis=0, keepdims=True)


def store_shares(target, value, cols):
    me, ways = lax.axis_index("narrow"), lax.axis_size("narrow")
    share = value.shape[0] // ways
    for place in range(ways):
        lower = pl.multiple_of(place_of(me, place) * share, share)
        target[pl.ds(lower, share), cols] = value[place * share : (place + 1) * share, :]


def place_of(me, other):
    core = lax.rem(me + other, 2)
    chip = lax.rem(me // 2 + other // 2, 2)
    return 2 * (1 - core) + 1 - chip


def owner_at(me, place):
    core, chip = 1 - place // 2, 1 - lax.rem(place, 2)
    return 2 * lax.rem(me // 2 + chip, 2) + lax.rem(me + core, 2)


def project(tokens, starts, lengths, embed, gain, modulation, weight, tables, seqs, block=512):
    rows, width = tokens.shape
    seq_length = rows // seqs
    block = min(block, seq_length)
    per_seq = seq_length // block
    pairs = width // PAIR

    def kernel(starts, lengths, tok, emb, gn, mod, w_q, w_k, w_v, cos, sin, out, nt):
        step = pl.program_id(0)
        seq = step // per_seq
        first = (step - seq * per_seq) * block
        start, _ = masked_rows(tok[...], emb[...], starts[seq], lengths[seq], first)
        hat, _ = normalized(start)
        shift = mod[pl.ds(seq, 1), 0:width]
        scale = mod[pl.ds(seq, 1), width : 2 * width]
        normed = (hat * (gn[...] * (1.0 + scale)) + shift).astype(BF16)
        store_shares(nt, jnp.transpose(normed), slice(None))
        for which, w in enumerate((w_q, w_k)):
            turned = mxu(normed, w[...])
            for part in range(pairs):
                v = turned[:, part * PAIR : (part + 1) * PAIR]
                v = v * cos[...] + partner_lanes(v) * sin[...]
                lower = which * width + part * PAIR
                out[:, lower : lower + PAIR] = v.astype(BF16)
        out[:, 2 * width :] = mxu(normed, w_v[...]).astype(BF16)

    table = pl.BlockSpec((block, PAIR), lambda i: (lax.rem(i, per_seq), 0))
    return call(
        kernel,
        "project",
        (rows // block,),
        [
            smem(),
            smem(),
            pl.BlockSpec((block, width), lambda i: (i, 0)),
            whole((1, width)),
            whole((1, width)),
            whole(modulation.shape),
            column_third(0, width),
            column_third(1, width),
            column_third(2, width),
            table,
            table,
        ],
        (
            pl.BlockSpec((block, 3 * width), lambda i: (i, 0)),
            pl.BlockSpec((width, block), lambda i: (0, i)),
        ),
        (
            jax.ShapeDtypeStruct((rows, 3 * width), BF16),
            jax.ShapeDtypeStruct((width, rows), BF16),
        ),
        [],
        2 * rows * width * 3 * width,
        rows * width * 10 + 6 * width * width,
    )(starts, lengths, tokens, embed, gain, modulation, weight, weight, weight, *tables)


def flip(index, stride):
    return index + stride * (1 - 2 * lax.rem(index // stride, 2))


def exchange_stages():
    count = lax.axis_size("wide")
    strides = [1 << bit for bit in range(1, count.bit_length() - 1)]
    return [("pair", "narrow", 1), ("chip", "narrow", 2), ("split", "wide", 1)] + [
        ("full", "wide", stride) for stride in strides
    ] + [("join", "wide", 1)]


class Steps:
    def in_specs(self):
        return [pl.BlockSpec(memory_space=pl.ANY)] * self.count

    out_specs = in_specs

    def locate(self):
        self.at = {axis: lax.axis_index(axis) for axis in ("wide", "narrow")}
        self.odd = lax.rem(self.at["wide"], 2)

    def half_of(self, rows, which, lower=0):
        side = self.odd if which == 0 else 1 - self.odd
        return pl.ds(pl.multiple_of(lower + side * (rows // 2), rows // 2), rows // 2)

    def greet(self):
        barrier = pltpu.get_barrier_semaphore()
        for axis, stride in self.partners:
            pl.semaphore_signal(
                barrier,
                inc=1,
                device_id={axis: flip(self.at[axis], stride)},
                device_id_type=pl.DeviceIdType.MESH,
            )
        pl.semaphore_wait(barrier, len(self.partners))

    def push(self, source, target, sent, got, axis, stride):
        return pltpu.make_async_remote_copy(
            src_ref=source,
            dst_ref=target,
            send_sem=sent,
            recv_sem=got,
            device_id={axis: flip(self.at[axis], stride)},
            device_id_type=pl.DeviceIdType.MESH,
        )

    def tick(self, now, last):
        planned = sorted(self.plan(), key=lambda item: item[:3])
        for when in sorted({item[0] for item in planned if item[0] < last}):

            @pl.when(now == when)
            def _(when=when):
                if when == 0:
                    self.greet()
                for item in planned:
                    if item[0] == when:
                        item[3]()

    def rest(self, last):
        for item in sorted(self.plan(), key=lambda item: item[:3]):
            if item[0] >= last:
                item[3]()


class Gather(Steps):
    partners = (("narrow", 1), ("narrow", 2), ("wide", 1))

    def __init__(self, shapes, begins, waits, columns=None):
        columns = columns or [(k, 0, shape[1]) for k, shape in enumerate(shapes)]
        self.arrays, self.columns = shapes, columns
        self.shapes = [(shapes[k][0], upper - lower) for k, lower, upper in columns]
        self.begins, self.waits = begins, waits
        self.count = len(columns)

    def in_specs(self):
        return [pl.BlockSpec(memory_space=pl.ANY)] * len(self.arrays)

    out_specs = in_specs

    def out_shape(self):
        return [jax.ShapeDtypeStruct((4 * rows, cols), BF16) for rows, cols in self.arrays]

    def scratch(self):
        dma, held = pltpu.SemaphoreType.DMA, []
        for shape in self.shapes:
            held += [dma((5,)), dma((5,)), dma((2,)), pltpu.VMEM(shape, BF16)]
        return held

    def bind(self, ins, outs, held):
        self.refs = [
            (ins[k].at[:, lower:upper], outs[k].at[:, lower:upper])
            + tuple(held[4 * part : 4 * part + 4])
            for part, (k, lower, upper) in enumerate(self.columns)
        ]
        self.locate()

    def block(self, k, index, which=None):
        rows = self.shapes[k][0]
        if which is None:
            return pl.ds(pl.multiple_of(index * rows, rows), rows)
        return self.half_of(rows, which, index * rows)

    def remote(self, k, step):
        source, out, sent, got, _, _ = self.refs[k]
        me, across = self.at["narrow"], flip(self.at["narrow"], 2)
        axis, stride = (("narrow", 1), ("narrow", 2), ("wide", 1), ("narrow", 1), ("narrow", 1))[step]
        if step == 0:
            ends = (source, out.at[self.block(k, me), :])
        elif step == 1:
            half = self.half_of(self.shapes[k][0], 0)
            ends = (source.at[half, :], out.at[self.block(k, me, 0), :])
        else:
            spot = self.block(k, across, 1 if step == 4 else 0)
            ends = (out.at[spot, :], out.at[spot, :])
        return self.push(*ends, sent.at[step], got.at[step], axis, stride)

    def local(self, k, which):
        source, out, _, _, near, kept = self.refs[k]
        if which == 0:
            return pltpu.make_async_copy(source, kept, near.at[0])
        return pltpu.make_async_copy(
            kept, out.at[self.block(k, self.at["narrow"]), :], near.at[1]
        )

    def begin(self, k):
        self.remote(k, 1).start()
        self.remote(k, 0).start()
        self.local(k, 0).start()

    def relay(self, k):
        self.local(k, 0).wait()
        self.local(k, 1).start()
        self.remote(k, 1).wait()
        self.remote(k, 2).start()
        self.remote(k, 3).start()

    def share(self, k):
        self.remote(k, 2).wait()
        self.remote(k, 4).start()

    def close(self, k):
        self.remote(k, 0).wait()
        self.remote(k, 3).wait()
        self.remote(k, 4).wait()
        self.local(k, 1).wait()

    def plan(self):
        planned = []
        for k in range(self.count):
            when = self.begins[k]
            planned.append((when, 0, k, lambda k=k: self.begin(k)))
            for wait, act in zip(self.waits, (self.relay, self.share, self.close)):
                when += wait
                planned.append((when, 1, k, lambda k=k, act=act: act(k)))
        return planned


class Exchange(Steps):
    def __init__(self, shapes, times):
        self.stages = exchange_stages()
        self.shapes = [shape[1:] for shape in shapes]
        self.times = times
        self.count = len(shapes)
        self.partners = sorted({(axis, stride) for _, axis, stride in self.stages})

    def out_shape(self):
        return [jax.ShapeDtypeStruct(shape, BF16) for shape in self.shapes]

    def scratch(self):
        held = []
        for rows, cols in self.shapes:
            held += [
                pltpu.VMEM((2, rows, cols), BF16),
                pltpu.VMEM((2, rows, cols), BF16),
                pltpu.VMEM((rows, cols), BF16),
                pltpu.VMEM((len(self.stages) - 3, rows // 2, cols), BF16),
                pltpu.VMEM((rows // 2, cols), BF16),
                pltpu.SemaphoreType.DMA((len(self.stages),)),
                pltpu.SemaphoreType.DMA((len(self.stages),)),
                pltpu.SemaphoreType.DMA((2,)),
            ]
        return held

    def bind(self, ins, outs, held):
        self.refs = [
            (ins[k], outs[k]) + tuple(held[8 * k : 8 * k + 8]) for k in range(self.count)
        ]
        self.locate()

    def remote(self, k, step):
        source, out, pair, kept, chip, halves, mine, sent, got, _ = self.refs[k]
        kind, axis, stride = self.stages[step]
        rows = self.shapes[k][0]
        if kind == "pair":
            ends = (source.at[0:2], pair)
        elif kind == "chip":
            ends = (kept.at[0], chip)
        elif kind == "split":
            ends = (kept.at[1, self.half_of(rows, 1), :], halves.at[0])
        elif kind == "full":
            ends = (mine, halves.at[step - 2])
        else:
            ends = (mine, out.at[self.half_of(rows, 0), :])
        return self.push(*ends, sent.at[step], got.at[step], axis, stride)

    def local(self, k, which):
        source, out, _, kept, _, _, mine, _, _, near = self.refs[k]
        if which == 0:
            return pltpu.make_async_copy(source.at[2:4], kept, near.at[0])
        half = self.half_of(self.shapes[k][0], 0)
        return pltpu.make_async_copy(mine, out.at[half, :], near.at[1])

    def start(self, k, step):
        self.remote(k, step).start()
        if step == 0:
            self.local(k, 0).start()
        if step == len(self.stages) - 1:
            self.local(k, 1).start()

    def end(self, k, step):
        _, _, pair, kept, chip, halves, mine, _, _, _ = self.refs[k]
        kind = self.stages[step][0]
        self.remote(k, step).wait()
        if kind == "pair":
            self.local(k, 0).wait()
            kept[...] = (kept[...].astype(F32) + pair[...].astype(F32)).astype(BF16)
        elif kind == "chip":
            kept[1] = (kept[1].astype(F32) + chip[...].astype(F32)).astype(BF16)
        elif kind == "split":
            own = self.half_of(self.shapes[k][0], 0)
            mine[...] = (kept[1, own, :].astype(F32) + halves[0].astype(F32)).astype(BF16)
        elif kind == "full":
            mine[...] = (mine[...].astype(F32) + halves[step - 2].astype(F32)).astype(BF16)
        else:
            self.local(k, 1).wait()
        if step + 1 < len(self.stages):
            self.start(k, step + 1)

    def plan(self):
        planned = []
        last = len(self.stages) - 1
        for k, (begin, *ends) in enumerate(self.times):
            planned.append((begin, 0, k, lambda k=k: self.start(k, 0)))
            for step in range(last + 1):
                when = ends[-1] if step == last else ends[min(step, 4)]
                planned.append((when, 1, k, lambda k=k, step=step: self.end(k, step)))
        return planned


def paced(begins, waits):
    return [[begin + sum(waits[:count]) for count in range(len(waits) + 1)] for begin in begins]


def head_mask(v, half):
    lane = lax.broadcasted_iota(jnp.int32, (1, PAIR), 1)
    keep = (lane < HEAD) if half == 0 else (lane >= HEAD)
    return jnp.where(keep, v, jnp.zeros_like(v))


def attend(qkv, shares, begins, waits, columns, ident, seqs, block=512, per=3):
    rows, width = qkv.shape[0], qkv.shape[1] // 3
    seq_length = rows // seqs
    block = min(block, seq_length)
    pairs = width // PAIR
    count = seq_length // block
    steps = pairs // per
    items = per * count
    wide = per * PAIR

    gathering = Gather([v.shape for v in shares], begins, waits, columns)
    many = len(shares)
    ticks = seqs * steps * items

    def kernel(*refs):
        q_ref, k_ref, v_ref = refs[:3]
        out, total = refs[3 + many : 5 + many]
        v_turned, out_turned, held = refs[5 + 2 * many : 8 + 2 * many]
        gathering.bind(refs[3 : 3 + many], refs[5 + many : 5 + 2 * many], refs[8 + 2 * many :])
        spot = pl.program_id(0) * steps + pl.program_id(1)
        v_turned[...] = jnp.transpose(v_ref[...])

        def place(i):
            pair = i // count
            part = i - pair * count
            return (
                pair,
                pl.ds(pl.multiple_of(pair * PAIR, PAIR), PAIR),
                pl.ds(pl.multiple_of(part * block, block), block),
            )

        def score(i, half):
            _, cols, part = place(i)
            held[half] = mxu(k_ref[:, cols], head_mask(q_ref[part, cols], half), TRANSPOSED)

        def finish(i, half):
            pair, _, part = place(i)
            scores = held[half]
            top = jnp.max(scores, axis=0, keepdims=True)
            exponent = jnp.exp2(scores * SCALE2 - top * SCALE2).astype(BF16)
            head = pl.ds(pl.multiple_of(pair * PAIR + half * HEAD, HEAD), HEAD)
            left = jnp.concatenate([v_turned[head, :], jnp.ones((16, seq_length), BF16)], axis=0)
            mixed = mxu(left, exponent)
            denominator = mixed[HEAD : HEAD + 1]
            out_turned[head, part] = mixed[:HEAD] * (1.0 / denominator)
            total[0, pair, half : half + 1, part] = top * SCALE2 + jnp.log2(denominator)

        score(0, 0)

        def body(i, carry):
            gathering.tick(spot * items + i, ticks)
            score(i, 1)
            finish(i, 0)
            score(jnp.minimum(i + 1, items - 1), 0)
            finish(i, 1)
            return carry

        lax.fori_loop(0, items, body, 0)
        out[...] = jnp.transpose(out_turned[...]).astype(BF16)

        @pl.when(spot == seqs * steps - 1)
        def _():
            gathering.rest(ticks)

    def part_of(which):
        return pl.BlockSpec((seq_length, wide), lambda s, p: (s, which * steps + p))

    return call(
        kernel,
        "attend",
        (seqs, steps),
        [part_of(0), part_of(1), part_of(2)] + gathering.in_specs(),
        [part_of(0), pl.BlockSpec((1, per, 2, seq_length), lambda s, p: (s, p, 0, 0))]
        + gathering.out_specs(),
        [
            jax.ShapeDtypeStruct((rows, width), BF16),
            jax.ShapeDtypeStruct((seqs, pairs, 2, seq_length), F32),
        ]
        + gathering.out_shape(),
        [
            pltpu.VMEM((wide, seq_length), BF16),
            pltpu.VMEM((wide, seq_length), F32),
            pltpu.VMEM((2, seq_length, block), F32),
        ]
        + gathering.scratch(),
        16 * rows * seq_length * width,
        rows * width * 8,
        rows * seq_length * width // HEAD,
        ident,
    )(qkv, qkv, qkv, *shares)


def attend_back(
    qkv, mixture, d_mixture, total, tables, pieces, times, ident, seqs, block=512, per=3
):
    rows, width = mixture.shape
    seq_length = rows // seqs
    block = min(block, seq_length)
    pairs = width // PAIR
    count = seq_length // block
    steps = pairs // per
    items = per * count
    wide = per * PAIR
    exchange = Exchange([v.shape for v in pieces], times)
    many = len(pieces)
    ticks = seqs * steps * items

    def kernel(*refs):
        q_ref, k_ref, v_ref, mix, grad, tot, cos, sin = refs[:8]
        dq, dk, dv = refs[8 + many : 11 + many]
        k_turned, dq_turned, dk_sum, dv_sum, inner, s_held, p_held = refs[
            11 + 2 * many : 18 + 2 * many
        ]
        exchange.bind(refs[8 : 8 + many], refs[11 + many : 11 + 2 * many], refs[18 + 2 * many :])
        spot = pl.program_id(0) * steps + pl.program_id(1)
        k_turned[...] = jnp.transpose(k_ref[...])
        product = jnp.transpose(mix[...].astype(F32) * grad[...].astype(F32))
        for pair in range(per):
            for half in range(2):
                lower = pair * PAIR + half * HEAD
                inner[pair, half : half + 1, :] = column_sum(product[lower : lower + HEAD, :])
        dk_sum[...] = jnp.zeros_like(dk_sum)
        dv_sum[...] = jnp.zeros_like(dv_sum)

        def body(i, carry):
            exchange.tick(spot * items + i, ticks)
            pair = i // count
            part = i - pair * count
            cols = pl.ds(pl.multiple_of(pair * PAIR, PAIR), PAIR)
            part = pl.ds(pl.multiple_of(part * block, block), block)
            for half in range(2):
                head = pl.ds(pl.multiple_of(pair * PAIR + half * HEAD, HEAD), HEAD)
                query = head_mask(q_ref[part, cols], half)
                cot = head_mask(grad[part, cols], half)
                s_held[half] = mxu(k_ref[:, cols], query, TRANSPOSED)
                p_held[half] = mxu(v_ref[:, cols], cot, TRANSPOSED)
                probs = jnp.exp2(s_held[half] * SCALE2 - tot[0, pair, half : half + 1, part])
                d_scores = (probs * (p_held[half] - inner[pair, half : half + 1, part])).astype(BF16)
                dv_sum[:, cols] += mxu(probs.astype(BF16), cot)
                dk_sum[:, cols] += mxu(d_scores, query)
                dq_turned[head, part] = mxu(k_turned[head, :], d_scores)
            return carry

        lax.fori_loop(0, items, body, 0)
        d_queries = jnp.transpose(dq_turned[...])
        for source, target in ((d_queries, dq), (dk_sum, dk)):
            for pair in range(per):
                v = source[:, pair * PAIR : (pair + 1) * PAIR] * SCALE
                v = v * cos[...] - partner_lanes(v) * sin[...]
                target[:, pair * PAIR : (pair + 1) * PAIR] = v.astype(BF16)
        dv[...] = dv_sum[...].astype(BF16)

        @pl.when(spot == seqs * steps - 1)
        def _():
            exchange.rest(ticks)

    def part_of(which):
        return pl.BlockSpec((seq_length, wide), lambda s, p: (s, which * steps + p))

    table = whole((seq_length, PAIR))
    grads = jax.ShapeDtypeStruct((rows, width), BF16)
    return call(
        kernel,
        "attend_back",
        (seqs, steps),
        [part_of(0), part_of(1), part_of(2), part_of(0), part_of(0)]
        + [pl.BlockSpec((1, per, 2, seq_length), lambda s, p: (s, p, 0, 0))]
        + [table] * 2
        + exchange.in_specs(),
        [part_of(0), part_of(0), part_of(0)] + exchange.out_specs(),
        [grads, grads, grads] + exchange.out_shape(),
        [
            pltpu.VMEM((wide, seq_length), BF16),
            pltpu.VMEM((wide, seq_length), F32),
            pltpu.VMEM((seq_length, wide), F32),
            pltpu.VMEM((seq_length, wide), F32),
            pltpu.VMEM((per, 2, seq_length), F32),
            pltpu.VMEM((2, seq_length, block), F32),
            pltpu.VMEM((2, seq_length, block), F32),
        ]
        + exchange.scratch(),
        40 * rows * seq_length * width,
        rows * width * 16,
        rows * seq_length * width // HEAD,
        ident,
    )(qkv, qkv, qkv, mixture, d_mixture, total, *tables, *pieces)


def middle_norm(mixture, tokens, starts, lengths, embed, gain, modulation, weight, seqs, block=512):
    rows, width = tokens.shape
    seq_length = rows // seqs
    block = min(block, seq_length)
    per_seq = seq_length // block

    def kernel(starts, lengths, mix, tok, emb, gn, mod, w, out):
        step = pl.program_id(0)
        seq = step // per_seq
        first = (step - seq * per_seq) * block
        start, _ = masked_rows(tok[...], emb[...], starts[seq], lengths[seq], first)
        middle = start + mod[pl.ds(seq, 1), 2 * width : 3 * width] * mxu(mix[...], w[...])
        hat, _ = normalized(middle)
        shift = mod[pl.ds(seq, 1), 3 * width : 4 * width]
        scale = mod[pl.ds(seq, 1), 4 * width : 5 * width]
        out[...] = (hat * (gn[...] * (1.0 + scale)) + shift).astype(BF16)

    row = pl.BlockSpec((block, width), lambda i: (i, 0))
    return call(
        kernel,
        "middle_norm",
        (rows // block,),
        [smem(), smem(), row, row, whole((1, width)), whole((1, width)), whole(modulation.shape)]
        + [whole(weight.shape)],
        row,
        jax.ShapeDtypeStruct((rows, width), BF16),
        [],
        2 * rows * width * width,
        rows * width * 6,
    )(starts, lengths, mixture, tokens, embed, gain, modulation, weight)


def gelu_pair(v):
    root = math.sqrt(2.0 / math.pi)
    square = v * v
    bent = jnp.tanh(v * (root + (root * 0.044715) * square))
    near = 0.5 + 0.5 * bent
    slope = near + (0.5 * v) * (1.0 - bent * bent) * (root + (3.0 * root * 0.044715) * square)
    return v * near, slope


def group_rows(ref, group, ways):
    part = ref.shape[0] // (ways * GROUPS)
    lowers = [(way * GROUPS + group) * part for way in range(ways)]
    return jnp.concatenate([ref[lower : lower + part, :] for lower in lowers], axis=0)


def group_columns(ref, group, ways):
    part = ref.shape[1] // (ways * GROUPS)
    lowers = [(way * GROUPS + group) * part for way in range(ways)]
    return jnp.concatenate([ref[:, lower : lower + part] for lower in lowers], axis=1)


def hidden_units(normed, cot, modulation, up, up_bias, down, group, seqs, block=512):
    rows, width = normed.shape
    ways = lax.axis_size("narrow")
    units = up.shape[1] // GROUPS
    share, part_units = width // ways, units // ways
    seq_length = rows // seqs
    block = min(block, seq_length)
    per_seq = seq_length // block
    steps = rows // block

    def kernel(*refs):
        nrm, g, mod, b_up = refs[:4]
        w_ups, w_downs = refs[4 : 4 + ways], refs[4 + ways : 4 + 2 * ways]
        act, d_up, g_up, g_down, g_bias, d_gate, g_sum = refs[4 + 2 * ways : 11 + 2 * ways]
        n_turned, g_turned, a_held, u_held, down_held = refs[11 + 2 * ways :]
        step = pl.program_id(0)

        @pl.when(step == 0)
        def _():
            g_bias[...] = jnp.zeros_like(g_bias)
            d_gate[...] = jnp.zeros_like(d_gate)
            g_sum[...] = jnp.zeros_like(g_sum)
            for way in range(ways):
                down_held[way] = w_downs[way][...]

        @pl.when(step < steps)
        def _():
            seq = step // per_seq
            part = pl.ds(pl.multiple_of(step * block, block), block)
            cotangent = g[...].astype(F32)
            d_branch = (mod[pl.ds(seq, 1), 5 * width : 6 * width] * cotangent).astype(BF16)
            for way in range(ways):
                cols = slice(way * part_units, (way + 1) * part_units)
                upper = mxu(nrm[...], w_ups[way][...]) + b_up[:, cols]
                d_active = mxu(d_branch, w_downs[way][...], TRANSPOSED)
                active, slope = gelu_pair(upper)
                active = active.astype(BF16)
                d_upper = (d_active * slope).astype(BF16)
                act[:, cols] = active
                a_held[part, cols] = active
                d_up[:, cols] = d_upper
                u_held[part, cols] = d_upper
                g_bias[:, cols] += column_sum(d_upper.astype(F32))
            store_shares(n_turned, jnp.transpose(nrm[...]), part)
            g_turned[:, part] = jnp.transpose(g[...])
            g_sum[pl.ds(seq, 1), :] += column_sum(cotangent)

        @pl.when(step >= steps)
        def _():
            place = step - steps
            owner = owner_at(lax.axis_index("narrow"), place)
            cols = pl.ds(pl.multiple_of(owner * part_units, part_units), part_units)
            product = mxu(n_turned[...], u_held[:, cols]).astype(BF16)
            g_up[:, :, cols] = product.reshape(ways, share, part_units)
            own = down_held[owner].astype(F32)
            total = jnp.zeros((part_units, width), F32)
            for seq in range(seqs):
                lower, upper = seq * seq_length, (seq + 1) * seq_length
                product = mxu(g_turned[:, lower:upper], a_held[lower:upper, cols])
                product = jnp.transpose(product)
                total += product * mod[seq : seq + 1, 5 * width : 6 * width]
                d_gate[seq : seq + 1, :] += column_sum(product * own)
            g_down[0] = total.astype(BF16)

    def early(i):
        return (jnp.minimum(i, steps - 1), 0)

    def fixed(shape):
        return pl.BlockSpec(shape, lambda i: (0,) * len(shape))

    def piece(shape, index):
        return pl.BlockSpec(shape, lambda i: index, pipeline_mode=pl.Buffered(1))

    spots = [way * GROUPS + group for way in range(ways)]
    return call(
        kernel,
        "hidden_units",
        (steps + ways,),
        [pl.BlockSpec((block, width), early)] * 2
        + [whole(modulation.shape), whole(up_bias.shape)]
        + [piece((width, part_units), (0, spot)) for spot in spots]
        + [piece((part_units, width), (spot, 0)) for spot in spots],
        (
            pl.BlockSpec((block, units), early),
            pl.BlockSpec((block, units), early),
            fixed((ways, share, units)),
            pl.BlockSpec(
                (1, part_units, width), lambda i: (jnp.maximum(i - steps, 0), 0, 0)
            ),
            fixed((1, units)),
            fixed((seqs, width)),
            fixed((seqs, width)),
        ),
        (
            jax.ShapeDtypeStruct((rows, units), BF16),
            jax.ShapeDtypeStruct((rows, units), BF16),
            jax.ShapeDtypeStruct((ways, share, units), BF16),
            jax.ShapeDtypeStruct((ways, part_units, width), BF16),
            jax.ShapeDtypeStruct((1, units), F32),
            jax.ShapeDtypeStruct((seqs, width), F32),
            jax.ShapeDtypeStruct((seqs, width), F32),
        ),
        [
            pltpu.VMEM((width, rows), BF16),
            pltpu.VMEM((width, rows), BF16),
            pltpu.VMEM((rows, units), BF16),
            pltpu.VMEM((rows, units), BF16),
            pltpu.VMEM((ways, part_units, width), BF16),
        ],
        8 * rows * width * units,
        rows * (width * 4 + units * 4) + 8 * width * units,
        rows * units,
    )(normed, cot, modulation, up_bias, *[up] * ways, *[down] * ways)


def middle_back(
    mixture, tokens, cot, starts, lengths, embed, gain, modulation, out_weight, d_uppers, up,
    pieces, times, ident, seqs, block=256,
):
    rows, width = tokens.shape
    ways = lax.axis_size("narrow")
    seq_length = rows // seqs
    block = min(block, seq_length)
    per_seq = seq_length // block
    steps = rows // block
    groups = len(d_uppers)
    units = d_uppers[0].shape[1]
    share = width // ways
    exchange = Exchange([v.shape for v in pieces], times)
    many = len(pieces)

    def kernel(*refs):
        starts, lengths, mix, tok, g, emb, gn, mod, w_out, w_up = refs[:10]
        d_ups, spot = refs[10 : 10 + groups], 10 + groups
        ins, spot = refs[spot : spot + many], spot + many
        d_middle_out, d_mix, g_out, sums = refs[spot : spot + 4]
        outs, spot = refs[spot + 4 : spot + 4 + many], spot + 4 + many
        g_sum = refs[spot]
        exchange.bind(ins, outs, refs[spot + 1 :])
        step = pl.program_id(0)
        seq = step // per_seq
        first = (step - seq * per_seq) * block
        exchange.tick(step, steps)

        @pl.when(step == 0)
        def _():
            g_sum[...] = jnp.zeros_like(g_sum)

        @pl.when(step == seq * per_seq)
        def _():
            sums[...] = jnp.zeros_like(sums)

        def vector(which):
            return mod[pl.ds(seq, 1), which * width : (which + 1) * width]

        attended = mxu(mix[...], w_out[...])
        start, _ = masked_rows(tok[...], emb[...], starts[seq], lengths[seq], first)
        hat, inverse = normalized(start + vector(2) * attended)
        d_normed = mxu(d_ups[0][...], group_columns(w_up, 0, ways), TRANSPOSED)
        for group in range(1, groups):
            d_normed += mxu(d_ups[group][...], group_columns(w_up, group, ways), TRANSPOSED)
        d_middle = g[...].astype(F32) + norm_back(
            d_normed * (gn[...] * (1.0 + vector(4))), hat, inverse
        )
        d_middle_out[...] = d_middle
        d_attended = (vector(2) * d_middle).astype(BF16)
        d_mix[...] = mxu(d_attended, w_out[...], TRANSPOSED).astype(BF16)
        g_sum[...] += mxu(jnp.transpose(mix[...]), d_attended)
        sums[0, 0:1, :] += column_sum(d_normed)
        sums[0, 1:2, :] += column_sum(d_normed * hat)
        sums[0, 2:3, :] += column_sum(d_middle * attended)

        @pl.when(step == steps - 1)
        def _():
            for place in range(ways):
                owner = owner_at(exchange.at["narrow"], place)
                spot = pl.ds(pl.multiple_of(owner * share, share), share)
                g_out[place] = g_sum[spot, :].astype(BF16)
            exchange.rest(steps)

    row = pl.BlockSpec((block, width), lambda i: (i, 0))
    unit_row = pl.BlockSpec((block, units), lambda i: (i, 0))
    return call(
        kernel,
        "middle_back",
        (steps,),
        [smem(), smem(), row, row, row, whole((1, width)), whole((1, width))]
        + [whole(modulation.shape), whole(out_weight.shape), whole(up.shape)]
        + [unit_row] * groups
        + exchange.in_specs(),
        [
            row,
            row,
            pl.BlockSpec((ways, share, width), lambda i: (0, 0, 0)),
            pl.BlockSpec((1, 8, width), lambda i: (i // per_seq, 0, 0)),
        ]
        + exchange.out_specs(),
        [
            jax.ShapeDtypeStruct((rows, width), F32),
            jax.ShapeDtypeStruct((rows, width), BF16),
            jax.ShapeDtypeStruct((ways, share, width), BF16),
            jax.ShapeDtypeStruct((seqs, 8, width), F32),
        ]
        + exchange.out_shape(),
        [pltpu.VMEM((width, width), F32)] + exchange.scratch(),
        rows * width * (2 * units * groups + 6 * width),
        rows * (width * 12 + units * groups * 2) + 2 * width * units * groups,
        0,
        ident,
    )(
        starts, lengths, mixture, tokens, cot, embed, gain, modulation, out_weight, up,
        *d_uppers, *pieces,
    )


class Finale(Steps):
    def __init__(self, ways):
        self.ways = ways
        self.wide = lax.axis_size("wide")

    def scratch(self, columns):
        dma = pltpu.SemaphoreType.DMA
        return [
            pltpu.VMEM((self.ways, 8, columns), F32),
            pltpu.VMEM((self.ways, 8, columns), F32),
            pltpu.VMEM((self.wide, 8, columns), F32),
            dma((self.ways,)),
            dma((self.ways,)),
            dma((self.wide,)),
            dma((self.wide,)),
        ]

    def bind(self, held):
        self.parts, self.narrow_got, self.wide_got, *self.sems = held
        self.locate()

    def others(self):
        targets = []
        for offset in range(1, self.ways):
            targets.append({"narrow": lax.rem(self.at["narrow"] + offset, self.ways)})
        for offset in range(1, self.wide):
            targets.append({"wide": lax.rem(self.at["wide"] + offset, self.wide)})
        return targets

    def greet(self):
        barrier = pltpu.get_barrier_semaphore()
        targets = self.others()
        for target in targets:
            pl.semaphore_signal(
                barrier, inc=1, device_id=target, device_id_type=pl.DeviceIdType.MESH
            )
        pl.semaphore_wait(barrier, len(targets))

    def along_narrow(self, offset):
        target = lax.rem(self.at["narrow"] + offset, self.ways)
        return pltpu.make_async_remote_copy(
            src_ref=self.parts.at[target],
            dst_ref=self.narrow_got.at[self.at["narrow"]],
            send_sem=self.sems[0].at[offset],
            recv_sem=self.sems[1].at[offset],
            device_id={"narrow": target},
            device_id_type=pl.DeviceIdType.MESH,
        )

    def along_wide(self, offset):
        me = self.at["wide"]
        return pltpu.make_async_remote_copy(
            src_ref=self.wide_got.at[me],
            dst_ref=self.wide_got.at[me],
            send_sem=self.sems[2].at[offset],
            recv_sem=self.sems[3].at[offset],
            device_id={"wide": lax.rem(me + offset, self.wide)},
            device_id_type=pl.DeviceIdType.MESH,
        )

    def begin(self):
        for offset in range(1, self.ways):
            self.along_narrow(offset).start()
        me = self.at["narrow"]
        self.narrow_got[pl.ds(me, 1)] = self.parts[pl.ds(me, 1)]

    def spread(self, seqs, row_lanes):
        for offset in range(1, self.ways):
            self.along_narrow(offset).wait()
        me = self.at["wide"]
        for way in range(self.ways):
            self.wide_got[pl.ds(me, 1), way * seqs : (way + 1) * seqs, 0:row_lanes] = (
                self.narrow_got[way : way + 1, 0:seqs, 0:row_lanes]
            )
        total = self.narrow_got[0:1, :, row_lanes:]
        for way in range(1, self.ways):
            total += self.narrow_got[way : way + 1, :, row_lanes:]
        self.wide_got[pl.ds(me, 1), :, row_lanes:] = total
        for offset in range(1, self.wide):
            self.along_wide(offset).start()

    def close(self):
        for offset in range(1, self.wide):
            self.along_wide(offset).wait()


def finish(
    turned, d_parts, tokens, d_middle, mixture, starts, lengths, embed, gain, modulation, weight,
    out_weight, down_bias, actives, down, features, rows_two, vectors_two, times, ident, seqs,
    tile=256, block=512, late_block=256,
):
    rows, width = tokens.shape
    ways = lax.axis_size("narrow")
    share = width // ways
    seq_length = rows // seqs
    block, late_block = min(block, seq_length), min(late_block, seq_length)
    per_seq, late_per_seq = seq_length // block, seq_length // late_block
    tiles = width // tile
    columns, group_units = modulation.shape[1] // ways, actives[0].shape[1]
    groups = len(actives)
    time_width = features.shape[1]
    window = 2 * PAIR
    lanes = columns + time_width + window
    early, middle, late = 3 * tiles, rows // block, rows // late_block
    steps = early + middle + late
    exchange = Exchange([(ways, share, width)] * 3, times)
    finale = Finale(ways)

    def kernel(*refs):
        (
            starts, lengths, left, c_q, c_k, c_v, tok, d_mid, r_q, r_k, r_v, emb, gn, mod, w_q, w_k, w_v,
            tok_late, mix, w_out, b_down, feat, two, vec,
        ) = refs[:24]
        acts, w_down = refs[24 : 24 + groups], refs[24 + groups]
        spot = 25 + groups
        g_tok, block_out, g_ada, g_ada_bias, g_vec = refs[spot : spot + 5]
        outs = refs[spot + 5 : spot + 8]
        grads, sums = refs[spot + 8 : spot + 10]
        small = 7
        exchange.bind(
            [grads.at[part] for part in range(3)], outs, refs[spot + 10 + small :]
        )
        finale.bind(refs[spot + 10 : spot + 10 + small])
        step = pl.program_id(0)

        @pl.when(step == 0)
        def _():
            finale.greet()
            sums[...] = jnp.zeros_like(sums)

        exchange.tick(step, steps)

        for part, source in enumerate((c_q, c_k, c_v)):

            @pl.when((step >= part * tiles) & (step < (part + 1) * tiles))
            def _(part=part, source=source):
                cols = pl.ds(pl.multiple_of((step - part * tiles) * tile, tile), tile)
                product = mxu(left[...], source[...]).astype(BF16)
                grads[part, :, :, cols] = product.reshape(ways, share, tile)

        @pl.when((step >= early) & (step < early + middle))
        def _():
            at = step - early
            seq = at // per_seq
            first = (at - seq * per_seq) * block
            start, inside = masked_rows(
                tok[...], emb[...], starts[seq], lengths[seq], first
            )
            hat, inverse = normalized(start)
            d_normed = mxu(r_q[...], w_q[...], TRANSPOSED)
            d_normed += mxu(r_k[...], w_k[...], TRANSPOSED)
            d_normed += mxu(r_v[...], w_v[...], TRANSPOSED)
            scale = mod[pl.ds(seq, 1), width : 2 * width]
            d_start = d_mid[...] + norm_back(d_normed * (gn[...] * (1.0 + scale)), hat, inverse)
            g_tok[...] = jnp.where(inside, 0.0, d_start)
            sums[seq, 0:1, :] += column_sum(d_normed)
            sums[seq, 1:2, :] += column_sum(d_normed * hat)
            sums[seq, 2:3, :] += column_sum(jnp.where(inside, d_start, 0.0))

        @pl.when(step == early + middle)
        def _():
            parts = finale.parts
            embed_sum = jnp.zeros((1, width), F32)
            gain_sum = jnp.zeros((1, width), F32)
            for seq in range(seqs):
                shift, scale = sums[seq, 0:1, :], sums[seq, 1:2, :]
                gain_sum += scale * (1.0 + mod[seq : seq + 1, width : 2 * width])
                embed_sum += sums[seq, 2:3, :]
                row = jnp.concatenate([shift, scale * gn[...], two[seq : seq + 1, :]], axis=1)
                for way in range(ways):
                    parts[way, seq : seq + 1, 0:columns] = row[
                        :, way * columns : (way + 1) * columns
                    ]
            for way in range(ways):
                parts[way, 0:seqs, columns : columns + time_width] = feat[...]
                lower = PAIR * (share * way // PAIR)
                parts[way, 0:1, columns + time_width :] = embed_sum[:, lower : lower + window]
                parts[way, 1:2, columns + time_width :] = gain_sum[:, lower : lower + window]
                parts[way, 2:8, columns + time_width :] = vec[way, 2:8, :]
            finale.begin()

        @pl.when(step == early + middle + 2)
        def _():
            finale.spread(seqs, columns + time_width)

        @pl.when(step >= early + middle)
        def _():
            at = step - early - middle
            seq = at // late_per_seq
            first = (at - seq * late_per_seq) * late_block
            start, _ = masked_rows(
                tok_late[...], emb[...], starts[seq], lengths[seq], first
            )
            attended = mxu(mix[...], w_out[...])
            branch = mxu(acts[0][...], group_rows(w_down, 0, ways))
            for group in range(1, groups):
                branch += mxu(acts[group][...], group_rows(w_down, group, ways))
            branch += b_down[...]
            hidden = start + mod[pl.ds(seq, 1), 2 * width : 3 * width] * attended
            block_out[...] = (
                hidden + mod[pl.ds(seq, 1), 5 * width : 6 * width] * branch
            ).astype(BF16)

        @pl.when(step == steps - 1)
        def _():
            finale.close()
            got = finale.wide_got
            every = got[...].reshape(finale.wide * 8, lanes)
            d_mods, feats = every[:, 0:columns], every[:, columns : columns + time_width]
            g_ada[...] = lax.dot_general(
                jnp.transpose(feats), d_mods, PLAIN, precision=FULL_PRECISION,
                preferred_element_type=F32,
            )
            g_ada_bias[...] = column_sum(d_mods)
            total = got[0, :, columns + time_width :]
            for index in range(1, finale.wide):
                total += got[index, :, columns + time_width :]
            g_vec[...] = total
            exchange.rest(steps)

    def column(part):
        return pl.BlockSpec((rows, tile), lambda i: (0, jnp.clip(i - part * tiles, 0, tiles - 1)))

    row = pl.BlockSpec((block, width), lambda i: (jnp.clip(i - early, 0, middle - 1), 0))

    def late_row(wide):
        return pl.BlockSpec(
            (late_block, wide), lambda i: (jnp.maximum(i - early - middle, 0), 0)
        )

    def fixed(shape):
        return pl.BlockSpec(shape, lambda i: (0,) * len(shape))

    return call(
        kernel,
        "finish",
        (steps,),
        [smem(), smem(), whole(turned.shape), column(0), column(1), column(2), row, row, row, row, row]
        + [whole((1, width)), whole((1, width)), whole(modulation.shape)]
        + [column_third(which, width) for which in range(3)]
        + [late_row(width), late_row(width), whole((width, width)), whole((1, width))]
        + [whole(features.shape), whole(rows_two.shape), whole(vectors_two.shape)]
        + [late_row(group_units)] * groups
        + [whole(down.shape)],
        [
            row,
            late_row(width),
            fixed((time_width, columns)),
            fixed((1, columns)),
            fixed((8, window)),
        ]
        + exchange.out_specs(),
        [
            jax.ShapeDtypeStruct((rows, width), F32),
            jax.ShapeDtypeStruct((rows, width), BF16),
            jax.ShapeDtypeStruct((time_width, columns), F32),
            jax.ShapeDtypeStruct((1, columns), F32),
            jax.ShapeDtypeStruct((8, window), F32),
        ]
        + exchange.out_shape(),
        [pltpu.VMEM((3, ways, share, width), BF16), pltpu.VMEM((seqs, 8, width), F32)]
        + finale.scratch(lanes)
        + exchange.scratch(),
        2 * rows * width * (7 * width + group_units * groups),
        rows * (width * 24 + 2 * group_units * groups),
        0,
        ident,
    )(
        starts, lengths, turned, *d_parts, tokens, d_middle, *d_parts, embed, gain, modulation, weight, weight,
        weight,        tokens, mixture, out_weight, down_bias, features, rows_two, vectors_two, *actives, down,
    )


def gather_first(small, ada, weight, ident):
    share, wide = weight.shape
    width = wide // 3
    columns = [(0, 0, small.shape[1]), (1, 0, ada.shape[1])]
    columns += [(2, k * width, (k + 1) * width) for k in range(3)]
    gathering = Gather([small.shape, ada.shape, weight.shape], [0] * 5, [0] * 3, columns)

    def kernel(*refs):
        gathering.bind(refs[0:3], refs[3:6], refs[6:])
        gathering.greet()
        gathering.begin(0)
        gathering.begin(1)
        gathering.begin(2)
        for k in range(5):
            gathering.relay(k)
            if k + 3 < 5:
                gathering.begin(k + 3)
            if k > 0:
                gathering.share(k - 1)
        gathering.share(4)
        for k in range(5):
            gathering.close(k)

    return call(
        kernel,
        "gather_first",
        (),
        gathering.in_specs(),
        gathering.out_specs(),
        gathering.out_shape(),
        gathering.scratch(),
        0,
        8 * share * wide,
        0,
        ident,
    )(small, ada, weight)


def assemble(ups, downs, out, qkv):
    share, units = ups[0].shape
    part, width = downs[0].shape
    ways = units // part
    groups = len(ups)

    def kernel(*refs):
        up_in, down_in = refs[:groups], refs[groups : 2 * groups]
        out_in, qkv_in = refs[2 * groups], refs[2 * groups + 1 : 2 * groups + 4]
        g_up, g_down, g_out, g_qkv = refs[2 * groups + 4 :]
        for group in range(groups):
            for way in range(ways):
                lower = (way * groups + group) * part
                g_up[:, lower : lower + part] = up_in[group][
                    :, way * part : (way + 1) * part
                ].astype(F32)
            g_down[group] = down_in[group][...].astype(F32)
        g_out[...] = out_in[...].astype(F32)
        for which in range(3):
            g_qkv[:, which * width : (which + 1) * width] = qkv_in[which][...].astype(F32)

    pace = 4
    small, tall = share // pace, part // pace

    def rows(count, columns):
        return pl.BlockSpec((count, columns), lambda i: (i, 0))

    g_up, g_down, g_out, g_qkv = call(
        kernel,
        "assemble",
        (pace,),
        [rows(small, units)] * groups
        + [rows(tall, width)] * groups
        + [rows(small, width)] * 4,
        (
            rows(small, units * groups),
            pl.BlockSpec((groups, tall, width), lambda i: (0, i, 0)),
            rows(small, width),
            rows(small, 3 * width),
        ),
        (
            jax.ShapeDtypeStruct((share, units * groups), F32),
            jax.ShapeDtypeStruct((groups, part, width), F32),
            jax.ShapeDtypeStruct((share, width), F32),
            jax.ShapeDtypeStruct((share, 3 * width), F32),
        ),
        [],
        0,
        12 * share * units * groups,
    )(*ups, *downs, out, *qkv)
    return g_up, g_down.reshape(groups * part, width), g_out, g_qkv


def per_device(
    tokens,
    timestep,
    span_start,
    span_length,
    mask_embed,
    ada_weight,
    ada_bias,
    norm_first,
    query_key_value_weight,
    output_weight,
    norm_second,
    up_projection_weight,
    up_projection_bias,
    down_projection_weight,
    down_projection_bias,
    cotangent,
):
    seqs = timestep.shape[0]
    rows, width = tokens.shape
    seq_length = rows // seqs
    ways = lax.axis_size("narrow")
    me = lax.axis_index("narrow")
    share = width // ways
    unit_share = down_projection_weight.shape[0]
    part = unit_share // GROUPS
    units = ways * part
    time_width, columns = ada_weight.shape

    vectors = (
        ada_bias, mask_embed, norm_first, norm_second, down_projection_bias, up_projection_bias,
    )
    filled, lower = jnp.zeros((32 * PAIR,), BF16), 0
    for v in vectors:
        filled += jnp.pad(v, (lower, filled.shape[0] - lower - v.shape[0]))
        lower += v.shape[0]
    small = filled.reshape(32, PAIR)
    small, ada, w_qkv = gather_first(small, ada_weight, query_key_value_weight, 0)

    small = small.reshape(ways, -1).astype(F32)
    smalls, lower = [], 0
    for v in vectors:
        smalls.append(small[:, lower : lower + v.shape[0]].reshape(1, -1))
        lower += v.shape[0]
    bias_ada, embed, gain_one, gain_two, bias_down, bias_up = smalls
    features = time_features(timestep, time_width)
    modulation = jnp.einsum(
        "sf,wfc->swc",
        features,
        ada.reshape(ways, time_width, columns).astype(F32),
        precision=FULL_PRECISION,
    ).reshape(seqs, -1) + bias_ada
    tables = rotary_tables(seq_length)

    qkv, turned_one = project(
        tokens, span_start, span_length, embed, gain_one, modulation, w_qkv, tables, seqs
    )
    thirds = [
        (which, third * size, (third + 1) * size)
        for which, size in ((1, unit_share * ways // 3), (2, width // 3))
        for third in range(3)
    ]
    mixture, total, w_out, w_up, w_down = attend(
        qkv,
        [output_weight, up_projection_weight, down_projection_weight],
        [0, 1, 3, 6, 8, 11, 13],
        [5, 5, 2],
        [(0, 0, width)] + thirds,
        1,
        seqs,
    )
    normed_two = middle_norm(
        mixture, tokens, span_start, span_length, embed, gain_two, modulation, w_out, seqs
    )
    bias_parts = bias_up.reshape(ways, GROUPS, part)
    actives, d_uppers, pieces, g_biases, d_gate_two = [], [], [], [], 0.0
    for group in range(GROUPS):
        active, d_upper, g_up, g_down, g_bias, d_gate, g_sum = hidden_units(
            normed_two,
            cotangent,
            modulation,
            w_up,
            bias_parts[:, group].reshape(1, units),
            w_down,
            group,
            seqs,
        )
        actives.append(active)
        d_uppers.append(d_upper)
        pieces += [g_up, g_down]
        g_biases.append(g_bias)
        d_gate_two += d_gate
    d_gate_two += bias_down * g_sum
    d_middle, d_mixture, g_out, sums_two, *done_first = middle_back(
        mixture, tokens, cotangent, span_start, span_length, embed, gain_two, modulation, w_out,
        d_uppers, w_up, pieces[:2], paced([0, 1], [1, 2, 1, 1, 2, 1]), 2, seqs,
    )
    d_q, d_k, d_v, *done_second = attend_back(
        qkv, mixture, d_mixture, total, tables, pieces[2:] + [g_out],
        paced([0, 2, 4, 6, 8], [1, 5, 3, 3, 5, 3]), 3, seqs,
    )
    scale_two = modulation[:, 4 * width : 5 * width]
    rows_two = jnp.concatenate(
        [sums_two[:, 2], sums_two[:, 0], sums_two[:, 1] * gain_two, d_gate_two], axis=1
    )
    g_norm_two = jnp.sum(sums_two[:, 1] * (1.0 + scale_two), axis=0)
    g_bias_down = jnp.sum(modulation[:, 5 * width :] * g_sum, axis=0)
    lowers = [PAIR * (share * way // PAIR) for way in range(ways)]
    vectors_two = jnp.stack(
        [
            jnp.stack([v[lower : lower + 2 * PAIR] for lower in lowers])
            for v in (g_norm_two, g_norm_two, g_norm_two, g_bias_down)
        ]
        + [v.reshape(ways, part) for v in g_biases]
        + [jnp.zeros((ways, 2 * PAIR), F32)],
        axis=1,
    )
    grad_tokens, block_out, grad_ada_weight, grad_ada_bias, vectors, *g_qkv = finish(
        turned_one, (d_q, d_k, d_v), tokens, d_middle, mixture, span_start, span_length, embed,
        gain_one, modulation, w_qkv, w_out, bias_down, actives, w_down, features, rows_two,
        vectors_two,
        [[3, 5, 11, 12, 13, 16, 18], [6, 8, 12, 13, 15, 18, 20], [9, 10, 14, 16, 18, 20, 21]],
        4, seqs,
    )
    skip = lax.rem(share * me, PAIR)
    own = lax.dynamic_slice_in_dim(vectors[:4], skip, share, 1)
    g_ups, g_downs = zip(*[done_first] + [done_second[2 * k : 2 * k + 2] for k in range(2)])
    g_up, g_down, g_out, g_qkv = assemble(g_ups, g_downs, done_second[4], g_qkv)
    return (
        block_out,
        grad_tokens,
        own[0],
        grad_ada_weight,
        grad_ada_bias[0],
        own[1],
        g_qkv,
        g_out,
        own[2],
        g_up,
        vectors[4 : 4 + GROUPS].reshape(-1),
        g_down,
        own[3],
    )


def solution(mesh):
    rows = P(("wide", "narrow"), None)
    per_seq = P(("wide", "narrow"))
    vector, matrix, columns = P("narrow"), P("narrow", None), P(None, "narrow")
    return jax.shard_map(
        per_device,
        mesh=mesh,
        in_specs=(
            rows, per_seq, per_seq, per_seq, vector, columns, vector, vector,
            matrix, matrix, vector, matrix, vector, matrix, vector, rows,
        ),
        out_specs=(
            rows, rows, vector, columns, vector, vector, matrix, matrix, vector, matrix,
            vector, matrix, vector,
        ),
        check_vma=False,
    )
```

```python
import math

import jax
import jax.numpy as jnp
import numpy as np
from jax import lax
from jax.experimental import pallas as pl
from jax.experimental.pallas import tpu as pltpu
from jax.sharding import PartitionSpec as P

HEAD = 64
PAIR = 2 * HEAD
GROUPS = 3
FINISH_TIMES = [
    [3, 5, 11, 12, 13, 16, 18], [6, 8, 12, 13, 15, 18, 20], [9, 10, 14, 16, 18, 20, 21],
]
EPSILON = 1e-05
FULL_PRECISION = lax.Precision.HIGHEST
F32 = jnp.float32
BF16 = jnp.bfloat16
SCALE = 1.0 / math.sqrt(HEAD)
SCALE2 = SCALE * math.log2(math.e)
VMEM_BYTES = 60 << 20
PLAIN = (((1,), (0,)), ((), ()))
TRANSPOSED = (((1,), (1,)), ((), ()))


def mxu(left, right, dims=PLAIN):
    return lax.dot_general(left, right, dims, preferred_element_type=F32)


def call(
    kernel, name, grid, in_specs, out_specs, out_shape, scratch, flops, moved, exps=0, ident=None
):
    return pl.pallas_call(
        kernel,
        name=name,
        grid=grid,
        in_specs=in_specs,
        out_specs=out_specs,
        out_shape=out_shape,
        scratch_shapes=scratch,
        compiler_params=pltpu.CompilerParams(
            vmem_limit_bytes=VMEM_BYTES, collective_id=ident, has_side_effects=ident is not None
        ),
        cost_estimate=pl.CostEstimate(flops=flops, bytes_accessed=moved, transcendentals=exps),
    )


def whole(shape):
    return pl.BlockSpec(shape, lambda *_: (0,) * len(shape), pipeline_mode=pl.Buffered(1))


def column_third(which, width):
    return pl.BlockSpec((width, width), lambda *_: (0, which), pipeline_mode=pl.Buffered(1))


def smem():
    return pl.BlockSpec(memory_space=pltpu.SMEM)


def time_features(step_ids, feature_count):
    halfway = feature_count // 2
    spacing = jnp.exp(-math.log(10000.0) * jnp.arange(halfway, dtype=F32) / halfway)
    angles = step_ids.astype(F32)[:, None] * spacing[None, :]
    return jax.nn.silu(jnp.concatenate([jnp.cos(angles), jnp.sin(angles)], axis=-1))


def rotary_tables(seq_length):
    halfway = HEAD // 2
    spacing = np.exp(-math.log(10000.0) * np.arange(halfway, dtype=np.float32) / halfway)
    angles = np.arange(seq_length, dtype=np.float32)[:, None] * spacing.astype(np.float32)
    cosine, sine = np.cos(angles), np.sin(angles)
    signed = np.concatenate([-sine, sine] * 2, axis=-1)
    return np.concatenate([cosine] * 4, axis=-1), signed


def partner_lanes(v):
    lane = lax.broadcasted_iota(jnp.int32, (1, PAIR), 1)
    return jnp.where(lax.rem(lane, HEAD) < HEAD // 2, from_ahead(v), from_behind(v))


def from_ahead(v):
    return pltpu.roll(v, PAIR - HEAD // 2, 1)


def from_behind(v):
    return pltpu.roll(v, HEAD // 2, 1)


def masked_rows(tokens, embed, start, length, first_row):
    rows = tokens.shape[0]
    position = lax.broadcasted_iota(jnp.int32, (rows, 1), 0) + first_row
    inside = (position >= start) & (position < start + length)
    return jnp.where(inside, embed, tokens.astype(F32)), inside


def normalized(rows):
    centre = rows - jnp.mean(rows, axis=-1, keepdims=True)
    spread = jnp.mean(centre * centre, axis=-1, keepdims=True)
    inverse = lax.rsqrt(spread + EPSILON)
    return centre * inverse, inverse


def norm_back(d_out, hat, inverse):
    return inverse * (
        d_out
        - jnp.mean(d_out, axis=-1, keepdims=True)
        - hat * jnp.mean(d_out * hat, axis=-1, keepdims=True)
    )


def column_sum(v):
    return jnp.sum(v, axis=0, keepdims=True)


def store_shares(target, value, cols):
    me, ways = lax.axis_index("narrow"), lax.axis_size("narrow")
    share = value.shape[0] // ways
    for place in range(ways):
        lower = pl.multiple_of(place_of(me, place) * share, share)
        target[pl.ds(lower, share), cols] = value[place * share : (place + 1) * share, :]


def place_of(me, other):
    core = lax.rem(me + other, 2)
    chip = lax.rem(me // 2 + other // 2, 2)
    return 2 * (1 - core) + 1 - chip


def owner_at(me, place):
    core, chip = 1 - place // 2, 1 - lax.rem(place, 2)
    return 2 * lax.rem(me // 2 + chip, 2) + lax.rem(me + core, 2)


def project(tokens, starts, lengths, embed, gain, modulation, weight, tables, seqs, block=512):
    rows, width = tokens.shape
    seq_length = rows // seqs
    block = min(block, seq_length)
    per_seq = seq_length // block
    pairs = width // PAIR

    def kernel(starts, lengths, tok, emb, gn, mod, w_q, w_k, w_v, cos, sin, out, nt):
        step = pl.program_id(0)
        seq = step // per_seq
        first = (step - seq * per_seq) * block
        start, _ = masked_rows(tok[...], emb[...], starts[seq], lengths[seq], first)
        hat, _ = normalized(start)
        shift = mod[pl.ds(seq, 1), 0:width]
        scale = mod[pl.ds(seq, 1), width : 2 * width]
        normed = (hat * (gn[...] * (1.0 + scale)) + shift).astype(BF16)
        store_shares(nt, jnp.transpose(normed), slice(None))
        for which, w in enumerate((w_q, w_k)):
            turned = mxu(normed, w[...])
            for part in range(pairs):
                v = turned[:, part * PAIR : (part + 1) * PAIR]
                v = v * cos[...] + partner_lanes(v) * sin[...]
                lower = which * width + part * PAIR
                out[:, lower : lower + PAIR] = v.astype(BF16)
        out[:, 2 * width :] = mxu(normed, w_v[...]).astype(BF16)

    table = pl.BlockSpec((block, PAIR), lambda i: (lax.rem(i, per_seq), 0))
    return call(
        kernel,
        "project",
        (rows // block,),
        [
            smem(),
            smem(),
            pl.BlockSpec((block, width), lambda i: (i, 0)),
            whole((1, width)),
            whole((1, width)),
            whole(modulation.shape),
            column_third(0, width),
            column_third(1, width),
            column_third(2, width),
            table,
            table,
        ],
        (
            pl.BlockSpec((block, 3 * width), lambda i: (i, 0)),
            pl.BlockSpec((width, block), lambda i: (0, i)),
        ),
        (
            jax.ShapeDtypeStruct((rows, 3 * width), BF16),
            jax.ShapeDtypeStruct((width, rows), BF16),
        ),
        [],
        2 * rows * width * 3 * width,
        rows * width * 10 + 6 * width * width,
    )(starts, lengths, tokens, embed, gain, modulation, weight, weight, weight, *tables)


def flip(index, stride):
    return index + stride * (1 - 2 * lax.rem(index // stride, 2))


def exchange_stages():
    count = lax.axis_size("wide")
    strides = [1 << bit for bit in range(1, count.bit_length() - 1)]
    return [("pair", "narrow", 1), ("chip", "narrow", 2), ("split", "wide", 1)] + [
        ("full", "wide", stride) for stride in strides
    ] + [("join", "wide", 1)]


class Steps:
    def in_specs(self):
        return [pl.BlockSpec(memory_space=pl.ANY)] * self.count

    out_specs = in_specs

    def locate(self):
        self.at = {axis: lax.axis_index(axis) for axis in ("wide", "narrow")}
        self.odd = lax.rem(self.at["wide"], 2)

    def half_of(self, rows, which, lower=0):
        side = self.odd if which == 0 else 1 - self.odd
        return pl.ds(pl.multiple_of(lower + side * (rows // 2), rows // 2), rows // 2)

    def greet(self):
        barrier = pltpu.get_barrier_semaphore()
        for axis, stride in self.partners:
            pl.semaphore_signal(
                barrier,
                inc=1,
                device_id={axis: flip(self.at[axis], stride)},
                device_id_type=pl.DeviceIdType.MESH,
            )
        pl.semaphore_wait(barrier, len(self.partners))

    def push(self, source, target, sent, got, axis, stride):
        return pltpu.make_async_remote_copy(
            src_ref=source,
            dst_ref=target,
            send_sem=sent,
            recv_sem=got,
            device_id={axis: flip(self.at[axis], stride)},
            device_id_type=pl.DeviceIdType.MESH,
        )

    def tick(self, now, last):
        planned = sorted(self.plan(), key=lambda item: item[:3])
        for when in sorted({item[0] for item in planned if item[0] < last}):

            @pl.when(now == when)
            def _(when=when):
                if when == 0:
                    self.greet()
                for item in planned:
                    if item[0] == when:
                        item[3]()

    def rest(self, last):
        for item in sorted(self.plan(), key=lambda item: item[:3]):
            if item[0] >= last:
                item[3]()


class Gather(Steps):
    partners = (("narrow", 1), ("narrow", 2), ("wide", 1))

    def __init__(self, shapes, begins, waits, columns=None):
        columns = columns or [(k, 0, shape[1]) for k, shape in enumerate(shapes)]
        self.arrays, self.columns = shapes, columns
        self.shapes = [(shapes[k][0], upper - lower) for k, lower, upper in columns]
        self.begins, self.waits = begins, waits
        self.count = len(columns)

    def in_specs(self):
        return [pl.BlockSpec(memory_space=pl.ANY)] * len(self.arrays)

    out_specs = in_specs

    def out_shape(self):
        return [jax.ShapeDtypeStruct((4 * rows, cols), BF16) for rows, cols in self.arrays]

    def scratch(self):
        dma, held = pltpu.SemaphoreType.DMA, []
        for shape in self.shapes:
            held += [dma((5,)), dma((5,)), dma((2,)), pltpu.VMEM(shape, BF16)]
        return held

    def bind(self, ins, outs, held):
        self.refs = [
            (ins[k].at[:, lower:upper], outs[k].at[:, lower:upper])
            + tuple(held[4 * part : 4 * part + 4])
            for part, (k, lower, upper) in enumerate(self.columns)
        ]
        self.locate()

    def block(self, k, index, which=None):
        rows = self.shapes[k][0]
        if which is None:
            return pl.ds(pl.multiple_of(index * rows, rows), rows)
        return self.half_of(rows, which, index * rows)

    def remote(self, k, step):
        source, out, sent, got, _, _ = self.refs[k]
        me, across = self.at["narrow"], flip(self.at["narrow"], 2)
        axis, stride = (("narrow", 1), ("narrow", 2), ("wide", 1), ("narrow", 1), ("narrow", 1))[step]
        if step == 0:
            ends = (source, out.at[self.block(k, me), :])
        elif step == 1:
            half = self.half_of(self.shapes[k][0], 0)
            ends = (source.at[half, :], out.at[self.block(k, me, 0), :])
        else:
            spot = self.block(k, across, 1 if step == 4 else 0)
            ends = (out.at[spot, :], out.at[spot, :])
        return self.push(*ends, sent.at[step], got.at[step], axis, stride)

    def local(self, k, which):
        source, out, _, _, near, kept = self.refs[k]
        if which == 0:
            return pltpu.make_async_copy(source, kept, near.at[0])
        return pltpu.make_async_copy(
            kept, out.at[self.block(k, self.at["narrow"]), :], near.at[1]
        )

    def begin(self, k):
        self.remote(k, 1).start()
        self.remote(k, 0).start()
        self.local(k, 0).start()

    def relay(self, k):
        self.local(k, 0).wait()
        self.local(k, 1).start()
        self.remote(k, 1).wait()
        self.remote(k, 2).start()
        self.remote(k, 3).start()

    def share(self, k):
        self.remote(k, 2).wait()
        self.remote(k, 4).start()

    def close(self, k):
        self.remote(k, 0).wait()
        self.remote(k, 3).wait()
        self.remote(k, 4).wait()
        self.local(k, 1).wait()

    def plan(self):
        planned = []
        for k in range(self.count):
            when = self.begins[k]
            planned.append((when, 0, k, lambda k=k: self.begin(k)))
            for wait, act in zip(self.waits, (self.relay, self.share, self.close)):
                when += wait
                planned.append((when, 1, k, lambda k=k, act=act: act(k)))
        return planned


class Exchange(Steps):
    def __init__(self, shapes, times, columns=None, spans=None):
        columns = columns or [(k, 0, shape[-1]) for k, shape in enumerate(shapes)]
        spans = spans or ["whole"] * len(shapes)
        self.stages = exchange_stages()
        self.arrays, self.columns = [shape[-2:] for shape in shapes], columns
        self.shapes = [(self.arrays[k][0], upper - lower) for k, lower, upper in columns]
        self.spans = [spans[k] for k, _, _ in columns]
        self.firsts = [2 if span == "tail" else 0 for span in self.spans]
        self.lasts = [1 if span == "head" else len(self.stages) - 1 for span in self.spans]
        self.times = times
        self.count = len(columns)
        self.partners = sorted({(axis, stride) for _, axis, stride in self.stages})

    def in_specs(self):
        return [pl.BlockSpec(memory_space=pl.ANY)] * len(self.arrays)

    out_specs = in_specs

    def out_shape(self):
        return [jax.ShapeDtypeStruct(shape, BF16) for shape in self.arrays]

    def scratch(self):
        held = []
        dma = pltpu.SemaphoreType.DMA
        for (rows, cols), span in zip(self.shapes, self.spans):
            early, late = span != "tail", span != "head"
            held += [
                pltpu.VMEM((2, rows, cols) if early else (2, 16, PAIR), BF16),
                pltpu.VMEM((2 if early else 1, rows, cols), BF16),
                pltpu.VMEM((rows, cols) if early else (16, PAIR), BF16),
                pltpu.VMEM((len(self.stages) - 3, rows // 2, cols) if late else (1, 16, PAIR), BF16),
                pltpu.VMEM((rows // 2, cols) if late else (16, PAIR), BF16),
                dma((len(self.stages),)),
                dma((len(self.stages),)),
                dma((2,)),
            ]
        return held

    def bind(self, ins, outs, held):
        self.refs = []
        for part, (k, lower, upper) in enumerate(self.columns):
            every = (slice(None),) * (1 if self.spans[part] == "tail" else 2)
            self.refs.append(
                (ins[k].at[every + (slice(lower, upper),)], outs[k].at[:, lower:upper])
                + tuple(held[8 * part : 8 * part + 8])
            )
        self.locate()

    def own(self, k):
        kept = self.refs[k][3]
        return kept.at[0 if self.spans[k] == "tail" else 1]

    def remote(self, k, step):
        source, out, pair, kept, chip, halves, mine, sent, got, _ = self.refs[k]
        kind, axis, stride = self.stages[step]
        rows = self.shapes[k][0]
        if kind == "pair":
            ends = (source.at[0:2], pair)
        elif kind == "chip":
            ends = (kept.at[0], chip)
        elif kind == "split":
            ends = (self.own(k).at[self.half_of(rows, 1), :], halves.at[0])
        elif kind == "full":
            ends = (mine, halves.at[step - 2])
        else:
            ends = (mine, out.at[self.half_of(rows, 0), :])
        return self.push(*ends, sent.at[step], got.at[step], axis, stride)

    def load(self, k):
        source, kept, near = self.refs[k][0], self.refs[k][3], self.refs[k][9]
        if self.spans[k] == "tail":
            return pltpu.make_async_copy(source, kept.at[0], near.at[0])
        return pltpu.make_async_copy(source.at[2:4], kept, near.at[0])

    def store(self, k):
        out, mine, near = self.refs[k][1], self.refs[k][6], self.refs[k][9]
        if self.spans[k] == "head":
            return pltpu.make_async_copy(self.own(k), out, near.at[1])
        half = self.half_of(self.shapes[k][0], 0)
        return pltpu.make_async_copy(mine, out.at[half, :], near.at[1])

    def begin(self, k):
        self.load(k).start()
        if self.spans[k] != "tail":
            self.remote(k, 0).start()

    def enter(self, k):
        self.load(k).wait()
        self.remote(k, 2).start()

    def end(self, k, step):
        _, _, pair, kept, chip, halves, mine, _, _, _ = self.refs[k]
        kind = self.stages[step][0]
        self.remote(k, step).wait()
        if kind == "pair":
            self.load(k).wait()
            kept[...] = (kept[...].astype(F32) + pair[...].astype(F32)).astype(BF16)
        elif kind == "chip":
            kept[1] = (kept[1].astype(F32) + chip[...].astype(F32)).astype(BF16)
        elif kind == "split":
            half = self.half_of(self.shapes[k][0], 0)
            own = self.own(k)[half, :].astype(F32)
            mine[...] = (own + halves[0].astype(F32)).astype(BF16)
        elif kind == "full":
            mine[...] = (mine[...].astype(F32) + halves[step - 2].astype(F32)).astype(BF16)
        if step < self.lasts[k]:
            self.remote(k, step + 1).start()
        if step == max(self.lasts[k] - 1, 1):
            self.store(k).start()
        if step == self.lasts[k]:
            self.store(k).wait()

    def plan(self):
        planned = []
        for k, (begin, *ends) in enumerate(self.times):
            first, last = self.firsts[k], self.lasts[k]
            planned.append((begin, 0, k, lambda k=k: self.begin(k)))
            if first:
                planned.append((ends[0], 1, k, lambda k=k: self.enter(k)))
                ends = [0] + ends
            for step in range(first, last + 1):
                when = ends[-1] if step == last else ends[min(step, 4)]
                planned.append((when, 1, k, lambda k=k, step=step: self.end(k, step)))
        return planned


def paced(begins, waits):
    return [[begin + sum(waits[:count]) for count in range(len(waits) + 1)] for begin in begins]


def head_mask(v, half):
    lane = lax.broadcasted_iota(jnp.int32, (1, PAIR), 1)
    keep = (lane < HEAD) if half == 0 else (lane >= HEAD)
    return jnp.where(keep, v, jnp.zeros_like(v))


def attend(qkv, shares, begins, waits, columns, ident, seqs, block=512, per=3):
    rows, width = qkv.shape[0], qkv.shape[1] // 3
    seq_length = rows // seqs
    block = min(block, seq_length)
    pairs = width // PAIR
    count = seq_length // block
    steps = pairs // per
    items = per * count
    wide = per * PAIR

    gathering = Gather([v.shape for v in shares], begins, waits, columns)
    many = len(shares)
    ticks = seqs * steps * items

    def kernel(*refs):
        q_ref, k_ref, v_ref = refs[:3]
        out, total = refs[3 + many : 5 + many]
        v_turned, out_turned, held = refs[5 + 2 * many : 8 + 2 * many]
        gathering.bind(refs[3 : 3 + many], refs[5 + many : 5 + 2 * many], refs[8 + 2 * many :])
        spot = pl.program_id(0) * steps + pl.program_id(1)
        v_turned[...] = jnp.transpose(v_ref[...])

        def place(i):
            pair = i // count
            part = i - pair * count
            return (
                pair,
                pl.ds(pl.multiple_of(pair * PAIR, PAIR), PAIR),
                pl.ds(pl.multiple_of(part * block, block), block),
            )

        def score(i, half):
            _, cols, part = place(i)
            held[half] = mxu(k_ref[:, cols], head_mask(q_ref[part, cols], half), TRANSPOSED)

        def finish(i, half):
            pair, _, part = place(i)
            scores = held[half]
            top = jnp.max(scores, axis=0, keepdims=True)
            exponent = jnp.exp2(scores * SCALE2 - top * SCALE2).astype(BF16)
            head = pl.ds(pl.multiple_of(pair * PAIR + half * HEAD, HEAD), HEAD)
            left = jnp.concatenate([v_turned[head, :], jnp.ones((16, seq_length), BF16)], axis=0)
            mixed = mxu(left, exponent)
            denominator = mixed[HEAD : HEAD + 1]
            out_turned[head, part] = mixed[:HEAD] * (1.0 / denominator)
            total[0, pair, half : half + 1, part] = top * SCALE2 + jnp.log2(denominator)

        score(0, 0)

        def body(i, carry):
            gathering.tick(spot * items + i, ticks)
            score(i, 1)
            finish(i, 0)
            score(jnp.minimum(i + 1, items - 1), 0)
            finish(i, 1)
            return carry

        lax.fori_loop(0, items, body, 0)
        out[...] = jnp.transpose(out_turned[...]).astype(BF16)

        @pl.when(spot == seqs * steps - 1)
        def _():
            gathering.rest(ticks)

    def part_of(which):
        return pl.BlockSpec((seq_length, wide), lambda s, p: (s, which * steps + p))

    return call(
        kernel,
        "attend",
        (seqs, steps),
        [part_of(0), part_of(1), part_of(2)] + gathering.in_specs(),
        [part_of(0), pl.BlockSpec((1, per, 2, seq_length), lambda s, p: (s, p, 0, 0))]
        + gathering.out_specs(),
        [
            jax.ShapeDtypeStruct((rows, width), BF16),
            jax.ShapeDtypeStruct((seqs, pairs, 2, seq_length), F32),
        ]
        + gathering.out_shape(),
        [
            pltpu.VMEM((wide, seq_length), BF16),
            pltpu.VMEM((wide, seq_length), F32),
            pltpu.VMEM((2, seq_length, block), F32),
        ]
        + gathering.scratch(),
        16 * rows * seq_length * width,
        rows * width * 8,
        rows * seq_length * width // HEAD,
        ident,
    )(qkv, qkv, qkv, *shares)


def attend_back(
    qkv, mixture, d_mixture, total, tables, pieces, spans, columns, times, ident, seqs, block=512,
    per=3,
):
    rows, width = mixture.shape
    seq_length = rows // seqs
    block = min(block, seq_length)
    pairs = width // PAIR
    count = seq_length // block
    steps = pairs // per
    items = per * count
    wide = per * PAIR
    exchange = Exchange([v.shape for v in pieces], times, columns, spans)
    many = len(pieces)
    ticks = seqs * steps * items

    def kernel(*refs):
        q_ref, k_ref, v_ref, mix, grad, tot, cos, sin = refs[:8]
        dq, dk, dv = refs[8 + many : 11 + many]
        k_turned, dq_turned, dk_sum, dv_sum, inner, s_held, p_held = refs[
            11 + 2 * many : 18 + 2 * many
        ]
        exchange.bind(refs[8 : 8 + many], refs[11 + many : 11 + 2 * many], refs[18 + 2 * many :])
        spot = pl.program_id(0) * steps + pl.program_id(1)
        k_turned[...] = jnp.transpose(k_ref[...])
        product = jnp.transpose(mix[...].astype(F32) * grad[...].astype(F32))
        for pair in range(per):
            for half in range(2):
                lower = pair * PAIR + half * HEAD
                inner[pair, half : half + 1, :] = column_sum(product[lower : lower + HEAD, :])
        dk_sum[...] = jnp.zeros_like(dk_sum)
        dv_sum[...] = jnp.zeros_like(dv_sum)

        def body(i, carry):
            exchange.tick(spot * items + i, ticks)
            pair = i // count
            part = i - pair * count
            cols = pl.ds(pl.multiple_of(pair * PAIR, PAIR), PAIR)
            part = pl.ds(pl.multiple_of(part * block, block), block)
            for half in range(2):
                head = pl.ds(pl.multiple_of(pair * PAIR + half * HEAD, HEAD), HEAD)
                query = head_mask(q_ref[part, cols], half)
                cot = head_mask(grad[part, cols], half)
                s_held[half] = mxu(k_ref[:, cols], query, TRANSPOSED)
                p_held[half] = mxu(v_ref[:, cols], cot, TRANSPOSED)
                probs = jnp.exp2(s_held[half] * SCALE2 - tot[0, pair, half : half + 1, part])
                d_scores = (probs * (p_held[half] - inner[pair, half : half + 1, part])).astype(BF16)
                dv_sum[:, cols] += mxu(probs.astype(BF16), cot)
                dk_sum[:, cols] += mxu(d_scores, query)
                dq_turned[head, part] = mxu(k_turned[head, :], d_scores)
            return carry

        lax.fori_loop(0, items, body, 0)
        d_queries = jnp.transpose(dq_turned[...])
        for source, target in ((d_queries, dq), (dk_sum, dk)):
            for pair in range(per):
                v = source[:, pair * PAIR : (pair + 1) * PAIR] * SCALE
                v = v * cos[...] - partner_lanes(v) * sin[...]
                target[:, pair * PAIR : (pair + 1) * PAIR] = v.astype(BF16)
        dv[...] = dv_sum[...].astype(BF16)

        @pl.when(spot == seqs * steps - 1)
        def _():
            exchange.rest(ticks)

    def part_of(which):
        return pl.BlockSpec((seq_length, wide), lambda s, p: (s, which * steps + p))

    table = whole((seq_length, PAIR))
    grads = jax.ShapeDtypeStruct((rows, width), BF16)
    return call(
        kernel,
        "attend_back",
        (seqs, steps),
        [part_of(0), part_of(1), part_of(2), part_of(0), part_of(0)]
        + [pl.BlockSpec((1, per, 2, seq_length), lambda s, p: (s, p, 0, 0))]
        + [table] * 2
        + exchange.in_specs(),
        [part_of(0), part_of(0), part_of(0)] + exchange.out_specs(),
        [grads, grads, grads] + exchange.out_shape(),
        [
            pltpu.VMEM((wide, seq_length), BF16),
            pltpu.VMEM((wide, seq_length), F32),
            pltpu.VMEM((seq_length, wide), F32),
            pltpu.VMEM((seq_length, wide), F32),
            pltpu.VMEM((per, 2, seq_length), F32),
            pltpu.VMEM((2, seq_length, block), F32),
            pltpu.VMEM((2, seq_length, block), F32),
        ]
        + exchange.scratch(),
        40 * rows * seq_length * width,
        rows * width * 16,
        rows * seq_length * width // HEAD,
        ident,
    )(qkv, qkv, qkv, mixture, d_mixture, total, *tables, *pieces)


def middle_norm(mixture, tokens, starts, lengths, embed, gain, modulation, weight, seqs, block=512):
    rows, width = tokens.shape
    seq_length = rows // seqs
    block = min(block, seq_length)
    per_seq = seq_length // block

    def kernel(starts, lengths, mix, tok, emb, gn, mod, w, out):
        step = pl.program_id(0)
        seq = step // per_seq
        first = (step - seq * per_seq) * block
        start, _ = masked_rows(tok[...], emb[...], starts[seq], lengths[seq], first)
        middle = start + mod[pl.ds(seq, 1), 2 * width : 3 * width] * mxu(mix[...], w[...])
        hat, _ = normalized(middle)
        shift = mod[pl.ds(seq, 1), 3 * width : 4 * width]
        scale = mod[pl.ds(seq, 1), 4 * width : 5 * width]
        out[...] = (hat * (gn[...] * (1.0 + scale)) + shift).astype(BF16)

    row = pl.BlockSpec((block, width), lambda i: (i, 0))
    return call(
        kernel,
        "middle_norm",
        (rows // block,),
        [smem(), smem(), row, row, whole((1, width)), whole((1, width)), whole(modulation.shape)]
        + [whole(weight.shape)],
        row,
        jax.ShapeDtypeStruct((rows, width), BF16),
        [],
        2 * rows * width * width,
        rows * width * 6,
    )(starts, lengths, mixture, tokens, embed, gain, modulation, weight)


def gelu_pair(v):
    root = math.sqrt(2.0 / math.pi)
    square = v * v
    bent = jnp.tanh(v * (root + (root * 0.044715) * square))
    near = 0.5 + 0.5 * bent
    slope = near + (0.5 * v) * (1.0 - bent * bent) * (root + (3.0 * root * 0.044715) * square)
    return v * near, slope


def group_rows(ref, group, ways):
    part = ref.shape[0] // (ways * GROUPS)
    lowers = [(way * GROUPS + group) * part for way in range(ways)]
    return jnp.concatenate([ref[lower : lower + part, :] for lower in lowers], axis=0)


def group_columns(ref, group, ways):
    part = ref.shape[1] // (ways * GROUPS)
    lowers = [(way * GROUPS + group) * part for way in range(ways)]
    return jnp.concatenate([ref[:, lower : lower + part] for lower in lowers], axis=1)


def grouped_rows(ref, ways):
    part = ref.shape[0] // (ways * GROUPS)
    lowers = [(way * GROUPS + group) * part for group in range(GROUPS) for way in range(ways)]
    return jnp.concatenate([ref[lower : lower + part, :] for lower in lowers], axis=0)


def grouped_columns(ref, ways):
    part = ref.shape[1] // (ways * GROUPS)
    lowers = [(way * GROUPS + group) * part for group in range(GROUPS) for way in range(ways)]
    return jnp.concatenate([ref[:, lower : lower + part] for lower in lowers], axis=1)


def halved(arrays):
    return [
        (k, half * v.shape[-1] // 2, (half + 1) * v.shape[-1] // 2)
        for k, v in enumerate(arrays)
        for half in range(2)
    ]


def hidden_units(normed, cot, modulation, up, up_bias, down, times, ident, seqs, block=512):
    rows, width = normed.shape
    ways = lax.axis_size("narrow")
    units = up.shape[1] // GROUPS
    share, part_units = width // ways, units // ways
    seq_length = rows // seqs
    block = min(block, seq_length)
    per_seq = seq_length // block
    steps = rows // block
    turn = steps + ways
    shape_up, shape_down = (ways, share, units), (ways, part_units, width)
    traded = [jax.ShapeDtypeStruct(v, BF16) for v in (shape_up, shape_down) * 2]
    exchange = Exchange(
        [v.shape for v in traded], times, halved(traded), ["whole"] * 2 + ["head"] * 2
    )

    def kernel(*refs):
        nrm, g, mod, b_up = refs[:4]
        w_ups, w_downs = refs[4 : 4 + ways], refs[4 + ways : 4 + 2 * ways]
        act, d_up, g_bias, d_gate, g_sum = refs[4 + 2 * ways : 9 + 2 * ways]
        outs, left = refs[9 + 2 * ways : 15 + 2 * ways], refs[15 + 2 * ways :]
        n_turned, g_turned, a_held, u_held, down_held, g_up, g_down, near = left[:8]
        exchange.bind(
            [g_up.at[0], g_down.at[0], g_up.at[1], g_down.at[1]], outs[:4], left[8:]
        )
        step = pl.program_id(0)
        group = step // turn
        at = step - group * turn

        @pl.when(step == 0)
        def _():
            exchange.greet()
            d_gate[...] = jnp.zeros_like(d_gate)
            g_sum[...] = jnp.zeros_like(g_sum)

        exchange.tick(step, GROUPS * turn)

        @pl.when(at == 0)
        def _():
            g_bias[...] = jnp.zeros_like(g_bias)
            for way in range(ways):
                down_held[way] = w_downs[way][...]

        part = pl.ds(pl.multiple_of(jnp.minimum(at, steps - 1) * block, block), block)

        @pl.when(at < steps)
        def _():
            seq = at // per_seq
            cotangent = g[...].astype(F32)
            d_branch = (mod[pl.ds(seq, 1), 5 * width : 6 * width] * cotangent).astype(BF16)
            for way in range(ways):
                cols = slice(way * part_units, (way + 1) * part_units)
                upper = mxu(nrm[...], w_ups[way][...]) + b_up[:, cols]
                d_active = mxu(d_branch, w_downs[way][...], TRANSPOSED)
                active, slope = gelu_pair(upper)
                active = active.astype(BF16)
                d_upper = (d_active * slope).astype(BF16)
                act[:, cols] = active
                a_held[part, cols] = active
                d_up[:, cols] = d_upper
                u_held[part, cols] = d_upper
                g_bias[:, cols] += column_sum(d_upper.astype(F32))

        @pl.when(step < steps)
        def _():
            store_shares(n_turned, jnp.transpose(nrm[...]), part)
            g_turned[:, part] = jnp.transpose(g[...])
            g_sum[pl.ds(at // per_seq, 1), :] += column_sum(g[...].astype(F32))

        @pl.when(at >= steps)
        def _():
            place = at - steps
            owner = owner_at(exchange.at["narrow"], place)
            cols = pl.ds(pl.multiple_of(owner * part_units, part_units), part_units)
            product = mxu(n_turned[...], u_held[:, cols]).astype(BF16)
            g_up[group, :, :, cols] = product.reshape(ways, share, part_units)
            own = down_held[owner].astype(F32)
            total = jnp.zeros((part_units, width), F32)
            for seq in range(seqs):
                lower, upper = seq * seq_length, (seq + 1) * seq_length
                product = mxu(g_turned[:, lower:upper], a_held[lower:upper, cols])
                product = jnp.transpose(product)
                total += product * mod[seq : seq + 1, 5 * width : 6 * width]
                d_gate[seq : seq + 1, :] += column_sum(product * own)
            g_down[group, place] = total.astype(BF16)

        @pl.when(step == GROUPS * turn - 1)
        def _():
            copies = [
                pltpu.make_async_copy(source.at[GROUPS - 1], target, near.at[k])
                for k, (source, target) in enumerate(((g_up, outs[4]), (g_down, outs[5])))
            ]
            for copy in copies:
                copy.start()
            exchange.rest(GROUPS * turn)
            for copy in copies:
                copy.wait()

    def early(i):
        return (jnp.minimum(lax.rem(i, turn), steps - 1), 0)

    def fixed(shape):
        return pl.BlockSpec(shape, lambda i: (0,) * len(shape))

    by_rows = pl.BlockSpec(
        (block, units), lambda i: (jnp.minimum(lax.rem(i, turn), steps - 1), i // turn)
    )
    by_group = pl.BlockSpec((1, units), lambda i: (0, i // turn))

    def up_piece(way):
        return pl.BlockSpec((width, part_units), lambda i: (0, way * GROUPS + i // turn))

    def down_piece(way):
        return pl.BlockSpec((part_units, width), lambda i: (way * GROUPS + i // turn, 0))

    assert GROUPS == 3
    anywhere = pl.BlockSpec(memory_space=pl.ANY)
    return call(
        kernel,
        "hidden_units",
        (GROUPS * turn,),
        [pl.BlockSpec((block, width), early)] * 2
        + [whole(modulation.shape), by_group]
        + [up_piece(way) for way in range(ways)]
        + [down_piece(way) for way in range(ways)],
        [by_rows, by_rows, by_group, fixed((seqs, width)), fixed((seqs, width))]
        + exchange.out_specs()
        + [anywhere] * 2,
        [
            jax.ShapeDtypeStruct((rows, units * GROUPS), BF16),
            jax.ShapeDtypeStruct((rows, units * GROUPS), BF16),
            jax.ShapeDtypeStruct((1, units * GROUPS), F32),
            jax.ShapeDtypeStruct((seqs, width), F32),
            jax.ShapeDtypeStruct((seqs, width), F32),
        ]
        + exchange.out_shape()
        + [jax.ShapeDtypeStruct(shape_up, BF16), jax.ShapeDtypeStruct(shape_down, BF16)],
        [
            pltpu.VMEM((width, rows), BF16),
            pltpu.VMEM((width, rows), BF16),
            pltpu.VMEM((rows, units), BF16),
            pltpu.VMEM((rows, units), BF16),
            pltpu.VMEM((ways, part_units, width), BF16),
            pltpu.VMEM((GROUPS,) + shape_up, BF16),
            pltpu.VMEM((GROUPS,) + shape_down, BF16),
            pltpu.SemaphoreType.DMA((2,)),
        ]
        + exchange.scratch(),
        8 * rows * width * units * GROUPS,
        GROUPS * (rows * (width * 4 + units * 4) + 8 * width * units),
        rows * units * GROUPS,
        ident,
    )(normed, cot, modulation, up_bias, *[up] * ways, *[down] * ways)


def middle_back(
    mixture, tokens, cot, starts, lengths, embed, gain, modulation, out_weight, d_upper, up, seqs,
    block=256,
):
    rows, width = tokens.shape
    ways = lax.axis_size("narrow")
    seq_length = rows // seqs
    block = min(block, seq_length)
    per_seq = seq_length // block
    steps = rows // block
    hidden_width = d_upper.shape[1]
    share = width // ways

    def kernel(
        starts, lengths, mix, tok, g, emb, gn, mod, w_out, w_up, d_ups, d_middle_out, d_mix, g_out,
        sums, g_sum,
    ):
        step = pl.program_id(0)
        seq = step // per_seq
        first = (step - seq * per_seq) * block

        @pl.when(step == 0)
        def _():
            g_sum[...] = jnp.zeros_like(g_sum)

        @pl.when(step == seq * per_seq)
        def _():
            sums[...] = jnp.zeros_like(sums)

        def vector(which):
            return mod[pl.ds(seq, 1), which * width : (which + 1) * width]

        attended = mxu(mix[...], w_out[...])
        start, _ = masked_rows(tok[...], emb[...], starts[seq], lengths[seq], first)
        hat, inverse = normalized(start + vector(2) * attended)
        d_normed = mxu(d_ups[...], grouped_columns(w_up, ways), TRANSPOSED)
        d_middle = g[...].astype(F32) + norm_back(
            d_normed * (gn[...] * (1.0 + vector(4))), hat, inverse
        )
        d_middle_out[...] = d_middle
        d_attended = (vector(2) * d_middle).astype(BF16)
        d_mix[...] = mxu(d_attended, w_out[...], TRANSPOSED).astype(BF16)
        g_sum[...] += mxu(jnp.transpose(mix[...]), d_attended)
        sums[0, 0:1, :] += column_sum(d_normed)
        sums[0, 1:2, :] += column_sum(d_normed * hat)
        sums[0, 2:3, :] += column_sum(d_middle * attended)

        @pl.when(step == steps - 1)
        def _():
            for place in range(ways):
                owner = owner_at(lax.axis_index("narrow"), place)
                spot = pl.ds(pl.multiple_of(owner * share, share), share)
                g_out[place] = g_sum[spot, :].astype(BF16)

    row = pl.BlockSpec((block, width), lambda i: (i, 0))
    return call(
        kernel,
        "middle_back",
        (steps,),
        [smem(), smem(), row, row, row, whole((1, width)), whole((1, width))]
        + [whole(modulation.shape), whole(out_weight.shape), whole(up.shape)]
        + [pl.BlockSpec((block, hidden_width), lambda i: (i, 0))],
        (
            row,
            row,
            pl.BlockSpec((ways, share, width), lambda i: (0, 0, 0)),
            pl.BlockSpec((1, 8, width), lambda i: (i // per_seq, 0, 0)),
        ),
        (
            jax.ShapeDtypeStruct((rows, width), F32),
            jax.ShapeDtypeStruct((rows, width), BF16),
            jax.ShapeDtypeStruct((ways, share, width), BF16),
            jax.ShapeDtypeStruct((seqs, 8, width), F32),
        ),
        [pltpu.VMEM((width, width), F32)],
        rows * width * (2 * hidden_width + 6 * width),
        rows * (width * 12 + hidden_width * 2) + 2 * width * hidden_width,
    )(
        starts, lengths, mixture, tokens, cot, embed, gain, modulation, out_weight, up, d_upper,
    )


class Finale(Steps):
    def __init__(self, ways):
        self.ways = ways
        self.wide = lax.axis_size("wide")

    def scratch(self, columns):
        dma = pltpu.SemaphoreType.DMA
        return [
            pltpu.VMEM((self.ways, 8, columns), F32),
            pltpu.VMEM((self.ways, 8, columns), F32),
            pltpu.VMEM((self.wide, 8, columns), F32),
            dma((self.ways,)),
            dma((self.ways,)),
            dma((self.wide,)),
            dma((self.wide,)),
        ]

    def bind(self, held):
        self.parts, self.narrow_got, self.wide_got, *self.sems = held
        self.locate()

    def others(self):
        targets = []
        for offset in range(1, self.ways):
            targets.append({"narrow": lax.rem(self.at["narrow"] + offset, self.ways)})
        for offset in range(1, self.wide):
            targets.append({"wide": lax.rem(self.at["wide"] + offset, self.wide)})
        return targets

    def greet(self):
        barrier = pltpu.get_barrier_semaphore()
        targets = self.others()
        for target in targets:
            pl.semaphore_signal(
                barrier, inc=1, device_id=target, device_id_type=pl.DeviceIdType.MESH
            )
        pl.semaphore_wait(barrier, len(targets))

    def along_narrow(self, offset):
        target = lax.rem(self.at["narrow"] + offset, self.ways)
        return pltpu.make_async_remote_copy(
            src_ref=self.parts.at[target],
            dst_ref=self.narrow_got.at[self.at["narrow"]],
            send_sem=self.sems[0].at[offset],
            recv_sem=self.sems[1].at[offset],
            device_id={"narrow": target},
            device_id_type=pl.DeviceIdType.MESH,
        )

    def along_wide(self, offset):
        me = self.at["wide"]
        return pltpu.make_async_remote_copy(
            src_ref=self.wide_got.at[me],
            dst_ref=self.wide_got.at[me],
            send_sem=self.sems[2].at[offset],
            recv_sem=self.sems[3].at[offset],
            device_id={"wide": lax.rem(me + offset, self.wide)},
            device_id_type=pl.DeviceIdType.MESH,
        )

    def begin(self):
        for offset in range(1, self.ways):
            self.along_narrow(offset).start()
        me = self.at["narrow"]
        self.narrow_got[pl.ds(me, 1)] = self.parts[pl.ds(me, 1)]

    def spread(self, seqs, row_lanes):
        for offset in range(1, self.ways):
            self.along_narrow(offset).wait()
        me = self.at["wide"]
        for way in range(self.ways):
            self.wide_got[pl.ds(me, 1), way * seqs : (way + 1) * seqs, 0:row_lanes] = (
                self.narrow_got[way : way + 1, 0:seqs, 0:row_lanes]
            )
        total = self.narrow_got[0:1, :, row_lanes:]
        for way in range(1, self.ways):
            total += self.narrow_got[way : way + 1, :, row_lanes:]
        self.wide_got[pl.ds(me, 1), :, row_lanes:] = total
        for offset in range(1, self.wide):
            self.along_wide(offset).start()

    def close(self):
        for offset in range(1, self.wide):
            self.along_wide(offset).wait()


def finish(
    turned, d_parts, tokens, d_middle, mixture, starts, lengths, embed, gain, modulation, weight,
    out_weight, down_bias, active, down, features, rows_two, vectors_two, times, ident, seqs,
    exchange_columns=None, tile=256, block=512, late_block=256,
):
    rows, width = tokens.shape
    ways = lax.axis_size("narrow")
    share = width // ways
    seq_length = rows // seqs
    block, late_block = min(block, seq_length), min(late_block, seq_length)
    per_seq, late_per_seq = seq_length // block, seq_length // late_block
    tiles = width // tile
    columns, hidden_width = modulation.shape[1] // ways, active.shape[1]
    time_width = features.shape[1]
    window = 2 * PAIR
    lanes = columns + time_width + window
    early, middle, late = 3 * tiles, rows // block, rows // late_block
    steps = early + middle + late
    exchange = Exchange([(ways, share, width)] * 3, times, exchange_columns)
    finale = Finale(ways)

    def kernel(*refs):
        (
            starts, lengths, left, c_q, c_k, c_v, tok, d_mid, r_q, r_k, r_v, emb, gn, mod, w_q, w_k, w_v,
            tok_late, mix, w_out, b_down, feat, two, vec,
        ) = refs[:24]
        act, w_down = refs[24:26]
        spot = 26
        g_tok, block_out, g_ada, g_ada_bias, g_vec = refs[spot : spot + 5]
        outs = refs[spot + 5 : spot + 8]
        grads, sums = refs[spot + 8 : spot + 10]
        small = 7
        exchange.bind(
            [grads.at[part] for part in range(3)], outs, refs[spot + 10 + small :]
        )
        finale.bind(refs[spot + 10 : spot + 10 + small])
        step = pl.program_id(0)

        @pl.when(step == 0)
        def _():
            finale.greet()
            sums[...] = jnp.zeros_like(sums)

        exchange.tick(step, steps)

        for part, source in enumerate((c_q, c_k, c_v)):

            @pl.when((step >= part * tiles) & (step < (part + 1) * tiles))
            def _(part=part, source=source):
                cols = pl.ds(pl.multiple_of((step - part * tiles) * tile, tile), tile)
                product = mxu(left[...], source[...]).astype(BF16)
                grads[part, :, :, cols] = product.reshape(ways, share, tile)

        @pl.when((step >= early) & (step < early + middle))
        def _():
            at = step - early
            seq = at // per_seq
            first = (at - seq * per_seq) * block
            start, inside = masked_rows(
                tok[...], emb[...], starts[seq], lengths[seq], first
            )
            hat, inverse = normalized(start)
            d_normed = mxu(r_q[...], w_q[...], TRANSPOSED)
            d_normed += mxu(r_k[...], w_k[...], TRANSPOSED)
            d_normed += mxu(r_v[...], w_v[...], TRANSPOSED)
            scale = mod[pl.ds(seq, 1), width : 2 * width]
            d_start = d_mid[...] + norm_back(d_normed * (gn[...] * (1.0 + scale)), hat, inverse)
            g_tok[...] = jnp.where(inside, 0.0, d_start)
            sums[seq, 0:1, :] += column_sum(d_normed)
            sums[seq, 1:2, :] += column_sum(d_normed * hat)
            sums[seq, 2:3, :] += column_sum(jnp.where(inside, d_start, 0.0))

        @pl.when(step == early + middle)
        def _():
            parts = finale.parts
            embed_sum = jnp.zeros((1, width), F32)
            gain_sum = jnp.zeros((1, width), F32)
            for seq in range(seqs):
                shift, scale = sums[seq, 0:1, :], sums[seq, 1:2, :]
                gain_sum += scale * (1.0 + mod[seq : seq + 1, width : 2 * width])
                embed_sum += sums[seq, 2:3, :]
                row = jnp.concatenate([shift, scale * gn[...], two[seq : seq + 1, :]], axis=1)
                for way in range(ways):
                    parts[way, seq : seq + 1, 0:columns] = row[
                        :, way * columns : (way + 1) * columns
                    ]
            for way in range(ways):
                parts[way, 0:seqs, columns : columns + time_width] = feat[...]
                lower = PAIR * (share * way // PAIR)
                parts[way, 0:1, columns + time_width :] = embed_sum[:, lower : lower + window]
                parts[way, 1:2, columns + time_width :] = gain_sum[:, lower : lower + window]
                parts[way, 2:8, columns + time_width :] = vec[way, 2:8, :]
            finale.begin()

        @pl.when(step == early + middle + 2)
        def _():
            finale.spread(seqs, columns + time_width)

        @pl.when(step >= early + middle)
        def _():
            at = step - early - middle
            seq = at // late_per_seq
            first = (at - seq * late_per_seq) * late_block
            start, _ = masked_rows(
                tok_late[...], emb[...], starts[seq], lengths[seq], first
            )
            attended = mxu(mix[...], w_out[...])
            branch = mxu(act[...], grouped_rows(w_down, ways)) + b_down[...]
            hidden = start + mod[pl.ds(seq, 1), 2 * width : 3 * width] * attended
            block_out[...] = (
                hidden + mod[pl.ds(seq, 1), 5 * width : 6 * width] * branch
            ).astype(BF16)

        @pl.when(step == steps - 1)
        def _():
            finale.close()
            got = finale.wide_got
            every = got[...].reshape(finale.wide * 8, lanes)
            d_mods, feats = every[:, 0:columns], every[:, columns : columns + time_width]
            g_ada[...] = lax.dot_general(
                jnp.transpose(feats), d_mods, PLAIN, precision=FULL_PRECISION,
                preferred_element_type=F32,
            )
            g_ada_bias[...] = column_sum(d_mods)
            total = got[0, :, columns + time_width :]
            for index in range(1, finale.wide):
                total += got[index, :, columns + time_width :]
            g_vec[...] = total
            exchange.rest(steps)

    def column(part):
        return pl.BlockSpec((rows, tile), lambda i: (0, jnp.clip(i - part * tiles, 0, tiles - 1)))

    row = pl.BlockSpec((block, width), lambda i: (jnp.clip(i - early, 0, middle - 1), 0))

    def late_row(wide):
        return pl.BlockSpec(
            (late_block, wide), lambda i: (jnp.maximum(i - early - middle, 0), 0)
        )

    def fixed(shape):
        return pl.BlockSpec(shape, lambda i: (0,) * len(shape))

    return call(
        kernel,
        "finish",
        (steps,),
        [smem(), smem(), whole(turned.shape), column(0), column(1), column(2), row, row, row, row, row]
        + [whole((1, width)), whole((1, width)), whole(modulation.shape)]
        + [column_third(which, width) for which in range(3)]
        + [late_row(width), late_row(width), whole((width, width)), whole((1, width))]
        + [whole(features.shape), whole(rows_two.shape), whole(vectors_two.shape)]
        + [late_row(hidden_width), whole(down.shape)],
        [
            row,
            late_row(width),
            fixed((time_width, columns)),
            fixed((1, columns)),
            fixed((8, window)),
        ]
        + exchange.out_specs(),
        [
            jax.ShapeDtypeStruct((rows, width), F32),
            jax.ShapeDtypeStruct((rows, width), BF16),
            jax.ShapeDtypeStruct((time_width, columns), F32),
            jax.ShapeDtypeStruct((1, columns), F32),
            jax.ShapeDtypeStruct((8, window), F32),
        ]
        + exchange.out_shape(),
        [pltpu.VMEM((3, ways, share, width), BF16), pltpu.VMEM((seqs, 8, width), F32)]
        + finale.scratch(lanes)
        + exchange.scratch(),
        2 * rows * width * (7 * width + hidden_width),
        rows * (width * 24 + 2 * hidden_width),
        0,
        ident,
    )(
        starts, lengths, turned, *d_parts, tokens, d_middle, *d_parts, embed, gain, modulation, weight, weight,
        weight,        tokens, mixture, out_weight, down_bias, features, rows_two, vectors_two, active, down,
    )


def gather_first(small, ada, weight, ident):
    share, wide = weight.shape
    width = wide // 3
    columns = [(0, 0, small.shape[1]), (1, 0, ada.shape[1])]
    columns += [(2, k * width, (k + 1) * width) for k in range(3)]
    gathering = Gather([small.shape, ada.shape, weight.shape], [0] * 5, [0] * 3, columns)

    def kernel(*refs):
        gathering.bind(refs[0:3], refs[3:6], refs[6:])
        gathering.greet()
        gathering.begin(0)
        gathering.begin(1)
        gathering.begin(2)
        for k in range(5):
            gathering.relay(k)
            if k + 3 < 5:
                gathering.begin(k + 3)
            if k > 0:
                gathering.share(k - 1)
        gathering.share(4)
        for k in range(5):
            gathering.close(k)

    return call(
        kernel,
        "gather_first",
        (),
        gathering.in_specs(),
        gathering.out_specs(),
        gathering.out_shape(),
        gathering.scratch(),
        0,
        8 * share * wide,
        0,
        ident,
    )(small, ada, weight)


def assemble(ups, downs, out, qkv):
    share, units = ups[0].shape
    part, width = downs[0].shape
    ways = units // part
    groups = len(ups)

    def kernel(*refs):
        up_in, down_in = refs[:groups], refs[groups : 2 * groups]
        out_in, qkv_in = refs[2 * groups], refs[2 * groups + 1 : 2 * groups + 4]
        g_up, g_down, g_out, g_qkv = refs[2 * groups + 4 :]
        for group in range(groups):
            for way in range(ways):
                lower = (way * groups + group) * part
                g_up[:, lower : lower + part] = up_in[group][
                    :, way * part : (way + 1) * part
                ].astype(F32)
            g_down[group] = down_in[group][...].astype(F32)
        g_out[...] = out_in[...].astype(F32)
        for which in range(3):
            g_qkv[:, which * width : (which + 1) * width] = qkv_in[which][...].astype(F32)

    pace = 4
    small, tall = share // pace, part // pace

    def rows(count, columns):
        return pl.BlockSpec((count, columns), lambda i: (i, 0))

    g_up, g_down, g_out, g_qkv = call(
        kernel,
        "assemble",
        (pace,),
        [rows(small, units)] * groups
        + [rows(tall, width)] * groups
        + [rows(small, width)] * 4,
        (
            rows(small, units * groups),
            pl.BlockSpec((groups, tall, width), lambda i: (0, i, 0)),
            rows(small, width),
            rows(small, 3 * width),
        ),
        (
            jax.ShapeDtypeStruct((share, units * groups), F32),
            jax.ShapeDtypeStruct((groups, part, width), F32),
            jax.ShapeDtypeStruct((share, width), F32),
            jax.ShapeDtypeStruct((share, 3 * width), F32),
        ),
        [],
        0,
        12 * share * units * groups,
    )(*ups, *downs, out, *qkv)
    return g_up, g_down.reshape(groups * part, width), g_out, g_qkv


def per_device(
    tokens,
    timestep,
    span_start,
    span_length,
    mask_embed,
    ada_weight,
    ada_bias,
    norm_first,
    query_key_value_weight,
    output_weight,
    norm_second,
    up_projection_weight,
    up_projection_bias,
    down_projection_weight,
    down_projection_bias,
    cotangent,
):
    seqs = timestep.shape[0]
    rows, width = tokens.shape
    seq_length = rows // seqs
    ways = lax.axis_size("narrow")
    me = lax.axis_index("narrow")
    share = width // ways
    unit_share = down_projection_weight.shape[0]
    part = unit_share // GROUPS
    units = ways * part
    time_width, columns = ada_weight.shape

    vectors = (
        ada_bias, mask_embed, norm_first, norm_second, down_projection_bias, up_projection_bias,
    )
    filled, lower = jnp.zeros((32 * PAIR,), BF16), 0
    for v in vectors:
        filled += jnp.pad(v, (lower, filled.shape[0] - lower - v.shape[0]))
        lower += v.shape[0]
    small = filled.reshape(32, PAIR)
    small, ada, w_qkv = gather_first(small, ada_weight, query_key_value_weight, 0)

    small = small.reshape(ways, -1).astype(F32)
    smalls, lower = [], 0
    for v in vectors:
        smalls.append(small[:, lower : lower + v.shape[0]].reshape(1, -1))
        lower += v.shape[0]
    bias_ada, embed, gain_one, gain_two, bias_down, bias_up = smalls
    features = time_features(timestep, time_width)
    modulation = jnp.einsum(
        "sf,wfc->swc",
        features,
        ada.reshape(ways, time_width, columns).astype(F32),
        precision=FULL_PRECISION,
    ).reshape(seqs, -1) + bias_ada
    tables = rotary_tables(seq_length)

    qkv, turned_one = project(
        tokens, span_start, span_length, embed, gain_one, modulation, w_qkv, tables, seqs
    )
    thirds = [
        (which, third * size, (third + 1) * size)
        for which, size in ((1, unit_share * ways // 3), (2, width // 3))
        for third in range(3)
    ]
    mixture, total, w_out, w_up, w_down = attend(
        qkv,
        [output_weight, up_projection_weight, down_projection_weight],
        [0, 1, 3, 6, 8, 11, 13],
        [5, 5, 2],
        [(0, 0, width)] + thirds,
        1,
        seqs,
    )
    normed_two = middle_norm(
        mixture, tokens, span_start, span_length, embed, gain_two, modulation, w_out, seqs
    )
    bias_up = jnp.swapaxes(bias_up.reshape(ways, GROUPS, part), 0, 1).reshape(1, -1)
    head_times = paced([8, 9, 10, 11], [1, 3, 2, 2, 2, 1]) + paced([16, 17, 18, 19], [1, 3])
    active, d_upper, g_bias, d_gate_two, g_sum, *swaps = hidden_units(
        normed_two, cotangent, modulation, w_up, bias_up, w_down, head_times, 2, seqs
    )
    d_gate_two += bias_down * g_sum
    d_middle, d_mixture, g_out, sums_two = middle_back(
        mixture, tokens, cotangent, span_start, span_length, embed, gain_two, modulation, w_out,
        d_upper, w_up, seqs,
    )
    d_q, d_k, d_v, *done = attend_back(
        qkv, mixture, d_mixture, total, tables, swaps[2:] + [g_out],
        ["tail"] * 2 + ["whole"] * 3, halved(swaps[2:] + [g_out]),
        [[k, k + 1] + [k + 1 + n for n in (3, 5, 7, 9)] for k in range(4)]
        + paced([0, 1, 2, 4, 5, 7], [2, 3, 2, 2, 3, 2]),
        3, seqs,
    )
    scale_two = modulation[:, 4 * width : 5 * width]
    rows_two = jnp.concatenate(
        [sums_two[:, 2], sums_two[:, 0], sums_two[:, 1] * gain_two, d_gate_two], axis=1
    )
    g_norm_two = jnp.sum(sums_two[:, 1] * (1.0 + scale_two), axis=0)
    g_bias_down = jnp.sum(modulation[:, 5 * width :] * g_sum, axis=0)
    lowers = [PAIR * (share * way // PAIR) for way in range(ways)]
    vectors_two = jnp.stack(
        [
            jnp.stack([v[lower : lower + 2 * PAIR] for lower in lowers])
            for v in (g_norm_two, g_norm_two, g_norm_two, g_bias_down)
        ]
        + [g_bias[0].reshape(GROUPS, ways, part)[group] for group in range(GROUPS)]
        + [jnp.zeros((ways, 2 * PAIR), F32)],
        axis=1,
    )
    grad_tokens, block_out, grad_ada_weight, grad_ada_bias, vectors, *g_qkv = finish(
        turned_one, (d_q, d_k, d_v), tokens, d_middle, mixture, span_start, span_length, embed,
        gain_one, modulation, w_qkv, w_out, bias_down, active, w_down, features, rows_two,
        vectors_two,
        FINISH_TIMES, 4, seqs,
    )
    skip = lax.rem(share * me, PAIR)
    own = lax.dynamic_slice_in_dim(vectors[:4], skip, share, 1)
    g_ups, g_downs = (swaps[0], *done[0:4:2]), (swaps[1], *done[1:4:2])
    g_up, g_down, g_out, g_qkv = assemble(g_ups, g_downs, done[4], g_qkv)
    return (
        block_out,
        grad_tokens,
        own[0],
        grad_ada_weight,
        grad_ada_bias[0],
        own[1],
        g_qkv,
        g_out,
        own[2],
        g_up,
        vectors[4 : 4 + GROUPS].reshape(-1),
        g_down,
        own[3],
    )


def solution(mesh):
    rows = P(("wide", "narrow"), None)
    per_seq = P(("wide", "narrow"))
    vector, matrix, columns = P("narrow"), P("narrow", None), P(None, "narrow")
    return jax.shard_map(
        per_device,
        mesh=mesh,
        in_specs=(
            rows, per_seq, per_seq, per_seq, vector, columns, vector, vector,
            matrix, matrix, vector, matrix, vector, matrix, vector, rows,
        ),
        out_specs=(
            rows, rows, vector, columns, vector, vector, matrix, matrix, vector, matrix,
            vector, matrix, vector,
        ),
        check_vma=False,
    )
```

```python
import math

import jax
import jax.numpy as jnp
import numpy as np
from jax import lax
from jax.experimental import pallas as pl
from jax.experimental.pallas import tpu as pltpu
from jax.sharding import PartitionSpec as P

HEAD = 64
PAIR = 2 * HEAD
GROUPS = 3
FINISH_TIMES = [
    [1, 3, 7, 8, 9, 11, 13], [2, 4, 8, 9, 10, 13, 15], [3, 5, 9, 10, 12, 15, 17],
    [4, 6, 10, 12, 14, 17, 18], [5, 6, 10, 12, 14, 17, 18], [6, 7, 12, 14, 16, 18, 18],
]
EPSILON = 1e-05
FULL_PRECISION = lax.Precision.HIGHEST
F32 = jnp.float32
BF16 = jnp.bfloat16
SCALE = 1.0 / math.sqrt(HEAD)
SCALE2 = SCALE * math.log2(math.e)
VMEM_BYTES = 60 << 20
PLAIN = (((1,), (0,)), ((), ()))
TRANSPOSED = (((1,), (1,)), ((), ()))


def mxu(left, right, dims=PLAIN):
    return lax.dot_general(left, right, dims, preferred_element_type=F32)


def call(
    kernel, name, grid, in_specs, out_specs, out_shape, scratch, flops, moved, exps=0, ident=None
):
    return pl.pallas_call(
        kernel,
        name=name,
        grid=grid,
        in_specs=in_specs,
        out_specs=out_specs,
        out_shape=out_shape,
        scratch_shapes=scratch,
        compiler_params=pltpu.CompilerParams(
            vmem_limit_bytes=VMEM_BYTES, collective_id=ident, has_side_effects=ident is not None
        ),
        cost_estimate=pl.CostEstimate(flops=flops, bytes_accessed=moved, transcendentals=exps),
    )


def whole(shape):
    return pl.BlockSpec(shape, lambda *_: (0,) * len(shape), pipeline_mode=pl.Buffered(1))


def column_third(which, width):
    return pl.BlockSpec((width, width), lambda *_: (0, which), pipeline_mode=pl.Buffered(1))


def smem():
    return pl.BlockSpec(memory_space=pltpu.SMEM)


def time_features(step_ids, feature_count):
    halfway = feature_count // 2
    spacing = jnp.exp(-math.log(10000.0) * jnp.arange(halfway, dtype=F32) / halfway)
    angles = step_ids.astype(F32)[:, None] * spacing[None, :]
    return jax.nn.silu(jnp.concatenate([jnp.cos(angles), jnp.sin(angles)], axis=-1))


def rotary_tables(seq_length):
    halfway = HEAD // 2
    spacing = np.exp(-math.log(10000.0) * np.arange(halfway, dtype=np.float32) / halfway)
    angles = np.arange(seq_length, dtype=np.float32)[:, None] * spacing.astype(np.float32)
    cosine, sine = np.cos(angles), np.sin(angles)
    signed = np.concatenate([-sine, sine] * 2, axis=-1)
    return np.concatenate([cosine] * 4, axis=-1), signed


def partner_lanes(v):
    lane = lax.broadcasted_iota(jnp.int32, (1, PAIR), 1)
    return jnp.where(lax.rem(lane, HEAD) < HEAD // 2, from_ahead(v), from_behind(v))


def from_ahead(v):
    return pltpu.roll(v, PAIR - HEAD // 2, 1)


def from_behind(v):
    return pltpu.roll(v, HEAD // 2, 1)


def masked_rows(tokens, embed, start, length, first_row):
    rows = tokens.shape[0]
    position = lax.broadcasted_iota(jnp.int32, (rows, 1), 0) + first_row
    inside = (position >= start) & (position < start + length)
    return jnp.where(inside, embed, tokens.astype(F32)), inside


def normalized(rows):
    centre = rows - jnp.mean(rows, axis=-1, keepdims=True)
    spread = jnp.mean(centre * centre, axis=-1, keepdims=True)
    inverse = lax.rsqrt(spread + EPSILON)
    return centre * inverse, inverse


def norm_back(d_out, hat, inverse):
    return inverse * (
        d_out
        - jnp.mean(d_out, axis=-1, keepdims=True)
        - hat * jnp.mean(d_out * hat, axis=-1, keepdims=True)
    )


def column_sum(v):
    return jnp.sum(v, axis=0, keepdims=True)


def store_shares(target, value, cols):
    me, ways = lax.axis_index("narrow"), lax.axis_size("narrow")
    share = value.shape[0] // ways
    for place in range(ways):
        lower = pl.multiple_of(place_of(me, place) * share, share)
        target[pl.ds(lower, share), cols] = value[place * share : (place + 1) * share, :]


def place_of(me, other):
    core = lax.rem(me + other, 2)
    chip = lax.rem(me // 2 + other // 2, 2)
    return 2 * (1 - core) + 1 - chip


def owner_at(me, place):
    core, chip = 1 - place // 2, 1 - lax.rem(place, 2)
    return 2 * lax.rem(me // 2 + chip, 2) + lax.rem(me + core, 2)


def project(tokens, starts, lengths, embed, gain, modulation, weight, tables, seqs, block=512):
    rows, width = tokens.shape
    seq_length = rows // seqs
    block = min(block, seq_length)
    per_seq = seq_length // block
    pairs = width // PAIR

    def kernel(starts, lengths, tok, emb, gn, mod, w_q, w_k, w_v, cos, sin, out, nt):
        step = pl.program_id(0)
        seq = step // per_seq
        first = (step - seq * per_seq) * block
        start, _ = masked_rows(tok[...], emb[...], starts[seq], lengths[seq], first)
        hat, _ = normalized(start)
        shift = mod[pl.ds(seq, 1), 0:width]
        scale = mod[pl.ds(seq, 1), width : 2 * width]
        normed = (hat * (gn[...] * (1.0 + scale)) + shift).astype(BF16)
        store_shares(nt, jnp.transpose(normed), slice(None))
        for which, w in enumerate((w_q, w_k)):
            turned = mxu(normed, w[...])
            for part in range(pairs):
                v = turned[:, part * PAIR : (part + 1) * PAIR]
                v = v * cos[...] + partner_lanes(v) * sin[...]
                lower = which * width + part * PAIR
                out[:, lower : lower + PAIR] = v.astype(BF16)
        out[:, 2 * width :] = mxu(normed, w_v[...]).astype(BF16)

    table = pl.BlockSpec((block, PAIR), lambda i: (lax.rem(i, per_seq), 0))
    return call(
        kernel,
        "project",
        (rows // block,),
        [
            smem(),
            smem(),
            pl.BlockSpec((block, width), lambda i: (i, 0)),
            whole((1, width)),
            whole((1, width)),
            whole(modulation.shape),
            column_third(0, width),
            column_third(1, width),
            column_third(2, width),
            table,
            table,
        ],
        (
            pl.BlockSpec((block, 3 * width), lambda i: (i, 0)),
            pl.BlockSpec((width, block), lambda i: (0, i)),
        ),
        (
            jax.ShapeDtypeStruct((rows, 3 * width), BF16),
            jax.ShapeDtypeStruct((width, rows), BF16),
        ),
        [],
        2 * rows * width * 3 * width,
        rows * width * 10 + 6 * width * width,
    )(starts, lengths, tokens, embed, gain, modulation, weight, weight, weight, *tables)


def flip(index, stride):
    return index + stride * (1 - 2 * lax.rem(index // stride, 2))


def exchange_stages():
    count = lax.axis_size("wide")
    strides = [1 << bit for bit in range(1, count.bit_length() - 1)]
    return [("pair", "narrow", 1), ("chip", "narrow", 2), ("split", "wide", 1)] + [
        ("full", "wide", stride) for stride in strides
    ] + [("join", "wide", 1)]


class Steps:
    def in_specs(self):
        return [pl.BlockSpec(memory_space=pl.ANY)] * self.count

    out_specs = in_specs

    def locate(self):
        self.at = {axis: lax.axis_index(axis) for axis in ("wide", "narrow")}
        self.odd = lax.rem(self.at["wide"], 2)

    def half_of(self, rows, which, lower=0):
        side = self.odd if which == 0 else 1 - self.odd
        return pl.ds(pl.multiple_of(lower + side * (rows // 2), rows // 2), rows // 2)

    def greet(self):
        barrier = pltpu.get_barrier_semaphore()
        for axis, stride in self.partners:
            pl.semaphore_signal(
                barrier,
                inc=1,
                device_id={axis: flip(self.at[axis], stride)},
                device_id_type=pl.DeviceIdType.MESH,
            )
        pl.semaphore_wait(barrier, len(self.partners))

    def push(self, source, target, sent, got, axis, stride):
        return pltpu.make_async_remote_copy(
            src_ref=source,
            dst_ref=target,
            send_sem=sent,
            recv_sem=got,
            device_id={axis: flip(self.at[axis], stride)},
            device_id_type=pl.DeviceIdType.MESH,
        )

    def tick(self, now, last, bunch=6):
        planned = sorted(self.plan(), key=lambda item: item[:3])
        times = sorted({item[0] for item in planned if item[0] < last})
        for lower in sorted({when - when % bunch for when in times}):

            @pl.when((now >= lower) & (now < lower + bunch))
            def _(lower=lower):
                for when in times:
                    if lower <= when < lower + bunch:
                        pl.when(now == when)(lambda when=when: self.take(planned, when))

    def take(self, planned, when):
        if when == 0:
            self.greet()
        for item in planned:
            if item[0] == when:
                item[3]()

    def rest(self, last):
        for item in sorted(self.plan(), key=lambda item: item[:3]):
            if item[0] >= last:
                item[3]()


class Gather(Steps):
    partners = (("narrow", 1), ("narrow", 2), ("wide", 1))

    def __init__(self, shapes, begins, waits, columns=None):
        columns = columns or [(k, 0, shape[1]) for k, shape in enumerate(shapes)]
        self.arrays, self.columns = shapes, columns
        self.shapes = [(shapes[k][0], upper - lower) for k, lower, upper in columns]
        self.begins, self.waits = begins, waits
        self.count = len(columns)

    def in_specs(self):
        return [pl.BlockSpec(memory_space=pl.ANY)] * len(self.arrays)

    out_specs = in_specs

    def out_shape(self):
        return [jax.ShapeDtypeStruct((4 * rows, cols), BF16) for rows, cols in self.arrays]

    def scratch(self):
        dma, held = pltpu.SemaphoreType.DMA, []
        for shape in self.shapes:
            held += [dma((5,)), dma((5,)), dma((2,)), pltpu.VMEM(shape, BF16)]
        return held

    def bind(self, ins, outs, held):
        self.refs = [
            (ins[k].at[:, lower:upper], outs[k].at[:, lower:upper])
            + tuple(held[4 * part : 4 * part + 4])
            for part, (k, lower, upper) in enumerate(self.columns)
        ]
        self.locate()

    def block(self, k, index, which=None):
        rows = self.shapes[k][0]
        if which is None:
            return pl.ds(pl.multiple_of(index * rows, rows), rows)
        return self.half_of(rows, which, index * rows)

    def remote(self, k, step):
        source, out, sent, got, _, _ = self.refs[k]
        me, across = self.at["narrow"], flip(self.at["narrow"], 2)
        axis, stride = (("narrow", 1), ("narrow", 2), ("wide", 1), ("narrow", 1), ("narrow", 1))[step]
        if step == 0:
            ends = (source, out.at[self.block(k, me), :])
        elif step == 1:
            half = self.half_of(self.shapes[k][0], 0)
            ends = (source.at[half, :], out.at[self.block(k, me, 0), :])
        else:
            spot = self.block(k, across, 1 if step == 4 else 0)
            ends = (out.at[spot, :], out.at[spot, :])
        return self.push(*ends, sent.at[step], got.at[step], axis, stride)

    def local(self, k, which):
        source, out, _, _, near, kept = self.refs[k]
        if which == 0:
            return pltpu.make_async_copy(source, kept, near.at[0])
        return pltpu.make_async_copy(
            kept, out.at[self.block(k, self.at["narrow"]), :], near.at[1]
        )

    def begin(self, k):
        self.remote(k, 1).start()
        self.remote(k, 0).start()
        self.local(k, 0).start()

    def relay(self, k):
        self.local(k, 0).wait()
        self.local(k, 1).start()
        self.remote(k, 1).wait()
        self.remote(k, 2).start()
        self.remote(k, 3).start()

    def share(self, k):
        self.remote(k, 2).wait()
        self.remote(k, 4).start()

    def close(self, k):
        self.remote(k, 0).wait()
        self.remote(k, 3).wait()
        self.remote(k, 4).wait()
        self.local(k, 1).wait()

    def plan(self):
        planned = []
        for k in range(self.count):
            when = self.begins[k]
            planned.append((when, 0, k, lambda k=k: self.begin(k)))
            for wait, act in zip(self.waits, (self.relay, self.share, self.close)):
                when += wait
                planned.append((when, 1, k, lambda k=k, act=act: act(k)))
        return planned


class Exchange(Steps):
    def __init__(self, shapes, times, columns=None, spans=None):
        columns = columns or [(k, 0, shape[-1]) for k, shape in enumerate(shapes)]
        spans = spans or ["whole"] * len(shapes)
        self.stages = exchange_stages()
        self.arrays, self.columns = [shape[-2:] for shape in shapes], columns
        self.shapes = [(self.arrays[k][0], upper - lower) for k, lower, upper in columns]
        self.spans = [spans[k] for k, _, _ in columns]
        self.firsts = [2 if span == "tail" else 0 for span in self.spans]
        self.lasts = [1 if span == "head" else len(self.stages) - 1 for span in self.spans]
        self.times = times
        self.count = len(columns)
        self.partners = sorted({(axis, stride) for _, axis, stride in self.stages})

    def in_specs(self):
        return [pl.BlockSpec(memory_space=pl.ANY)] * len(self.arrays)

    out_specs = in_specs

    def out_shape(self):
        return [jax.ShapeDtypeStruct(shape, BF16) for shape in self.arrays]

    def scratch(self):
        held = []
        dma = pltpu.SemaphoreType.DMA
        for (rows, cols), span in zip(self.shapes, self.spans):
            early, late = span != "tail", span != "head"
            held += [
                pltpu.VMEM((2, rows, cols) if early else (2, 16, PAIR), BF16),
                pltpu.VMEM((2 if early else 1, rows, cols), BF16),
                pltpu.VMEM((rows, cols) if early else (16, PAIR), BF16),
                pltpu.VMEM((len(self.stages) - 3, rows // 2, cols) if late else (1, 16, PAIR), BF16),
                pltpu.VMEM((rows // 2, cols) if late else (16, PAIR), BF16),
                dma((len(self.stages),)),
                dma((len(self.stages),)),
                dma((2,)),
            ]
        return held

    def bind(self, ins, outs, held):
        self.refs = []
        for part, (k, lower, upper) in enumerate(self.columns):
            every = (slice(None),) * (1 if self.spans[part] == "tail" else 2)
            self.refs.append(
                (ins[k].at[every + (slice(lower, upper),)], outs[k].at[:, lower:upper])
                + tuple(held[8 * part : 8 * part + 8])
            )
        self.locate()

    def own(self, k):
        kept = self.refs[k][3]
        return kept.at[0 if self.spans[k] == "tail" else 1]

    def remote(self, k, step):
        source, out, pair, kept, chip, halves, mine, sent, got, _ = self.refs[k]
        kind, axis, stride = self.stages[step]
        rows = self.shapes[k][0]
        if kind == "pair":
            ends = (source.at[0:2], pair)
        elif kind == "chip":
            ends = (kept.at[0], chip)
        elif kind == "split":
            ends = (self.own(k).at[self.half_of(rows, 1), :], halves.at[0])
        elif kind == "full":
            ends = (mine, halves.at[step - 2])
        else:
            ends = (mine, out.at[self.half_of(rows, 0), :])
        return self.push(*ends, sent.at[step], got.at[step], axis, stride)

    def load(self, k):
        source, kept, near = self.refs[k][0], self.refs[k][3], self.refs[k][9]
        if self.spans[k] == "tail":
            return pltpu.make_async_copy(source, kept.at[0], near.at[0])
        return pltpu.make_async_copy(source.at[2:4], kept, near.at[0])

    def store(self, k):
        out, mine, near = self.refs[k][1], self.refs[k][6], self.refs[k][9]
        if self.spans[k] == "head":
            return pltpu.make_async_copy(self.own(k), out, near.at[1])
        half = self.half_of(self.shapes[k][0], 0)
        return pltpu.make_async_copy(mine, out.at[half, :], near.at[1])

    def begin(self, k):
        self.load(k).start()
        if self.spans[k] != "tail":
            self.remote(k, 0).start()

    def enter(self, k):
        self.load(k).wait()
        self.remote(k, 2).start()

    def end(self, k, step):
        _, _, pair, kept, chip, halves, mine, _, _, _ = self.refs[k]
        kind = self.stages[step][0]
        self.remote(k, step).wait()
        if kind == "pair":
            self.load(k).wait()
            kept[...] = (kept[...].astype(F32) + pair[...].astype(F32)).astype(BF16)
        elif kind == "chip":
            kept[1] = (kept[1].astype(F32) + chip[...].astype(F32)).astype(BF16)
        elif kind == "split":
            half = self.half_of(self.shapes[k][0], 0)
            own = self.own(k)[half, :].astype(F32)
            mine[...] = (own + halves[0].astype(F32)).astype(BF16)
        elif kind == "full":
            mine[...] = (mine[...].astype(F32) + halves[step - 2].astype(F32)).astype(BF16)
        if step < self.lasts[k]:
            self.remote(k, step + 1).start()
        if step == max(self.lasts[k] - 1, 1):
            self.store(k).start()
        if step == self.lasts[k]:
            self.store(k).wait()

    def plan(self):
        planned = []
        for k, (begin, *ends) in enumerate(self.times):
            first, last = self.firsts[k], self.lasts[k]
            planned.append((begin, 0, k, lambda k=k: self.begin(k)))
            if first:
                planned.append((ends[0], 1, k, lambda k=k: self.enter(k)))
                ends = [0] + ends
            for step in range(first, last + 1):
                when = ends[-1] if step == last else ends[min(step, 4)]
                planned.append((when, 1, k, lambda k=k, step=step: self.end(k, step)))
        return planned


def paced(begins, waits):
    return [[begin + sum(waits[:count]) for count in range(len(waits) + 1)] for begin in begins]


def head_mask(v, half):
    lane = lax.broadcasted_iota(jnp.int32, (1, PAIR), 1)
    keep = (lane < HEAD) if half == 0 else (lane >= HEAD)
    return jnp.where(keep, v, jnp.zeros_like(v))


def attend(qkv, shares, begins, waits, columns, ident, seqs, block=512, per=3):
    rows, width = qkv.shape[0], qkv.shape[1] // 3
    seq_length = rows // seqs
    block = min(block, seq_length)
    pairs = width // PAIR
    count = seq_length // block
    steps = pairs // per
    items = per * count
    wide = per * PAIR

    gathering = Gather([v.shape for v in shares], begins, waits, columns)
    many = len(shares)
    ticks = seqs * steps * items

    def kernel(*refs):
        q_ref, k_ref, v_ref = refs[:3]
        out, total = refs[3 + many : 5 + many]
        v_turned, out_turned, held = refs[5 + 2 * many : 8 + 2 * many]
        gathering.bind(refs[3 : 3 + many], refs[5 + many : 5 + 2 * many], refs[8 + 2 * many :])
        spot = pl.program_id(0) * steps + pl.program_id(1)
        v_turned[...] = jnp.transpose(v_ref[...])

        def place(i):
            pair = i // count
            part = i - pair * count
            return (
                pair,
                pl.ds(pl.multiple_of(pair * PAIR, PAIR), PAIR),
                pl.ds(pl.multiple_of(part * block, block), block),
            )

        def score(i, half):
            _, cols, part = place(i)
            held[half] = mxu(k_ref[:, cols], head_mask(q_ref[part, cols], half), TRANSPOSED)

        def finish(i, half):
            pair, _, part = place(i)
            scores = held[half]
            top = jnp.max(scores, axis=0, keepdims=True)
            exponent = jnp.exp2(scores * SCALE2 - top * SCALE2).astype(BF16)
            head = pl.ds(pl.multiple_of(pair * PAIR + half * HEAD, HEAD), HEAD)
            left = jnp.concatenate([v_turned[head, :], jnp.ones((16, seq_length), BF16)], axis=0)
            mixed = mxu(left, exponent)
            denominator = mixed[HEAD : HEAD + 1]
            out_turned[head, part] = mixed[:HEAD] * (1.0 / denominator)
            total[0, pair, half : half + 1, part] = top * SCALE2 + jnp.log2(denominator)

        score(0, 0)

        def body(i, carry):
            gathering.tick(spot * items + i, ticks)
            score(i, 1)
            finish(i, 0)
            score(jnp.minimum(i + 1, items - 1), 0)
            finish(i, 1)
            return carry

        lax.fori_loop(0, items, body, 0)
        out[...] = jnp.transpose(out_turned[...]).astype(BF16)

        @pl.when(spot == seqs * steps - 1)
        def _():
            gathering.rest(ticks)

    def part_of(which):
        return pl.BlockSpec((seq_length, wide), lambda s, p: (s, which * steps + p))

    return call(
        kernel,
        "attend",
        (seqs, steps),
        [part_of(0), part_of(1), part_of(2)] + gathering.in_specs(),
        [part_of(0), pl.BlockSpec((1, per, 2, seq_length), lambda s, p: (s, p, 0, 0))]
        + gathering.out_specs(),
        [
            jax.ShapeDtypeStruct((rows, width), BF16),
            jax.ShapeDtypeStruct((seqs, pairs, 2, seq_length), F32),
        ]
        + gathering.out_shape(),
        [
            pltpu.VMEM((wide, seq_length), BF16),
            pltpu.VMEM((wide, seq_length), F32),
            pltpu.VMEM((2, seq_length, block), F32),
        ]
        + gathering.scratch(),
        16 * rows * seq_length * width,
        rows * width * 8,
        rows * seq_length * width // HEAD,
        ident,
    )(qkv, qkv, qkv, *shares)


def attend_back(
    qkv, mixture, d_mixture, total, tables, pieces, spans, columns, times, ident, seqs, block=512,
    per=3,
):
    rows, width = mixture.shape
    seq_length = rows // seqs
    block = min(block, seq_length)
    pairs = width // PAIR
    count = seq_length // block
    steps = pairs // per
    items = per * count
    wide = per * PAIR
    exchange = Exchange([v.shape for v in pieces], times, columns, spans)
    many = len(pieces)
    ticks = seqs * steps * items

    def kernel(*refs):
        q_ref, k_ref, v_ref, mix, grad, tot, cos, sin = refs[:8]
        dq, dk, dv = refs[8 + many : 11 + many]
        k_turned, dq_turned, dk_sum, dv_sum, inner, s_held, p_held = refs[
            11 + 2 * many : 18 + 2 * many
        ]
        exchange.bind(refs[8 : 8 + many], refs[11 + many : 11 + 2 * many], refs[18 + 2 * many :])
        spot = pl.program_id(0) * steps + pl.program_id(1)
        k_turned[...] = jnp.transpose(k_ref[...])
        product = jnp.transpose(mix[...].astype(F32) * grad[...].astype(F32))
        for pair in range(per):
            for half in range(2):
                lower = pair * PAIR + half * HEAD
                inner[pair, half : half + 1, :] = column_sum(product[lower : lower + HEAD, :])
        dk_sum[...] = jnp.zeros_like(dk_sum)
        dv_sum[...] = jnp.zeros_like(dv_sum)

        def body(i, carry):
            exchange.tick(spot * items + i, ticks)
            pair = i // count
            part = i - pair * count
            cols = pl.ds(pl.multiple_of(pair * PAIR, PAIR), PAIR)
            part = pl.ds(pl.multiple_of(part * block, block), block)
            for half in range(2):
                head = pl.ds(pl.multiple_of(pair * PAIR + half * HEAD, HEAD), HEAD)
                query = head_mask(q_ref[part, cols], half)
                cot = head_mask(grad[part, cols], half)
                s_held[half] = mxu(k_ref[:, cols], query, TRANSPOSED)
                p_held[half] = mxu(v_ref[:, cols], cot, TRANSPOSED)
                probs = jnp.exp2(s_held[half] * SCALE2 - tot[0, pair, half : half + 1, part])
                d_scores = (probs * (p_held[half] - inner[pair, half : half + 1, part])).astype(BF16)
                dv_sum[:, cols] += mxu(probs.astype(BF16), cot)
                dk_sum[:, cols] += mxu(d_scores, query)
                dq_turned[head, part] = mxu(k_turned[head, :], d_scores)
            return carry

        lax.fori_loop(0, items, body, 0)
        d_queries = jnp.transpose(dq_turned[...])
        for source, target in ((d_queries, dq), (dk_sum, dk)):
            for pair in range(per):
                v = source[:, pair * PAIR : (pair + 1) * PAIR] * SCALE
                v = v * cos[...] - partner_lanes(v) * sin[...]
                target[:, pair * PAIR : (pair + 1) * PAIR] = v.astype(BF16)
        dv[...] = dv_sum[...].astype(BF16)

        @pl.when(spot == seqs * steps - 1)
        def _():
            exchange.rest(ticks)

    def part_of(which):
        return pl.BlockSpec((seq_length, wide), lambda s, p: (s, which * steps + p))

    table = whole((seq_length, PAIR))
    grads = jax.ShapeDtypeStruct((rows, width), BF16)
    return call(
        kernel,
        "attend_back",
        (seqs, steps),
        [part_of(0), part_of(1), part_of(2), part_of(0), part_of(0)]
        + [pl.BlockSpec((1, per, 2, seq_length), lambda s, p: (s, p, 0, 0))]
        + [table] * 2
        + exchange.in_specs(),
        [part_of(0), part_of(0), part_of(0)] + exchange.out_specs(),
        [grads, grads, grads] + exchange.out_shape(),
        [
            pltpu.VMEM((wide, seq_length), BF16),
            pltpu.VMEM((wide, seq_length), F32),
            pltpu.VMEM((seq_length, wide), F32),
            pltpu.VMEM((seq_length, wide), F32),
            pltpu.VMEM((per, 2, seq_length), F32),
            pltpu.VMEM((2, seq_length, block), F32),
            pltpu.VMEM((2, seq_length, block), F32),
        ]
        + exchange.scratch(),
        40 * rows * seq_length * width,
        rows * width * 16,
        rows * seq_length * width // HEAD,
        ident,
    )(qkv, qkv, qkv, mixture, d_mixture, total, *tables, *pieces)


def middle_norm(mixture, tokens, starts, lengths, embed, gain, modulation, weight, seqs, block=512):
    rows, width = tokens.shape
    seq_length = rows // seqs
    block = min(block, seq_length)
    per_seq = seq_length // block

    def kernel(starts, lengths, mix, tok, emb, gn, mod, w, out):
        step = pl.program_id(0)
        seq = step // per_seq
        first = (step - seq * per_seq) * block
        start, _ = masked_rows(tok[...], emb[...], starts[seq], lengths[seq], first)
        middle = start + mod[pl.ds(seq, 1), 2 * width : 3 * width] * mxu(mix[...], w[...])
        hat, _ = normalized(middle)
        shift = mod[pl.ds(seq, 1), 3 * width : 4 * width]
        scale = mod[pl.ds(seq, 1), 4 * width : 5 * width]
        out[...] = (hat * (gn[...] * (1.0 + scale)) + shift).astype(BF16)

    row = pl.BlockSpec((block, width), lambda i: (i, 0))
    return call(
        kernel,
        "middle_norm",
        (rows // block,),
        [smem(), smem(), row, row, whole((1, width)), whole((1, width)), whole(modulation.shape)]
        + [whole(weight.shape)],
        row,
        jax.ShapeDtypeStruct((rows, width), BF16),
        [],
        2 * rows * width * width,
        rows * width * 6,
    )(starts, lengths, mixture, tokens, embed, gain, modulation, weight)


def gelu_pair(v):
    root = math.sqrt(2.0 / math.pi)
    square = v * v
    near = 0.5 + 0.5 * jnp.tanh(v * (root + (root * 0.044715) * square))
    active = v * near
    bend = 2.0 * root + (6.0 * root * 0.044715) * square
    return active, near + (active * (1.0 - near)) * bend


def grouped_rows(ref, ways):
    part = ref.shape[0] // (ways * GROUPS)
    lowers = [(way * GROUPS + group) * part for group in range(GROUPS) for way in range(ways)]
    return jnp.concatenate([ref[lower : lower + part, :] for lower in lowers], axis=0)


def grouped_columns(ref, ways):
    part = ref.shape[1] // (ways * GROUPS)
    lowers = [(way * GROUPS + group) * part for group in range(GROUPS) for way in range(ways)]
    return jnp.concatenate([ref[:, lower : lower + part] for lower in lowers], axis=1)


def halved(arrays):
    return [
        (k, half * v.shape[-1] // 2, (half + 1) * v.shape[-1] // 2)
        for k, v in enumerate(arrays)
        for half in range(2)
    ]


def hidden_units(normed, cot, modulation, up, up_bias, down, times, ident, seqs, block=512):
    rows, width = normed.shape
    ways = lax.axis_size("narrow")
    units = up.shape[1] // GROUPS
    share, part_units = width // ways, units // ways
    seq_length = rows // seqs
    block = min(block, seq_length)
    per_seq = seq_length // block
    steps = rows // block
    turn = steps + ways
    shape_up, shape_down = (ways, share, units), (ways, part_units, width)
    traded = [jax.ShapeDtypeStruct(v, BF16) for v in (shape_up, shape_down) * 2]
    exchange = Exchange(
        [v.shape for v in traded], times, halved(traded), ["whole"] * 2 + ["head"] * 2
    )

    def kernel(*refs):
        nrm, g, mod, b_up = refs[:4]
        w_ups, w_downs = refs[4 : 4 + ways], refs[4 + ways : 4 + 2 * ways]
        act, d_up, g_bias, d_gate, g_sum = refs[4 + 2 * ways : 9 + 2 * ways]
        outs, left = refs[9 + 2 * ways : 15 + 2 * ways], refs[15 + 2 * ways :]
        n_turned, g_turned, a_held, u_held, down_held, g_up, g_down, near = left[:8]
        exchange.bind(
            [g_up.at[0], g_down.at[0], g_up.at[1], g_down.at[1]], outs[:4], left[8:]
        )
        step = pl.program_id(0)
        group = step // turn
        at = step - group * turn

        @pl.when(step == 0)
        def _():
            exchange.greet()
            n_turned[width:, :] = jnp.ones((16, rows), BF16)
            d_gate[...] = jnp.zeros_like(d_gate)
            g_sum[...] = jnp.zeros_like(g_sum)

        exchange.tick(step, GROUPS * turn)

        @pl.when(at == 0)
        def _():
            for way in range(ways):
                down_held[way] = w_downs[way][...]

        part = pl.ds(pl.multiple_of(jnp.minimum(at, steps - 1) * block, block), block)

        @pl.when(at < steps)
        def _():
            seq = at // per_seq
            cotangent = g[...].astype(F32)
            d_branch = (mod[pl.ds(seq, 1), 5 * width : 6 * width] * cotangent).astype(BF16)
            for way in range(ways):
                cols = slice(way * part_units, (way + 1) * part_units)
                upper = mxu(nrm[...], w_ups[way][...]) + b_up[:, cols]
                d_active = mxu(d_branch, w_downs[way][...], TRANSPOSED)
                active, slope = gelu_pair(upper)
                active = active.astype(BF16)
                d_upper = (d_active * slope).astype(BF16)
                act[:, cols] = active
                a_held[part, cols] = active
                d_up[:, cols] = d_upper
                u_held[part, cols] = d_upper

        @pl.when(step < steps)
        def _():
            store_shares(n_turned, jnp.transpose(nrm[...]), part)
            g_turned[:, part] = jnp.transpose(g[...])
            g_sum[pl.ds(at // per_seq, 1), :] += column_sum(g[...].astype(F32))

        @pl.when(at >= steps)
        def _():
            place = at - steps
            owner = owner_at(exchange.at["narrow"], place)
            cols = pl.ds(pl.multiple_of(owner * part_units, part_units), part_units)
            product = mxu(n_turned[...], u_held[:, cols])
            g_bias[:, cols] = product[width : width + 1]
            g_up[group, :, :, cols] = product[:width].astype(BF16).reshape(
                ways, share, part_units
            )
            own = down_held[owner].astype(F32)
            total = jnp.zeros((part_units, width), F32)
            for seq in range(seqs):
                lower, upper = seq * seq_length, (seq + 1) * seq_length
                product = mxu(g_turned[:, lower:upper], a_held[lower:upper, cols])
                product = jnp.transpose(product)
                total += product * mod[seq : seq + 1, 5 * width : 6 * width]
                d_gate[seq : seq + 1, :] += column_sum(product * own)
            g_down[group, place] = total.astype(BF16)

        @pl.when(step == GROUPS * turn - 1)
        def _():
            copies = [
                pltpu.make_async_copy(source.at[GROUPS - 1], target, near.at[k])
                for k, (source, target) in enumerate(((g_up, outs[4]), (g_down, outs[5])))
            ]
            for copy in copies:
                copy.start()
            exchange.rest(GROUPS * turn)
            for copy in copies:
                copy.wait()

    def early(i):
        return (jnp.minimum(lax.rem(i, turn), steps - 1), 0)

    def fixed(shape):
        return pl.BlockSpec(shape, lambda i: (0,) * len(shape))

    by_rows = pl.BlockSpec(
        (block, units), lambda i: (jnp.minimum(lax.rem(i, turn), steps - 1), i // turn)
    )
    by_group = pl.BlockSpec((1, units), lambda i: (0, i // turn))

    def up_piece(way):
        return pl.BlockSpec((width, part_units), lambda i: (0, way * GROUPS + i // turn))

    def down_piece(way):
        return pl.BlockSpec((part_units, width), lambda i: (way * GROUPS + i // turn, 0))

    assert GROUPS == 3
    anywhere = pl.BlockSpec(memory_space=pl.ANY)
    return call(
        kernel,
        "hidden_units",
        (GROUPS * turn,),
        [pl.BlockSpec((block, width), early)] * 2
        + [whole(modulation.shape), by_group]
        + [up_piece(way) for way in range(ways)]
        + [down_piece(way) for way in range(ways)],
        [by_rows, by_rows, by_group, fixed((seqs, width)), fixed((seqs, width))]
        + exchange.out_specs()
        + [anywhere] * 2,
        [
            jax.ShapeDtypeStruct((rows, units * GROUPS), BF16),
            jax.ShapeDtypeStruct((rows, units * GROUPS), BF16),
            jax.ShapeDtypeStruct((1, units * GROUPS), F32),
            jax.ShapeDtypeStruct((seqs, width), F32),
            jax.ShapeDtypeStruct((seqs, width), F32),
        ]
        + exchange.out_shape()
        + [jax.ShapeDtypeStruct(shape_up, BF16), jax.ShapeDtypeStruct(shape_down, BF16)],
        [
            pltpu.VMEM((width + 16, rows), BF16),
            pltpu.VMEM((width, rows), BF16),
            pltpu.VMEM((rows, units), BF16),
            pltpu.VMEM((rows, units), BF16),
            pltpu.VMEM((ways, part_units, width), BF16),
            pltpu.VMEM((GROUPS,) + shape_up, BF16),
            pltpu.VMEM((GROUPS,) + shape_down, BF16),
            pltpu.SemaphoreType.DMA((2,)),
        ]
        + exchange.scratch(),
        8 * rows * width * units * GROUPS,
        GROUPS * (rows * (width * 4 + units * 4) + 8 * width * units),
        rows * units * GROUPS,
        ident,
    )(normed, cot, modulation, up_bias, *[up] * ways, *[down] * ways)


def middle_back(
    mixture, tokens, cot, starts, lengths, embed, gain, modulation, out_weight, d_upper, up, seqs,
    block=256,
):
    rows, width = tokens.shape
    ways = lax.axis_size("narrow")
    seq_length = rows // seqs
    block = min(block, seq_length)
    per_seq = seq_length // block
    steps = rows // block
    hidden_width = d_upper.shape[1]
    share = width // ways

    def kernel(
        starts, lengths, mix, tok, g, emb, gn, mod, w_out, w_up, d_ups, d_middle_out, d_mix, g_out,
        sums, g_sum,
    ):
        step = pl.program_id(0)
        seq = step // per_seq
        first = (step - seq * per_seq) * block

        @pl.when(step == 0)
        def _():
            g_sum[...] = jnp.zeros_like(g_sum)

        @pl.when(step == seq * per_seq)
        def _():
            sums[...] = jnp.zeros_like(sums)

        def vector(which):
            return mod[pl.ds(seq, 1), which * width : (which + 1) * width]

        attended = mxu(mix[...], w_out[...])
        start, _ = masked_rows(tok[...], emb[...], starts[seq], lengths[seq], first)
        hat, inverse = normalized(start + vector(2) * attended)
        d_normed = mxu(d_ups[...], grouped_columns(w_up, ways), TRANSPOSED)
        d_middle = g[...].astype(F32) + norm_back(
            d_normed * (gn[...] * (1.0 + vector(4))), hat, inverse
        )
        d_middle_out[...] = d_middle
        d_attended = (vector(2) * d_middle).astype(BF16)
        d_mix[...] = mxu(d_attended, w_out[...], TRANSPOSED).astype(BF16)
        g_sum[...] += mxu(jnp.transpose(mix[...]), d_attended)
        sums[0, 0:1, :] += column_sum(d_normed)
        sums[0, 1:2, :] += column_sum(d_normed * hat)
        sums[0, 2:3, :] += column_sum(d_middle * attended)

        @pl.when(step == steps - 1)
        def _():
            for place in range(ways):
                owner = owner_at(lax.axis_index("narrow"), place)
                spot = pl.ds(pl.multiple_of(owner * share, share), share)
                g_out[place] = g_sum[spot, :].astype(BF16)

    row = pl.BlockSpec((block, width), lambda i: (i, 0))
    return call(
        kernel,
        "middle_back",
        (steps,),
        [smem(), smem(), row, row, row, whole((1, width)), whole((1, width))]
        + [whole(modulation.shape), whole(out_weight.shape), whole(up.shape)]
        + [pl.BlockSpec((block, hidden_width), lambda i: (i, 0))],
        (
            row,
            row,
            pl.BlockSpec((ways, share, width), lambda i: (0, 0, 0)),
            pl.BlockSpec((1, 8, width), lambda i: (i // per_seq, 0, 0)),
        ),
        (
            jax.ShapeDtypeStruct((rows, width), F32),
            jax.ShapeDtypeStruct((rows, width), BF16),
            jax.ShapeDtypeStruct((ways, share, width), BF16),
            jax.ShapeDtypeStruct((seqs, 8, width), F32),
        ),
        [pltpu.VMEM((width, width), F32)],
        rows * width * (2 * hidden_width + 6 * width),
        rows * (width * 12 + hidden_width * 2) + 2 * width * hidden_width,
    )(
        starts, lengths, mixture, tokens, cot, embed, gain, modulation, out_weight, up, d_upper,
    )


class Finale(Steps):
    def __init__(self, ways):
        self.ways = ways
        self.wide = lax.axis_size("wide")

    def scratch(self, columns):
        dma = pltpu.SemaphoreType.DMA
        return [
            pltpu.VMEM((self.ways, 8, columns), F32),
            pltpu.VMEM((self.ways, 8, columns), F32),
            pltpu.VMEM((self.wide, 8, columns), F32),
            dma((self.ways,)),
            dma((self.ways,)),
            dma((self.wide,)),
            dma((self.wide,)),
        ]

    def bind(self, held):
        self.parts, self.narrow_got, self.wide_got, *self.sems = held
        self.locate()

    def others(self):
        targets = []
        for offset in range(1, self.ways):
            targets.append({"narrow": lax.rem(self.at["narrow"] + offset, self.ways)})
        for offset in range(1, self.wide):
            targets.append({"wide": lax.rem(self.at["wide"] + offset, self.wide)})
        return targets

    def greet(self):
        barrier = pltpu.get_barrier_semaphore()
        targets = self.others()
        for target in targets:
            pl.semaphore_signal(
                barrier, inc=1, device_id=target, device_id_type=pl.DeviceIdType.MESH
            )
        pl.semaphore_wait(barrier, len(targets))

    def along_narrow(self, offset):
        target = lax.rem(self.at["narrow"] + offset, self.ways)
        return pltpu.make_async_remote_copy(
            src_ref=self.parts.at[target],
            dst_ref=self.narrow_got.at[self.at["narrow"]],
            send_sem=self.sems[0].at[offset],
            recv_sem=self.sems[1].at[offset],
            device_id={"narrow": target},
            device_id_type=pl.DeviceIdType.MESH,
        )

    def along_wide(self, offset):
        me = self.at["wide"]
        return pltpu.make_async_remote_copy(
            src_ref=self.wide_got.at[me],
            dst_ref=self.wide_got.at[me],
            send_sem=self.sems[2].at[offset],
            recv_sem=self.sems[3].at[offset],
            device_id={"wide": lax.rem(me + offset, self.wide)},
            device_id_type=pl.DeviceIdType.MESH,
        )

    def begin(self):
        for offset in range(1, self.ways):
            self.along_narrow(offset).start()
        me = self.at["narrow"]
        self.narrow_got[pl.ds(me, 1)] = self.parts[pl.ds(me, 1)]

    def spread(self, seqs, row_lanes):
        for offset in range(1, self.ways):
            self.along_narrow(offset).wait()
        me = self.at["wide"]
        for way in range(self.ways):
            self.wide_got[pl.ds(me, 1), way * seqs : (way + 1) * seqs, 0:row_lanes] = (
                self.narrow_got[way : way + 1, 0:seqs, 0:row_lanes]
            )
        total = self.narrow_got[0:1, :, row_lanes:]
        for way in range(1, self.ways):
            total += self.narrow_got[way : way + 1, :, row_lanes:]
        self.wide_got[pl.ds(me, 1), :, row_lanes:] = total
        for offset in range(1, self.wide):
            self.along_wide(offset).start()

    def close(self):
        for offset in range(1, self.wide):
            self.along_wide(offset).wait()


def finish(
    turned, d_parts, tokens, d_middle, mixture, starts, lengths, embed, gain, modulation, weight,
    out_weight, down_bias, active, down, features, rows_two, vectors_two, times, ident, seqs,
    tile=384, block=512, late_block=256,
):
    rows, width = tokens.shape
    ways = lax.axis_size("narrow")
    share = width // ways
    seq_length = rows // seqs
    block, late_block = min(block, seq_length), min(late_block, seq_length)
    per_seq, late_per_seq = seq_length // block, seq_length // late_block
    tiles = width // tile
    columns, hidden_width = modulation.shape[1] // ways, active.shape[1]
    time_width = features.shape[1]
    window = 2 * PAIR
    lanes = columns + time_width + window
    early, middle, late = 3 * tiles, rows // block, rows // late_block
    steps = early + middle + late
    parts = [jax.ShapeDtypeStruct((ways, share, width), BF16)] * 3
    exchange = Exchange([v.shape for v in parts], times, halved(parts))
    finale = Finale(ways)

    def kernel(*refs):
        (
            starts, lengths, left, q_all, k_all, v_all, tok, d_mid, emb, gn, mod, w_qkv_all,
            tok_late, mix, w_out_all, b_down, feat, two, vec, act, w_down_all,
        ) = refs[:21]
        spot = 21
        g_tok, block_out, g_ada, g_ada_bias, g_vec = refs[spot : spot + 5]
        outs = refs[spot + 5 : spot + 8]
        grads, sums = refs[spot + 8 : spot + 10]
        d_held, w_qkv, w_out, w_down, near = refs[spot + 10 : spot + 15]
        small = spot + 15 + 7
        exchange.bind([grads.at[part] for part in range(3)], outs, refs[small:])
        finale.bind(refs[spot + 15 : small])
        step = pl.program_id(0)
        loads = [
            pltpu.make_async_copy(source, d_held.at[part], near.at[part])
            for part, source in enumerate((q_all, k_all, v_all))
        ]
        loads += [
            pltpu.make_async_copy(source, target, near.at[3 + which])
            for which, (source, target) in enumerate(
                ((w_qkv_all, w_qkv), (w_out_all, w_out), (w_down_all, w_down))
            )
        ]

        @pl.when(step == 0)
        def _():
            for load in loads:
                load.start()
            finale.greet()
            sums[...] = jnp.zeros_like(sums)

        exchange.tick(step, steps)

        for part in range(3):
            pl.when(step == part * tiles)(loads[part].wait)
        pl.when(step == early)(loads[3].wait)

        @pl.when(step == early + middle)
        def _():
            loads[4].wait()
            loads[5].wait()

        @pl.when(step < early)
        def _():
            part = step // tiles
            cols = pl.ds(pl.multiple_of((step - part * tiles) * tile, tile), tile)
            product = mxu(left[...], d_held[part, :, cols]).astype(BF16)
            grads[part, :, :, cols] = product.reshape(ways, share, tile)

        @pl.when((step >= early) & (step < early + middle))
        def _():
            at = step - early
            seq = at // per_seq
            first = (at - seq * per_seq) * block
            start, inside = masked_rows(
                tok[...], emb[...], starts[seq], lengths[seq], first
            )
            hat, inverse = normalized(start)
            here = pl.ds(pl.multiple_of(at * block, block), block)
            d_normed = mxu(d_held[0, here, :], w_qkv[:, 0:width], TRANSPOSED)
            d_normed += mxu(d_held[1, here, :], w_qkv[:, width : 2 * width], TRANSPOSED)
            d_normed += mxu(d_held[2, here, :], w_qkv[:, 2 * width :], TRANSPOSED)
            scale = mod[pl.ds(seq, 1), width : 2 * width]
            d_start = d_mid[...] + norm_back(d_normed * (gn[...] * (1.0 + scale)), hat, inverse)
            g_tok[...] = jnp.where(inside, 0.0, d_start)
            sums[seq, 0:1, :] += column_sum(d_normed)
            sums[seq, 1:2, :] += column_sum(d_normed * hat)
            sums[seq, 2:3, :] += column_sum(jnp.where(inside, d_start, 0.0))

        @pl.when(step == early + middle)
        def _():
            parts = finale.parts
            embed_sum = jnp.zeros((1, width), F32)
            gain_sum = jnp.zeros((1, width), F32)
            for seq in range(seqs):
                shift, scale = sums[seq, 0:1, :], sums[seq, 1:2, :]
                gain_sum += scale * (1.0 + mod[seq : seq + 1, width : 2 * width])
                embed_sum += sums[seq, 2:3, :]
                row = jnp.concatenate([shift, scale * gn[...], two[seq : seq + 1, :]], axis=1)
                for way in range(ways):
                    parts[way, seq : seq + 1, 0:columns] = row[
                        :, way * columns : (way + 1) * columns
                    ]
            for way in range(ways):
                parts[way, 0:seqs, columns : columns + time_width] = feat[...]
                lower = PAIR * (share * way // PAIR)
                parts[way, 0:1, columns + time_width :] = embed_sum[:, lower : lower + window]
                parts[way, 1:2, columns + time_width :] = gain_sum[:, lower : lower + window]
                parts[way, 2:8, columns + time_width :] = vec[way, 2:8, :]
            finale.begin()

        @pl.when(step == early + middle + 2)
        def _():
            finale.spread(seqs, columns + time_width)

        @pl.when(step >= early + middle)
        def _():
            at = step - early - middle
            seq = at // late_per_seq
            first = (at - seq * late_per_seq) * late_block
            start, _ = masked_rows(
                tok_late[...], emb[...], starts[seq], lengths[seq], first
            )
            attended = mxu(mix[...], w_out[...])
            branch = mxu(act[...], grouped_rows(w_down, ways)) + b_down[...]
            hidden = start + mod[pl.ds(seq, 1), 2 * width : 3 * width] * attended
            block_out[...] = (
                hidden + mod[pl.ds(seq, 1), 5 * width : 6 * width] * branch
            ).astype(BF16)

        @pl.when(step == steps - 1)
        def _():
            finale.close()
            got = finale.wide_got
            every = got[...].reshape(finale.wide * 8, lanes)
            d_mods, feats = every[:, 0:columns], every[:, columns : columns + time_width]
            g_ada[...] = lax.dot_general(
                jnp.transpose(feats), d_mods, PLAIN, precision=FULL_PRECISION,
                preferred_element_type=F32,
            )
            g_ada_bias[...] = column_sum(d_mods)
            total = got[0, :, columns + time_width :]
            for index in range(1, finale.wide):
                total += got[index, :, columns + time_width :]
            g_vec[...] = total
            exchange.rest(steps)

    row = pl.BlockSpec((block, width), lambda i: (jnp.clip(i - early, 0, middle - 1), 0))

    def late_row(wide):
        return pl.BlockSpec(
            (late_block, wide), lambda i: (jnp.maximum(i - early - middle, 0), 0)
        )

    def fixed(shape):
        return pl.BlockSpec(shape, lambda i: (0,) * len(shape))

    anywhere = pl.BlockSpec(memory_space=pl.ANY)
    return call(
        kernel,
        "finish",
        (steps,),
        [smem(), smem(), whole(turned.shape)]
        + [anywhere] * 3
        + [row, row, whole((1, width)), whole((1, width)), whole(modulation.shape), anywhere]
        + [late_row(width), late_row(width), anywhere, whole((1, width))]
        + [whole(features.shape), whole(rows_two.shape), whole(vectors_two.shape)]
        + [late_row(hidden_width), anywhere],
        [
            row,
            late_row(width),
            fixed((time_width, columns)),
            fixed((1, columns)),
            fixed((8, window)),
        ]
        + exchange.out_specs(),
        [
            jax.ShapeDtypeStruct((rows, width), F32),
            jax.ShapeDtypeStruct((rows, width), BF16),
            jax.ShapeDtypeStruct((time_width, columns), F32),
            jax.ShapeDtypeStruct((1, columns), F32),
            jax.ShapeDtypeStruct((8, window), F32),
        ]
        + exchange.out_shape(),
        [
            pltpu.VMEM((3, ways, share, width), BF16),
            pltpu.VMEM((seqs, 8, width), F32),
            pltpu.VMEM((3, rows, width), BF16),
            pltpu.VMEM(weight.shape, BF16),
            pltpu.VMEM(out_weight.shape, BF16),
            pltpu.VMEM(down.shape, BF16),
            pltpu.SemaphoreType.DMA((6,)),
        ]
        + finale.scratch(lanes)
        + exchange.scratch(),
        2 * rows * width * (7 * width + hidden_width),
        rows * (width * 24 + 2 * hidden_width),
        0,
        ident,
    )(
        starts, lengths, turned, *d_parts, tokens, d_middle, embed, gain, modulation, weight,        tokens, mixture, out_weight, down_bias, features, rows_two, vectors_two, active, down,
    )


def gather_first(small, ada, weight, ident):
    share, wide = weight.shape
    width = wide // 3
    columns = [(0, 0, small.shape[1]), (1, 0, ada.shape[1])]
    columns += [(2, k * width, (k + 1) * width) for k in range(3)]
    gathering = Gather([small.shape, ada.shape, weight.shape], [0] * 5, [0] * 3, columns)

    def kernel(*refs):
        gathering.bind(refs[0:3], refs[3:6], refs[6:])
        gathering.greet()
        gathering.begin(0)
        gathering.begin(1)
        gathering.begin(2)
        for k in range(5):
            gathering.relay(k)
            if k + 3 < 5:
                gathering.begin(k + 3)
            if k > 0:
                gathering.share(k - 1)
        gathering.share(4)
        for k in range(5):
            gathering.close(k)

    return call(
        kernel,
        "gather_first",
        (),
        gathering.in_specs(),
        gathering.out_specs(),
        gathering.out_shape(),
        gathering.scratch(),
        0,
        8 * share * wide,
        0,
        ident,
    )(small, ada, weight)


def assemble(ups, downs, out, qkv):
    share, units = ups[0].shape
    part, width = downs[0].shape
    ways = units // part
    groups = len(ups)

    def kernel(*refs):
        up_in, down_in = refs[:groups], refs[groups : 2 * groups]
        out_in, qkv_in = refs[2 * groups], refs[2 * groups + 1 : 2 * groups + 4]
        g_up, g_down, g_out, g_qkv = refs[2 * groups + 4 :]
        for group in range(groups):
            for way in range(ways):
                lower = (way * groups + group) * part
                g_up[:, lower : lower + part] = up_in[group][
                    :, way * part : (way + 1) * part
                ].astype(F32)
            g_down[group] = down_in[group][...].astype(F32)
        g_out[...] = out_in[...].astype(F32)
        for which in range(3):
            g_qkv[:, which * width : (which + 1) * width] = qkv_in[which][...].astype(F32)

    pace = 4
    small, tall = share // pace, part // pace

    def rows(count, columns):
        return pl.BlockSpec((count, columns), lambda i: (i, 0))

    g_up, g_down, g_out, g_qkv = call(
        kernel,
        "assemble",
        (pace,),
        [rows(small, units)] * groups
        + [rows(tall, width)] * groups
        + [rows(small, width)] * 4,
        (
            rows(small, units * groups),
            pl.BlockSpec((groups, tall, width), lambda i: (0, i, 0)),
            rows(small, width),
            rows(small, 3 * width),
        ),
        (
            jax.ShapeDtypeStruct((share, units * groups), F32),
            jax.ShapeDtypeStruct((groups, part, width), F32),
            jax.ShapeDtypeStruct((share, width), F32),
            jax.ShapeDtypeStruct((share, 3 * width), F32),
        ),
        [],
        0,
        12 * share * units * groups,
    )(*ups, *downs, out, *qkv)
    return g_up, g_down.reshape(groups * part, width), g_out, g_qkv


def per_device(
    tokens,
    timestep,
    span_start,
    span_length,
    mask_embed,
    ada_weight,
    ada_bias,
    norm_first,
    query_key_value_weight,
    output_weight,
    norm_second,
    up_projection_weight,
    up_projection_bias,
    down_projection_weight,
    down_projection_bias,
    cotangent,
):
    seqs = timestep.shape[0]
    rows, width = tokens.shape
    seq_length = rows // seqs
    ways = lax.axis_size("narrow")
    me = lax.axis_index("narrow")
    share = width // ways
    unit_share = down_projection_weight.shape[0]
    part = unit_share // GROUPS
    units = ways * part
    time_width, columns = ada_weight.shape

    vectors = (
        ada_bias, mask_embed, norm_first, norm_second, down_projection_bias, up_projection_bias,
    )
    filled, lower = jnp.zeros((32 * PAIR,), BF16), 0
    for v in vectors:
        filled += jnp.pad(v, (lower, filled.shape[0] - lower - v.shape[0]))
        lower += v.shape[0]
    small = filled.reshape(32, PAIR)
    small, ada, w_qkv = gather_first(small, ada_weight, query_key_value_weight, 0)

    small = small.reshape(ways, -1).astype(F32)
    smalls, lower = [], 0
    for v in vectors:
        smalls.append(small[:, lower : lower + v.shape[0]].reshape(1, -1))
        lower += v.shape[0]
    bias_ada, embed, gain_one, gain_two, bias_down, bias_up = smalls
    features = time_features(timestep, time_width)
    modulation = jnp.einsum(
        "sf,wfc->swc",
        features,
        ada.reshape(ways, time_width, columns).astype(F32),
        precision=FULL_PRECISION,
    ).reshape(seqs, -1) + bias_ada
    tables = rotary_tables(seq_length)

    qkv, turned_one = project(
        tokens, span_start, span_length, embed, gain_one, modulation, w_qkv, tables, seqs
    )
    thirds = [
        (which, third * size, (third + 1) * size)
        for which, size in ((1, unit_share * ways // 3), (2, width // 3))
        for third in range(3)
    ]
    mixture, total, w_out, w_up, w_down = attend(
        qkv,
        [output_weight, up_projection_weight, down_projection_weight],
        [0, 1, 3, 6, 8, 11, 13],
        [5, 5, 2],
        [(0, 0, width)] + thirds,
        1,
        seqs,
    )
    normed_two = middle_norm(
        mixture, tokens, span_start, span_length, embed, gain_two, modulation, w_out, seqs
    )
    bias_up = jnp.swapaxes(bias_up.reshape(ways, GROUPS, part), 0, 1).reshape(1, -1)
    head_times = paced([8, 9, 10, 11], [1, 5, 2, 2, 2, 1]) + paced([17, 17, 18, 19], [1, 4])
    active, d_upper, g_bias, d_gate_two, g_sum, *swaps = hidden_units(
        normed_two, cotangent, modulation, w_up, bias_up, w_down, head_times, 2, seqs
    )
    d_gate_two += bias_down * g_sum
    d_middle, d_mixture, g_out, sums_two = middle_back(
        mixture, tokens, cotangent, span_start, span_length, embed, gain_two, modulation, w_out,
        d_upper, w_up, seqs,
    )
    d_q, d_k, d_v, *done = attend_back(
        qkv, mixture, d_mixture, total, tables, swaps[2:] + [g_out],
        ["tail"] * 2 + ["whole"] * 3, halved(swaps[2:] + [g_out]),
        [[1, 2, 5, 8, 11, 13], [2, 3, 6, 9, 12, 14], [3, 4, 7, 10, 13, 15], [4, 5, 8, 11, 14, 16]]
        + paced([0, 1, 3, 5, 6, 8], [1, 4, 3, 3, 4, 2]),
        3, seqs,
    )
    scale_two = modulation[:, 4 * width : 5 * width]
    rows_two = jnp.concatenate(
        [sums_two[:, 2], sums_two[:, 0], sums_two[:, 1] * gain_two, d_gate_two], axis=1
    )
    g_norm_two = jnp.sum(sums_two[:, 1] * (1.0 + scale_two), axis=0)
    g_bias_down = jnp.sum(modulation[:, 5 * width :] * g_sum, axis=0)
    lowers = [PAIR * (share * way // PAIR) for way in range(ways)]
    vectors_two = jnp.stack(
        [
            jnp.stack([v[lower : lower + 2 * PAIR] for lower in lowers])
            for v in (g_norm_two, g_norm_two, g_norm_two, g_bias_down)
        ]
        + [g_bias[0].reshape(GROUPS, ways, part)[group] for group in range(GROUPS)]
        + [jnp.zeros((ways, 2 * PAIR), F32)],
        axis=1,
    )
    grad_tokens, block_out, grad_ada_weight, grad_ada_bias, vectors, *g_qkv = finish(
        turned_one, (d_q, d_k, d_v), tokens, d_middle, mixture, span_start, span_length, embed,
        gain_one, modulation, w_qkv, w_out, bias_down, active, w_down, features, rows_two,
        vectors_two,
        FINISH_TIMES, 4, seqs,
    )
    skip = lax.rem(share * me, PAIR)
    own = lax.dynamic_slice_in_dim(vectors[:4], skip, share, 1)
    g_ups, g_downs = (swaps[0], *done[0:4:2]), (swaps[1], *done[1:4:2])
    g_up, g_down, g_out, g_qkv = assemble(g_ups, g_downs, done[4], g_qkv)
    return (
        block_out,
        grad_tokens,
        own[0],
        grad_ada_weight,
        grad_ada_bias[0],
        own[1],
        g_qkv,
        g_out,
        own[2],
        g_up,
        vectors[4 : 4 + GROUPS].reshape(-1),
        g_down,
        own[3],
    )


def solution(mesh):
    rows = P(("wide", "narrow"), None)
    per_seq = P(("wide", "narrow"))
    vector, matrix, columns = P("narrow"), P("narrow", None), P(None, "narrow")
    return jax.shard_map(
        per_device,
        mesh=mesh,
        in_specs=(
            rows, per_seq, per_seq, per_seq, vector, columns, vector, vector,
            matrix, matrix, vector, matrix, vector, matrix, vector, rows,
        ),
        out_specs=(
            rows, rows, vector, columns, vector, vector, matrix, matrix, vector, matrix,
            vector, matrix, vector,
        ),
        check_vma=False,
    )
```

```python
import math

import jax
import jax.numpy as jnp
import numpy as np
from jax import lax
from jax.experimental import pallas as pl
from jax.experimental.pallas import tpu as pltpu
from jax.sharding import PartitionSpec as P

HEAD = 64
PAIR = 2 * HEAD
GROUPS = 3
FINISH_TIMES = [
    [1, 3, 5, 6, 7, 10, 12], [2, 4, 6, 7, 9, 12, 14], [3, 4, 7, 9, 11, 14, 15],
]
EPSILON = 1e-05
FULL_PRECISION = lax.Precision.HIGHEST
F32 = jnp.float32
BF16 = jnp.bfloat16
SCALE = 1.0 / math.sqrt(HEAD)
SCALE2 = SCALE * math.log2(math.e)
VMEM_BYTES = 60 << 20
PLAIN = (((1,), (0,)), ((), ()))
TRANSPOSED = (((1,), (1,)), ((), ()))


def mxu(left, right, dims=PLAIN):
    return lax.dot_general(left, right, dims, preferred_element_type=F32)


def call(
    kernel, name, grid, in_specs, out_specs, out_shape, scratch, flops, moved, exps=0, ident=None
):
    return pl.pallas_call(
        kernel,
        name=name,
        grid=grid,
        in_specs=in_specs,
        out_specs=out_specs,
        out_shape=out_shape,
        scratch_shapes=scratch,
        compiler_params=pltpu.CompilerParams(
            vmem_limit_bytes=VMEM_BYTES, collective_id=ident, has_side_effects=ident is not None
        ),
        cost_estimate=pl.CostEstimate(flops=flops, bytes_accessed=moved, transcendentals=exps),
    )


def whole(shape):
    return pl.BlockSpec(shape, lambda *_: (0,) * len(shape), pipeline_mode=pl.Buffered(1))


def column_third(which, width):
    return pl.BlockSpec((width, width), lambda *_: (0, which), pipeline_mode=pl.Buffered(1))


def smem():
    return pl.BlockSpec(memory_space=pltpu.SMEM)


def time_features(step_ids, feature_count):
    halfway = feature_count // 2
    spacing = jnp.exp(-math.log(10000.0) * jnp.arange(halfway, dtype=F32) / halfway)
    angles = step_ids.astype(F32)[:, None] * spacing[None, :]
    return jax.nn.silu(jnp.concatenate([jnp.cos(angles), jnp.sin(angles)], axis=-1))


def rotary_tables(seq_length):
    halfway = HEAD // 2
    spacing = np.exp(-math.log(10000.0) * np.arange(halfway, dtype=np.float32) / halfway)
    angles = np.arange(seq_length, dtype=np.float32)[:, None] * spacing.astype(np.float32)
    cosine, sine = np.cos(angles), np.sin(angles)
    signed = np.concatenate([-sine, sine] * 2, axis=-1)
    return np.concatenate([cosine] * 4, axis=-1), signed


def partner_lanes(v):
    lane = lax.broadcasted_iota(jnp.int32, (1, PAIR), 1)
    return jnp.where(lax.rem(lane, HEAD) < HEAD // 2, from_ahead(v), from_behind(v))


def from_ahead(v):
    return pltpu.roll(v, PAIR - HEAD // 2, 1)


def from_behind(v):
    return pltpu.roll(v, HEAD // 2, 1)


def masked_rows(tokens, embed, start, length, first_row):
    rows = tokens.shape[0]
    position = lax.broadcasted_iota(jnp.int32, (rows, 1), 0) + first_row
    inside = (position >= start) & (position < start + length)
    return jnp.where(inside, embed, tokens.astype(F32)), inside


def normalized(rows):
    centre = rows - jnp.mean(rows, axis=-1, keepdims=True)
    spread = jnp.mean(centre * centre, axis=-1, keepdims=True)
    inverse = lax.rsqrt(spread + EPSILON)
    return centre * inverse, inverse


def norm_back(d_out, hat, inverse):
    return inverse * (
        d_out
        - jnp.mean(d_out, axis=-1, keepdims=True)
        - hat * jnp.mean(d_out * hat, axis=-1, keepdims=True)
    )


def column_sum(v):
    return jnp.sum(v, axis=0, keepdims=True)


def store_shares(target, value, cols):
    me, ways = lax.axis_index("narrow"), lax.axis_size("narrow")
    share = value.shape[0] // ways
    for place in range(ways):
        lower = pl.multiple_of(place_of(me, place) * share, share)
        target[pl.ds(lower, share), cols] = value[place * share : (place + 1) * share, :]


def place_of(me, other):
    core = lax.rem(me + other, 2)
    chip = lax.rem(me // 2 + other // 2, 2)
    return 2 * (1 - core) + 1 - chip


def owner_at(me, place):
    core, chip = 1 - place // 2, 1 - lax.rem(place, 2)
    return 2 * lax.rem(me // 2 + chip, 2) + lax.rem(me + core, 2)


def project(tokens, starts, lengths, embed, gain, modulation, weight, tables, seqs, block=512):
    rows, width = tokens.shape
    seq_length = rows // seqs
    block = min(block, seq_length)
    per_seq = seq_length // block
    pairs = width // PAIR

    def kernel(starts, lengths, tok, emb, gn, mod, w_q, w_k, w_v, cos, sin, out, nt):
        step = pl.program_id(0)
        seq = step // per_seq
        first = (step - seq * per_seq) * block
        start, _ = masked_rows(tok[...], emb[...], starts[seq], lengths[seq], first)
        hat, _ = normalized(start)
        shift = mod[pl.ds(seq, 1), 0:width]
        scale = mod[pl.ds(seq, 1), width : 2 * width]
        normed = (hat * (gn[...] * (1.0 + scale)) + shift).astype(BF16)
        store_shares(nt, jnp.transpose(normed), slice(None))
        for which, w in enumerate((w_q, w_k)):
            turned = mxu(normed, w[...])
            for part in range(pairs):
                v = turned[:, part * PAIR : (part + 1) * PAIR]
                v = v * cos[...] + partner_lanes(v) * sin[...]
                lower = which * width + part * PAIR
                out[:, lower : lower + PAIR] = v.astype(BF16)
        out[:, 2 * width :] = mxu(normed, w_v[...]).astype(BF16)

    table = pl.BlockSpec((block, PAIR), lambda i: (lax.rem(i, per_seq), 0))
    return call(
        kernel,
        "project",
        (rows // block,),
        [
            smem(),
            smem(),
            pl.BlockSpec((block, width), lambda i: (i, 0)),
            whole((1, width)),
            whole((1, width)),
            whole(modulation.shape),
            column_third(0, width),
            column_third(1, width),
            column_third(2, width),
            table,
            table,
        ],
        (
            pl.BlockSpec((block, 3 * width), lambda i: (i, 0)),
            pl.BlockSpec((width, block), lambda i: (0, i)),
        ),
        (
            jax.ShapeDtypeStruct((rows, 3 * width), BF16),
            jax.ShapeDtypeStruct((width, rows), BF16),
        ),
        [],
        2 * rows * width * 3 * width,
        rows * width * 10 + 6 * width * width,
    )(starts, lengths, tokens, embed, gain, modulation, weight, weight, weight, *tables)


def flip(index, stride):
    return index + stride * (1 - 2 * lax.rem(index // stride, 2))


def exchange_stages():
    count = lax.axis_size("wide")
    strides = [1 << bit for bit in range(1, count.bit_length() - 1)]
    return [("pair", "narrow", 1), ("chip", "narrow", 2), ("split", "wide", 1)] + [
        ("full", "wide", stride) for stride in strides
    ] + [("join", "wide", 1)]


class Steps:
    def in_specs(self):
        return [pl.BlockSpec(memory_space=pl.ANY)] * self.count

    out_specs = in_specs

    def locate(self):
        self.at = {axis: lax.axis_index(axis) for axis in ("wide", "narrow")}
        self.odd = lax.rem(self.at["wide"], 2)

    def half_of(self, rows, which, lower=0):
        side = self.odd if which == 0 else 1 - self.odd
        return pl.ds(pl.multiple_of(lower + side * (rows // 2), rows // 2), rows // 2)

    def greet(self):
        barrier = pltpu.get_barrier_semaphore()
        for axis, stride in self.partners:
            pl.semaphore_signal(
                barrier,
                inc=1,
                device_id={axis: flip(self.at[axis], stride)},
                device_id_type=pl.DeviceIdType.MESH,
            )
        pl.semaphore_wait(barrier, len(self.partners))

    def push(self, source, target, sent, got, axis, stride):
        return pltpu.make_async_remote_copy(
            src_ref=source,
            dst_ref=target,
            send_sem=sent,
            recv_sem=got,
            device_id={axis: flip(self.at[axis], stride)},
            device_id_type=pl.DeviceIdType.MESH,
        )

    def tick(self, now, last, bunch=6):
        planned = sorted(self.plan(), key=lambda item: item[:3])
        times = sorted({item[0] for item in planned if item[0] < last})
        for lower in sorted({when - when % bunch for when in times}):

            @pl.when((now >= lower) & (now < lower + bunch))
            def _(lower=lower):
                for when in times:
                    if lower <= when < lower + bunch:
                        pl.when(now == when)(lambda when=when: self.take(planned, when))

    def take(self, planned, when):
        if when == 0:
            self.greet()
        for item in planned:
            if item[0] == when:
                item[3]()

    def rest(self, last):
        for item in sorted(self.plan(), key=lambda item: item[:3]):
            if item[0] >= last:
                item[3]()


class Gather(Steps):
    partners = (("narrow", 1), ("narrow", 2), ("wide", 1))

    def __init__(self, shapes, begins, waits, columns=None):
        columns = columns or [(k, 0, shape[1]) for k, shape in enumerate(shapes)]
        self.arrays, self.columns = shapes, columns
        self.shapes = [(shapes[k][0], upper - lower) for k, lower, upper in columns]
        self.begins, self.waits = begins, waits
        self.count = len(columns)

    def in_specs(self):
        return [pl.BlockSpec(memory_space=pl.ANY)] * len(self.arrays)

    out_specs = in_specs

    def out_shape(self):
        return [jax.ShapeDtypeStruct((4 * rows, cols), BF16) for rows, cols in self.arrays]

    def scratch(self):
        dma, held = pltpu.SemaphoreType.DMA, []
        for shape in self.shapes:
            held += [dma((5,)), dma((5,)), dma((2,)), pltpu.VMEM(shape, BF16)]
        return held

    def bind(self, ins, outs, held):
        self.refs = [
            (ins[k].at[:, lower:upper], outs[k].at[:, lower:upper])
            + tuple(held[4 * part : 4 * part + 4])
            for part, (k, lower, upper) in enumerate(self.columns)
        ]
        self.locate()

    def block(self, k, index, which=None):
        rows = self.shapes[k][0]
        if which is None:
            return pl.ds(pl.multiple_of(index * rows, rows), rows)
        return self.half_of(rows, which, index * rows)

    def remote(self, k, step):
        source, out, sent, got, _, _ = self.refs[k]
        me, across = self.at["narrow"], flip(self.at["narrow"], 2)
        axis, stride = (("narrow", 1), ("narrow", 2), ("wide", 1), ("narrow", 1), ("narrow", 1))[step]
        if step == 0:
            ends = (source, out.at[self.block(k, me), :])
        elif step == 1:
            half = self.half_of(self.shapes[k][0], 0)
            ends = (source.at[half, :], out.at[self.block(k, me, 0), :])
        else:
            spot = self.block(k, across, 1 if step == 4 else 0)
            ends = (out.at[spot, :], out.at[spot, :])
        return self.push(*ends, sent.at[step], got.at[step], axis, stride)

    def local(self, k, which):
        source, out, _, _, near, kept = self.refs[k]
        if which == 0:
            return pltpu.make_async_copy(source, kept, near.at[0])
        return pltpu.make_async_copy(
            kept, out.at[self.block(k, self.at["narrow"]), :], near.at[1]
        )

    def begin(self, k):
        self.remote(k, 1).start()
        self.remote(k, 0).start()
        self.local(k, 0).start()

    def relay(self, k):
        self.local(k, 0).wait()
        self.local(k, 1).start()
        self.remote(k, 1).wait()
        self.remote(k, 2).start()
        self.remote(k, 3).start()

    def share(self, k):
        self.remote(k, 2).wait()
        self.remote(k, 4).start()

    def close(self, k):
        self.remote(k, 0).wait()
        self.remote(k, 3).wait()
        self.remote(k, 4).wait()
        self.local(k, 1).wait()

    def plan(self):
        planned = []
        for k in range(self.count):
            when = self.begins[k]
            planned.append((when, 0, k, lambda k=k: self.begin(k)))
            for wait, act in zip(self.waits, (self.relay, self.share, self.close)):
                when += wait
                planned.append((when, 1, k, lambda k=k, act=act: act(k)))
        return planned


class Exchange(Steps):
    def __init__(self, shapes, times, columns=None, spans=None):
        columns = columns or [(k, 0, shape[-1]) for k, shape in enumerate(shapes)]
        spans = spans or ["whole"] * len(shapes)
        self.stages = exchange_stages()
        self.arrays, self.columns = [shape[-2:] for shape in shapes], columns
        self.shapes = [(self.arrays[k][0], upper - lower) for k, lower, upper in columns]
        self.spans = [spans[k] for k, _, _ in columns]
        self.firsts = [2 if span == "tail" else 0 for span in self.spans]
        self.lasts = [1 if span == "head" else len(self.stages) - 1 for span in self.spans]
        self.times = times
        self.count = len(columns)
        self.partners = sorted({(axis, stride) for _, axis, stride in self.stages})

    def in_specs(self):
        return [pl.BlockSpec(memory_space=pl.ANY)] * len(self.arrays)

    out_specs = in_specs

    def out_shape(self):
        return [jax.ShapeDtypeStruct(shape, BF16) for shape in self.arrays]

    def scratch(self):
        held = []
        dma = pltpu.SemaphoreType.DMA
        for (rows, cols), span in zip(self.shapes, self.spans):
            early, late = span != "tail", span != "head"
            held += [
                pltpu.VMEM((2, rows, cols) if early else (2, 16, PAIR), BF16),
                pltpu.VMEM((2 if early else 1, rows, cols), BF16),
                pltpu.VMEM((rows, cols) if early else (16, PAIR), BF16),
                pltpu.VMEM((len(self.stages) - 3, rows // 2, cols) if late else (1, 16, PAIR), BF16),
                pltpu.VMEM((rows // 2, cols) if late else (16, PAIR), BF16),
                dma((len(self.stages),)),
                dma((len(self.stages),)),
                dma((2,)),
            ]
        return held

    def bind(self, ins, outs, held):
        self.refs = []
        for part, (k, lower, upper) in enumerate(self.columns):
            every = (slice(None),) * (1 if self.spans[part] == "tail" else 2)
            self.refs.append(
                (ins[k].at[every + (slice(lower, upper),)], outs[k].at[:, lower:upper])
                + tuple(held[8 * part : 8 * part + 8])
            )
        self.locate()

    def own(self, k):
        kept = self.refs[k][3]
        return kept.at[0 if self.spans[k] == "tail" else 1]

    def remote(self, k, step):
        source, out, pair, kept, chip, halves, mine, sent, got, _ = self.refs[k]
        kind, axis, stride = self.stages[step]
        rows = self.shapes[k][0]
        if kind == "pair":
            ends = (source.at[0:2], pair)
        elif kind == "chip":
            ends = (kept.at[0], chip)
        elif kind == "split":
            ends = (self.own(k).at[self.half_of(rows, 1), :], halves.at[0])
        elif kind == "full":
            ends = (mine, halves.at[step - 2])
        else:
            ends = (mine, out.at[self.half_of(rows, 0), :])
        return self.push(*ends, sent.at[step], got.at[step], axis, stride)

    def load(self, k):
        source, kept, near = self.refs[k][0], self.refs[k][3], self.refs[k][9]
        if self.spans[k] == "tail":
            return pltpu.make_async_copy(source, kept.at[0], near.at[0])
        return pltpu.make_async_copy(source.at[2:4], kept, near.at[0])

    def store(self, k):
        out, mine, near = self.refs[k][1], self.refs[k][6], self.refs[k][9]
        if self.spans[k] == "head":
            return pltpu.make_async_copy(self.own(k), out, near.at[1])
        half = self.half_of(self.shapes[k][0], 0)
        return pltpu.make_async_copy(mine, out.at[half, :], near.at[1])

    def begin(self, k):
        self.load(k).start()
        if self.spans[k] != "tail":
            self.remote(k, 0).start()

    def enter(self, k):
        self.load(k).wait()
        self.remote(k, 2).start()

    def end(self, k, step):
        _, _, pair, kept, chip, halves, mine, _, _, _ = self.refs[k]
        kind = self.stages[step][0]
        self.remote(k, step).wait()
        if kind == "pair":
            self.load(k).wait()
            kept[...] = (kept[...].astype(F32) + pair[...].astype(F32)).astype(BF16)
        elif kind == "chip":
            kept[1] = (kept[1].astype(F32) + chip[...].astype(F32)).astype(BF16)
        elif kind == "split":
            half = self.half_of(self.shapes[k][0], 0)
            own = self.own(k)[half, :].astype(F32)
            mine[...] = (own + halves[0].astype(F32)).astype(BF16)
        elif kind == "full":
            mine[...] = (mine[...].astype(F32) + halves[step - 2].astype(F32)).astype(BF16)
        if step < self.lasts[k]:
            self.remote(k, step + 1).start()
        if step == max(self.lasts[k] - 1, 1):
            self.store(k).start()
        if step == self.lasts[k]:
            self.store(k).wait()

    def plan(self):
        planned = []
        for k, (begin, *ends) in enumerate(self.times):
            first, last = self.firsts[k], self.lasts[k]
            planned.append((begin, 0, k, lambda k=k: self.begin(k)))
            if first:
                planned.append((ends[0], 1, k, lambda k=k: self.enter(k)))
                ends = [0] + ends
            for step in range(first, last + 1):
                when = ends[-1] if step == last else ends[min(step, 4)]
                planned.append((when, 1, k, lambda k=k, step=step: self.end(k, step)))
        return planned


def paced(begins, waits):
    return [[begin + sum(waits[:count]) for count in range(len(waits) + 1)] for begin in begins]


def head_mask(v, half):
    lane = lax.broadcasted_iota(jnp.int32, (1, PAIR), 1)
    keep = (lane < HEAD) if half == 0 else (lane >= HEAD)
    return jnp.where(keep, v, jnp.zeros_like(v))


def attend(qkv, shares, begins, waits, columns, ident, seqs, block=512, per=3):
    rows, width = qkv.shape[0], qkv.shape[1] // 3
    seq_length = rows // seqs
    block = min(block, seq_length)
    pairs = width // PAIR
    count = seq_length // block
    steps = pairs // per
    items = per * count
    wide = per * PAIR

    gathering = Gather([v.shape for v in shares], begins, waits, columns)
    many = len(shares)
    ticks = seqs * steps * items

    def kernel(*refs):
        q_ref, k_ref, v_ref = refs[:3]
        out, total = refs[3 + many : 5 + many]
        v_turned, out_turned, held = refs[5 + 2 * many : 8 + 2 * many]
        gathering.bind(refs[3 : 3 + many], refs[5 + many : 5 + 2 * many], refs[8 + 2 * many :])
        spot = pl.program_id(0) * steps + pl.program_id(1)
        v_turned[...] = jnp.transpose(v_ref[...])

        def place(i):
            pair = i // count
            part = i - pair * count
            return (
                pair,
                pl.ds(pl.multiple_of(pair * PAIR, PAIR), PAIR),
                pl.ds(pl.multiple_of(part * block, block), block),
            )

        def score(i, half):
            _, cols, part = place(i)
            held[half] = mxu(k_ref[:, cols], head_mask(q_ref[part, cols], half), TRANSPOSED)

        def finish(i, half):
            pair, _, part = place(i)
            scores = held[half]
            top = jnp.max(scores, axis=0, keepdims=True)
            exponent = jnp.exp2(scores * SCALE2 - top * SCALE2).astype(BF16)
            head = pl.ds(pl.multiple_of(pair * PAIR + half * HEAD, HEAD), HEAD)
            left = jnp.concatenate([v_turned[head, :], jnp.ones((16, seq_length), BF16)], axis=0)
            mixed = mxu(left, exponent)
            denominator = mixed[HEAD : HEAD + 1]
            out_turned[head, part] = mixed[:HEAD] * (1.0 / denominator)
            total[0, pair, half : half + 1, part] = top * SCALE2 + jnp.log2(denominator)

        score(0, 0)

        def body(i, carry):
            gathering.tick(spot * items + i, ticks)
            score(i, 1)
            finish(i, 0)
            score(jnp.minimum(i + 1, items - 1), 0)
            finish(i, 1)
            return carry

        lax.fori_loop(0, items, body, 0)
        out[...] = jnp.transpose(out_turned[...]).astype(BF16)

        @pl.when(spot == seqs * steps - 1)
        def _():
            gathering.rest(ticks)

    def part_of(which):
        return pl.BlockSpec((seq_length, wide), lambda s, p: (s, which * steps + p))

    return call(
        kernel,
        "attend",
        (seqs, steps),
        [part_of(0), part_of(1), part_of(2)] + gathering.in_specs(),
        [part_of(0), pl.BlockSpec((1, per, 2, seq_length), lambda s, p: (s, p, 0, 0))]
        + gathering.out_specs(),
        [
            jax.ShapeDtypeStruct((rows, width), BF16),
            jax.ShapeDtypeStruct((seqs, pairs, 2, seq_length), F32),
        ]
        + gathering.out_shape(),
        [
            pltpu.VMEM((wide, seq_length), BF16),
            pltpu.VMEM((wide, seq_length), F32),
            pltpu.VMEM((2, seq_length, block), F32),
        ]
        + gathering.scratch(),
        16 * rows * seq_length * width,
        rows * width * 8,
        rows * seq_length * width // HEAD,
        ident,
    )(qkv, qkv, qkv, *shares)


def attend_back(
    qkv, mixture, d_mixture, total, tables, turned, pieces, spans, columns, times, ident, seqs,
    block=512, per=3,
):
    rows, width = mixture.shape
    seq_length = rows // seqs
    block = min(block, seq_length)
    pairs = width // PAIR
    count = seq_length // block
    steps = pairs // per
    items = per * count
    wide = per * PAIR
    ways = lax.axis_size("narrow")
    share = width // ways
    own = [jax.ShapeDtypeStruct((ways, share, wide), BF16)] * 3
    traded = list(pieces) + own
    exchange = Exchange(
        [v.shape for v in traded],
        times,
        list(columns) + [(len(pieces) + part, 0, wide) for part in range(3)],
        list(spans) + ["whole"] * 3,
    )
    many, outs = len(pieces), len(traded)
    assert steps == 2
    ticks = seqs * steps * items

    def kernel(*refs):
        q_ref, k_ref, v_ref, mix, grad, tot, cos, sin, turned_all = refs[:9]
        lower = 9 + many
        dq, dk, dv = refs[lower : lower + 3]
        out_refs, lower = refs[lower + 3 : lower + 3 + outs], lower + 3 + outs
        k_turned, dq_turned, dk_sum, dv_sum, inner, s_held, p_held = refs[lower : lower + 7]
        left, d_held, grads, near = refs[lower + 7 : lower + 11]
        exchange.bind(
            list(refs[9 : 9 + many]) + [grads.at[part] for part in range(3)],
            out_refs,
            refs[lower + 11 :],
        )
        seq = pl.program_id(1)
        spot = pl.program_id(0) * seqs + seq
        load = pltpu.make_async_copy(turned_all, left, near.at[0])
        pl.when(spot == 0)(load.start)

        @pl.when(spot == seqs)
        def _():
            load.wait()
            for part in range(3):
                product = mxu(left[...], d_held[part]).astype(BF16)
                grads[part] = product.reshape(ways, share, wide)

        k_turned[...] = jnp.transpose(k_ref[...])
        product = jnp.transpose(mix[...].astype(F32) * grad[...].astype(F32))
        for pair in range(per):
            for half in range(2):
                lower = pair * PAIR + half * HEAD
                inner[pair, half : half + 1, :] = column_sum(product[lower : lower + HEAD, :])
        dk_sum[...] = jnp.zeros_like(dk_sum)
        dv_sum[...] = jnp.zeros_like(dv_sum)

        def body(i, carry):
            exchange.tick(spot * items + i, ticks)
            pair = i // count
            part = i - pair * count
            cols = pl.ds(pl.multiple_of(pair * PAIR, PAIR), PAIR)
            part = pl.ds(pl.multiple_of(part * block, block), block)
            for half in range(2):
                head = pl.ds(pl.multiple_of(pair * PAIR + half * HEAD, HEAD), HEAD)
                query = head_mask(q_ref[part, cols], half)
                cot = head_mask(grad[part, cols], half)
                s_held[half] = mxu(k_ref[:, cols], query, TRANSPOSED)
                p_held[half] = mxu(v_ref[:, cols], cot, TRANSPOSED)
                probs = jnp.exp2(s_held[half] * SCALE2 - tot[0, pair, half : half + 1, part])
                d_scores = (probs * (p_held[half] - inner[pair, half : half + 1, part])).astype(BF16)
                dv_sum[:, cols] += mxu(probs.astype(BF16), cot)
                dk_sum[:, cols] += mxu(d_scores, query)
                dq_turned[head, part] = mxu(k_turned[head, :], d_scores)
            return carry

        lax.fori_loop(0, items, body, 0)
        d_queries = jnp.transpose(dq_turned[...])
        for source, target in ((d_queries, dq), (dk_sum, dk)):
            for pair in range(per):
                v = source[:, pair * PAIR : (pair + 1) * PAIR] * SCALE
                v = v * cos[...] - partner_lanes(v) * sin[...]
                target[:, pair * PAIR : (pair + 1) * PAIR] = v.astype(BF16)
        dv[...] = dv_sum[...].astype(BF16)

        @pl.when(spot < seqs)
        def _():
            here = pl.ds(pl.multiple_of(seq * seq_length, seq_length), seq_length)
            for part, target in enumerate((dq, dk, dv)):
                d_held[part, here, :] = target[...]

        @pl.when(spot == seqs * steps - 1)
        def _():
            exchange.rest(ticks)

    def part_of(which):
        return pl.BlockSpec((seq_length, wide), lambda p, s: (s, which * steps + p))

    table = whole((seq_length, PAIR))
    grads = jax.ShapeDtypeStruct((rows, width), BF16)
    return call(
        kernel,
        "attend_back",
        (steps, seqs),
        [part_of(0), part_of(1), part_of(2), part_of(0), part_of(0)]
        + [pl.BlockSpec((1, per, 2, seq_length), lambda p, s: (s, p, 0, 0))]
        + [table] * 2
        + [pl.BlockSpec(memory_space=pl.ANY)] * (1 + many),
        [part_of(0), part_of(0), part_of(0)] + exchange.out_specs(),
        [grads, grads, grads] + exchange.out_shape(),
        [
            pltpu.VMEM((wide, seq_length), BF16),
            pltpu.VMEM((wide, seq_length), F32),
            pltpu.VMEM((seq_length, wide), F32),
            pltpu.VMEM((seq_length, wide), F32),
            pltpu.VMEM((per, 2, seq_length), F32),
            pltpu.VMEM((2, seq_length, block), F32),
            pltpu.VMEM((2, seq_length, block), F32),
            pltpu.VMEM(turned.shape, BF16),
            pltpu.VMEM((3, rows, wide), BF16),
            pltpu.VMEM((3, ways, share, wide), BF16),
            pltpu.SemaphoreType.DMA((1,)),
        ]
        + exchange.scratch(),
        40 * rows * seq_length * width,
        rows * width * 16,
        rows * seq_length * width // HEAD,
        ident,
    )(qkv, qkv, qkv, mixture, d_mixture, total, *tables, turned, *pieces)


def middle_norm(mixture, tokens, starts, lengths, embed, gain, modulation, weight, seqs, block=512):
    rows, width = tokens.shape
    seq_length = rows // seqs
    block = min(block, seq_length)
    per_seq = seq_length // block

    def kernel(starts, lengths, mix, tok, emb, gn, mod, w, out):
        step = pl.program_id(0)
        seq = step // per_seq
        first = (step - seq * per_seq) * block
        start, _ = masked_rows(tok[...], emb[...], starts[seq], lengths[seq], first)
        middle = start + mod[pl.ds(seq, 1), 2 * width : 3 * width] * mxu(mix[...], w[...])
        hat, _ = normalized(middle)
        shift = mod[pl.ds(seq, 1), 3 * width : 4 * width]
        scale = mod[pl.ds(seq, 1), 4 * width : 5 * width]
        out[...] = (hat * (gn[...] * (1.0 + scale)) + shift).astype(BF16)

    row = pl.BlockSpec((block, width), lambda i: (i, 0))
    return call(
        kernel,
        "middle_norm",
        (rows // block,),
        [smem(), smem(), row, row, whole((1, width)), whole((1, width)), whole(modulation.shape)]
        + [whole(weight.shape)],
        row,
        jax.ShapeDtypeStruct((rows, width), BF16),
        [],
        2 * rows * width * width,
        rows * width * 6,
    )(starts, lengths, mixture, tokens, embed, gain, modulation, weight)


def gelu_pair(v):
    root = math.sqrt(2.0 / math.pi)
    square = v * v
    near = 0.5 + 0.5 * jnp.tanh(v * (root + (root * 0.044715) * square))
    active = v * near
    bend = 2.0 * root + (6.0 * root * 0.044715) * square
    return active, near + (active * (1.0 - near)) * bend


def grouped_rows(ref, ways):
    part = ref.shape[0] // (ways * GROUPS)
    lowers = [(way * GROUPS + group) * part for group in range(GROUPS) for way in range(ways)]
    return jnp.concatenate([ref[lower : lower + part, :] for lower in lowers], axis=0)


def grouped_columns(ref, ways):
    part = ref.shape[1] // (ways * GROUPS)
    lowers = [(way * GROUPS + group) * part for group in range(GROUPS) for way in range(ways)]
    return jnp.concatenate([ref[:, lower : lower + part] for lower in lowers], axis=1)


def halved(arrays):
    return [
        (k, half * v.shape[-1] // 2, (half + 1) * v.shape[-1] // 2)
        for k, v in enumerate(arrays)
        for half in range(2)
    ]


def hidden_units(normed, cot, modulation, up, up_bias, down, times, ident, seqs, block=512):
    rows, width = normed.shape
    ways = lax.axis_size("narrow")
    units = up.shape[1] // GROUPS
    share, part_units = width // ways, units // ways
    seq_length = rows // seqs
    block = min(block, seq_length)
    per_seq = seq_length // block
    steps = rows // block
    turn = steps + ways
    shape_up, shape_down = (ways, share, units), (ways, part_units, width)
    traded = [jax.ShapeDtypeStruct(v, BF16) for v in (shape_up, shape_down) * 2]
    exchange = Exchange(
        [v.shape for v in traded], times, halved(traded), ["whole"] * 2 + ["head"] * 2
    )

    def kernel(*refs):
        nrm, g, mod, b_up = refs[:4]
        w_ups, w_downs = refs[4 : 4 + ways], refs[4 + ways : 4 + 2 * ways]
        act, d_up, g_bias, d_gate, g_sum = refs[4 + 2 * ways : 9 + 2 * ways]
        outs, left = refs[9 + 2 * ways : 15 + 2 * ways], refs[15 + 2 * ways :]
        n_turned, g_turned, a_held, u_held, down_held, g_up, g_down, near = left[:8]
        exchange.bind(
            [g_up.at[0], g_down.at[0], g_up.at[1], g_down.at[1]], outs[:4], left[8:]
        )
        step = pl.program_id(0)
        group = step // turn
        at = step - group * turn

        @pl.when(step == 0)
        def _():
            exchange.greet()
            n_turned[width:, :] = jnp.ones((16, rows), BF16)
            d_gate[...] = jnp.zeros_like(d_gate)
            g_sum[...] = jnp.zeros_like(g_sum)

        exchange.tick(step, GROUPS * turn)

        @pl.when(at == 0)
        def _():
            for way in range(ways):
                down_held[way] = w_downs[way][...]

        part = pl.ds(pl.multiple_of(jnp.minimum(at, steps - 1) * block, block), block)

        @pl.when(at < steps)
        def _():
            seq = at // per_seq
            cotangent = g[...].astype(F32)
            d_branch = (mod[pl.ds(seq, 1), 5 * width : 6 * width] * cotangent).astype(BF16)
            for way in range(ways):
                cols = slice(way * part_units, (way + 1) * part_units)
                upper = mxu(nrm[...], w_ups[way][...]) + b_up[:, cols]
                d_active = mxu(d_branch, w_downs[way][...], TRANSPOSED)
                active, slope = gelu_pair(upper)
                active = active.astype(BF16)
                d_upper = (d_active * slope).astype(BF16)
                act[:, cols] = active
                a_held[part, cols] = active
                d_up[:, cols] = d_upper
                u_held[part, cols] = d_upper

        @pl.when(step < steps)
        def _():
            store_shares(n_turned, jnp.transpose(nrm[...]), part)
            g_turned[:, part] = jnp.transpose(g[...])
            g_sum[pl.ds(at // per_seq, 1), :] += column_sum(g[...].astype(F32))

        @pl.when(at >= steps)
        def _():
            place = at - steps
            owner = owner_at(exchange.at["narrow"], place)
            cols = pl.ds(pl.multiple_of(owner * part_units, part_units), part_units)
            product = mxu(n_turned[...], u_held[:, cols])
            g_bias[:, cols] = product[width : width + 1]
            g_up[group, :, :, cols] = product[:width].astype(BF16).reshape(
                ways, share, part_units
            )
            own = down_held[owner].astype(F32)
            total = jnp.zeros((part_units, width), F32)
            for seq in range(seqs):
                lower, upper = seq * seq_length, (seq + 1) * seq_length
                product = mxu(g_turned[:, lower:upper], a_held[lower:upper, cols])
                product = jnp.transpose(product)
                total += product * mod[seq : seq + 1, 5 * width : 6 * width]
                d_gate[seq : seq + 1, :] += column_sum(product * own)
            g_down[group, place] = total.astype(BF16)

        @pl.when(step == GROUPS * turn - 1)
        def _():
            copies = [
                pltpu.make_async_copy(source.at[GROUPS - 1], target, near.at[k])
                for k, (source, target) in enumerate(((g_up, outs[4]), (g_down, outs[5])))
            ]
            for copy in copies:
                copy.start()
            exchange.rest(GROUPS * turn)
            for copy in copies:
                copy.wait()

    def early(i):
        return (jnp.minimum(lax.rem(i, turn), steps - 1), 0)

    def fixed(shape):
        return pl.BlockSpec(shape, lambda i: (0,) * len(shape))

    by_rows = pl.BlockSpec(
        (block, units), lambda i: (jnp.minimum(lax.rem(i, turn), steps - 1), i // turn)
    )
    by_group = pl.BlockSpec((1, units), lambda i: (0, i // turn))

    def up_piece(way):
        return pl.BlockSpec((width, part_units), lambda i: (0, way * GROUPS + i // turn))

    def down_piece(way):
        return pl.BlockSpec((part_units, width), lambda i: (way * GROUPS + i // turn, 0))

    assert GROUPS == 3
    anywhere = pl.BlockSpec(memory_space=pl.ANY)
    return call(
        kernel,
        "hidden_units",
        (GROUPS * turn,),
        [pl.BlockSpec((block, width), early)] * 2
        + [whole(modulation.shape), by_group]
        + [up_piece(way) for way in range(ways)]
        + [down_piece(way) for way in range(ways)],
        [by_rows, by_rows, by_group, fixed((seqs, width)), fixed((seqs, width))]
        + exchange.out_specs()
        + [anywhere] * 2,
        [
            jax.ShapeDtypeStruct((rows, units * GROUPS), BF16),
            jax.ShapeDtypeStruct((rows, units * GROUPS), BF16),
            jax.ShapeDtypeStruct((1, units * GROUPS), F32),
            jax.ShapeDtypeStruct((seqs, width), F32),
            jax.ShapeDtypeStruct((seqs, width), F32),
        ]
        + exchange.out_shape()
        + [jax.ShapeDtypeStruct(shape_up, BF16), jax.ShapeDtypeStruct(shape_down, BF16)],
        [
            pltpu.VMEM((width + 16, rows), BF16),
            pltpu.VMEM((width, rows), BF16),
            pltpu.VMEM((rows, units), BF16),
            pltpu.VMEM((rows, units), BF16),
            pltpu.VMEM((ways, part_units, width), BF16),
            pltpu.VMEM((GROUPS,) + shape_up, BF16),
            pltpu.VMEM((GROUPS,) + shape_down, BF16),
            pltpu.SemaphoreType.DMA((2,)),
        ]
        + exchange.scratch(),
        8 * rows * width * units * GROUPS,
        GROUPS * (rows * (width * 4 + units * 4) + 8 * width * units),
        rows * units * GROUPS,
        ident,
    )(normed, cot, modulation, up_bias, *[up] * ways, *[down] * ways)


def middle_back(
    mixture, tokens, cot, starts, lengths, embed, gain, modulation, out_weight, d_upper, up, seqs,
    block=256,
):
    rows, width = tokens.shape
    ways = lax.axis_size("narrow")
    seq_length = rows // seqs
    block = min(block, seq_length)
    per_seq = seq_length // block
    steps = rows // block
    hidden_width = d_upper.shape[1]
    share = width // ways

    def kernel(
        starts, lengths, mix, tok, g, emb, gn, mod, w_out, w_up, d_ups, d_middle_out, d_mix, g_out,
        sums, g_sum,
    ):
        step = pl.program_id(0)
        seq = step // per_seq
        first = (step - seq * per_seq) * block

        @pl.when(step == 0)
        def _():
            g_sum[...] = jnp.zeros_like(g_sum)

        @pl.when(step == seq * per_seq)
        def _():
            sums[...] = jnp.zeros_like(sums)

        def vector(which):
            return mod[pl.ds(seq, 1), which * width : (which + 1) * width]

        attended = mxu(mix[...], w_out[...])
        start, _ = masked_rows(tok[...], emb[...], starts[seq], lengths[seq], first)
        hat, inverse = normalized(start + vector(2) * attended)
        d_normed = mxu(d_ups[...], grouped_columns(w_up, ways), TRANSPOSED)
        d_middle = g[...].astype(F32) + norm_back(
            d_normed * (gn[...] * (1.0 + vector(4))), hat, inverse
        )
        d_middle_out[...] = d_middle
        d_attended = (vector(2) * d_middle).astype(BF16)
        d_mix[...] = mxu(d_attended, w_out[...], TRANSPOSED).astype(BF16)
        g_sum[...] += mxu(jnp.transpose(mix[...]), d_attended)
        sums[0, 0:1, :] += column_sum(d_normed)
        sums[0, 1:2, :] += column_sum(d_normed * hat)
        sums[0, 2:3, :] += column_sum(d_middle * attended)

        @pl.when(step == steps - 1)
        def _():
            for place in range(ways):
                owner = owner_at(lax.axis_index("narrow"), place)
                spot = pl.ds(pl.multiple_of(owner * share, share), share)
                g_out[place] = g_sum[spot, :].astype(BF16)

    row = pl.BlockSpec((block, width), lambda i: (i, 0))
    return call(
        kernel,
        "middle_back",
        (steps,),
        [smem(), smem(), row, row, row, whole((1, width)), whole((1, width))]
        + [whole(modulation.shape), whole(out_weight.shape), whole(up.shape)]
        + [pl.BlockSpec((block, hidden_width), lambda i: (i, 0))],
        (
            row,
            row,
            pl.BlockSpec((ways, share, width), lambda i: (0, 0, 0)),
            pl.BlockSpec((1, 8, width), lambda i: (i // per_seq, 0, 0)),
        ),
        (
            jax.ShapeDtypeStruct((rows, width), F32),
            jax.ShapeDtypeStruct((rows, width), BF16),
            jax.ShapeDtypeStruct((ways, share, width), BF16),
            jax.ShapeDtypeStruct((seqs, 8, width), F32),
        ),
        [pltpu.VMEM((width, width), F32)],
        rows * width * (2 * hidden_width + 6 * width),
        rows * (width * 12 + hidden_width * 2) + 2 * width * hidden_width,
    )(
        starts, lengths, mixture, tokens, cot, embed, gain, modulation, out_weight, up, d_upper,
    )


class Finale(Steps):
    def __init__(self, ways):
        self.ways = ways
        self.wide = lax.axis_size("wide")

    def scratch(self, columns):
        dma = pltpu.SemaphoreType.DMA
        return [
            pltpu.VMEM((self.ways, 8, columns), F32),
            pltpu.VMEM((self.ways, 8, columns), F32),
            pltpu.VMEM((self.wide, 8, columns), F32),
            dma((self.ways,)),
            dma((self.ways,)),
            dma((self.wide,)),
            dma((self.wide,)),
        ]

    def bind(self, held):
        self.parts, self.narrow_got, self.wide_got, *self.sems = held
        self.locate()

    def others(self):
        targets = []
        for offset in range(1, self.ways):
            targets.append({"narrow": lax.rem(self.at["narrow"] + offset, self.ways)})
        for offset in range(1, self.wide):
            targets.append({"wide": lax.rem(self.at["wide"] + offset, self.wide)})
        return targets

    def greet(self):
        barrier = pltpu.get_barrier_semaphore()
        targets = self.others()
        for target in targets:
            pl.semaphore_signal(
                barrier, inc=1, device_id=target, device_id_type=pl.DeviceIdType.MESH
            )
        pl.semaphore_wait(barrier, len(targets))

    def along_narrow(self, offset):
        target = lax.rem(self.at["narrow"] + offset, self.ways)
        return pltpu.make_async_remote_copy(
            src_ref=self.parts.at[target],
            dst_ref=self.narrow_got.at[self.at["narrow"]],
            send_sem=self.sems[0].at[offset],
            recv_sem=self.sems[1].at[offset],
            device_id={"narrow": target},
            device_id_type=pl.DeviceIdType.MESH,
        )

    def along_wide(self, offset):
        me = self.at["wide"]
        return pltpu.make_async_remote_copy(
            src_ref=self.wide_got.at[me],
            dst_ref=self.wide_got.at[me],
            send_sem=self.sems[2].at[offset],
            recv_sem=self.sems[3].at[offset],
            device_id={"wide": lax.rem(me + offset, self.wide)},
            device_id_type=pl.DeviceIdType.MESH,
        )

    def begin(self):
        for offset in range(1, self.ways):
            self.along_narrow(offset).start()
        me = self.at["narrow"]
        self.narrow_got[pl.ds(me, 1)] = self.parts[pl.ds(me, 1)]

    def spread(self, seqs, row_lanes):
        for offset in range(1, self.ways):
            self.along_narrow(offset).wait()
        me = self.at["wide"]
        for way in range(self.ways):
            self.wide_got[pl.ds(me, 1), way * seqs : (way + 1) * seqs, 0:row_lanes] = (
                self.narrow_got[way : way + 1, 0:seqs, 0:row_lanes]
            )
        total = self.narrow_got[0:1, :, row_lanes:]
        for way in range(1, self.ways):
            total += self.narrow_got[way : way + 1, :, row_lanes:]
        self.wide_got[pl.ds(me, 1), :, row_lanes:] = total
        for offset in range(1, self.wide):
            self.along_wide(offset).start()

    def close(self):
        for offset in range(1, self.wide):
            self.along_wide(offset).wait()


def finish(
    turned, d_parts, tokens, d_middle, mixture, starts, lengths, embed, gain, modulation, weight,
    out_weight, down_bias, active, down, features, rows_two, vectors_two, times, ident, seqs,
    wide=384, block=512, late_block=256,
):
    rows, width = tokens.shape
    ways = lax.axis_size("narrow")
    share = width // ways
    seq_length = rows // seqs
    block, late_block = min(block, seq_length), min(late_block, seq_length)
    per_seq, late_per_seq = seq_length // block, seq_length // late_block
    columns, hidden_width = modulation.shape[1] // ways, active.shape[1]
    time_width = features.shape[1]
    window = 2 * PAIR
    lanes = columns + time_width + window
    early, middle, late = 3, rows // block, rows // late_block
    steps = early + middle + late
    exchange = Exchange([(ways, share, wide)] * 3, times)
    finale = Finale(ways)

    def kernel(*refs):
        (
            starts, lengths, left, q_all, k_all, v_all, tok, d_mid, emb, gn, mod, w_qkv_all,
            tok_late, mix, w_out_all, b_down, feat, two, vec, act, w_down_all,
        ) = refs[:21]
        spot = 21
        g_tok, block_out, g_ada, g_ada_bias, g_vec = refs[spot : spot + 5]
        outs = refs[spot + 5 : spot + 8]
        grads, sums = refs[spot + 8 : spot + 10]
        d_held, w_qkv, w_out, w_down, near = refs[spot + 10 : spot + 15]
        small = spot + 15 + 7
        exchange.bind([grads.at[part] for part in range(3)], outs, refs[small:])
        finale.bind(refs[spot + 15 : small])
        step = pl.program_id(0)
        loads = [
            pltpu.make_async_copy(source, d_held.at[part], near.at[part])
            for part, source in enumerate((q_all, k_all, v_all))
        ]
        loads += [
            pltpu.make_async_copy(source, target, near.at[3 + which])
            for which, (source, target) in enumerate(
                ((w_qkv_all, w_qkv), (w_out_all, w_out), (w_down_all, w_down))
            )
        ]

        @pl.when(step == 0)
        def _():
            for load in loads:
                load.start()
            finale.greet()
            sums[...] = jnp.zeros_like(sums)

        exchange.tick(step, steps)

        for part in range(3):
            pl.when(step == part)(loads[part].wait)
        pl.when(step == early)(loads[3].wait)

        @pl.when(step == early + middle)
        def _():
            loads[4].wait()
            loads[5].wait()

        @pl.when(step < early)
        def _():
            product = mxu(left[...], d_held[step, :, width - wide :]).astype(BF16)
            grads[step] = product.reshape(ways, share, wide)

        @pl.when((step >= early) & (step < early + middle))
        def _():
            at = step - early
            seq = at // per_seq
            first = (at - seq * per_seq) * block
            start, inside = masked_rows(
                tok[...], emb[...], starts[seq], lengths[seq], first
            )
            hat, inverse = normalized(start)
            here = pl.ds(pl.multiple_of(at * block, block), block)
            d_normed = mxu(d_held[0, here, :], w_qkv[:, 0:width], TRANSPOSED)
            d_normed += mxu(d_held[1, here, :], w_qkv[:, width : 2 * width], TRANSPOSED)
            d_normed += mxu(d_held[2, here, :], w_qkv[:, 2 * width :], TRANSPOSED)
            scale = mod[pl.ds(seq, 1), width : 2 * width]
            d_start = d_mid[...] + norm_back(d_normed * (gn[...] * (1.0 + scale)), hat, inverse)
            g_tok[...] = jnp.where(inside, 0.0, d_start)
            sums[seq, 0:1, :] += column_sum(d_normed)
            sums[seq, 1:2, :] += column_sum(d_normed * hat)
            sums[seq, 2:3, :] += column_sum(jnp.where(inside, d_start, 0.0))

        @pl.when(step == early + middle)
        def _():
            parts = finale.parts
            embed_sum = jnp.zeros((1, width), F32)
            gain_sum = jnp.zeros((1, width), F32)
            for seq in range(seqs):
                shift, scale = sums[seq, 0:1, :], sums[seq, 1:2, :]
                gain_sum += scale * (1.0 + mod[seq : seq + 1, width : 2 * width])
                embed_sum += sums[seq, 2:3, :]
                row = jnp.concatenate([shift, scale * gn[...], two[seq : seq + 1, :]], axis=1)
                for way in range(ways):
                    parts[way, seq : seq + 1, 0:columns] = row[
                        :, way * columns : (way + 1) * columns
                    ]
            for way in range(ways):
                parts[way, 0:seqs, columns : columns + time_width] = feat[...]
                lower = PAIR * (share * way // PAIR)
                parts[way, 0:1, columns + time_width :] = embed_sum[:, lower : lower + window]
                parts[way, 1:2, columns + time_width :] = gain_sum[:, lower : lower + window]
                parts[way, 2:8, columns + time_width :] = vec[way, 2:8, :]
            finale.begin()

        @pl.when(step == early + middle + 2)
        def _():
            finale.spread(seqs, columns + time_width)

        @pl.when(step >= early + middle)
        def _():
            at = step - early - middle
            seq = at // late_per_seq
            first = (at - seq * late_per_seq) * late_block
            start, _ = masked_rows(
                tok_late[...], emb[...], starts[seq], lengths[seq], first
            )
            attended = mxu(mix[...], w_out[...])
            branch = mxu(act[...], grouped_rows(w_down, ways)) + b_down[...]
            hidden = start + mod[pl.ds(seq, 1), 2 * width : 3 * width] * attended
            block_out[...] = (
                hidden + mod[pl.ds(seq, 1), 5 * width : 6 * width] * branch
            ).astype(BF16)

        @pl.when(step == steps - 1)
        def _():
            finale.close()
            got = finale.wide_got
            every = got[...].reshape(finale.wide * 8, lanes)
            d_mods, feats = every[:, 0:columns], every[:, columns : columns + time_width]
            g_ada[...] = lax.dot_general(
                jnp.transpose(feats), d_mods, PLAIN, precision=FULL_PRECISION,
                preferred_element_type=F32,
            )
            g_ada_bias[...] = column_sum(d_mods)
            total = got[0, :, columns + time_width :]
            for index in range(1, finale.wide):
                total += got[index, :, columns + time_width :]
            g_vec[...] = total
            exchange.rest(steps)

    row = pl.BlockSpec((block, width), lambda i: (jnp.clip(i - early, 0, middle - 1), 0))

    def late_row(wide):
        return pl.BlockSpec(
            (late_block, wide), lambda i: (jnp.maximum(i - early - middle, 0), 0)
        )

    def fixed(shape):
        return pl.BlockSpec(shape, lambda i: (0,) * len(shape))

    anywhere = pl.BlockSpec(memory_space=pl.ANY)
    return call(
        kernel,
        "finish",
        (steps,),
        [smem(), smem(), whole(turned.shape)]
        + [anywhere] * 3
        + [row, row, whole((1, width)), whole((1, width)), whole(modulation.shape), anywhere]
        + [late_row(width), late_row(width), anywhere, whole((1, width))]
        + [whole(features.shape), whole(rows_two.shape), whole(vectors_two.shape)]
        + [late_row(hidden_width), anywhere],
        [
            row,
            late_row(width),
            fixed((time_width, columns)),
            fixed((1, columns)),
            fixed((8, window)),
        ]
        + exchange.out_specs(),
        [
            jax.ShapeDtypeStruct((rows, width), F32),
            jax.ShapeDtypeStruct((rows, width), BF16),
            jax.ShapeDtypeStruct((time_width, columns), F32),
            jax.ShapeDtypeStruct((1, columns), F32),
            jax.ShapeDtypeStruct((8, window), F32),
        ]
        + exchange.out_shape(),
        [
            pltpu.VMEM((3, ways, share, wide), BF16),
            pltpu.VMEM((seqs, 8, width), F32),
            pltpu.VMEM((3, rows, width), BF16),
            pltpu.VMEM(weight.shape, BF16),
            pltpu.VMEM(out_weight.shape, BF16),
            pltpu.VMEM(down.shape, BF16),
            pltpu.SemaphoreType.DMA((6,)),
        ]
        + finale.scratch(lanes)
        + exchange.scratch(),
        2 * rows * width * (7 * width + hidden_width),
        rows * (width * 24 + 2 * hidden_width),
        0,
        ident,
    )(
        starts, lengths, turned, *d_parts, tokens, d_middle, embed, gain, modulation, weight,        tokens, mixture, out_weight, down_bias, features, rows_two, vectors_two, active, down,
    )


def gather_first(small, ada, weight, ident):
    share, wide = weight.shape
    width = wide // 3
    columns = [(0, 0, small.shape[1]), (1, 0, ada.shape[1])]
    columns += [(2, k * width, (k + 1) * width) for k in range(3)]
    gathering = Gather([small.shape, ada.shape, weight.shape], [0] * 5, [0] * 3, columns)

    def kernel(*refs):
        gathering.bind(refs[0:3], refs[3:6], refs[6:])
        gathering.greet()
        gathering.begin(0)
        gathering.begin(1)
        gathering.begin(2)
        for k in range(5):
            gathering.relay(k)
            if k + 3 < 5:
                gathering.begin(k + 3)
            if k > 0:
                gathering.share(k - 1)
        gathering.share(4)
        for k in range(5):
            gathering.close(k)

    return call(
        kernel,
        "gather_first",
        (),
        gathering.in_specs(),
        gathering.out_specs(),
        gathering.out_shape(),
        gathering.scratch(),
        0,
        8 * share * wide,
        0,
        ident,
    )(small, ada, weight)


def assemble(ups, downs, out, qkv):
    share, units = ups[0].shape
    part, width = downs[0].shape
    ways = units // part
    groups = len(ups)

    def kernel(*refs):
        up_in, down_in = refs[:groups], refs[groups : 2 * groups]
        out_in, qkv_in = refs[2 * groups], refs[2 * groups + 1 : 2 * groups + 7]
        g_up, g_down, g_out, g_qkv = refs[2 * groups + 7 :]
        for group in range(groups):
            for way in range(ways):
                lower = (way * groups + group) * part
                g_up[:, lower : lower + part] = up_in[group][
                    :, way * part : (way + 1) * part
                ].astype(F32)
            g_down[group] = down_in[group][...].astype(F32)
        g_out[...] = out_in[...].astype(F32)
        for which in range(6):
            lower = (which % 3) * width + (which // 3) * (width // 2)
            g_qkv[:, lower : lower + width // 2] = qkv_in[which][...].astype(F32)

    pace = 4
    small, tall = share // pace, part // pace

    def rows(count, columns):
        return pl.BlockSpec((count, columns), lambda i: (i, 0))

    g_up, g_down, g_out, g_qkv = call(
        kernel,
        "assemble",
        (pace,),
        [rows(small, units)] * groups
        + [rows(tall, width)] * groups
        + [rows(small, width)]
        + [rows(small, width // 2)] * 6,
        (
            rows(small, units * groups),
            pl.BlockSpec((groups, tall, width), lambda i: (0, i, 0)),
            rows(small, width),
            rows(small, 3 * width),
        ),
        (
            jax.ShapeDtypeStruct((share, units * groups), F32),
            jax.ShapeDtypeStruct((groups, part, width), F32),
            jax.ShapeDtypeStruct((share, width), F32),
            jax.ShapeDtypeStruct((share, 3 * width), F32),
        ),
        [],
        0,
        12 * share * units * groups,
    )(*ups, *downs, out, *qkv)
    return g_up, g_down.reshape(groups * part, width), g_out, g_qkv


def per_device(
    tokens,
    timestep,
    span_start,
    span_length,
    mask_embed,
    ada_weight,
    ada_bias,
    norm_first,
    query_key_value_weight,
    output_weight,
    norm_second,
    up_projection_weight,
    up_projection_bias,
    down_projection_weight,
    down_projection_bias,
    cotangent,
):
    seqs = timestep.shape[0]
    rows, width = tokens.shape
    seq_length = rows // seqs
    ways = lax.axis_size("narrow")
    me = lax.axis_index("narrow")
    share = width // ways
    unit_share = down_projection_weight.shape[0]
    part = unit_share // GROUPS
    units = ways * part
    time_width, columns = ada_weight.shape

    vectors = (
        ada_bias, mask_embed, norm_first, norm_second, down_projection_bias, up_projection_bias,
    )
    filled, lower = jnp.zeros((32 * PAIR,), BF16), 0
    for v in vectors:
        filled += jnp.pad(v, (lower, filled.shape[0] - lower - v.shape[0]))
        lower += v.shape[0]
    small = filled.reshape(32, PAIR)
    small, ada, w_qkv = gather_first(small, ada_weight, query_key_value_weight, 0)

    small = small.reshape(ways, -1).astype(F32)
    smalls, lower = [], 0
    for v in vectors:
        smalls.append(small[:, lower : lower + v.shape[0]].reshape(1, -1))
        lower += v.shape[0]
    bias_ada, embed, gain_one, gain_two, bias_down, bias_up = smalls
    features = time_features(timestep, time_width)
    modulation = jnp.einsum(
        "sf,wfc->swc",
        features,
        ada.reshape(ways, time_width, columns).astype(F32),
        precision=FULL_PRECISION,
    ).reshape(seqs, -1) + bias_ada
    tables = rotary_tables(seq_length)

    qkv, turned_one = project(
        tokens, span_start, span_length, embed, gain_one, modulation, w_qkv, tables, seqs
    )
    thirds = [
        (which, third * size, (third + 1) * size)
        for which, size in ((1, unit_share * ways // 3), (2, width // 3))
        for third in range(3)
    ]
    mixture, total, w_out, w_up, w_down = attend(
        qkv,
        [output_weight, up_projection_weight, down_projection_weight],
        [0, 1, 3, 6, 8, 11, 13],
        [5, 5, 2],
        [(0, 0, width)] + thirds,
        1,
        seqs,
    )
    normed_two = middle_norm(
        mixture, tokens, span_start, span_length, embed, gain_two, modulation, w_out, seqs
    )
    bias_up = jnp.swapaxes(bias_up.reshape(ways, GROUPS, part), 0, 1).reshape(1, -1)
    head_times = paced([8, 9, 10, 11], [1, 5, 2, 2, 2, 1]) + paced([17, 17, 18, 19], [1, 4])
    active, d_upper, g_bias, d_gate_two, g_sum, *swaps = hidden_units(
        normed_two, cotangent, modulation, w_up, bias_up, w_down, head_times, 2, seqs
    )
    d_gate_two += bias_down * g_sum
    d_middle, d_mixture, g_out, sums_two = middle_back(
        mixture, tokens, cotangent, span_start, span_length, embed, gain_two, modulation, w_out,
        d_upper, w_up, seqs,
    )
    d_q, d_k, d_v, *done = attend_back(
        qkv, mixture, d_mixture, total, tables, turned_one, swaps[2:] + [g_out],
        ["tail"] * 2 + ["whole"] * 3, halved(swaps[2:] + [g_out]),
        [[1, 2, 5, 8, 11, 13], [2, 3, 6, 9, 12, 14], [3, 4, 7, 10, 13, 15], [4, 5, 8, 11, 14, 16]]
        + paced([0, 1, 3, 5], [1, 4, 3, 3, 4, 2])
        + paced([6, 8], [1, 3, 3, 3, 3, 2])
        + paced([12, 12, 13], [1, 3, 2, 2, 3, 1]),
        3, seqs,
    )
    scale_two = modulation[:, 4 * width : 5 * width]
    rows_two = jnp.concatenate(
        [sums_two[:, 2], sums_two[:, 0], sums_two[:, 1] * gain_two, d_gate_two], axis=1
    )
    g_norm_two = jnp.sum(sums_two[:, 1] * (1.0 + scale_two), axis=0)
    g_bias_down = jnp.sum(modulation[:, 5 * width :] * g_sum, axis=0)
    lowers = [PAIR * (share * way // PAIR) for way in range(ways)]
    vectors_two = jnp.stack(
        [
            jnp.stack([v[lower : lower + 2 * PAIR] for lower in lowers])
            for v in (g_norm_two, g_norm_two, g_norm_two, g_bias_down)
        ]
        + [g_bias[0].reshape(GROUPS, ways, part)[group] for group in range(GROUPS)]
        + [jnp.zeros((ways, 2 * PAIR), F32)],
        axis=1,
    )
    grad_tokens, block_out, grad_ada_weight, grad_ada_bias, vectors, *g_qkv = finish(
        turned_one, (d_q, d_k, d_v), tokens, d_middle, mixture, span_start, span_length, embed,
        gain_one, modulation, w_qkv, w_out, bias_down, active, w_down, features, rows_two,
        vectors_two,
        FINISH_TIMES, 4, seqs,
    )
    skip = lax.rem(share * me, PAIR)
    own = lax.dynamic_slice_in_dim(vectors[:4], skip, share, 1)
    g_ups, g_downs = (swaps[0], *done[0:4:2]), (swaps[1], *done[1:4:2])
    g_up, g_down, g_out, g_qkv = assemble(g_ups, g_downs, done[4], done[5:] + g_qkv)
    return (
        block_out,
        grad_tokens,
        own[0],
        grad_ada_weight,
        grad_ada_bias[0],
        own[1],
        g_qkv,
        g_out,
        own[2],
        g_up,
        vectors[4 : 4 + GROUPS].reshape(-1),
        g_down,
        own[3],
    )


def solution(mesh):
    rows = P(("wide", "narrow"), None)
    per_seq = P(("wide", "narrow"))
    vector, matrix, columns = P("narrow"), P("narrow", None), P(None, "narrow")
    return jax.shard_map(
        per_device,
        mesh=mesh,
        in_specs=(
            rows, per_seq, per_seq, per_seq, vector, columns, vector, vector,
            matrix, matrix, vector, matrix, vector, matrix, vector, rows,
        ),
        out_specs=(
            rows, rows, vector, columns, vector, vector, matrix, matrix, vector, matrix,
            vector, matrix, vector,
        ),
        check_vma=False,
    )
```

```python
import math

import jax
import jax.numpy as jnp
import numpy as np
from jax import lax
from jax.experimental import pallas as pl
from jax.experimental.pallas import tpu as pltpu
from jax.sharding import PartitionSpec as P

HEAD = 64
PAIR = 2 * HEAD
GROUPS = 3
HIDDEN_TIMES = [
    [8, 10, 13, 16, 18, 21, 24], [8, 10, 15, 17, 19, 23, 24], [9, 11, 17], [10, 12, 18],
    [16, 18, 21], [16, 18, 23], [17, 19, 24], [18, 20, 24],
]
MIDDLE_TIMES = [
    [0, 1, 3, 5, 7, 8], [0, 1, 3, 5, 8, 8],
]
BACK_TIMES = [
    [0, 1, 3, 5, 8, 10], [0, 1, 4, 6, 9, 11], [1, 2, 4, 7, 10, 12], [1, 2, 5, 7, 11, 14],
    [0, 2, 5, 7, 9, 13, 15], [1, 3, 6, 8, 10, 14, 16], [2, 4, 7, 9, 11, 15, 17],
    [3, 5, 8, 11, 13, 17, 19], [4, 6, 9, 12, 14, 17, 20], [5, 7, 10, 13, 15, 18, 20],
    [12, 14, 16], [12, 14, 17], [13, 15, 18],
]
FINISH_TIMES = [
    [0, 2, 4, 6, 9, 12], [0, 2, 5, 7, 10, 13], [0, 2, 5, 7, 12, 15], [1, 4, 6, 8, 11, 14, 15],
    [2, 4, 7, 10, 13, 15, 15], [3, 4, 8, 11, 14, 15, 15],
]
EPSILON = 1e-05
FULL_PRECISION = lax.Precision.HIGHEST
F32 = jnp.float32
BF16 = jnp.bfloat16
SCALE = 1.0 / math.sqrt(HEAD)
SCALE2 = SCALE * math.log2(math.e)
VMEM_BYTES = 60 << 20
PLAIN = (((1,), (0,)), ((), ()))
TRANSPOSED = (((1,), (1,)), ((), ()))


def mxu(left, right, dims=PLAIN):
    return lax.dot_general(left, right, dims, preferred_element_type=F32)


def call(
    kernel, name, grid, in_specs, out_specs, out_shape, scratch, flops, moved, exps=0, ident=None
):
    return pl.pallas_call(
        kernel,
        name=name,
        grid=grid,
        in_specs=in_specs,
        out_specs=out_specs,
        out_shape=out_shape,
        scratch_shapes=scratch,
        compiler_params=pltpu.CompilerParams(
            vmem_limit_bytes=VMEM_BYTES, collective_id=ident, has_side_effects=ident is not None
        ),
        cost_estimate=pl.CostEstimate(flops=flops, bytes_accessed=moved, transcendentals=exps),
    )


def whole(shape):
    return pl.BlockSpec(shape, lambda *_: (0,) * len(shape), pipeline_mode=pl.Buffered(1))


def column_third(which, width):
    return pl.BlockSpec((width, width), lambda *_: (0, which), pipeline_mode=pl.Buffered(1))


def smem():
    return pl.BlockSpec(memory_space=pltpu.SMEM)


def time_features(step_ids, feature_count):
    halfway = feature_count // 2
    spacing = jnp.exp(-math.log(10000.0) * jnp.arange(halfway, dtype=F32) / halfway)
    angles = step_ids.astype(F32)[:, None] * spacing[None, :]
    return jax.nn.silu(jnp.concatenate([jnp.cos(angles), jnp.sin(angles)], axis=-1))


def rotary_tables(seq_length):
    halfway = HEAD // 2
    spacing = np.exp(-math.log(10000.0) * np.arange(halfway, dtype=np.float32) / halfway)
    angles = np.arange(seq_length, dtype=np.float32)[:, None] * spacing.astype(np.float32)
    cosine, sine = np.cos(angles), np.sin(angles)
    signed = np.concatenate([-sine, sine] * 2, axis=-1)
    return np.concatenate([cosine] * 4, axis=-1), signed


def partner_lanes(v):
    lane = lax.broadcasted_iota(jnp.int32, (1, PAIR), 1)
    return jnp.where(lax.rem(lane, HEAD) < HEAD // 2, from_ahead(v), from_behind(v))


def from_ahead(v):
    return pltpu.roll(v, PAIR - HEAD // 2, 1)


def from_behind(v):
    return pltpu.roll(v, HEAD // 2, 1)


def masked_rows(tokens, embed, start, length, first_row):
    rows = tokens.shape[0]
    position = lax.broadcasted_iota(jnp.int32, (rows, 1), 0) + first_row
    inside = (position >= start) & (position < start + length)
    return jnp.where(inside, embed, tokens.astype(F32)), inside


def normalized(rows):
    centre = rows - jnp.mean(rows, axis=-1, keepdims=True)
    spread = jnp.mean(centre * centre, axis=-1, keepdims=True)
    inverse = lax.rsqrt(spread + EPSILON)
    return centre * inverse, inverse


def norm_back(d_out, hat, inverse):
    return inverse * (
        d_out
        - jnp.mean(d_out, axis=-1, keepdims=True)
        - hat * jnp.mean(d_out * hat, axis=-1, keepdims=True)
    )


def column_sum(v):
    return jnp.sum(v, axis=0, keepdims=True)


def store_shares(target, value, cols):
    me, ways = lax.axis_index("narrow"), lax.axis_size("narrow")
    share = value.shape[0] // ways
    for place in range(ways):
        lower = pl.multiple_of(place_of(me, place) * share, share)
        target[pl.ds(lower, share), cols] = value[place * share : (place + 1) * share, :]


def place_of(me, other):
    core = lax.rem(me + other, 2)
    chip = lax.rem(me // 2 + other // 2, 2)
    return 2 * (1 - core) + 1 - chip


def owner_at(me, place):
    core, chip = 1 - place // 2, 1 - lax.rem(place, 2)
    return 2 * lax.rem(me // 2 + chip, 2) + lax.rem(me + core, 2)


def project(tokens, starts, lengths, embed, gain, modulation, weight, tables, seqs, block=512):
    rows, width = tokens.shape
    seq_length = rows // seqs
    block = min(block, seq_length)
    per_seq = seq_length // block
    pairs = width // PAIR

    def kernel(starts, lengths, tok, emb, gn, mod, w_q, w_k, w_v, cos, sin, out, nt):
        step = pl.program_id(0)
        seq = step // per_seq
        first = (step - seq * per_seq) * block
        start, _ = masked_rows(tok[...], emb[...], starts[seq], lengths[seq], first)
        hat, _ = normalized(start)
        shift = mod[pl.ds(seq, 1), 0:width]
        scale = mod[pl.ds(seq, 1), width : 2 * width]
        normed = (hat * (gn[...] * (1.0 + scale)) + shift).astype(BF16)
        store_shares(nt, jnp.transpose(normed), slice(None))
        for which, w in enumerate((w_q, w_k)):
            turned = mxu(normed, w[...])
            for part in range(pairs):
                v = turned[:, part * PAIR : (part + 1) * PAIR]
                v = v * cos[...] + partner_lanes(v) * sin[...]
                lower = which * width + part * PAIR
                out[:, lower : lower + PAIR] = v.astype(BF16)
        out[:, 2 * width :] = mxu(normed, w_v[...]).astype(BF16)

    table = pl.BlockSpec((block, PAIR), lambda i: (lax.rem(i, per_seq), 0))
    return call(
        kernel,
        "project",
        (rows // block,),
        [
            smem(),
            smem(),
            pl.BlockSpec((block, width), lambda i: (i, 0)),
            whole((1, width)),
            whole((1, width)),
            whole(modulation.shape),
            column_third(0, width),
            column_third(1, width),
            column_third(2, width),
            table,
            table,
        ],
        (
            pl.BlockSpec((block, 3 * width), lambda i: (i, 0)),
            pl.BlockSpec((width, block), lambda i: (0, i)),
        ),
        (
            jax.ShapeDtypeStruct((rows, 3 * width), BF16),
            jax.ShapeDtypeStruct((width, rows), BF16),
        ),
        [],
        2 * rows * width * 3 * width,
        rows * width * 10 + 6 * width * width,
    )(starts, lengths, tokens, embed, gain, modulation, weight, weight, weight, *tables)


def flip(index, stride):
    return index + stride * (1 - 2 * lax.rem(index // stride, 2))


def exchange_stages():
    count = lax.axis_size("wide")
    strides = [1 << bit for bit in range(1, count.bit_length() - 1)]
    return [("pair", "narrow", 1), ("chip", "narrow", 2), ("split", "wide", 1)] + [
        ("full", "wide", stride) for stride in strides
    ] + [("join", "wide", 1)]


class Steps:
    def in_specs(self):
        return [pl.BlockSpec(memory_space=pl.ANY)] * self.count

    out_specs = in_specs

    def locate(self):
        self.at = {axis: lax.axis_index(axis) for axis in ("wide", "narrow")}
        self.odd = lax.rem(self.at["wide"], 2)

    def half_of(self, rows, which, lower=0):
        side = self.odd if which == 0 else 1 - self.odd
        return pl.ds(pl.multiple_of(lower + side * (rows // 2), rows // 2), rows // 2)

    def greet(self):
        barrier = pltpu.get_barrier_semaphore()
        for axis, stride in self.partners:
            pl.semaphore_signal(
                barrier,
                inc=1,
                device_id={axis: flip(self.at[axis], stride)},
                device_id_type=pl.DeviceIdType.MESH,
            )
        pl.semaphore_wait(barrier, len(self.partners))

    def push(self, source, target, sent, got, axis, stride):
        return pltpu.make_async_remote_copy(
            src_ref=source,
            dst_ref=target,
            send_sem=sent,
            recv_sem=got,
            device_id={axis: flip(self.at[axis], stride)},
            device_id_type=pl.DeviceIdType.MESH,
        )

    def tick(self, now, last, bunch=6, greet=True):
        planned = sorted(self.plan(), key=lambda item: item[:3])
        times = sorted({item[0] for item in planned if item[0] < last})
        for lower in sorted({when - when % bunch for when in times}):

            @pl.when((now >= lower) & (now < lower + bunch))
            def _(lower=lower):
                for when in times:
                    if lower <= when < lower + bunch:
                        pl.when(now == when)(
                            lambda when=when: self.take(planned, when, greet)
                        )

    def take(self, planned, when, greet):
        if when == 0 and greet:
            self.greet()
        for item in planned:
            if item[0] == when:
                item[3]()

    def rest(self, last):
        for item in sorted(self.plan(), key=lambda item: item[:3]):
            if item[0] >= last:
                item[3]()


class Gather(Steps):
    partners = (("narrow", 1), ("narrow", 2), ("wide", 1))

    def __init__(self, shapes, begins, waits, columns=None):
        columns = columns or [(k, 0, shape[1]) for k, shape in enumerate(shapes)]
        self.arrays, self.columns = shapes, columns
        self.shapes = [(shapes[k][0], upper - lower) for k, lower, upper in columns]
        self.begins, self.waits = begins, waits
        self.count = len(columns)

    def in_specs(self):
        return [pl.BlockSpec(memory_space=pl.ANY)] * len(self.arrays)

    out_specs = in_specs

    def out_shape(self):
        return [jax.ShapeDtypeStruct((4 * rows, cols), BF16) for rows, cols in self.arrays]

    def scratch(self):
        dma, held = pltpu.SemaphoreType.DMA, []
        for shape in self.shapes:
            held += [dma((5,)), dma((5,)), dma((2,)), pltpu.VMEM(shape, BF16)]
        return held

    def bind(self, ins, outs, held):
        self.refs = [
            (ins[k].at[:, lower:upper], outs[k].at[:, lower:upper])
            + tuple(held[4 * part : 4 * part + 4])
            for part, (k, lower, upper) in enumerate(self.columns)
        ]
        self.locate()

    def block(self, k, index, which=None):
        rows = self.shapes[k][0]
        if which is None:
            return pl.ds(pl.multiple_of(index * rows, rows), rows)
        return self.half_of(rows, which, index * rows)

    def remote(self, k, step):
        source, out, sent, got, _, _ = self.refs[k]
        me, across = self.at["narrow"], flip(self.at["narrow"], 2)
        axis, stride = (("narrow", 1), ("narrow", 2), ("wide", 1), ("narrow", 1), ("narrow", 1))[step]
        if step == 0:
            ends = (source, out.at[self.block(k, me), :])
        elif step == 1:
            half = self.half_of(self.shapes[k][0], 0)
            ends = (source.at[half, :], out.at[self.block(k, me, 0), :])
        else:
            spot = self.block(k, across, 1 if step == 4 else 0)
            ends = (out.at[spot, :], out.at[spot, :])
        return self.push(*ends, sent.at[step], got.at[step], axis, stride)

    def local(self, k, which):
        source, out, _, _, near, kept = self.refs[k]
        if which == 0:
            return pltpu.make_async_copy(source, kept, near.at[0])
        return pltpu.make_async_copy(
            kept, out.at[self.block(k, self.at["narrow"]), :], near.at[1]
        )

    def begin(self, k):
        self.remote(k, 1).start()
        self.remote(k, 0).start()
        self.local(k, 0).start()

    def relay(self, k):
        self.local(k, 0).wait()
        self.local(k, 1).start()
        self.remote(k, 1).wait()
        self.remote(k, 2).start()
        self.remote(k, 3).start()

    def share(self, k):
        self.remote(k, 2).wait()
        self.remote(k, 4).start()

    def close(self, k):
        self.remote(k, 0).wait()
        self.remote(k, 3).wait()
        self.remote(k, 4).wait()
        self.local(k, 1).wait()

    def plan(self):
        planned = []
        for k in range(self.count):
            when = self.begins[k]
            planned.append((when, 0, k, lambda k=k: self.begin(k)))
            for wait, act in zip(self.waits, (self.relay, self.share, self.close)):
                when += wait
                planned.append((when, 1, k, lambda k=k, act=act: act(k)))
        return planned


class Exchange(Steps):
    def __init__(self, shapes, times, columns=None, spans=None):
        columns = columns or [(k, 0, shape[-1]) for k, shape in enumerate(shapes)]
        spans = spans or ["whole"] * len(shapes)
        self.stages = exchange_stages()
        self.arrays, self.columns = [shape[-2:] for shape in shapes], columns
        self.shapes = [(self.arrays[k][0], upper - lower) for k, lower, upper in columns]
        self.spans = [spans[k] for k, _, _ in columns]
        self.firsts = [2 if span == "tail" else 0 for span in self.spans]
        self.lasts = [1 if span == "head" else len(self.stages) - 1 for span in self.spans]
        self.times = times
        self.count = len(columns)
        self.partners = sorted({(axis, stride) for _, axis, stride in self.stages})

    def in_specs(self):
        return [pl.BlockSpec(memory_space=pl.ANY)] * len(self.arrays)

    out_specs = in_specs

    def out_shape(self):
        return [jax.ShapeDtypeStruct(shape, BF16) for shape in self.arrays]

    def scratch(self):
        held = []
        dma = pltpu.SemaphoreType.DMA
        for (rows, cols), span in zip(self.shapes, self.spans):
            early, late = span != "tail", span != "head"
            held += [
                pltpu.VMEM((2, rows, cols) if early else (2, 16, PAIR), BF16),
                pltpu.VMEM((2 if early else 1, rows, cols), BF16),
                pltpu.VMEM((rows, cols) if early else (16, PAIR), BF16),
                pltpu.VMEM((len(self.stages) - 3, rows // 2, cols) if late else (1, 16, PAIR), BF16),
                pltpu.VMEM((rows // 2, cols) if late else (16, PAIR), BF16),
                dma((len(self.stages),)),
                dma((len(self.stages),)),
                dma((2,)),
            ]
        return held

    def bind(self, ins, outs, held):
        self.refs = []
        for part, (k, lower, upper) in enumerate(self.columns):
            every = (slice(None),) * (1 if self.spans[part] == "tail" else 2)
            self.refs.append(
                (ins[k].at[every + (slice(lower, upper),)], outs[k].at[:, lower:upper])
                + tuple(held[8 * part : 8 * part + 8])
            )
        self.locate()

    def own(self, k):
        kept = self.refs[k][3]
        return kept.at[0 if self.spans[k] == "tail" else 1]

    def remote(self, k, step):
        source, out, pair, kept, chip, halves, mine, sent, got, _ = self.refs[k]
        kind, axis, stride = self.stages[step]
        rows = self.shapes[k][0]
        if kind == "pair":
            ends = (source.at[0:2], pair)
        elif kind == "chip":
            ends = (kept.at[0], chip)
        elif kind == "split":
            ends = (self.own(k).at[self.half_of(rows, 1), :], halves.at[0])
        elif kind == "full":
            ends = (mine, halves.at[step - 2])
        else:
            ends = (mine, out.at[self.half_of(rows, 0), :])
        return self.push(*ends, sent.at[step], got.at[step], axis, stride)

    def load(self, k):
        source, kept, near = self.refs[k][0], self.refs[k][3], self.refs[k][9]
        if self.spans[k] == "tail":
            return pltpu.make_async_copy(source, kept.at[0], near.at[0])
        return pltpu.make_async_copy(source.at[2:4], kept, near.at[0])

    def store(self, k):
        out, mine, near = self.refs[k][1], self.refs[k][6], self.refs[k][9]
        if self.spans[k] == "head":
            return pltpu.make_async_copy(self.own(k), out, near.at[1])
        half = self.half_of(self.shapes[k][0], 0)
        return pltpu.make_async_copy(mine, out.at[half, :], near.at[1])

    def begin(self, k):
        self.load(k).start()
        if self.spans[k] != "tail":
            self.remote(k, 0).start()

    def enter(self, k):
        self.load(k).wait()
        self.remote(k, 2).start()

    def end(self, k, step):
        _, _, pair, kept, chip, halves, mine, _, _, _ = self.refs[k]
        kind = self.stages[step][0]
        self.remote(k, step).wait()
        if kind == "pair":
            self.load(k).wait()
            kept[...] = kept[...] + pair[...]
        elif kind == "chip":
            kept[1] = kept[1] + chip[...]
        elif kind == "split":
            half = self.half_of(self.shapes[k][0], 0)
            mine[...] = self.own(k)[half, :] + halves[0]
        elif kind == "full":
            mine[...] = mine[...] + halves[step - 2]
        if step < self.lasts[k]:
            self.remote(k, step + 1).start()
        if step == max(self.lasts[k] - 1, 1):
            self.store(k).start()
        if step == self.lasts[k]:
            self.store(k).wait()

    def plan(self):
        planned = []
        for k, (begin, *ends) in enumerate(self.times):
            first, last = self.firsts[k], self.lasts[k]
            planned.append((begin, 0, k, lambda k=k: self.begin(k)))
            if first:
                planned.append((ends[0], 1, k, lambda k=k: self.enter(k)))
                ends = [0] + ends
            for step in range(first, last + 1):
                when = ends[-1] if step == last else ends[min(step, 4)]
                planned.append((when, 1, k, lambda k=k, step=step: self.end(k, step)))
        return planned


def paced(begins, waits):
    return [[begin + sum(waits[:count]) for count in range(len(waits) + 1)] for begin in begins]


def head_mask(v, half):
    lane = lax.broadcasted_iota(jnp.int32, (1, PAIR), 1)
    keep = (lane < HEAD) if half == 0 else (lane >= HEAD)
    return jnp.where(keep, v, jnp.zeros_like(v))


def attend(qkv, shares, begins, waits, columns, ident, seqs, block=512, per=3):
    rows, width = qkv.shape[0], qkv.shape[1] // 3
    seq_length = rows // seqs
    block = min(block, seq_length)
    pairs = width // PAIR
    count = seq_length // block
    steps = pairs // per
    items = per * count
    wide = per * PAIR

    gathering = Gather([v.shape for v in shares], begins, waits, columns)
    many = len(shares)
    ticks = seqs * steps * items

    def kernel(*refs):
        q_ref, k_ref, v_ref = refs[:3]
        out, total = refs[3 + many : 5 + many]
        v_turned, out_turned, held = refs[5 + 2 * many : 8 + 2 * many]
        gathering.bind(refs[3 : 3 + many], refs[5 + many : 5 + 2 * many], refs[8 + 2 * many :])
        spot = pl.program_id(0) * steps + pl.program_id(1)
        v_turned[...] = jnp.transpose(v_ref[...])

        def place(i):
            pair = i // count
            part = i - pair * count
            return (
                pair,
                pl.ds(pl.multiple_of(pair * PAIR, PAIR), PAIR),
                pl.ds(pl.multiple_of(part * block, block), block),
            )

        def score(i, half):
            _, cols, part = place(i)
            held[half] = mxu(k_ref[:, cols], head_mask(q_ref[part, cols], half), TRANSPOSED)

        def finish(i, half):
            pair, _, part = place(i)
            scores = held[half]
            top = jnp.max(scores, axis=0, keepdims=True)
            exponent = jnp.exp2(scores * SCALE2 - top * SCALE2).astype(BF16)
            head = pl.ds(pl.multiple_of(pair * PAIR + half * HEAD, HEAD), HEAD)
            left = jnp.concatenate([v_turned[head, :], jnp.ones((16, seq_length), BF16)], axis=0)
            mixed = mxu(left, exponent)
            denominator = mixed[HEAD : HEAD + 1]
            out_turned[head, part] = mixed[:HEAD] * (1.0 / denominator)
            total[0, pair, half : half + 1, part] = top * SCALE2 + jnp.log2(denominator)

        score(0, 0)

        def body(i, carry):
            gathering.tick(spot * items + i, ticks)
            score(i, 1)
            finish(i, 0)
            score(jnp.minimum(i + 1, items - 1), 0)
            finish(i, 1)
            return carry

        lax.fori_loop(0, items, body, 0)
        out[...] = jnp.transpose(out_turned[...]).astype(BF16)

        @pl.when(spot == seqs * steps - 1)
        def _():
            gathering.rest(ticks)

    def part_of(which):
        return pl.BlockSpec((seq_length, wide), lambda s, p: (s, which * steps + p))

    return call(
        kernel,
        "attend",
        (seqs, steps),
        [part_of(0), part_of(1), part_of(2)] + gathering.in_specs(),
        [part_of(0), pl.BlockSpec((1, per, 2, seq_length), lambda s, p: (s, p, 0, 0))]
        + gathering.out_specs(),
        [
            jax.ShapeDtypeStruct((rows, width), BF16),
            jax.ShapeDtypeStruct((seqs, pairs, 2, seq_length), F32),
        ]
        + gathering.out_shape(),
        [
            pltpu.VMEM((wide, seq_length), BF16),
            pltpu.VMEM((wide, seq_length), F32),
            pltpu.VMEM((2, seq_length, block), F32),
        ]
        + gathering.scratch(),
        16 * rows * seq_length * width,
        rows * width * 8,
        rows * seq_length * width // HEAD,
        ident,
    )(qkv, qkv, qkv, *shares)


def attend_back(
    qkv, mixture, d_mixture, total, tables, turned, pieces, spans, columns, times, ident, seqs,
    block=512, per=3,
):
    rows, width = mixture.shape
    seq_length = rows // seqs
    block = min(block, seq_length)
    pairs = width // PAIR
    count = seq_length // block
    steps = pairs // per
    items = per * count
    wide = per * PAIR
    ways = lax.axis_size("narrow")
    share = width // ways
    own = [jax.ShapeDtypeStruct((ways, share, wide), BF16)] * 3
    traded = list(pieces) + own
    exchange = Exchange(
        [v.shape for v in traded],
        times,
        list(columns) + [(len(pieces) + part, 0, wide) for part in range(3)],
        list(spans) + ["head"] * 3,
    )
    many, outs = len(pieces), len(traded)
    assert steps == 2
    ticks = seqs * steps * items

    def kernel(*refs):
        q_ref, k_ref, v_ref, mix, grad, tot, cos, sin, turned_all = refs[:9]
        lower = 9 + many
        dq, dk, dv = refs[lower : lower + 3]
        out_refs, lower = refs[lower + 3 : lower + 3 + outs], lower + 3 + outs
        k_turned, dq_turned, dk_sum, dv_sum, inner, s_held, p_held = refs[lower : lower + 7]
        left, d_held, grads, near = refs[lower + 7 : lower + 11]
        exchange.bind(
            list(refs[9 : 9 + many]) + [grads.at[part] for part in range(3)],
            out_refs,
            refs[lower + 11 :],
        )
        seq = pl.program_id(1)
        spot = pl.program_id(0) * seqs + seq
        load = pltpu.make_async_copy(turned_all, left, near.at[0])
        pl.when(spot == 0)(load.start)

        @pl.when(spot == seqs)
        def _():
            load.wait()
            for part in range(3):
                product = mxu(left[...], d_held[part]).astype(BF16)
                grads[part] = product.reshape(ways, share, wide)

        k_turned[...] = jnp.transpose(k_ref[...])
        product = jnp.transpose(mix[...].astype(F32) * grad[...].astype(F32))
        for pair in range(per):
            for half in range(2):
                lower = pair * PAIR + half * HEAD
                inner[pair, half : half + 1, :] = column_sum(product[lower : lower + HEAD, :])
        dk_sum[...] = jnp.zeros_like(dk_sum)
        dv_sum[...] = jnp.zeros_like(dv_sum)

        def body(i, carry):
            exchange.tick(spot * items + i, ticks)
            pair = i // count
            part = i - pair * count
            cols = pl.ds(pl.multiple_of(pair * PAIR, PAIR), PAIR)
            part = pl.ds(pl.multiple_of(part * block, block), block)
            for half in range(2):
                head = pl.ds(pl.multiple_of(pair * PAIR + half * HEAD, HEAD), HEAD)
                query = head_mask(q_ref[part, cols], half)
                cot = head_mask(grad[part, cols], half)
                s_held[half] = mxu(k_ref[:, cols], query, TRANSPOSED)
                p_held[half] = mxu(v_ref[:, cols], cot, TRANSPOSED)
                probs = jnp.exp2(s_held[half] * SCALE2 - tot[0, pair, half : half + 1, part])
                d_scores = (probs * (p_held[half] - inner[pair, half : half + 1, part])).astype(BF16)
                dv_sum[:, cols] += mxu(probs.astype(BF16), cot)
                dk_sum[:, cols] += mxu(d_scores, query)
                dq_turned[head, part] = mxu(k_turned[head, :], d_scores)
            return carry

        lax.fori_loop(0, items, body, 0)
        d_queries = jnp.transpose(dq_turned[...])
        for source, target in ((d_queries, dq), (dk_sum, dk)):
            for pair in range(per):
                v = source[:, pair * PAIR : (pair + 1) * PAIR] * SCALE
                v = v * cos[...] - partner_lanes(v) * sin[...]
                target[:, pair * PAIR : (pair + 1) * PAIR] = v.astype(BF16)
        dv[...] = dv_sum[...].astype(BF16)

        @pl.when(spot < seqs)
        def _():
            here = pl.ds(pl.multiple_of(seq * seq_length, seq_length), seq_length)
            for part, target in enumerate((dq, dk, dv)):
                d_held[part, here, :] = target[...]

        @pl.when(spot == seqs * steps - 1)
        def _():
            exchange.rest(ticks)

    def part_of(which):
        return pl.BlockSpec((seq_length, wide), lambda p, s: (s, which * steps + p))

    table = whole((seq_length, PAIR))
    grads = jax.ShapeDtypeStruct((rows, width), BF16)
    return call(
        kernel,
        "attend_back",
        (steps, seqs),
        [part_of(0), part_of(1), part_of(2), part_of(0), part_of(0)]
        + [pl.BlockSpec((1, per, 2, seq_length), lambda p, s: (s, p, 0, 0))]
        + [table] * 2
        + [pl.BlockSpec(memory_space=pl.ANY)] * (1 + many),
        [part_of(0), part_of(0), part_of(0)] + exchange.out_specs(),
        [grads, grads, grads] + exchange.out_shape(),
        [
            pltpu.VMEM((wide, seq_length), BF16),
            pltpu.VMEM((wide, seq_length), F32),
            pltpu.VMEM((seq_length, wide), F32),
            pltpu.VMEM((seq_length, wide), F32),
            pltpu.VMEM((per, 2, seq_length), F32),
            pltpu.VMEM((2, seq_length, block), F32),
            pltpu.VMEM((2, seq_length, block), F32),
            pltpu.VMEM(turned.shape, BF16),
            pltpu.VMEM((3, rows, wide), BF16),
            pltpu.VMEM((3, ways, share, wide), BF16),
            pltpu.SemaphoreType.DMA((1,)),
        ]
        + exchange.scratch(),
        40 * rows * seq_length * width,
        rows * width * 16,
        rows * seq_length * width // HEAD,
        ident,
    )(qkv, qkv, qkv, mixture, d_mixture, total, *tables, turned, *pieces)


def middle_norm(mixture, tokens, starts, lengths, embed, gain, modulation, weight, seqs, block=512):
    rows, width = tokens.shape
    seq_length = rows // seqs
    block = min(block, seq_length)
    per_seq = seq_length // block

    def kernel(starts, lengths, mix, tok, emb, gn, mod, w, out):
        step = pl.program_id(0)
        seq = step // per_seq
        first = (step - seq * per_seq) * block
        start, _ = masked_rows(tok[...], emb[...], starts[seq], lengths[seq], first)
        middle = start + mod[pl.ds(seq, 1), 2 * width : 3 * width] * mxu(mix[...], w[...])
        hat, _ = normalized(middle)
        shift = mod[pl.ds(seq, 1), 3 * width : 4 * width]
        scale = mod[pl.ds(seq, 1), 4 * width : 5 * width]
        out[...] = (hat * (gn[...] * (1.0 + scale)) + shift).astype(BF16)

    row = pl.BlockSpec((block, width), lambda i: (i, 0))
    return call(
        kernel,
        "middle_norm",
        (rows // block,),
        [smem(), smem(), row, row, whole((1, width)), whole((1, width)), whole(modulation.shape)]
        + [whole(weight.shape)],
        row,
        jax.ShapeDtypeStruct((rows, width), BF16),
        [],
        2 * rows * width * width,
        rows * width * 6,
    )(starts, lengths, mixture, tokens, embed, gain, modulation, weight)


def gelu_pair(v):
    root = math.sqrt(2.0 / math.pi)
    square = v * v
    near = 0.5 + 0.5 * jnp.tanh(v * (root + (root * 0.044715) * square))
    active = v * near
    bend = 2.0 * root + (6.0 * root * 0.044715) * square
    return active, near + (active * (1.0 - near)) * bend


def grouped_rows(ref, ways):
    part = ref.shape[0] // (ways * GROUPS)
    lowers = [(way * GROUPS + group) * part for group in range(GROUPS) for way in range(ways)]
    return jnp.concatenate([ref[lower : lower + part, :] for lower in lowers], axis=0)


def grouped_columns(ref, ways):
    part = ref.shape[1] // (ways * GROUPS)
    lowers = [(way * GROUPS + group) * part for group in range(GROUPS) for way in range(ways)]
    return jnp.concatenate([ref[:, lower : lower + part] for lower in lowers], axis=1)


def halved(arrays):
    return [
        (k, half * v.shape[-1] // 2, (half + 1) * v.shape[-1] // 2)
        for k, v in enumerate(arrays)
        for half in range(2)
    ]


def hidden_units(normed, cot, modulation, up, up_bias, down, times, ident, seqs, block=512):
    rows, width = normed.shape
    ways = lax.axis_size("narrow")
    units = up.shape[1] // GROUPS
    share, part_units = width // ways, units // ways
    seq_length = rows // seqs
    block = min(block, seq_length)
    per_seq = seq_length // block
    steps = rows // block
    turn = steps + ways
    shape_up, shape_down = (ways, share, units), (ways, part_units, width)
    traded = [jax.ShapeDtypeStruct(v, BF16) for v in (shape_up, shape_down) * 2]
    exchange = Exchange(
        [v.shape for v in traded], times, halved(traded), ["whole"] + ["head"] * 3
    )

    def kernel(*refs):
        nrm, g, mod, b_up = refs[:4]
        w_ups, w_downs = refs[4 : 4 + ways], refs[4 + ways : 4 + 2 * ways]
        act, d_up, g_bias, d_gate, g_sum = refs[4 + 2 * ways : 9 + 2 * ways]
        outs, left = refs[9 + 2 * ways : 15 + 2 * ways], refs[15 + 2 * ways :]
        n_turned, g_turned, a_held, u_held, down_held, g_up, g_down, near = left[:8]
        exchange.bind(
            [g_up.at[0], g_down.at[0], g_up.at[1], g_down.at[1]], outs[:4], left[8:]
        )
        step = pl.program_id(0)
        group = step // turn
        at = step - group * turn

        @pl.when(step == 0)
        def _():
            exchange.greet()
            n_turned[width:, :] = jnp.ones((16, rows), BF16)
            d_gate[...] = jnp.zeros_like(d_gate)
            g_sum[...] = jnp.zeros_like(g_sum)

        exchange.tick(step, GROUPS * turn)

        @pl.when(at == 0)
        def _():
            for way in range(ways):
                down_held[way] = w_downs[way][...]

        part = pl.ds(pl.multiple_of(jnp.minimum(at, steps - 1) * block, block), block)

        @pl.when(at < steps)
        def _():
            seq = at // per_seq
            cotangent = g[...].astype(F32)
            d_branch = (mod[pl.ds(seq, 1), 5 * width : 6 * width] * cotangent).astype(BF16)
            for way in range(ways):
                cols = slice(way * part_units, (way + 1) * part_units)
                upper = mxu(nrm[...], w_ups[way][...]) + b_up[:, cols]
                d_active = mxu(d_branch, w_downs[way][...], TRANSPOSED)
                active, slope = gelu_pair(upper)
                active = active.astype(BF16)
                d_upper = (d_active * slope).astype(BF16)
                act[:, cols] = active
                a_held[part, cols] = active
                d_up[:, cols] = d_upper
                u_held[part, cols] = d_upper

        @pl.when(step < steps)
        def _():
            store_shares(n_turned, jnp.transpose(nrm[...]), part)
            g_turned[:, part] = jnp.transpose(g[...])
            g_sum[pl.ds(at // per_seq, 1), :] += column_sum(g[...].astype(F32))

        @pl.when(at >= steps)
        def _():
            place = at - steps
            owner = owner_at(exchange.at["narrow"], place)
            cols = pl.ds(pl.multiple_of(owner * part_units, part_units), part_units)
            product = mxu(n_turned[...], u_held[:, cols])
            g_bias[:, cols] = product[width : width + 1]
            g_up[group, :, :, cols] = product[:width].astype(BF16).reshape(
                ways, share, part_units
            )
            own = down_held[owner].astype(F32)
            total = jnp.zeros((part_units, width), F32)
            for seq in range(seqs):
                lower, upper = seq * seq_length, (seq + 1) * seq_length
                product = mxu(g_turned[:, lower:upper], a_held[lower:upper, cols])
                product = jnp.transpose(product)
                total += product * mod[seq : seq + 1, 5 * width : 6 * width]
                d_gate[seq : seq + 1, :] += column_sum(product * own)
            g_down[group, place] = total.astype(BF16)

        @pl.when(step == GROUPS * turn - 1)
        def _():
            copies = [
                pltpu.make_async_copy(source.at[GROUPS - 1], target, near.at[k])
                for k, (source, target) in enumerate(((g_up, outs[4]), (g_down, outs[5])))
            ]
            for copy in copies:
                copy.start()
            exchange.rest(GROUPS * turn)
            for copy in copies:
                copy.wait()

    def early(i):
        return (jnp.minimum(lax.rem(i, turn), steps - 1), 0)

    def fixed(shape):
        return pl.BlockSpec(shape, lambda i: (0,) * len(shape))

    by_rows = pl.BlockSpec(
        (block, units), lambda i: (jnp.minimum(lax.rem(i, turn), steps - 1), i // turn)
    )
    by_group = pl.BlockSpec((1, units), lambda i: (0, i // turn))

    def up_piece(way):
        return pl.BlockSpec((width, part_units), lambda i: (0, way * GROUPS + i // turn))

    def down_piece(way):
        return pl.BlockSpec((part_units, width), lambda i: (way * GROUPS + i // turn, 0))

    assert GROUPS == 3
    anywhere = pl.BlockSpec(memory_space=pl.ANY)
    return call(
        kernel,
        "hidden_units",
        (GROUPS * turn,),
        [pl.BlockSpec((block, width), early)] * 2
        + [whole(modulation.shape), by_group]
        + [up_piece(way) for way in range(ways)]
        + [down_piece(way) for way in range(ways)],
        [by_rows, by_rows, by_group, fixed((seqs, width)), fixed((seqs, width))]
        + exchange.out_specs()
        + [anywhere] * 2,
        [
            jax.ShapeDtypeStruct((rows, units * GROUPS), BF16),
            jax.ShapeDtypeStruct((rows, units * GROUPS), BF16),
            jax.ShapeDtypeStruct((1, units * GROUPS), F32),
            jax.ShapeDtypeStruct((seqs, width), F32),
            jax.ShapeDtypeStruct((seqs, width), F32),
        ]
        + exchange.out_shape()
        + [jax.ShapeDtypeStruct(shape_up, BF16), jax.ShapeDtypeStruct(shape_down, BF16)],
        [
            pltpu.VMEM((width + 16, rows), BF16),
            pltpu.VMEM((width, rows), BF16),
            pltpu.VMEM((rows, units), BF16),
            pltpu.VMEM((rows, units), BF16),
            pltpu.VMEM((ways, part_units, width), BF16),
            pltpu.VMEM((GROUPS,) + shape_up, BF16),
            pltpu.VMEM((GROUPS,) + shape_down, BF16),
            pltpu.SemaphoreType.DMA((2,)),
        ]
        + exchange.scratch(),
        8 * rows * width * units * GROUPS,
        GROUPS * (rows * (width * 4 + units * 4) + 8 * width * units),
        rows * units * GROUPS,
        ident,
    )(normed, cot, modulation, up_bias, *[up] * ways, *[down] * ways)


def middle_back(
    mixture, tokens, cot, starts, lengths, embed, gain, modulation, out_weight, d_upper, up, pieces, times,
    ident, seqs, block=256,
):
    rows, width = tokens.shape
    ways = lax.axis_size("narrow")
    seq_length = rows // seqs
    block = min(block, seq_length)
    per_seq = seq_length // block
    steps = rows // block
    hidden_width = d_upper.shape[1]
    share = width // ways

    many = len(pieces)
    exchange = Exchange([v.shape for v in pieces], times, halved(pieces), ["tail"] * many)

    def kernel(*refs):
        starts, lengths, mix, tok, g, emb, gn, mod, w_out, w_up, d_ups = refs[:11]
        d_middle_out, d_mix, g_out, sums = refs[11 + many : 15 + many]
        g_sum = refs[15 + 2 * many]
        exchange.bind(refs[11 : 11 + many], refs[15 + many : 15 + 2 * many], refs[16 + 2 * many :])
        step = pl.program_id(0)
        seq = step // per_seq
        first = (step - seq * per_seq) * block
        exchange.tick(step, steps)

        @pl.when(step == 0)
        def _():
            g_sum[...] = jnp.zeros_like(g_sum)

        @pl.when(step == seq * per_seq)
        def _():
            sums[...] = jnp.zeros_like(sums)

        def vector(which):
            return mod[pl.ds(seq, 1), which * width : (which + 1) * width]

        attended = mxu(mix[...], w_out[...])
        start, _ = masked_rows(tok[...], emb[...], starts[seq], lengths[seq], first)
        hat, inverse = normalized(start + vector(2) * attended)
        d_normed = mxu(d_ups[...], grouped_columns(w_up, ways), TRANSPOSED)
        d_middle = g[...].astype(F32) + norm_back(
            d_normed * (gn[...] * (1.0 + vector(4))), hat, inverse
        )
        d_middle_out[...] = d_middle
        d_attended = (vector(2) * d_middle).astype(BF16)
        d_mix[...] = mxu(d_attended, w_out[...], TRANSPOSED).astype(BF16)
        g_sum[...] += mxu(jnp.transpose(mix[...]), d_attended)
        sums[0, 0:1, :] += column_sum(d_normed)
        sums[0, 1:2, :] += column_sum(d_normed * hat)
        sums[0, 2:3, :] += column_sum(d_middle * attended)

        @pl.when(step == steps - 1)
        def _():
            for place in range(ways):
                owner = owner_at(exchange.at["narrow"], place)
                spot = pl.ds(pl.multiple_of(owner * share, share), share)
                g_out[place] = g_sum[spot, :].astype(BF16)
            exchange.rest(steps)

    row = pl.BlockSpec((block, width), lambda i: (i, 0))
    return call(
        kernel,
        "middle_back",
        (steps,),
        [smem(), smem(), row, row, row, whole((1, width)), whole((1, width))]
        + [whole(modulation.shape), whole(out_weight.shape), whole(up.shape)]
        + [pl.BlockSpec((block, hidden_width), lambda i: (i, 0))]
        + exchange.in_specs(),
        [
            row,
            row,
            pl.BlockSpec((ways, share, width), lambda i: (0, 0, 0)),
            pl.BlockSpec((1, 8, width), lambda i: (i // per_seq, 0, 0)),
        ]
        + exchange.out_specs(),
        [
            jax.ShapeDtypeStruct((rows, width), F32),
            jax.ShapeDtypeStruct((rows, width), BF16),
            jax.ShapeDtypeStruct((ways, share, width), BF16),
            jax.ShapeDtypeStruct((seqs, 8, width), F32),
        ]
        + exchange.out_shape(),
        [pltpu.VMEM((width, width), F32)] + exchange.scratch(),
        rows * width * (2 * hidden_width + 6 * width),
        rows * (width * 12 + hidden_width * 2) + 2 * width * hidden_width,
        0,
        ident,
    )(
        starts, lengths, mixture, tokens, cot, embed, gain, modulation, out_weight, up, d_upper,
        *pieces,
    )


class Finale(Steps):
    def __init__(self, ways):
        self.ways = ways
        self.wide = lax.axis_size("wide")

    def scratch(self, columns):
        dma = pltpu.SemaphoreType.DMA
        return [
            pltpu.VMEM((self.ways, 8, columns), F32),
            pltpu.VMEM((self.ways, 8, columns), F32),
            pltpu.VMEM((self.wide, 8, columns), F32),
            dma((self.ways,)),
            dma((self.ways,)),
            dma((self.wide,)),
            dma((self.wide,)),
        ]

    def bind(self, held):
        self.parts, self.narrow_got, self.wide_got, *self.sems = held
        self.locate()

    def others(self):
        targets = []
        for offset in range(1, self.ways):
            targets.append({"narrow": lax.rem(self.at["narrow"] + offset, self.ways)})
        for offset in range(1, self.wide):
            targets.append({"wide": lax.rem(self.at["wide"] + offset, self.wide)})
        return targets

    def greet(self):
        barrier = pltpu.get_barrier_semaphore()
        targets = self.others()
        for target in targets:
            pl.semaphore_signal(
                barrier, inc=1, device_id=target, device_id_type=pl.DeviceIdType.MESH
            )
        pl.semaphore_wait(barrier, len(targets))

    def along_narrow(self, offset):
        target = lax.rem(self.at["narrow"] + offset, self.ways)
        return pltpu.make_async_remote_copy(
            src_ref=self.parts.at[target],
            dst_ref=self.narrow_got.at[self.at["narrow"]],
            send_sem=self.sems[0].at[offset],
            recv_sem=self.sems[1].at[offset],
            device_id={"narrow": target},
            device_id_type=pl.DeviceIdType.MESH,
        )

    def along_wide(self, offset):
        me = self.at["wide"]
        return pltpu.make_async_remote_copy(
            src_ref=self.wide_got.at[me],
            dst_ref=self.wide_got.at[me],
            send_sem=self.sems[2].at[offset],
            recv_sem=self.sems[3].at[offset],
            device_id={"wide": lax.rem(me + offset, self.wide)},
            device_id_type=pl.DeviceIdType.MESH,
        )

    def begin(self):
        for offset in range(1, self.ways):
            self.along_narrow(offset).start()
        me = self.at["narrow"]
        self.narrow_got[pl.ds(me, 1)] = self.parts[pl.ds(me, 1)]

    def spread(self, seqs, row_lanes):
        for offset in range(1, self.ways):
            self.along_narrow(offset).wait()
        me = self.at["wide"]
        for way in range(self.ways):
            self.wide_got[pl.ds(me, 1), way * seqs : (way + 1) * seqs, 0:row_lanes] = (
                self.narrow_got[way : way + 1, 0:seqs, 0:row_lanes]
            )
        total = self.narrow_got[0:1, :, row_lanes:]
        for way in range(1, self.ways):
            total += self.narrow_got[way : way + 1, :, row_lanes:]
        self.wide_got[pl.ds(me, 1), :, row_lanes:] = total
        for offset in range(1, self.wide):
            self.along_wide(offset).start()

    def close(self):
        for offset in range(1, self.wide):
            self.along_wide(offset).wait()


def finish(
    turned, d_parts, tokens, d_middle, mixture, starts, lengths, embed, gain, modulation, weight,
    out_weight, down_bias, active, down, features, rows_two, vectors_two, pieces, times,
    ident, seqs,
    wide=384, block=512, late_block=256,
):
    rows, width = tokens.shape
    ways = lax.axis_size("narrow")
    share = width // ways
    seq_length = rows // seqs
    block, late_block = min(block, seq_length), min(late_block, seq_length)
    per_seq, late_per_seq = seq_length // block, seq_length // late_block
    columns, hidden_width = modulation.shape[1] // ways, active.shape[1]
    time_width = features.shape[1]
    window = 2 * PAIR
    lanes = columns + time_width + window
    early, middle, late = 3, rows // block, rows // late_block
    steps = early + middle + late
    exchange = Exchange(
        [v.shape for v in pieces] + [(ways, share, wide)] * 3,
        times,
        None,
        ["tail"] * 3 + ["whole"] * 3,
    )
    finale = Finale(ways)

    def kernel(*refs):
        (
            starts, lengths, left, q_all, k_all, v_all, tok, d_mid, emb, gn, mod, w_qkv_all,
            tok_late, mix, w_out_all, b_down, feat, two, vec, act, w_down_all,
        ) = refs[:21]
        spot = 24
        g_tok, block_out, g_ada, g_ada_bias, g_vec = refs[spot : spot + 5]
        outs = refs[spot + 5 : spot + 11]
        grads, sums = refs[spot + 11 : spot + 13]
        d_held, w_qkv, w_out, w_down, near = refs[spot + 13 : spot + 18]
        small = spot + 18 + 7
        exchange.bind(
            list(refs[21:24]) + [grads.at[part] for part in range(3)], outs, refs[small:]
        )
        finale.bind(refs[spot + 18 : small])
        step = pl.program_id(0)
        loads = [
            pltpu.make_async_copy(source, d_held.at[part], near.at[part])
            for part, source in enumerate((q_all, k_all, v_all))
        ]
        loads += [
            pltpu.make_async_copy(source, target, near.at[3 + which])
            for which, (source, target) in enumerate(
                ((w_qkv_all, w_qkv), (w_out_all, w_out), (w_down_all, w_down))
            )
        ]

        @pl.when(step == 0)
        def _():
            for load in loads:
                load.start()
            finale.greet()
            sums[...] = jnp.zeros_like(sums)

        exchange.tick(step, steps, greet=False)

        for part in range(3):
            pl.when(step == part)(loads[part].wait)
        pl.when(step == early)(loads[3].wait)

        @pl.when(step == early + middle)
        def _():
            loads[4].wait()
            loads[5].wait()

        @pl.when(step < early)
        def _():
            product = mxu(left[...], d_held[step, :, width - wide :]).astype(BF16)
            grads[step] = product.reshape(ways, share, wide)

        @pl.when((step >= early) & (step < early + middle))
        def _():
            at = step - early
            seq = at // per_seq
            first = (at - seq * per_seq) * block
            start, inside = masked_rows(
                tok[...], emb[...], starts[seq], lengths[seq], first
            )
            hat, inverse = normalized(start)
            here = pl.ds(pl.multiple_of(at * block, block), block)
            d_normed = mxu(d_held[0, here, :], w_qkv[:, 0:width], TRANSPOSED)
            d_normed += mxu(d_held[1, here, :], w_qkv[:, width : 2 * width], TRANSPOSED)
            d_normed += mxu(d_held[2, here, :], w_qkv[:, 2 * width :], TRANSPOSED)
            scale = mod[pl.ds(seq, 1), width : 2 * width]
            d_start = d_mid[...] + norm_back(d_normed * (gn[...] * (1.0 + scale)), hat, inverse)
            g_tok[...] = jnp.where(inside, 0.0, d_start)
            sums[seq, 0:1, :] += column_sum(d_normed)
            sums[seq, 1:2, :] += column_sum(d_normed * hat)
            sums[seq, 2:3, :] += column_sum(jnp.where(inside, d_start, 0.0))

        @pl.when(step == early + middle)
        def _():
            parts = finale.parts
            embed_sum = jnp.zeros((1, width), F32)
            gain_sum = jnp.zeros((1, width), F32)
            for seq in range(seqs):
                shift, scale = sums[seq, 0:1, :], sums[seq, 1:2, :]
                gain_sum += scale * (1.0 + mod[seq : seq + 1, width : 2 * width])
                embed_sum += sums[seq, 2:3, :]
                row = jnp.concatenate([shift, scale * gn[...], two[seq : seq + 1, :]], axis=1)
                for way in range(ways):
                    parts[way, seq : seq + 1, 0:columns] = row[
                        :, way * columns : (way + 1) * columns
                    ]
            for way in range(ways):
                parts[way, 0:seqs, columns : columns + time_width] = feat[...]
                lower = PAIR * (share * way // PAIR)
                parts[way, 0:1, columns + time_width :] = embed_sum[:, lower : lower + window]
                parts[way, 1:2, columns + time_width :] = gain_sum[:, lower : lower + window]
                parts[way, 2:8, columns + time_width :] = vec[way, 2:8, :]
            finale.begin()

        @pl.when(step == early + middle + 2)
        def _():
            finale.spread(seqs, columns + time_width)

        @pl.when(step >= early + middle)
        def _():
            at = step - early - middle
            seq = at // late_per_seq
            first = (at - seq * late_per_seq) * late_block
            start, _ = masked_rows(
                tok_late[...], emb[...], starts[seq], lengths[seq], first
            )
            attended = mxu(mix[...], w_out[...])
            branch = mxu(act[...], grouped_rows(w_down, ways)) + b_down[...]
            hidden = start + mod[pl.ds(seq, 1), 2 * width : 3 * width] * attended
            block_out[...] = (
                hidden + mod[pl.ds(seq, 1), 5 * width : 6 * width] * branch
            ).astype(BF16)

        @pl.when(step == steps - 1)
        def _():
            finale.close()
            got = finale.wide_got
            every = got[...].reshape(finale.wide * 8, lanes)
            d_mods, feats = every[:, 0:columns], every[:, columns : columns + time_width]
            g_ada[...] = lax.dot_general(
                jnp.transpose(feats), d_mods, PLAIN, precision=FULL_PRECISION,
                preferred_element_type=F32,
            )
            g_ada_bias[...] = column_sum(d_mods)
            total = got[0, :, columns + time_width :]
            for index in range(1, finale.wide):
                total += got[index, :, columns + time_width :]
            g_vec[...] = total
            exchange.rest(steps)

    row = pl.BlockSpec((block, width), lambda i: (jnp.clip(i - early, 0, middle - 1), 0))

    def late_row(wide):
        return pl.BlockSpec(
            (late_block, wide), lambda i: (jnp.maximum(i - early - middle, 0), 0)
        )

    def fixed(shape):
        return pl.BlockSpec(shape, lambda i: (0,) * len(shape))

    anywhere = pl.BlockSpec(memory_space=pl.ANY)
    return call(
        kernel,
        "finish",
        (steps,),
        [smem(), smem(), whole(turned.shape)]
        + [anywhere] * 3
        + [row, row, whole((1, width)), whole((1, width)), whole(modulation.shape), anywhere]
        + [late_row(width), late_row(width), anywhere, whole((1, width))]
        + [whole(features.shape), whole(rows_two.shape), whole(vectors_two.shape)]
        + [late_row(hidden_width)]
        + [anywhere] * 4,
        [
            row,
            late_row(width),
            fixed((time_width, columns)),
            fixed((1, columns)),
            fixed((8, window)),
        ]
        + exchange.out_specs(),
        [
            jax.ShapeDtypeStruct((rows, width), F32),
            jax.ShapeDtypeStruct((rows, width), BF16),
            jax.ShapeDtypeStruct((time_width, columns), F32),
            jax.ShapeDtypeStruct((1, columns), F32),
            jax.ShapeDtypeStruct((8, window), F32),
        ]
        + exchange.out_shape(),
        [
            pltpu.VMEM((3, ways, share, wide), BF16),
            pltpu.VMEM((seqs, 8, width), F32),
            pltpu.VMEM((3, rows, width), BF16),
            pltpu.VMEM(weight.shape, BF16),
            pltpu.VMEM(out_weight.shape, BF16),
            pltpu.VMEM(down.shape, BF16),
            pltpu.SemaphoreType.DMA((6,)),
        ]
        + finale.scratch(lanes)
        + exchange.scratch(),
        2 * rows * width * (7 * width + hidden_width),
        rows * (width * 24 + 2 * hidden_width),
        0,
        ident,
    )(
        starts, lengths, turned, *d_parts, tokens, d_middle, embed, gain, modulation, weight,        tokens, mixture, out_weight, down_bias, features, rows_two, vectors_two, active, down, *pieces,
    )


def gather_first(small, ada, weight, ident):
    share, wide = weight.shape
    width = wide // 3
    columns = [(0, 0, small.shape[1]), (1, 0, ada.shape[1])]
    columns += [(2, k * width, (k + 1) * width) for k in range(3)]
    gathering = Gather([small.shape, ada.shape, weight.shape], [0] * 5, [0] * 3, columns)

    def kernel(*refs):
        gathering.bind(refs[0:3], refs[3:6], refs[6:])
        gathering.greet()
        gathering.begin(0)
        gathering.begin(1)
        gathering.begin(2)
        for k in range(5):
            gathering.relay(k)
            if k + 3 < 5:
                gathering.begin(k + 3)
            if k > 0:
                gathering.share(k - 1)
        gathering.share(4)
        for k in range(5):
            gathering.close(k)

    return call(
        kernel,
        "gather_first",
        (),
        gathering.in_specs(),
        gathering.out_specs(),
        gathering.out_shape(),
        gathering.scratch(),
        0,
        8 * share * wide,
        0,
        ident,
    )(small, ada, weight)


def assemble(ups, downs, out, qkv):
    share, units = ups[0].shape
    part, width = downs[0].shape
    ways = units // part
    groups = len(ups)

    def kernel(*refs):
        up_in, down_in = refs[:groups], refs[groups : 2 * groups]
        out_in, qkv_in = refs[2 * groups], refs[2 * groups + 1 : 2 * groups + 7]
        g_up, g_down, g_out, g_qkv = refs[2 * groups + 7 :]
        for group in range(groups):
            for way in range(ways):
                lower = (way * groups + group) * part
                g_up[:, lower : lower + part] = up_in[group][
                    :, way * part : (way + 1) * part
                ].astype(F32)
            g_down[group] = down_in[group][...].astype(F32)
        g_out[...] = out_in[...].astype(F32)
        for which in range(6):
            lower = (which % 3) * width + (which // 3) * (width // 2)
            g_qkv[:, lower : lower + width // 2] = qkv_in[which][...].astype(F32)

    pace = 4
    small, tall = share // pace, part // pace

    def rows(count, columns):
        return pl.BlockSpec((count, columns), lambda i: (i, 0))

    g_up, g_down, g_out, g_qkv = call(
        kernel,
        "assemble",
        (pace,),
        [rows(small, units)] * groups
        + [rows(tall, width)] * groups
        + [rows(small, width)]
        + [rows(small, width // 2)] * 6,
        (
            rows(small, units * groups),
            pl.BlockSpec((groups, tall, width), lambda i: (0, i, 0)),
            rows(small, width),
            rows(small, 3 * width),
        ),
        (
            jax.ShapeDtypeStruct((share, units * groups), F32),
            jax.ShapeDtypeStruct((groups, part, width), F32),
            jax.ShapeDtypeStruct((share, width), F32),
            jax.ShapeDtypeStruct((share, 3 * width), F32),
        ),
        [],
        0,
        12 * share * units * groups,
    )(*ups, *downs, out, *qkv)
    return g_up, g_down.reshape(groups * part, width), g_out, g_qkv


def per_device(
    tokens,
    timestep,
    span_start,
    span_length,
    mask_embed,
    ada_weight,
    ada_bias,
    norm_first,
    query_key_value_weight,
    output_weight,
    norm_second,
    up_projection_weight,
    up_projection_bias,
    down_projection_weight,
    down_projection_bias,
    cotangent,
):
    seqs = timestep.shape[0]
    rows, width = tokens.shape
    seq_length = rows // seqs
    ways = lax.axis_size("narrow")
    me = lax.axis_index("narrow")
    share = width // ways
    unit_share = down_projection_weight.shape[0]
    part = unit_share // GROUPS
    units = ways * part
    time_width, columns = ada_weight.shape

    vectors = (
        ada_bias, mask_embed, norm_first, norm_second, down_projection_bias, up_projection_bias,
    )
    filled, lower = jnp.zeros((32 * PAIR,), BF16), 0
    for v in vectors:
        filled += jnp.pad(v, (lower, filled.shape[0] - lower - v.shape[0]))
        lower += v.shape[0]
    small = filled.reshape(32, PAIR)
    small, ada, w_qkv = gather_first(small, ada_weight, query_key_value_weight, 0)

    small = small.reshape(ways, -1).astype(F32)
    smalls, lower = [], 0
    for v in vectors:
        smalls.append(small[:, lower : lower + v.shape[0]].reshape(1, -1))
        lower += v.shape[0]
    bias_ada, embed, gain_one, gain_two, bias_down, bias_up = smalls
    features = time_features(timestep, time_width)
    modulation = jnp.einsum(
        "sf,wfc->swc",
        features,
        ada.reshape(ways, time_width, columns).astype(F32),
        precision=FULL_PRECISION,
    ).reshape(seqs, -1) + bias_ada
    tables = rotary_tables(seq_length)

    qkv, turned_one = project(
        tokens, span_start, span_length, embed, gain_one, modulation, w_qkv, tables, seqs
    )
    thirds = [
        (which, third * size, (third + 1) * size)
        for which, size in ((1, unit_share * ways // 3), (2, width // 3))
        for third in range(3)
    ]
    mixture, total, w_out, w_up, w_down = attend(
        qkv,
        [output_weight, up_projection_weight, down_projection_weight],
        [0, 1, 3, 6, 8, 11, 13],
        [5, 5, 2],
        [(0, 0, width)] + thirds,
        1,
        seqs,
    )
    normed_two = middle_norm(
        mixture, tokens, span_start, span_length, embed, gain_two, modulation, w_out, seqs
    )
    bias_up = jnp.swapaxes(bias_up.reshape(ways, GROUPS, part), 0, 1).reshape(1, -1)
    head_times = HIDDEN_TIMES
    active, d_upper, g_bias, d_gate_two, g_sum, *swaps = hidden_units(
        normed_two, cotangent, modulation, w_up, bias_up, w_down, head_times, 2, seqs
    )
    d_gate_two += bias_down * g_sum
    d_middle, d_mixture, g_out, sums_two, g_down_first = middle_back(
        mixture, tokens, cotangent, span_start, span_length, embed, gain_two, modulation, w_out,
        d_upper, w_up, swaps[1:2], MIDDLE_TIMES, 5, seqs,
    )
    d_q, d_k, d_v, *done = attend_back(
        qkv, mixture, d_mixture, total, tables, turned_one, swaps[2:] + [g_out],
        ["tail"] * 2 + ["whole"] * 3, halved(swaps[2:] + [g_out]),
        BACK_TIMES,
        3, seqs,
    )
    scale_two = modulation[:, 4 * width : 5 * width]
    rows_two = jnp.concatenate(
        [sums_two[:, 2], sums_two[:, 0], sums_two[:, 1] * gain_two, d_gate_two], axis=1
    )
    g_norm_two = jnp.sum(sums_two[:, 1] * (1.0 + scale_two), axis=0)
    g_bias_down = jnp.sum(modulation[:, 5 * width :] * g_sum, axis=0)
    lowers = [PAIR * (share * way // PAIR) for way in range(ways)]
    vectors_two = jnp.stack(
        [
            jnp.stack([v[lower : lower + 2 * PAIR] for lower in lowers])
            for v in (g_norm_two, g_norm_two, g_norm_two, g_bias_down)
        ]
        + [g_bias[0].reshape(GROUPS, ways, part)[group] for group in range(GROUPS)]
        + [jnp.zeros((ways, 2 * PAIR), F32)],
        axis=1,
    )
    grad_tokens, block_out, grad_ada_weight, grad_ada_bias, vectors, *g_qkv = finish(
        turned_one, (d_q, d_k, d_v), tokens, d_middle, mixture, span_start, span_length, embed,
        gain_one, modulation, w_qkv, w_out, bias_down, active, w_down, features, rows_two,
        vectors_two,
        done[5:], FINISH_TIMES, 4, seqs,
    )
    skip = lax.rem(share * me, PAIR)
    own = lax.dynamic_slice_in_dim(vectors[:4], skip, share, 1)
    g_ups, g_downs = (swaps[0], *done[0:4:2]), (g_down_first, *done[1:4:2])
    g_up, g_down, g_out, g_qkv = assemble(g_ups, g_downs, done[4], g_qkv)
    return (
        block_out,
        grad_tokens,
        own[0],
        grad_ada_weight,
        grad_ada_bias[0],
        own[1],
        g_qkv,
        g_out,
        own[2],
        g_up,
        vectors[4 : 4 + GROUPS].reshape(-1),
        g_down,
        own[3],
    )


def solution(mesh):
    rows = P(("wide", "narrow"), None)
    per_seq = P(("wide", "narrow"))
    vector, matrix, columns = P("narrow"), P("narrow", None), P(None, "narrow")
    return jax.shard_map(
        per_device,
        mesh=mesh,
        in_specs=(
            rows, per_seq, per_seq, per_seq, vector, columns, vector, vector,
            matrix, matrix, vector, matrix, vector, matrix, vector, rows,
        ),
        out_specs=(
            rows, rows, vector, columns, vector, vector, matrix, matrix, vector, matrix,
            vector, matrix, vector,
        ),
        check_vma=False,
    )
```

```python
import math

import jax
import jax.numpy as jnp
import numpy as np
from jax import lax
from jax.experimental import pallas as pl
from jax.experimental.pallas import tpu as pltpu
from jax.sharding import PartitionSpec as P

HEAD = 64
PAIR = 2 * HEAD
GROUPS = 3
FINISH_TIMES = [
    [1, 3, 5, 6, 7, 10, 12], [2, 4, 6, 7, 9, 12, 14], [3, 4, 7, 9, 11, 14, 15],
]
EPSILON = 1e-05
FULL_PRECISION = lax.Precision.HIGHEST
F32 = jnp.float32
BF16 = jnp.bfloat16
SCALE = 1.0 / math.sqrt(HEAD)
SCALE2 = SCALE * math.log2(math.e)
VMEM_BYTES = 60 << 20
PLAIN = (((1,), (0,)), ((), ()))
TRANSPOSED = (((1,), (1,)), ((), ()))


def mxu(left, right, dims=PLAIN):
    return lax.dot_general(left, right, dims, preferred_element_type=F32)


def call(
    kernel, name, grid, in_specs, out_specs, out_shape, scratch, flops, moved, exps=0, ident=None
):
    return pl.pallas_call(
        kernel,
        name=name,
        grid=grid,
        in_specs=in_specs,
        out_specs=out_specs,
        out_shape=out_shape,
        scratch_shapes=scratch,
        compiler_params=pltpu.CompilerParams(
            vmem_limit_bytes=VMEM_BYTES, collective_id=ident, has_side_effects=ident is not None
        ),
        cost_estimate=pl.CostEstimate(flops=flops, bytes_accessed=moved, transcendentals=exps),
    )


def whole(shape):
    return pl.BlockSpec(shape, lambda *_: (0,) * len(shape), pipeline_mode=pl.Buffered(1))


def column_third(which, width):
    return pl.BlockSpec((width, width), lambda *_: (0, which), pipeline_mode=pl.Buffered(1))


def smem():
    return pl.BlockSpec(memory_space=pltpu.SMEM)


def time_features(step_ids, feature_count):
    halfway = feature_count // 2
    spacing = jnp.exp(-math.log(10000.0) * jnp.arange(halfway, dtype=F32) / halfway)
    angles = step_ids.astype(F32)[:, None] * spacing[None, :]
    return jax.nn.silu(jnp.concatenate([jnp.cos(angles), jnp.sin(angles)], axis=-1))


def rotary_tables(seq_length):
    halfway = HEAD // 2
    spacing = np.exp(-math.log(10000.0) * np.arange(halfway, dtype=np.float32) / halfway)
    angles = np.arange(seq_length, dtype=np.float32)[:, None] * spacing.astype(np.float32)
    cosine, sine = np.cos(angles), np.sin(angles)
    signed = np.concatenate([-sine, sine] * 2, axis=-1)
    return np.concatenate([cosine] * 4, axis=-1), signed


def partner_lanes(v):
    lane = lax.broadcasted_iota(jnp.int32, (1, PAIR), 1)
    return jnp.where(lax.rem(lane, HEAD) < HEAD // 2, from_ahead(v), from_behind(v))


def from_ahead(v):
    return pltpu.roll(v, PAIR - HEAD // 2, 1)


def from_behind(v):
    return pltpu.roll(v, HEAD // 2, 1)


def masked_rows(tokens, embed, start, length, first_row):
    rows = tokens.shape[0]
    position = lax.broadcasted_iota(jnp.int32, (rows, 1), 0) + first_row
    inside = (position >= start) & (position < start + length)
    return jnp.where(inside, embed, tokens.astype(F32)), inside


def normalized(rows):
    centre = rows - jnp.mean(rows, axis=-1, keepdims=True)
    spread = jnp.mean(centre * centre, axis=-1, keepdims=True)
    inverse = lax.rsqrt(spread + EPSILON)
    return centre * inverse, inverse


def norm_back(d_out, hat, inverse):
    return inverse * (
        d_out
        - jnp.mean(d_out, axis=-1, keepdims=True)
        - hat * jnp.mean(d_out * hat, axis=-1, keepdims=True)
    )


def column_sum(v):
    return jnp.sum(v, axis=0, keepdims=True)


def store_shares(target, value, cols):
    me, ways = lax.axis_index("narrow"), lax.axis_size("narrow")
    share = value.shape[0] // ways
    for place in range(ways):
        lower = pl.multiple_of(place_of(me, place) * share, share)
        target[pl.ds(lower, share), cols] = value[place * share : (place + 1) * share, :]


def place_of(me, other):
    core = lax.rem(me + other, 2)
    chip = lax.rem(me // 2 + other // 2, 2)
    return 2 * (1 - core) + 1 - chip


def owner_at(me, place):
    core, chip = 1 - place // 2, 1 - lax.rem(place, 2)
    return 2 * lax.rem(me // 2 + chip, 2) + lax.rem(me + core, 2)


def project(tokens, starts, lengths, embed, gain, modulation, weight, tables, seqs, block=512):
    rows, width = tokens.shape
    seq_length = rows // seqs
    block = min(block, seq_length)
    per_seq = seq_length // block
    pairs = width // PAIR

    def kernel(starts, lengths, tok, emb, gn, mod, w_q, w_k, w_v, cos, sin, out, nt):
        step = pl.program_id(0)
        seq = step // per_seq
        first = (step - seq * per_seq) * block
        start, _ = masked_rows(tok[...], emb[...], starts[seq], lengths[seq], first)
        hat, _ = normalized(start)
        shift = mod[pl.ds(seq, 1), 0:width]
        scale = mod[pl.ds(seq, 1), width : 2 * width]
        normed = (hat * (gn[...] * (1.0 + scale)) + shift).astype(BF16)
        store_shares(nt, jnp.transpose(normed), slice(None))
        for which, w in enumerate((w_q, w_k)):
            turned = mxu(normed, w[...])
            for part in range(pairs):
                v = turned[:, part * PAIR : (part + 1) * PAIR]
                v = v * cos[...] + partner_lanes(v) * sin[...]
                lower = which * width + part * PAIR
                out[:, lower : lower + PAIR] = v.astype(BF16)
        out[:, 2 * width :] = mxu(normed, w_v[...]).astype(BF16)

    table = pl.BlockSpec((block, PAIR), lambda i: (lax.rem(i, per_seq), 0))
    return call(
        kernel,
        "project",
        (rows // block,),
        [
            smem(),
            smem(),
            pl.BlockSpec((block, width), lambda i: (i, 0)),
            whole((1, width)),
            whole((1, width)),
            whole(modulation.shape),
            column_third(0, width),
            column_third(1, width),
            column_third(2, width),
            table,
            table,
        ],
        (
            pl.BlockSpec((block, 3 * width), lambda i: (i, 0)),
            pl.BlockSpec((width, block), lambda i: (0, i)),
        ),
        (
            jax.ShapeDtypeStruct((rows, 3 * width), BF16),
            jax.ShapeDtypeStruct((width, rows), BF16),
        ),
        [],
        2 * rows * width * 3 * width,
        rows * width * 10 + 6 * width * width,
    )(starts, lengths, tokens, embed, gain, modulation, weight, weight, weight, *tables)


def flip(index, stride):
    return index + stride * (1 - 2 * lax.rem(index // stride, 2))


def exchange_stages():
    count = lax.axis_size("wide")
    strides = [1 << bit for bit in range(1, count.bit_length() - 1)]
    return [("pair", "narrow", 1), ("chip", "narrow", 2), ("split", "wide", 1)] + [
        ("full", "wide", stride) for stride in strides
    ] + [("join", "wide", 1)]


class Steps:
    def in_specs(self):
        return [pl.BlockSpec(memory_space=pl.ANY)] * self.count

    out_specs = in_specs

    def locate(self):
        self.at = {axis: lax.axis_index(axis) for axis in ("wide", "narrow")}
        self.odd = lax.rem(self.at["wide"], 2)

    def half_of(self, rows, which, lower=0):
        side = self.odd if which == 0 else 1 - self.odd
        return pl.ds(pl.multiple_of(lower + side * (rows // 2), rows // 2), rows // 2)

    def greet(self):
        barrier = pltpu.get_barrier_semaphore()
        for axis, stride in self.partners:
            pl.semaphore_signal(
                barrier,
                inc=1,
                device_id={axis: flip(self.at[axis], stride)},
                device_id_type=pl.DeviceIdType.MESH,
            )
        pl.semaphore_wait(barrier, len(self.partners))

    def push(self, source, target, sent, got, axis, stride):
        return pltpu.make_async_remote_copy(
            src_ref=source,
            dst_ref=target,
            send_sem=sent,
            recv_sem=got,
            device_id={axis: flip(self.at[axis], stride)},
            device_id_type=pl.DeviceIdType.MESH,
        )

    def tick(self, now, last, bunch=6):
        planned = sorted(self.plan(), key=lambda item: item[:3])
        times = sorted({item[0] for item in planned if item[0] < last})
        for lower in sorted({when - when % bunch for when in times}):

            @pl.when((now >= lower) & (now < lower + bunch))
            def _(lower=lower):
                for when in times:
                    if lower <= when < lower + bunch:
                        pl.when(now == when)(lambda when=when: self.take(planned, when))

    def take(self, planned, when):
        if when == 0:
            self.greet()
        for item in planned:
            if item[0] == when:
                item[3]()

    def rest(self, last):
        for item in sorted(self.plan(), key=lambda item: item[:3]):
            if item[0] >= last:
                item[3]()


class Gather(Steps):
    partners = (("narrow", 1), ("narrow", 2), ("wide", 1))

    def __init__(self, shapes, begins, waits, columns=None):
        columns = columns or [(k, 0, shape[1]) for k, shape in enumerate(shapes)]
        self.arrays, self.columns = shapes, columns
        self.shapes = [(shapes[k][0], upper - lower) for k, lower, upper in columns]
        self.begins, self.waits = begins, waits
        self.count = len(columns)

    def in_specs(self):
        return [pl.BlockSpec(memory_space=pl.ANY)] * len(self.arrays)

    out_specs = in_specs

    def out_shape(self):
        return [jax.ShapeDtypeStruct((4 * rows, cols), BF16) for rows, cols in self.arrays]

    def scratch(self):
        dma, held = pltpu.SemaphoreType.DMA, []
        for shape in self.shapes:
            held += [dma((5,)), dma((5,)), dma((2,)), pltpu.VMEM(shape, BF16)]
        return held

    def bind(self, ins, outs, held):
        self.refs = [
            (ins[k].at[:, lower:upper], outs[k].at[:, lower:upper])
            + tuple(held[4 * part : 4 * part + 4])
            for part, (k, lower, upper) in enumerate(self.columns)
        ]
        self.locate()

    def block(self, k, index, which=None):
        rows = self.shapes[k][0]
        if which is None:
            return pl.ds(pl.multiple_of(index * rows, rows), rows)
        return self.half_of(rows, which, index * rows)

    def remote(self, k, step):
        source, out, sent, got, _, _ = self.refs[k]
        me, across = self.at["narrow"], flip(self.at["narrow"], 2)
        axis, stride = (("narrow", 1), ("narrow", 2), ("wide", 1), ("narrow", 1), ("narrow", 1))[step]
        if step == 0:
            ends = (source, out.at[self.block(k, me), :])
        elif step == 1:
            half = self.half_of(self.shapes[k][0], 0)
            ends = (source.at[half, :], out.at[self.block(k, me, 0), :])
        else:
            spot = self.block(k, across, 1 if step == 4 else 0)
            ends = (out.at[spot, :], out.at[spot, :])
        return self.push(*ends, sent.at[step], got.at[step], axis, stride)

    def local(self, k, which):
        source, out, _, _, near, kept = self.refs[k]
        if which == 0:
            return pltpu.make_async_copy(source, kept, near.at[0])
        return pltpu.make_async_copy(
            kept, out.at[self.block(k, self.at["narrow"]), :], near.at[1]
        )

    def begin(self, k):
        self.remote(k, 1).start()
        self.remote(k, 0).start()
        self.local(k, 0).start()

    def relay(self, k):
        self.local(k, 0).wait()
        self.local(k, 1).start()
        self.remote(k, 1).wait()
        self.remote(k, 2).start()
        self.remote(k, 3).start()

    def share(self, k):
        self.remote(k, 2).wait()
        self.remote(k, 4).start()

    def close(self, k):
        self.remote(k, 0).wait()
        self.remote(k, 3).wait()
        self.remote(k, 4).wait()
        self.local(k, 1).wait()

    def plan(self):
        planned = []
        for k in range(self.count):
            when = self.begins[k]
            planned.append((when, 0, k, lambda k=k: self.begin(k)))
            for wait, act in zip(self.waits, (self.relay, self.share, self.close)):
                when += wait
                planned.append((when, 1, k, lambda k=k, act=act: act(k)))
        return planned


class Exchange(Steps):
    def __init__(self, shapes, times, columns=None, spans=None, near=()):
        columns = columns or [(k, 0, shape[-1]) for k, shape in enumerate(shapes)]
        spans = spans or ["whole"] * len(shapes)
        self.stages = exchange_stages()
        self.arrays, self.columns = [shape[-2:] for shape in shapes], columns
        self.shapes = [(self.arrays[k][0], upper - lower) for k, lower, upper in columns]
        self.spans = [spans[k] for k, _, _ in columns]
        self.near = [k in near for k, _, _ in columns]
        self.firsts = [2 if span == "tail" else 0 for span in self.spans]
        self.lasts = [1 if span == "head" else len(self.stages) - 1 for span in self.spans]
        self.times = times
        self.count = len(columns)
        self.partners = sorted({(axis, stride) for _, axis, stride in self.stages})

    def in_specs(self):
        return [pl.BlockSpec(memory_space=pl.ANY)] * len(self.arrays)

    out_specs = in_specs

    def out_shape(self):
        return [jax.ShapeDtypeStruct(shape, BF16) for shape in self.arrays]

    def scratch(self):
        held = []
        dma = pltpu.SemaphoreType.DMA
        for (rows, cols), span, near in zip(self.shapes, self.spans, self.near):
            early, late = span != "tail", span != "head"
            held += [
                pltpu.VMEM((2, rows, cols) if early else (2, 16, PAIR), BF16),
                pltpu.VMEM((2, 16, PAIR) if near else (2 if early else 1, rows, cols), BF16),
                pltpu.VMEM((rows, cols) if early else (16, PAIR), BF16),
                pltpu.VMEM((len(self.stages) - 3, rows // 2, cols) if late else (1, 16, PAIR), BF16),
                pltpu.VMEM((rows // 2, cols) if late else (16, PAIR), BF16),
                dma((len(self.stages),)),
                dma((len(self.stages),)),
                dma((2,)),
            ]
        return held

    def bind(self, ins, outs, held):
        self.refs = []
        for part, (k, lower, upper) in enumerate(self.columns):
            every = (slice(None),) * (1 if self.spans[part] == "tail" else 2)
            source, own = ins[k].at[every + (slice(lower, upper),)], held[8 * part : 8 * part + 8]
            if self.near[part]:
                own = [own[0], source.at[2:4]] + list(own[2:])
            self.refs.append((source, outs[k].at[:, lower:upper], *own))
        self.locate()

    def own(self, k):
        kept = self.refs[k][3]
        return kept.at[0 if self.spans[k] == "tail" else 1]

    def remote(self, k, step):
        source, out, pair, kept, chip, halves, mine, sent, got, _ = self.refs[k]
        kind, axis, stride = self.stages[step]
        rows = self.shapes[k][0]
        if kind == "pair":
            ends = (source.at[0:2], pair)
        elif kind == "chip":
            ends = (kept.at[0], chip)
        elif kind == "split":
            ends = (self.own(k).at[self.half_of(rows, 1), :], halves.at[0])
        elif kind == "full":
            ends = (mine, halves.at[step - 2])
        else:
            ends = (mine, out.at[self.half_of(rows, 0), :])
        return self.push(*ends, sent.at[step], got.at[step], axis, stride)

    def load(self, k):
        source, kept, near = self.refs[k][0], self.refs[k][3], self.refs[k][9]
        if self.spans[k] == "tail":
            return pltpu.make_async_copy(source, kept.at[0], near.at[0])
        return pltpu.make_async_copy(source.at[2:4], kept, near.at[0])

    def store(self, k):
        out, mine, near = self.refs[k][1], self.refs[k][6], self.refs[k][9]
        if self.spans[k] == "head":
            return pltpu.make_async_copy(self.own(k), out, near.at[1])
        half = self.half_of(self.shapes[k][0], 0)
        return pltpu.make_async_copy(mine, out.at[half, :], near.at[1])

    def begin(self, k):
        if not self.near[k]:
            self.load(k).start()
        if self.spans[k] != "tail":
            self.remote(k, 0).start()

    def enter(self, k):
        self.load(k).wait()
        self.remote(k, 2).start()

    def end(self, k, step):
        _, _, pair, kept, chip, halves, mine, _, _, _ = self.refs[k]
        kind = self.stages[step][0]
        self.remote(k, step).wait()
        if kind == "pair":
            if not self.near[k]:
                self.load(k).wait()
            kept[...] = kept[...] + pair[...]
        elif kind == "chip":
            kept[1] = kept[1] + chip[...]
        elif kind == "split":
            half = self.half_of(self.shapes[k][0], 0)
            mine[...] = self.own(k)[half, :] + halves[0]
        elif kind == "full":
            mine[...] = mine[...] + halves[step - 2]
        if step < self.lasts[k]:
            self.remote(k, step + 1).start()
        if step == max(self.lasts[k] - 1, 1):
            self.store(k).start()
        if step == self.lasts[k]:
            self.store(k).wait()

    def plan(self):
        planned = []
        for k, (begin, *ends) in enumerate(self.times):
            first, last = self.firsts[k], self.lasts[k]
            planned.append((begin, 0, k, lambda k=k: self.begin(k)))
            if first:
                planned.append((ends[0], 1, k, lambda k=k: self.enter(k)))
                ends = [0] + ends
            for step in range(first, last + 1):
                when = ends[-1] if step == last else ends[min(step, 4)]
                planned.append((when, 1, k, lambda k=k, step=step: self.end(k, step)))
        return planned


def paced(begins, waits):
    return [[begin + sum(waits[:count]) for count in range(len(waits) + 1)] for begin in begins]


def head_mask(v, half):
    lane = lax.broadcasted_iota(jnp.int32, (1, PAIR), 1)
    keep = (lane < HEAD) if half == 0 else (lane >= HEAD)
    return jnp.where(keep, v, jnp.zeros_like(v))


def attend(qkv, shares, begins, waits, columns, ident, seqs, block=512, per=3):
    rows, width = qkv.shape[0], qkv.shape[1] // 3
    seq_length = rows // seqs
    block = min(block, seq_length)
    pairs = width // PAIR
    count = seq_length // block
    steps = pairs // per
    items = per * count
    wide = per * PAIR

    gathering = Gather([v.shape for v in shares], begins, waits, columns)
    many = len(shares)
    ticks = seqs * steps * items

    def kernel(*refs):
        q_ref, k_ref, v_ref = refs[:3]
        out, total = refs[3 + many : 5 + many]
        v_turned, out_turned, held = refs[5 + 2 * many : 8 + 2 * many]
        gathering.bind(refs[3 : 3 + many], refs[5 + many : 5 + 2 * many], refs[8 + 2 * many :])
        spot = pl.program_id(0) * steps + pl.program_id(1)
        v_turned[...] = jnp.transpose(v_ref[...])

        def place(i):
            pair = i // count
            part = i - pair * count
            return (
                pair,
                pl.ds(pl.multiple_of(pair * PAIR, PAIR), PAIR),
                pl.ds(pl.multiple_of(part * block, block), block),
            )

        def score(i, half):
            _, cols, part = place(i)
            held[half] = mxu(k_ref[:, cols], head_mask(q_ref[part, cols], half), TRANSPOSED)

        def finish(i, half):
            pair, _, part = place(i)
            scores = held[half]
            top = jnp.max(scores, axis=0, keepdims=True)
            exponent = jnp.exp2(scores * SCALE2 - top * SCALE2).astype(BF16)
            head = pl.ds(pl.multiple_of(pair * PAIR + half * HEAD, HEAD), HEAD)
            left = jnp.concatenate([v_turned[head, :], jnp.ones((16, seq_length), BF16)], axis=0)
            mixed = mxu(left, exponent)
            denominator = mixed[HEAD : HEAD + 1]
            out_turned[head, part] = mixed[:HEAD] * (1.0 / denominator)
            total[0, pair, half : half + 1, part] = top * SCALE2 + jnp.log2(denominator)

        score(0, 0)

        def body(i, carry):
            gathering.tick(spot * items + i, ticks)
            score(i, 1)
            finish(i, 0)
            score(jnp.minimum(i + 1, items - 1), 0)
            finish(i, 1)
            return carry

        lax.fori_loop(0, items, body, 0)
        out[...] = jnp.transpose(out_turned[...]).astype(BF16)

        @pl.when(spot == seqs * steps - 1)
        def _():
            gathering.rest(ticks)

    def part_of(which):
        return pl.BlockSpec((seq_length, wide), lambda s, p: (s, which * steps + p))

    return call(
        kernel,
        "attend",
        (seqs, steps),
        [part_of(0), part_of(1), part_of(2)] + gathering.in_specs(),
        [part_of(0), pl.BlockSpec((1, per, 2, seq_length), lambda s, p: (s, p, 0, 0))]
        + gathering.out_specs(),
        [
            jax.ShapeDtypeStruct((rows, width), BF16),
            jax.ShapeDtypeStruct((seqs, pairs, 2, seq_length), F32),
        ]
        + gathering.out_shape(),
        [
            pltpu.VMEM((wide, seq_length), BF16),
            pltpu.VMEM((wide, seq_length), F32),
            pltpu.VMEM((2, seq_length, block), F32),
        ]
        + gathering.scratch(),
        16 * rows * seq_length * width,
        rows * width * 8,
        rows * seq_length * width // HEAD,
        ident,
    )(qkv, qkv, qkv, *shares)


def attend_back(
    qkv, mixture, d_mixture, total, tables, turned, pieces, spans, columns, times, ident, seqs,
    block=512, per=3,
):
    rows, width = mixture.shape
    seq_length = rows // seqs
    block = min(block, seq_length)
    pairs = width // PAIR
    count = seq_length // block
    steps = pairs // per
    items = per * count
    wide = per * PAIR
    ways = lax.axis_size("narrow")
    share = width // ways
    own = [jax.ShapeDtypeStruct((ways, share, wide), BF16)] * 3
    traded = list(pieces) + own
    exchange = Exchange(
        [v.shape for v in traded],
        times,
        list(columns) + [(len(pieces) + part, 0, wide) for part in range(3)],
        list(spans) + ["whole"] * 3,
        [len(pieces) + part for part in range(3)],
    )
    many, outs = len(pieces), len(traded)
    assert steps == 2
    ticks = seqs * steps * items

    def kernel(*refs):
        q_ref, k_ref, v_ref, mix, grad, tot, cos, sin, turned_all = refs[:9]
        lower = 9 + many
        dq, dk, dv = refs[lower : lower + 3]
        out_refs, lower = refs[lower + 3 : lower + 3 + outs], lower + 3 + outs
        k_turned, dq_turned, dk_sum, dv_sum, inner, s_held, p_held = refs[lower : lower + 7]
        left, d_held, grads, near = refs[lower + 7 : lower + 11]
        exchange.bind(
            list(refs[9 : 9 + many]) + [grads.at[part] for part in range(3)],
            out_refs,
            refs[lower + 11 :],
        )
        seq = pl.program_id(1)
        spot = pl.program_id(0) * seqs + seq
        load = pltpu.make_async_copy(turned_all, left, near.at[0])
        pl.when(spot == 0)(load.start)

        @pl.when(spot == seqs)
        def _():
            load.wait()
            for part in range(3):
                product = mxu(left[...], d_held[part]).astype(BF16)
                grads[part] = product.reshape(ways, share, wide)

        k_turned[...] = jnp.transpose(k_ref[...])
        product = jnp.transpose(mix[...].astype(F32) * grad[...].astype(F32))
        for pair in range(per):
            for half in range(2):
                lower = pair * PAIR + half * HEAD
                inner[pair, half : half + 1, :] = column_sum(product[lower : lower + HEAD, :])
        dk_sum[...] = jnp.zeros_like(dk_sum)
        dv_sum[...] = jnp.zeros_like(dv_sum)

        def body(i, carry):
            exchange.tick(spot * items + i, ticks)
            pair = i // count
            part = i - pair * count
            cols = pl.ds(pl.multiple_of(pair * PAIR, PAIR), PAIR)
            part = pl.ds(pl.multiple_of(part * block, block), block)
            for half in range(2):
                head = pl.ds(pl.multiple_of(pair * PAIR + half * HEAD, HEAD), HEAD)
                query = head_mask(q_ref[part, cols], half)
                cot = head_mask(grad[part, cols], half)
                s_held[half] = mxu(k_ref[:, cols], query, TRANSPOSED)
                p_held[half] = mxu(v_ref[:, cols], cot, TRANSPOSED)
                probs = jnp.exp2(s_held[half] * SCALE2 - tot[0, pair, half : half + 1, part])
                d_scores = (probs * (p_held[half] - inner[pair, half : half + 1, part])).astype(BF16)
                dv_sum[:, cols] += mxu(probs.astype(BF16), cot)
                dk_sum[:, cols] += mxu(d_scores, query)
                dq_turned[head, part] = mxu(k_turned[head, :], d_scores)
            return carry

        lax.fori_loop(0, items, body, 0)
        d_queries = jnp.transpose(dq_turned[...])
        for source, target in ((d_queries, dq), (dk_sum, dk)):
            for pair in range(per):
                v = source[:, pair * PAIR : (pair + 1) * PAIR] * SCALE
                v = v * cos[...] - partner_lanes(v) * sin[...]
                target[:, pair * PAIR : (pair + 1) * PAIR] = v.astype(BF16)
        dv[...] = dv_sum[...].astype(BF16)

        @pl.when(spot < seqs)
        def _():
            here = pl.ds(pl.multiple_of(seq * seq_length, seq_length), seq_length)
            for part, target in enumerate((dq, dk, dv)):
                d_held[part, here, :] = target[...]

        @pl.when(spot == seqs * steps - 1)
        def _():
            exchange.rest(ticks)

    def part_of(which):
        return pl.BlockSpec((seq_length, wide), lambda p, s: (s, which * steps + p))

    table = whole((seq_length, PAIR))
    grads = jax.ShapeDtypeStruct((rows, width), BF16)
    return call(
        kernel,
        "attend_back",
        (steps, seqs),
        [part_of(0), part_of(1), part_of(2), part_of(0), part_of(0)]
        + [pl.BlockSpec((1, per, 2, seq_length), lambda p, s: (s, p, 0, 0))]
        + [table] * 2
        + [pl.BlockSpec(memory_space=pl.ANY)] * (1 + many),
        [part_of(0), part_of(0), part_of(0)] + exchange.out_specs(),
        [grads, grads, grads] + exchange.out_shape(),
        [
            pltpu.VMEM((wide, seq_length), BF16),
            pltpu.VMEM((wide, seq_length), F32),
            pltpu.VMEM((seq_length, wide), F32),
            pltpu.VMEM((seq_length, wide), F32),
            pltpu.VMEM((per, 2, seq_length), F32),
            pltpu.VMEM((2, seq_length, block), F32),
            pltpu.VMEM((2, seq_length, block), F32),
            pltpu.VMEM(turned.shape, BF16),
            pltpu.VMEM((3, rows, wide), BF16),
            pltpu.VMEM((3, ways, share, wide), BF16),
            pltpu.SemaphoreType.DMA((1,)),
        ]
        + exchange.scratch(),
        40 * rows * seq_length * width,
        rows * width * 16,
        rows * seq_length * width // HEAD,
        ident,
    )(qkv, qkv, qkv, mixture, d_mixture, total, *tables, turned, *pieces)


def gelu_pair(v):
    root = math.sqrt(2.0 / math.pi)
    square = v * v
    near = 0.5 + 0.5 * jnp.tanh(v * (root + (root * 0.044715) * square))
    active = v * near
    bend = 2.0 * root + (6.0 * root * 0.044715) * square
    return active, near + (active * (1.0 - near)) * bend


def grouped_rows(ref, ways):
    part = ref.shape[0] // (ways * GROUPS)
    lowers = [(way * GROUPS + group) * part for group in range(GROUPS) for way in range(ways)]
    return jnp.concatenate([ref[lower : lower + part, :] for lower in lowers], axis=0)


def grouped_columns(ref, ways):
    part = ref.shape[1] // (ways * GROUPS)
    lowers = [(way * GROUPS + group) * part for group in range(GROUPS) for way in range(ways)]
    return jnp.concatenate([ref[:, lower : lower + part] for lower in lowers], axis=1)


def halved(arrays):
    return [
        (k, half * v.shape[-1] // 2, (half + 1) * v.shape[-1] // 2)
        for k, v in enumerate(arrays)
        for half in range(2)
    ]


def hidden_units(
    mixture, tokens, cot, starts, lengths, embed, gain, modulation, out_weight, up, up_bias, down,
    times, ident, seqs, block=512,
):
    rows, width = tokens.shape
    ways = lax.axis_size("narrow")
    units = up.shape[1] // GROUPS
    share, part_units = width // ways, units // ways
    seq_length = rows // seqs
    block = min(block, seq_length)
    per_seq = seq_length // block
    steps = rows // block
    turn = steps + ways
    shape_up, shape_down = (ways, share, units), (ways, part_units, width)
    traded = [jax.ShapeDtypeStruct(v, BF16) for v in (shape_up, shape_down) * 2]
    exchange = Exchange(
        [v.shape for v in traded], times, halved(traded), ["whole"] * 2 + ["head"] * 2, range(4)
    )

    def kernel(*refs):
        starts, lengths, mix, tok, emb, gn, w_out, g, mod, b_up = refs[:10]
        w_ups, w_downs = refs[10 : 10 + ways], refs[10 + ways : 10 + 2 * ways]
        act, d_up, g_bias, d_gate, g_sum = refs[10 + 2 * ways : 15 + 2 * ways]
        outs, left = refs[15 + 2 * ways : 21 + 2 * ways], refs[21 + 2 * ways :]
        n_turned, g_turned, a_held, u_held, down_held, g_up, g_down, near, n_held = left[:9]
        exchange.bind(
            [g_up.at[0], g_down.at[0], g_up.at[1], g_down.at[1]], outs[:4], left[9:]
        )
        step = pl.program_id(0)
        group = step // turn
        at = step - group * turn

        @pl.when(step == 0)
        def _():
            exchange.greet()
            n_turned[width:, :] = jnp.ones((16, rows), BF16)
            d_gate[...] = jnp.zeros_like(d_gate)
            g_sum[...] = jnp.zeros_like(g_sum)

        exchange.tick(step, GROUPS * turn)

        @pl.when(at == 0)
        def _():
            for way in range(ways):
                down_held[way] = w_downs[way][...]

        part = pl.ds(pl.multiple_of(jnp.minimum(at, steps - 1) * block, block), block)

        @pl.when(step < steps)
        def _():
            seq = at // per_seq
            first = (at - seq * per_seq) * block
            start, _ = masked_rows(tok[...], emb[...], starts[seq], lengths[seq], first)
            gate = mod[pl.ds(seq, 1), 2 * width : 3 * width]
            hat, _ = normalized(start + gate * mxu(mix[...], w_out[...]))
            shift = mod[pl.ds(seq, 1), 3 * width : 4 * width]
            scale = mod[pl.ds(seq, 1), 4 * width : 5 * width]
            normed = (hat * (gn[...] * (1.0 + scale)) + shift).astype(BF16)
            n_held[part, :] = normed
            store_shares(n_turned, jnp.transpose(normed), part)
            g_turned[:, part] = jnp.transpose(g[...])
            g_sum[pl.ds(seq, 1), :] += column_sum(g[...].astype(F32))

        @pl.when(at < steps)
        def _():
            seq = at // per_seq
            nrm = n_held[part, :]
            cotangent = g[...].astype(F32)
            d_branch = (mod[pl.ds(seq, 1), 5 * width : 6 * width] * cotangent).astype(BF16)
            for way in range(ways):
                cols = slice(way * part_units, (way + 1) * part_units)
                upper = mxu(nrm, w_ups[way][...]) + b_up[:, cols]
                d_active = mxu(d_branch, w_downs[way][...], TRANSPOSED)
                active, slope = gelu_pair(upper)
                active = active.astype(BF16)
                d_upper = (d_active * slope).astype(BF16)
                act[:, cols] = active
                a_held[part, cols] = active
                d_up[:, cols] = d_upper
                u_held[part, cols] = d_upper

        @pl.when(at >= steps)
        def _():
            place = at - steps
            owner = owner_at(exchange.at["narrow"], place)
            cols = pl.ds(pl.multiple_of(owner * part_units, part_units), part_units)
            product = mxu(n_turned[...], u_held[:, cols])
            g_bias[:, cols] = product[width : width + 1]
            g_up[group, :, :, cols] = product[:width].astype(BF16).reshape(
                ways, share, part_units
            )
            own = down_held[owner].astype(F32)
            total = jnp.zeros((part_units, width), F32)
            for seq in range(seqs):
                lower, upper = seq * seq_length, (seq + 1) * seq_length
                product = mxu(g_turned[:, lower:upper], a_held[lower:upper, cols])
                product = jnp.transpose(product)
                total += product * mod[seq : seq + 1, 5 * width : 6 * width]
                d_gate[seq : seq + 1, :] += column_sum(product * own)
            g_down[group, place] = total.astype(BF16)

        @pl.when(step == GROUPS * turn - 1)
        def _():
            copies = [
                pltpu.make_async_copy(source.at[GROUPS - 1], target, near.at[k])
                for k, (source, target) in enumerate(((g_up, outs[4]), (g_down, outs[5])))
            ]
            for copy in copies:
                copy.start()
            exchange.rest(GROUPS * turn)
            for copy in copies:
                copy.wait()

    def early(i):
        return (jnp.minimum(lax.rem(i, turn), steps - 1), 0)

    def once(i):
        return (jnp.minimum(i, steps - 1), 0)

    def fixed(shape):
        return pl.BlockSpec(shape, lambda i: (0,) * len(shape))

    by_rows = pl.BlockSpec(
        (block, units), lambda i: (jnp.minimum(lax.rem(i, turn), steps - 1), i // turn)
    )
    by_group = pl.BlockSpec((1, units), lambda i: (0, i // turn))

    def up_piece(way):
        return pl.BlockSpec((width, part_units), lambda i: (0, way * GROUPS + i // turn))

    def down_piece(way):
        return pl.BlockSpec((part_units, width), lambda i: (way * GROUPS + i // turn, 0))

    assert GROUPS == 3
    anywhere = pl.BlockSpec(memory_space=pl.ANY)
    return call(
        kernel,
        "hidden_units",
        (GROUPS * turn,),
        [smem(), smem()]
        + [pl.BlockSpec((block, width), once)] * 2
        + [whole((1, width)), whole((1, width)), whole(out_weight.shape)]
        + [pl.BlockSpec((block, width), early)]
        + [whole(modulation.shape), by_group]
        + [up_piece(way) for way in range(ways)]
        + [down_piece(way) for way in range(ways)],
        [by_rows, by_rows, by_group, fixed((seqs, width)), fixed((seqs, width))]
        + exchange.out_specs()
        + [anywhere] * 2,
        [
            jax.ShapeDtypeStruct((rows, units * GROUPS), BF16),
            jax.ShapeDtypeStruct((rows, units * GROUPS), BF16),
            jax.ShapeDtypeStruct((1, units * GROUPS), F32),
            jax.ShapeDtypeStruct((seqs, width), F32),
            jax.ShapeDtypeStruct((seqs, width), F32),
        ]
        + exchange.out_shape()
        + [jax.ShapeDtypeStruct(shape_up, BF16), jax.ShapeDtypeStruct(shape_down, BF16)],
        [
            pltpu.VMEM((width + 16, rows), BF16),
            pltpu.VMEM((width, rows), BF16),
            pltpu.VMEM((rows, units), BF16),
            pltpu.VMEM((rows, units), BF16),
            pltpu.VMEM((ways, part_units, width), BF16),
            pltpu.VMEM((GROUPS,) + shape_up, BF16),
            pltpu.VMEM((GROUPS,) + shape_down, BF16),
            pltpu.SemaphoreType.DMA((2,)),
            pltpu.VMEM((rows, width), BF16),
        ]
        + exchange.scratch(),
        8 * rows * width * units * GROUPS,
        GROUPS * (rows * (width * 4 + units * 4) + 8 * width * units),
        rows * units * GROUPS,
        ident,
    )(
        starts, lengths, mixture, tokens, embed, gain, out_weight, cot, modulation, up_bias,
        *[up] * ways, *[down] * ways,
    )


def middle_back(
    mixture, tokens, cot, starts, lengths, embed, gain, modulation, out_weight, d_upper, up, seqs,
    block=256,
):
    rows, width = tokens.shape
    ways = lax.axis_size("narrow")
    seq_length = rows // seqs
    block = min(block, seq_length)
    per_seq = seq_length // block
    steps = rows // block
    hidden_width = d_upper.shape[1]
    share = width // ways

    def kernel(
        starts, lengths, mix, tok, g, emb, gn, mod, w_out, w_up, d_ups, d_middle_out, d_mix, g_out,
        sums, g_sum,
    ):
        step = pl.program_id(0)
        seq = step // per_seq
        first = (step - seq * per_seq) * block

        @pl.when(step == 0)
        def _():
            g_sum[...] = jnp.zeros_like(g_sum)

        @pl.when(step == seq * per_seq)
        def _():
            sums[...] = jnp.zeros_like(sums)

        def vector(which):
            return mod[pl.ds(seq, 1), which * width : (which + 1) * width]

        attended = mxu(mix[...], w_out[...])
        start, _ = masked_rows(tok[...], emb[...], starts[seq], lengths[seq], first)
        hat, inverse = normalized(start + vector(2) * attended)
        d_normed = mxu(d_ups[...], grouped_columns(w_up, ways), TRANSPOSED)
        d_middle = g[...].astype(F32) + norm_back(
            d_normed * (gn[...] * (1.0 + vector(4))), hat, inverse
        )
        d_middle_out[...] = d_middle
        d_attended = (vector(2) * d_middle).astype(BF16)
        d_mix[...] = mxu(d_attended, w_out[...], TRANSPOSED).astype(BF16)
        g_sum[...] += mxu(jnp.transpose(mix[...]), d_attended)
        sums[0, 0:1, :] += column_sum(d_normed)
        sums[0, 1:2, :] += column_sum(d_normed * hat)
        sums[0, 2:3, :] += column_sum(d_middle * attended)

        @pl.when(step == steps - 1)
        def _():
            for place in range(ways):
                owner = owner_at(lax.axis_index("narrow"), place)
                spot = pl.ds(pl.multiple_of(owner * share, share), share)
                g_out[place] = g_sum[spot, :].astype(BF16)

    row = pl.BlockSpec((block, width), lambda i: (i, 0))
    return call(
        kernel,
        "middle_back",
        (steps,),
        [smem(), smem(), row, row, row, whole((1, width)), whole((1, width))]
        + [whole(modulation.shape), whole(out_weight.shape), whole(up.shape)]
        + [pl.BlockSpec((block, hidden_width), lambda i: (i, 0))],
        (
            row,
            row,
            pl.BlockSpec((ways, share, width), lambda i: (0, 0, 0)),
            pl.BlockSpec((1, 8, width), lambda i: (i // per_seq, 0, 0)),
        ),
        (
            jax.ShapeDtypeStruct((rows, width), F32),
            jax.ShapeDtypeStruct((rows, width), BF16),
            jax.ShapeDtypeStruct((ways, share, width), BF16),
            jax.ShapeDtypeStruct((seqs, 8, width), F32),
        ),
        [pltpu.VMEM((width, width), F32)],
        rows * width * (2 * hidden_width + 6 * width),
        rows * (width * 12 + hidden_width * 2) + 2 * width * hidden_width,
    )(
        starts, lengths, mixture, tokens, cot, embed, gain, modulation, out_weight, up, d_upper,
    )


class Finale(Steps):
    def __init__(self, ways):
        self.ways = ways
        self.wide = lax.axis_size("wide")

    def scratch(self, columns):
        dma = pltpu.SemaphoreType.DMA
        return [
            pltpu.VMEM((self.ways, 8, columns), F32),
            pltpu.VMEM((self.ways, 8, columns), F32),
            pltpu.VMEM((self.wide, 8, columns), F32),
            dma((self.ways,)),
            dma((self.ways,)),
            dma((self.wide,)),
            dma((self.wide,)),
        ]

    def bind(self, held):
        self.parts, self.narrow_got, self.wide_got, *self.sems = held
        self.locate()

    def others(self):
        targets = []
        for offset in range(1, self.ways):
            targets.append({"narrow": lax.rem(self.at["narrow"] + offset, self.ways)})
        for offset in range(1, self.wide):
            targets.append({"wide": lax.rem(self.at["wide"] + offset, self.wide)})
        return targets

    def greet(self):
        barrier = pltpu.get_barrier_semaphore()
        targets = self.others()
        for target in targets:
            pl.semaphore_signal(
                barrier, inc=1, device_id=target, device_id_type=pl.DeviceIdType.MESH
            )
        pl.semaphore_wait(barrier, len(targets))

    def along_narrow(self, offset):
        target = lax.rem(self.at["narrow"] + offset, self.ways)
        return pltpu.make_async_remote_copy(
            src_ref=self.parts.at[target],
            dst_ref=self.narrow_got.at[self.at["narrow"]],
            send_sem=self.sems[0].at[offset],
            recv_sem=self.sems[1].at[offset],
            device_id={"narrow": target},
            device_id_type=pl.DeviceIdType.MESH,
        )

    def along_wide(self, offset):
        me = self.at["wide"]
        return pltpu.make_async_remote_copy(
            src_ref=self.wide_got.at[me],
            dst_ref=self.wide_got.at[me],
            send_sem=self.sems[2].at[offset],
            recv_sem=self.sems[3].at[offset],
            device_id={"wide": lax.rem(me + offset, self.wide)},
            device_id_type=pl.DeviceIdType.MESH,
        )

    def begin(self):
        for offset in range(1, self.ways):
            self.along_narrow(offset).start()
        me = self.at["narrow"]
        self.narrow_got[pl.ds(me, 1)] = self.parts[pl.ds(me, 1)]

    def spread(self, seqs, row_lanes):
        for offset in range(1, self.ways):
            self.along_narrow(offset).wait()
        me = self.at["wide"]
        for way in range(self.ways):
            self.wide_got[pl.ds(me, 1), way * seqs : (way + 1) * seqs, 0:row_lanes] = (
                self.narrow_got[way : way + 1, 0:seqs, 0:row_lanes]
            )
        total = self.narrow_got[0:1, :, row_lanes:]
        for way in range(1, self.ways):
            total += self.narrow_got[way : way + 1, :, row_lanes:]
        self.wide_got[pl.ds(me, 1), :, row_lanes:] = total
        for offset in range(1, self.wide):
            self.along_wide(offset).start()

    def close(self):
        for offset in range(1, self.wide):
            self.along_wide(offset).wait()


def finish(
    turned, d_parts, tokens, d_middle, mixture, starts, lengths, embed, gain, modulation, weight,
    out_weight, down_bias, active, down, features, rows_two, vectors_two, times, ident, seqs,
    wide=384, block=512, late_block=256,
):
    rows, width = tokens.shape
    ways = lax.axis_size("narrow")
    share = width // ways
    seq_length = rows // seqs
    block, late_block = min(block, seq_length), min(late_block, seq_length)
    per_seq, late_per_seq = seq_length // block, seq_length // late_block
    columns, hidden_width = modulation.shape[1] // ways, active.shape[1]
    time_width = features.shape[1]
    window = 2 * PAIR
    lanes = columns + time_width + window
    early, middle, late = 3, rows // block, rows // late_block
    steps = early + middle + late
    exchange = Exchange([(ways, share, wide)] * 3, times, near=range(3))
    finale = Finale(ways)

    def kernel(*refs):
        (
            starts, lengths, left, q_all, k_all, v_all, tok, d_mid, emb, gn, mod, w_qkv_all,
            tok_late, mix, w_out_all, b_down, feat, two, vec, act, w_down_all,
        ) = refs[:21]
        spot = 21
        g_tok, block_out, g_ada, g_ada_bias, g_vec = refs[spot : spot + 5]
        outs = refs[spot + 5 : spot + 8]
        grads, sums = refs[spot + 8 : spot + 10]
        d_held, w_qkv, w_out, w_down, near = refs[spot + 10 : spot + 15]
        small = spot + 15 + 7
        exchange.bind([grads.at[part] for part in range(3)], outs, refs[small:])
        finale.bind(refs[spot + 15 : small])
        step = pl.program_id(0)
        loads = [
            pltpu.make_async_copy(source, d_held.at[part], near.at[part])
            for part, source in enumerate((q_all, k_all, v_all))
        ]
        loads += [
            pltpu.make_async_copy(source, target, near.at[3 + which])
            for which, (source, target) in enumerate(
                ((w_qkv_all, w_qkv), (w_out_all, w_out), (w_down_all, w_down))
            )
        ]

        @pl.when(step == 0)
        def _():
            for load in loads:
                load.start()
            finale.greet()
            sums[...] = jnp.zeros_like(sums)

        exchange.tick(step, steps)

        for part in range(3):
            pl.when(step == part)(loads[part].wait)
        pl.when(step == early)(loads[3].wait)

        @pl.when(step == early + middle)
        def _():
            loads[4].wait()
            loads[5].wait()

        @pl.when(step < early)
        def _():
            product = mxu(left[...], d_held[step, :, width - wide :]).astype(BF16)
            grads[step] = product.reshape(ways, share, wide)

        @pl.when((step >= early) & (step < early + middle))
        def _():
            at = step - early
            seq = at // per_seq
            first = (at - seq * per_seq) * block
            start, inside = masked_rows(
                tok[...], emb[...], starts[seq], lengths[seq], first
            )
            hat, inverse = normalized(start)
            here = pl.ds(pl.multiple_of(at * block, block), block)
            d_normed = mxu(d_held[0, here, :], w_qkv[:, 0:width], TRANSPOSED)
            d_normed += mxu(d_held[1, here, :], w_qkv[:, width : 2 * width], TRANSPOSED)
            d_normed += mxu(d_held[2, here, :], w_qkv[:, 2 * width :], TRANSPOSED)
            scale = mod[pl.ds(seq, 1), width : 2 * width]
            d_start = d_mid[...] + norm_back(d_normed * (gn[...] * (1.0 + scale)), hat, inverse)
            g_tok[...] = jnp.where(inside, 0.0, d_start)
            sums[seq, 0:1, :] += column_sum(d_normed)
            sums[seq, 1:2, :] += column_sum(d_normed * hat)
            sums[seq, 2:3, :] += column_sum(jnp.where(inside, d_start, 0.0))

        @pl.when(step == early + middle)
        def _():
            parts = finale.parts
            embed_sum = jnp.zeros((1, width), F32)
            gain_sum = jnp.zeros((1, width), F32)
            for seq in range(seqs):
                shift, scale = sums[seq, 0:1, :], sums[seq, 1:2, :]
                gain_sum += scale * (1.0 + mod[seq : seq + 1, width : 2 * width])
                embed_sum += sums[seq, 2:3, :]
                row = jnp.concatenate([shift, scale * gn[...], two[seq : seq + 1, :]], axis=1)
                for way in range(ways):
                    parts[way, seq : seq + 1, 0:columns] = row[
                        :, way * columns : (way + 1) * columns
                    ]
            for way in range(ways):
                parts[way, 0:seqs, columns : columns + time_width] = feat[...]
                lower = PAIR * (share * way // PAIR)
                parts[way, 0:1, columns + time_width :] = embed_sum[:, lower : lower + window]
                parts[way, 1:2, columns + time_width :] = gain_sum[:, lower : lower + window]
                parts[way, 2:8, columns + time_width :] = vec[way, 2:8, :]
            finale.begin()

        @pl.when(step == early + middle + 2)
        def _():
            finale.spread(seqs, columns + time_width)

        @pl.when(step >= early + middle)
        def _():
            at = step - early - middle
            seq = at // late_per_seq
            first = (at - seq * late_per_seq) * late_block
            start, _ = masked_rows(
                tok_late[...], emb[...], starts[seq], lengths[seq], first
            )
            attended = mxu(mix[...], w_out[...])
            branch = mxu(act[...], grouped_rows(w_down, ways)) + b_down[...]
            hidden = start + mod[pl.ds(seq, 1), 2 * width : 3 * width] * attended
            block_out[...] = (
                hidden + mod[pl.ds(seq, 1), 5 * width : 6 * width] * branch
            ).astype(BF16)

        @pl.when(step == steps - 1)
        def _():
            finale.close()
            got = finale.wide_got
            every = got[...].reshape(finale.wide * 8, lanes)
            d_mods, feats = every[:, 0:columns], every[:, columns : columns + time_width]
            g_ada[...] = lax.dot_general(
                jnp.transpose(feats), d_mods, PLAIN, precision=FULL_PRECISION,
                preferred_element_type=F32,
            )
            g_ada_bias[...] = column_sum(d_mods)
            total = got[0, :, columns + time_width :]
            for index in range(1, finale.wide):
                total += got[index, :, columns + time_width :]
            g_vec[...] = total
            exchange.rest(steps)

    row = pl.BlockSpec((block, width), lambda i: (jnp.clip(i - early, 0, middle - 1), 0))

    def late_row(wide):
        return pl.BlockSpec(
            (late_block, wide), lambda i: (jnp.maximum(i - early - middle, 0), 0)
        )

    def fixed(shape):
        return pl.BlockSpec(shape, lambda i: (0,) * len(shape))

    anywhere = pl.BlockSpec(memory_space=pl.ANY)
    return call(
        kernel,
        "finish",
        (steps,),
        [smem(), smem(), whole(turned.shape)]
        + [anywhere] * 3
        + [row, row, whole((1, width)), whole((1, width)), whole(modulation.shape), anywhere]
        + [late_row(width), late_row(width), anywhere, whole((1, width))]
        + [whole(features.shape), whole(rows_two.shape), whole(vectors_two.shape)]
        + [late_row(hidden_width), anywhere],
        [
            row,
            late_row(width),
            fixed((time_width, columns)),
            fixed((1, columns)),
            fixed((8, window)),
        ]
        + exchange.out_specs(),
        [
            jax.ShapeDtypeStruct((rows, width), F32),
            jax.ShapeDtypeStruct((rows, width), BF16),
            jax.ShapeDtypeStruct((time_width, columns), F32),
            jax.ShapeDtypeStruct((1, columns), F32),
            jax.ShapeDtypeStruct((8, window), F32),
        ]
        + exchange.out_shape(),
        [
            pltpu.VMEM((3, ways, share, wide), BF16),
            pltpu.VMEM((seqs, 8, width), F32),
            pltpu.VMEM((3, rows, width), BF16),
            pltpu.VMEM(weight.shape, BF16),
            pltpu.VMEM(out_weight.shape, BF16),
            pltpu.VMEM(down.shape, BF16),
            pltpu.SemaphoreType.DMA((6,)),
        ]
        + finale.scratch(lanes)
        + exchange.scratch(),
        2 * rows * width * (7 * width + hidden_width),
        rows * (width * 24 + 2 * hidden_width),
        0,
        ident,
    )(
        starts, lengths, turned, *d_parts, tokens, d_middle, embed, gain, modulation, weight,        tokens, mixture, out_weight, down_bias, features, rows_two, vectors_two, active, down,
    )


def gather_first(small, ada, weight, ident):
    share, wide = weight.shape
    width = wide // 3
    columns = [(0, 0, small.shape[1]), (1, 0, ada.shape[1])]
    columns += [(2, k * width, (k + 1) * width) for k in range(3)]
    gathering = Gather([small.shape, ada.shape, weight.shape], [0] * 5, [0] * 3, columns)

    def kernel(*refs):
        gathering.bind(refs[0:3], refs[3:6], refs[6:])
        gathering.greet()
        gathering.begin(0)
        gathering.begin(1)
        gathering.begin(2)
        for k in range(5):
            gathering.relay(k)
            if k + 3 < 5:
                gathering.begin(k + 3)
            if k > 0:
                gathering.share(k - 1)
        gathering.share(4)
        for k in range(5):
            gathering.close(k)

    return call(
        kernel,
        "gather_first",
        (),
        gathering.in_specs(),
        gathering.out_specs(),
        gathering.out_shape(),
        gathering.scratch(),
        0,
        8 * share * wide,
        0,
        ident,
    )(small, ada, weight)


def assemble(ups, downs, out, qkv):
    share, units = ups[0].shape
    part, width = downs[0].shape
    ways = units // part
    groups = len(ups)

    def kernel(*refs):
        up_in, down_in = refs[:groups], refs[groups : 2 * groups]
        out_in, qkv_in = refs[2 * groups], refs[2 * groups + 1 : 2 * groups + 7]
        g_up, g_down, g_out, g_qkv = refs[2 * groups + 7 :]
        for group in range(groups):
            for way in range(ways):
                lower = (way * groups + group) * part
                g_up[:, lower : lower + part] = up_in[group][
                    :, way * part : (way + 1) * part
                ].astype(F32)
            g_down[group] = down_in[group][...].astype(F32)
        g_out[...] = out_in[...].astype(F32)
        for which in range(6):
            lower = (which % 3) * width + (which // 3) * (width // 2)
            g_qkv[:, lower : lower + width // 2] = qkv_in[which][...].astype(F32)

    pace = 4
    small, tall = share // pace, part // pace

    def rows(count, columns):
        return pl.BlockSpec((count, columns), lambda i: (i, 0))

    g_up, g_down, g_out, g_qkv = call(
        kernel,
        "assemble",
        (pace,),
        [rows(small, units)] * groups
        + [rows(tall, width)] * groups
        + [rows(small, width)]
        + [rows(small, width // 2)] * 6,
        (
            rows(small, units * groups),
            pl.BlockSpec((groups, tall, width), lambda i: (0, i, 0)),
            rows(small, width),
            rows(small, 3 * width),
        ),
        (
            jax.ShapeDtypeStruct((share, units * groups), F32),
            jax.ShapeDtypeStruct((groups, part, width), F32),
            jax.ShapeDtypeStruct((share, width), F32),
            jax.ShapeDtypeStruct((share, 3 * width), F32),
        ),
        [],
        0,
        12 * share * units * groups,
    )(*ups, *downs, out, *qkv)
    return g_up, g_down.reshape(groups * part, width), g_out, g_qkv


def per_device(
    tokens,
    timestep,
    span_start,
    span_length,
    mask_embed,
    ada_weight,
    ada_bias,
    norm_first,
    query_key_value_weight,
    output_weight,
    norm_second,
    up_projection_weight,
    up_projection_bias,
    down_projection_weight,
    down_projection_bias,
    cotangent,
):
    seqs = timestep.shape[0]
    rows, width = tokens.shape
    seq_length = rows // seqs
    ways = lax.axis_size("narrow")
    me = lax.axis_index("narrow")
    share = width // ways
    unit_share = down_projection_weight.shape[0]
    part = unit_share // GROUPS
    units = ways * part
    time_width, columns = ada_weight.shape

    vectors = (
        ada_bias, mask_embed, norm_first, norm_second, down_projection_bias, up_projection_bias,
    )
    filled, lower = jnp.zeros((32 * PAIR,), BF16), 0
    for v in vectors:
        filled += jnp.pad(v, (lower, filled.shape[0] - lower - v.shape[0]))
        lower += v.shape[0]
    small = filled.reshape(32, PAIR)
    small, ada, w_qkv = gather_first(small, ada_weight, query_key_value_weight, 0)

    small = small.reshape(ways, -1).astype(F32)
    smalls, lower = [], 0
    for v in vectors:
        smalls.append(small[:, lower : lower + v.shape[0]].reshape(1, -1))
        lower += v.shape[0]
    bias_ada, embed, gain_one, gain_two, bias_down, bias_up = smalls
    features = time_features(timestep, time_width)
    modulation = jnp.einsum(
        "sf,wfc->swc",
        features,
        ada.reshape(ways, time_width, columns).astype(F32),
        precision=FULL_PRECISION,
    ).reshape(seqs, -1) + bias_ada
    tables = rotary_tables(seq_length)

    qkv, turned_one = project(
        tokens, span_start, span_length, embed, gain_one, modulation, w_qkv, tables, seqs
    )
    thirds = [
        (which, third * size, (third + 1) * size)
        for which, size in ((1, unit_share * ways // 3), (2, width // 3))
        for third in range(3)
    ]
    mixture, total, w_out, w_up, w_down = attend(
        qkv,
        [output_weight, up_projection_weight, down_projection_weight],
        [0, 1, 3, 6, 8, 11, 13],
        [5, 5, 2],
        [(0, 0, width)] + thirds,
        1,
        seqs,
    )
    bias_up = jnp.swapaxes(bias_up.reshape(ways, GROUPS, part), 0, 1).reshape(1, -1)
    head_times = paced([8, 9, 10, 11], [1, 5, 2, 2, 2, 1]) + paced([17, 17, 18, 19], [1, 4])
    active, d_upper, g_bias, d_gate_two, g_sum, *swaps = hidden_units(
        mixture, tokens, cotangent, span_start, span_length, embed, gain_two, modulation, w_out,
        w_up, bias_up, w_down, head_times, 2, seqs,
    )
    d_gate_two += bias_down * g_sum
    d_middle, d_mixture, g_out, sums_two = middle_back(
        mixture, tokens, cotangent, span_start, span_length, embed, gain_two, modulation, w_out,
        d_upper, w_up, seqs,
    )
    d_q, d_k, d_v, *done = attend_back(
        qkv, mixture, d_mixture, total, tables, turned_one, swaps[2:] + [g_out],
        ["tail"] * 2 + ["whole"] * 3, halved(swaps[2:] + [g_out]),
        [[1, 2, 5, 8, 11, 13], [2, 3, 6, 9, 12, 14], [3, 4, 7, 10, 13, 15], [4, 5, 8, 11, 14, 16]]
        + paced([0, 1, 3, 5], [1, 4, 3, 3, 4, 2])
        + paced([6, 8], [1, 3, 3, 3, 3, 2])
        + paced([12, 12, 13], [1, 3, 2, 2, 3, 1]),
        3, seqs,
    )
    scale_two = modulation[:, 4 * width : 5 * width]
    rows_two = jnp.concatenate(
        [sums_two[:, 2], sums_two[:, 0], sums_two[:, 1] * gain_two, d_gate_two], axis=1
    )
    g_norm_two = jnp.sum(sums_two[:, 1] * (1.0 + scale_two), axis=0)
    g_bias_down = jnp.sum(modulation[:, 5 * width :] * g_sum, axis=0)
    lowers = [PAIR * (share * way // PAIR) for way in range(ways)]
    vectors_two = jnp.stack(
        [
            jnp.stack([v[lower : lower + 2 * PAIR] for lower in lowers])
            for v in (g_norm_two, g_norm_two, g_norm_two, g_bias_down)
        ]
        + [g_bias[0].reshape(GROUPS, ways, part)[group] for group in range(GROUPS)]
        + [jnp.zeros((ways, 2 * PAIR), F32)],
        axis=1,
    )
    grad_tokens, block_out, grad_ada_weight, grad_ada_bias, vectors, *g_qkv = finish(
        turned_one, (d_q, d_k, d_v), tokens, d_middle, mixture, span_start, span_length, embed,
        gain_one, modulation, w_qkv, w_out, bias_down, active, w_down, features, rows_two,
        vectors_two,
        FINISH_TIMES, 4, seqs,
    )
    skip = lax.rem(share * me, PAIR)
    own = lax.dynamic_slice_in_dim(vectors[:4], skip, share, 1)
    g_ups, g_downs = (swaps[0], *done[0:4:2]), (swaps[1], *done[1:4:2])
    g_up, g_down, g_out, g_qkv = assemble(g_ups, g_downs, done[4], done[5:] + g_qkv)
    return (
        block_out,
        grad_tokens,
        own[0],
        grad_ada_weight,
        grad_ada_bias[0],
        own[1],
        g_qkv,
        g_out,
        own[2],
        g_up,
        vectors[4 : 4 + GROUPS].reshape(-1),
        g_down,
        own[3],
    )


def solution(mesh):
    rows = P(("wide", "narrow"), None)
    per_seq = P(("wide", "narrow"))
    vector, matrix, columns = P("narrow"), P("narrow", None), P(None, "narrow")
    return jax.shard_map(
        per_device,
        mesh=mesh,
        in_specs=(
            rows, per_seq, per_seq, per_seq, vector, columns, vector, vector,
            matrix, matrix, vector, matrix, vector, matrix, vector, rows,
        ),
        out_specs=(
            rows, rows, vector, columns, vector, vector, matrix, matrix, vector, matrix,
            vector, matrix, vector,
        ),
        check_vma=False,
    )
```

```python
import math

import jax
import jax.numpy as jnp
import numpy as np
from jax import lax
from jax.experimental import pallas as pl
from jax.experimental.pallas import tpu as pltpu
from jax.sharding import PartitionSpec as P

HEAD = 64
PAIR = 2 * HEAD
GROUPS = 3
EMBED, GAIN_ONE, GAIN_TWO, BIAS_DOWN, BIAS_UP = range(5)
FINISH_TIMES = [
    [1, 3, 5, 6, 7, 10, 12], [2, 4, 6, 7, 9, 12, 14], [3, 4, 7, 9, 11, 14, 15],
]
EPSILON = 1e-05
FULL_PRECISION = lax.Precision.HIGHEST
F32 = jnp.float32
BF16 = jnp.bfloat16
SCALE = 1.0 / math.sqrt(HEAD)
SCALE2 = SCALE * math.log2(math.e)
VMEM_BYTES = 60 << 20
PLAIN = (((1,), (0,)), ((), ()))
TRANSPOSED = (((1,), (1,)), ((), ()))


def mxu(left, right, dims=PLAIN):
    return lax.dot_general(left, right, dims, preferred_element_type=F32)


def call(
    kernel, name, grid, in_specs, out_specs, out_shape, scratch, flops, moved, exps=0, ident=None
):
    return pl.pallas_call(
        kernel,
        name=name,
        grid=grid,
        in_specs=in_specs,
        out_specs=out_specs,
        out_shape=out_shape,
        scratch_shapes=scratch,
        compiler_params=pltpu.CompilerParams(
            vmem_limit_bytes=VMEM_BYTES, collective_id=ident, has_side_effects=ident is not None
        ),
        cost_estimate=pl.CostEstimate(flops=flops, bytes_accessed=moved, transcendentals=exps),
    )


def whole(shape):
    return pl.BlockSpec(shape, lambda *_: (0,) * len(shape), pipeline_mode=pl.Buffered(1))


def column_third(which, width):
    return pl.BlockSpec((width, width), lambda *_: (0, which), pipeline_mode=pl.Buffered(1))


def row_of(ref, which, width):
    return ref.at[which : which + 1, 0:width]


def smem():
    return pl.BlockSpec(memory_space=pltpu.SMEM)


def time_features(step_ids, feature_count):
    halfway = feature_count // 2
    spacing = jnp.exp(-math.log(10000.0) * jnp.arange(halfway, dtype=F32) / halfway)
    angles = step_ids.astype(F32)[:, None] * spacing[None, :]
    return jax.nn.silu(jnp.concatenate([jnp.cos(angles), jnp.sin(angles)], axis=-1))


def rotary_tables(seq_length):
    halfway = HEAD // 2
    spacing = np.exp(-math.log(10000.0) * np.arange(halfway, dtype=np.float32) / halfway)
    angles = np.arange(seq_length, dtype=np.float32)[:, None] * spacing.astype(np.float32)
    cosine, sine = np.cos(angles), np.sin(angles)
    signed = np.concatenate([-sine, sine] * 2, axis=-1)
    return np.concatenate([cosine] * 4, axis=-1), signed


def partner_lanes(v):
    lane = lax.broadcasted_iota(jnp.int32, (1, PAIR), 1)
    return jnp.where(lax.rem(lane, HEAD) < HEAD // 2, from_ahead(v), from_behind(v))


def from_ahead(v):
    return pltpu.roll(v, PAIR - HEAD // 2, 1)


def from_behind(v):
    return pltpu.roll(v, HEAD // 2, 1)


def masked_rows(tokens, embed, start, length, first_row):
    rows = tokens.shape[0]
    position = lax.broadcasted_iota(jnp.int32, (rows, 1), 0) + first_row
    inside = (position >= start) & (position < start + length)
    return jnp.where(inside, embed, tokens.astype(F32)), inside


def normalized(rows):
    centre = rows - jnp.mean(rows, axis=-1, keepdims=True)
    spread = jnp.mean(centre * centre, axis=-1, keepdims=True)
    inverse = lax.rsqrt(spread + EPSILON)
    return centre * inverse, inverse


def norm_back(d_out, hat, inverse):
    return inverse * (
        d_out
        - jnp.mean(d_out, axis=-1, keepdims=True)
        - hat * jnp.mean(d_out * hat, axis=-1, keepdims=True)
    )


def column_sum(v):
    return jnp.sum(v, axis=0, keepdims=True)


def store_shares(target, value, cols):
    me, ways = lax.axis_index("narrow"), lax.axis_size("narrow")
    share = value.shape[0] // ways
    for place in range(ways):
        lower = pl.multiple_of(place_of(me, place) * share, share)
        target[pl.ds(lower, share), cols] = value[place * share : (place + 1) * share, :]


def place_of(me, other):
    core = lax.rem(me + other, 2)
    chip = lax.rem(me // 2 + other // 2, 2)
    return 2 * (1 - core) + 1 - chip


def owner_at(me, place):
    core, chip = 1 - place // 2, 1 - lax.rem(place, 2)
    return 2 * lax.rem(me // 2 + chip, 2) + lax.rem(me + core, 2)


def project(tokens, starts, lengths, embed, gain, modulation, weight, tables, seqs, block=512):
    rows, width = tokens.shape
    seq_length = rows // seqs
    block = min(block, seq_length)
    per_seq = seq_length // block
    pairs = width // PAIR

    def kernel(starts, lengths, tok, emb, gn, mod, w_q, w_k, w_v, cos, sin, out, nt):
        emb, gn = row_of(emb, EMBED, width), row_of(gn, GAIN_ONE, width)
        step = pl.program_id(0)
        seq = step // per_seq
        first = (step - seq * per_seq) * block
        start, _ = masked_rows(tok[...], emb[...], starts[seq], lengths[seq], first)
        hat, _ = normalized(start)
        shift = mod[pl.ds(seq, 1), 0:width]
        scale = mod[pl.ds(seq, 1), width : 2 * width]
        normed = (hat * (gn[...] * (1.0 + scale)) + shift).astype(BF16)
        store_shares(nt, jnp.transpose(normed), slice(None))
        for which, w in enumerate((w_q, w_k)):
            turned = mxu(normed, w[...])
            for part in range(pairs):
                v = turned[:, part * PAIR : (part + 1) * PAIR]
                v = v * cos[...] + partner_lanes(v) * sin[...]
                lower = which * width + part * PAIR
                out[:, lower : lower + PAIR] = v.astype(BF16)
        out[:, 2 * width :] = mxu(normed, w_v[...]).astype(BF16)

    table = pl.BlockSpec((block, PAIR), lambda i: (lax.rem(i, per_seq), 0))
    return call(
        kernel,
        "project",
        (rows // block,),
        [
            smem(),
            smem(),
            pl.BlockSpec((block, width), lambda i: (i, 0)),
            whole(embed.shape),
            whole(gain.shape),
            whole(modulation.shape),
            column_third(0, width),
            column_third(1, width),
            column_third(2, width),
            table,
            table,
        ],
        (
            pl.BlockSpec((block, 3 * width), lambda i: (i, 0)),
            pl.BlockSpec((width, block), lambda i: (0, i)),
        ),
        (
            jax.ShapeDtypeStruct((rows, 3 * width), BF16),
            jax.ShapeDtypeStruct((width, rows), BF16),
        ),
        [],
        2 * rows * width * 3 * width,
        rows * width * 10 + 6 * width * width,
    )(starts, lengths, tokens, embed, gain, modulation, weight, weight, weight, *tables)


def flip(index, stride):
    return index + stride * (1 - 2 * lax.rem(index // stride, 2))


def exchange_stages():
    count = lax.axis_size("wide")
    strides = [1 << bit for bit in range(1, count.bit_length() - 1)]
    return [("pair", "narrow", 1), ("chip", "narrow", 2), ("split", "wide", 1)] + [
        ("full", "wide", stride) for stride in strides
    ] + [("join", "wide", 1)]


class Steps:
    def in_specs(self):
        return [pl.BlockSpec(memory_space=pl.ANY)] * self.count

    out_specs = in_specs

    def locate(self):
        self.at = {axis: lax.axis_index(axis) for axis in ("wide", "narrow")}
        self.odd = lax.rem(self.at["wide"], 2)

    def half_of(self, rows, which, lower=0):
        side = self.odd if which == 0 else 1 - self.odd
        return pl.ds(pl.multiple_of(lower + side * (rows // 2), rows // 2), rows // 2)

    def greet(self):
        barrier = pltpu.get_barrier_semaphore()
        for axis, stride in self.partners:
            pl.semaphore_signal(
                barrier,
                inc=1,
                device_id={axis: flip(self.at[axis], stride)},
                device_id_type=pl.DeviceIdType.MESH,
            )
        pl.semaphore_wait(barrier, len(self.partners))

    def push(self, source, target, sent, got, axis, stride):
        return pltpu.make_async_remote_copy(
            src_ref=source,
            dst_ref=target,
            send_sem=sent,
            recv_sem=got,
            device_id={axis: flip(self.at[axis], stride)},
            device_id_type=pl.DeviceIdType.MESH,
        )

    def tick(self, now, last, bunch=6):
        planned = sorted(self.plan(), key=lambda item: item[:3])
        times = sorted({item[0] for item in planned if item[0] < last})
        for lower in sorted({when - when % bunch for when in times}):

            @pl.when((now >= lower) & (now < lower + bunch))
            def _(lower=lower):
                for when in times:
                    if lower <= when < lower + bunch:
                        pl.when(now == when)(lambda when=when: self.take(planned, when))

    def take(self, planned, when):
        if when == 0:
            self.greet()
        for item in planned:
            if item[0] == when:
                item[3]()

    def rest(self, last):
        for item in sorted(self.plan(), key=lambda item: item[:3]):
            if item[0] >= last:
                item[3]()


class Gather(Steps):
    partners = (("narrow", 1), ("narrow", 2), ("wide", 1))

    def __init__(self, shapes, begins, waits, columns=None, sideways=()):
        columns = columns or [(k, 0, shape[1]) for k, shape in enumerate(shapes)]
        self.arrays, self.columns = shapes, columns
        self.shapes = [(shapes[k][0], upper - lower) for k, lower, upper in columns]
        self.begins, self.waits = begins, waits
        self.count = len(columns)
        self.sideways = sideways

    def in_specs(self):
        return [pl.BlockSpec(memory_space=pl.ANY)] * len(self.arrays)

    out_specs = in_specs

    def out_shape(self):
        return [
            jax.ShapeDtypeStruct((rows, 4 * cols) if k in self.sideways else (4 * rows, cols), BF16)
            for k, (rows, cols) in enumerate(self.arrays)
        ]

    def scratch(self):
        dma, held = pltpu.SemaphoreType.DMA, []
        for shape in self.shapes:
            held += [dma((5,)), dma((5,)), dma((2,)), pltpu.VMEM(shape, BF16)]
        return held

    def bind(self, ins, outs, held):
        self.refs = [
            (
                ins[k].at[:, lower:upper],
                outs[k] if k in self.sideways else outs[k].at[:, lower:upper],
            )
            + tuple(held[4 * part : 4 * part + 4])
            for part, (k, lower, upper) in enumerate(self.columns)
        ]
        self.locate()

    def block(self, k, index, which=None):
        rows, cols = self.shapes[k]
        if self.columns[k][0] in self.sideways:
            down = slice(None) if which is None else self.half_of(rows, which)
            return down, pl.ds(pl.multiple_of(index * cols, cols), cols)
        if which is None:
            return pl.ds(pl.multiple_of(index * rows, rows), rows), slice(None)
        return self.half_of(rows, which, index * rows), slice(None)

    def remote(self, k, step):
        source, out, sent, got, _, _ = self.refs[k]
        me, across = self.at["narrow"], flip(self.at["narrow"], 2)
        axis, stride = (("narrow", 1), ("narrow", 2), ("wide", 1), ("narrow", 1), ("narrow", 1))[step]
        if step == 0:
            ends = (source, out.at[self.block(k, me)])
        elif step == 1:
            half = self.half_of(self.shapes[k][0], 0)
            ends = (source.at[half, :], out.at[self.block(k, me, 0)])
        else:
            spot = self.block(k, across, 1 if step == 4 else 0)
            ends = (out.at[spot], out.at[spot])
        return self.push(*ends, sent.at[step], got.at[step], axis, stride)

    def local(self, k, which):
        source, out, _, _, near, kept = self.refs[k]
        if which == 0:
            return pltpu.make_async_copy(source, kept, near.at[0])
        return pltpu.make_async_copy(
            kept, out.at[self.block(k, self.at["narrow"])], near.at[1]
        )

    def begin(self, k):
        self.remote(k, 1).start()
        self.remote(k, 0).start()
        self.local(k, 0).start()

    def relay(self, k):
        self.local(k, 0).wait()
        self.local(k, 1).start()
        self.remote(k, 1).wait()
        self.remote(k, 2).start()
        self.remote(k, 3).start()

    def share(self, k):
        self.remote(k, 2).wait()
        self.remote(k, 4).start()

    def close(self, k):
        self.remote(k, 0).wait()
        self.remote(k, 3).wait()
        self.remote(k, 4).wait()
        self.local(k, 1).wait()

    def plan(self):
        planned = []
        for k in range(self.count):
            when = self.begins[k]
            planned.append((when, 0, k, lambda k=k: self.begin(k)))
            for wait, act in zip(self.waits, (self.relay, self.share, self.close)):
                when += wait
                planned.append((when, 1, k, lambda k=k, act=act: act(k)))
        return planned


class Exchange(Steps):
    def __init__(self, shapes, times, columns=None, spans=None, near=()):
        columns = columns or [(k, 0, shape[-1]) for k, shape in enumerate(shapes)]
        spans = spans or ["whole"] * len(shapes)
        self.stages = exchange_stages()
        self.arrays, self.columns = [shape[-2:] for shape in shapes], columns
        self.shapes = [(self.arrays[k][0], upper - lower) for k, lower, upper in columns]
        self.spans = [spans[k] for k, _, _ in columns]
        self.near = [k in near for k, _, _ in columns]
        self.firsts = [2 if span == "tail" else 0 for span in self.spans]
        self.lasts = [1 if span == "head" else len(self.stages) - 1 for span in self.spans]
        self.times = times
        self.count = len(columns)
        self.partners = sorted({(axis, stride) for _, axis, stride in self.stages})

    def in_specs(self):
        return [pl.BlockSpec(memory_space=pl.ANY)] * len(self.arrays)

    out_specs = in_specs

    def out_shape(self):
        return [jax.ShapeDtypeStruct(shape, BF16) for shape in self.arrays]

    def scratch(self):
        held = []
        dma = pltpu.SemaphoreType.DMA
        for (rows, cols), span, near in zip(self.shapes, self.spans, self.near):
            early, late = span != "tail", span != "head"
            held += [
                pltpu.VMEM((2, rows, cols) if early else (2, 16, PAIR), BF16),
                pltpu.VMEM((2, 16, PAIR) if near else (2 if early else 1, rows, cols), BF16),
                pltpu.VMEM((rows, cols) if early else (16, PAIR), BF16),
                pltpu.VMEM((len(self.stages) - 3, rows // 2, cols) if late else (1, 16, PAIR), BF16),
                pltpu.VMEM((rows // 2, cols) if late else (16, PAIR), BF16),
                dma((len(self.stages),)),
                dma((len(self.stages),)),
                dma((2,)),
            ]
        return held

    def bind(self, ins, outs, held):
        self.refs = []
        for part, (k, lower, upper) in enumerate(self.columns):
            every = (slice(None),) * (1 if self.spans[part] == "tail" else 2)
            source, own = ins[k].at[every + (slice(lower, upper),)], held[8 * part : 8 * part + 8]
            if self.near[part]:
                own = [own[0], source.at[2:4]] + list(own[2:])
            self.refs.append((source, outs[k].at[:, lower:upper], *own))
        self.locate()

    def own(self, k):
        kept = self.refs[k][3]
        return kept.at[0 if self.spans[k] == "tail" else 1]

    def remote(self, k, step):
        source, out, pair, kept, chip, halves, mine, sent, got, _ = self.refs[k]
        kind, axis, stride = self.stages[step]
        rows = self.shapes[k][0]
        if kind == "pair":
            ends = (source.at[0:2], pair)
        elif kind == "chip":
            ends = (kept.at[0], chip)
        elif kind == "split":
            ends = (self.own(k).at[self.half_of(rows, 1), :], halves.at[0])
        elif kind == "full":
            ends = (mine, halves.at[step - 2])
        else:
            ends = (mine, out.at[self.half_of(rows, 0), :])
        return self.push(*ends, sent.at[step], got.at[step], axis, stride)

    def load(self, k):
        source, kept, near = self.refs[k][0], self.refs[k][3], self.refs[k][9]
        if self.spans[k] == "tail":
            return pltpu.make_async_copy(source, kept.at[0], near.at[0])
        return pltpu.make_async_copy(source.at[2:4], kept, near.at[0])

    def store(self, k):
        out, mine, near = self.refs[k][1], self.refs[k][6], self.refs[k][9]
        if self.spans[k] == "head":
            return pltpu.make_async_copy(self.own(k), out, near.at[1])
        half = self.half_of(self.shapes[k][0], 0)
        return pltpu.make_async_copy(mine, out.at[half, :], near.at[1])

    def begin(self, k):
        if not self.near[k]:
            self.load(k).start()
        if self.spans[k] != "tail":
            self.remote(k, 0).start()

    def enter(self, k):
        self.load(k).wait()
        self.remote(k, 2).start()

    def end(self, k, step):
        _, _, pair, kept, chip, halves, mine, _, _, _ = self.refs[k]
        kind = self.stages[step][0]
        self.remote(k, step).wait()
        if kind == "pair":
            if not self.near[k]:
                self.load(k).wait()
            kept[...] = kept[...] + pair[...]
        elif kind == "chip":
            kept[1] = kept[1] + chip[...]
        elif kind == "split":
            half = self.half_of(self.shapes[k][0], 0)
            mine[...] = self.own(k)[half, :] + halves[0]
        elif kind == "full":
            mine[...] = mine[...] + halves[step - 2]
        if step < self.lasts[k]:
            self.remote(k, step + 1).start()
        if step == max(self.lasts[k] - 1, 1):
            self.store(k).start()
        if step == self.lasts[k]:
            self.store(k).wait()

    def plan(self):
        planned = []
        for k, (begin, *ends) in enumerate(self.times):
            first, last = self.firsts[k], self.lasts[k]
            planned.append((begin, 0, k, lambda k=k: self.begin(k)))
            if first:
                planned.append((ends[0], 1, k, lambda k=k: self.enter(k)))
                ends = [0] + ends
            for step in range(first, last + 1):
                when = ends[-1] if step == last else ends[min(step, 4)]
                planned.append((when, 1, k, lambda k=k, step=step: self.end(k, step)))
        return planned


def paced(begins, waits):
    return [[begin + sum(waits[:count]) for count in range(len(waits) + 1)] for begin in begins]


def head_mask(v, half):
    lane = lax.broadcasted_iota(jnp.int32, (1, PAIR), 1)
    keep = (lane < HEAD) if half == 0 else (lane >= HEAD)
    return jnp.where(keep, v, jnp.zeros_like(v))


def attend(qkv, shares, begins, waits, columns, ident, seqs, block=512, per=3):
    rows, width = qkv.shape[0], qkv.shape[1] // 3
    seq_length = rows // seqs
    block = min(block, seq_length)
    pairs = width // PAIR
    count = seq_length // block
    steps = pairs // per
    items = per * count
    wide = per * PAIR

    gathering = Gather([v.shape for v in shares], begins, waits, columns)
    many = len(shares)
    ticks = seqs * steps * items

    def kernel(*refs):
        q_ref, k_ref, v_ref = refs[:3]
        out, total = refs[3 + many : 5 + many]
        v_turned, out_turned, held = refs[5 + 2 * many : 8 + 2 * many]
        gathering.bind(refs[3 : 3 + many], refs[5 + many : 5 + 2 * many], refs[8 + 2 * many :])
        spot = pl.program_id(0) * steps + pl.program_id(1)
        v_turned[...] = jnp.transpose(v_ref[...])

        def place(i):
            pair = i // count
            part = i - pair * count
            return (
                pair,
                pl.ds(pl.multiple_of(pair * PAIR, PAIR), PAIR),
                pl.ds(pl.multiple_of(part * block, block), block),
            )

        def score(i, half):
            _, cols, part = place(i)
            held[half] = mxu(k_ref[:, cols], head_mask(q_ref[part, cols], half), TRANSPOSED)

        def finish(i, half):
            pair, _, part = place(i)
            scores = held[half]
            top = jnp.max(scores, axis=0, keepdims=True)
            exponent = jnp.exp2(scores * SCALE2 - top * SCALE2).astype(BF16)
            head = pl.ds(pl.multiple_of(pair * PAIR + half * HEAD, HEAD), HEAD)
            left = jnp.concatenate([v_turned[head, :], jnp.ones((16, seq_length), BF16)], axis=0)
            mixed = mxu(left, exponent)
            denominator = mixed[HEAD : HEAD + 1]
            out_turned[head, part] = mixed[:HEAD] * (1.0 / denominator)
            total[0, pair, half : half + 1, part] = top * SCALE2 + jnp.log2(denominator)

        score(0, 0)

        def body(i, carry):
            gathering.tick(spot * items + i, ticks)
            score(i, 1)
            finish(i, 0)
            score(jnp.minimum(i + 1, items - 1), 0)
            finish(i, 1)
            return carry

        lax.fori_loop(0, items, body, 0)
        out[...] = jnp.transpose(out_turned[...]).astype(BF16)

        @pl.when(spot == seqs * steps - 1)
        def _():
            gathering.rest(ticks)

    def part_of(which):
        return pl.BlockSpec((seq_length, wide), lambda s, p: (s, which * steps + p))

    return call(
        kernel,
        "attend",
        (seqs, steps),
        [part_of(0), part_of(1), part_of(2)] + gathering.in_specs(),
        [part_of(0), pl.BlockSpec((1, per, 2, seq_length), lambda s, p: (s, p, 0, 0))]
        + gathering.out_specs(),
        [
            jax.ShapeDtypeStruct((rows, width), BF16),
            jax.ShapeDtypeStruct((seqs, pairs, 2, seq_length), F32),
        ]
        + gathering.out_shape(),
        [
            pltpu.VMEM((wide, seq_length), BF16),
            pltpu.VMEM((wide, seq_length), F32),
            pltpu.VMEM((2, seq_length, block), F32),
        ]
        + gathering.scratch(),
        16 * rows * seq_length * width,
        rows * width * 8,
        rows * seq_length * width // HEAD,
        ident,
    )(qkv, qkv, qkv, *shares)


def attend_back(
    qkv, mixture, d_mixture, total, tables, turned, pieces, spans, columns, times, ident, seqs,
    block=512, per=3,
):
    rows, width = mixture.shape
    seq_length = rows // seqs
    block = min(block, seq_length)
    pairs = width // PAIR
    count = seq_length // block
    steps = pairs // per
    items = per * count
    wide = per * PAIR
    ways = lax.axis_size("narrow")
    share = width // ways
    own = [jax.ShapeDtypeStruct((ways, share, wide), BF16)] * 3
    traded = list(pieces) + own
    exchange = Exchange(
        [v.shape for v in traded],
        times,
        list(columns) + [(len(pieces) + part, 0, wide) for part in range(3)],
        list(spans) + ["whole"] * 3,
        [len(pieces) + part for part in range(3)],
    )
    many, outs = len(pieces), len(traded)
    assert steps == 2
    ticks = seqs * steps * items

    def kernel(*refs):
        q_ref, k_ref, v_ref, mix, grad, tot, cos, sin, turned_all = refs[:9]
        lower = 9 + many
        dq, dk, dv = refs[lower : lower + 3]
        out_refs, lower = refs[lower + 3 : lower + 3 + outs], lower + 3 + outs
        k_turned, dq_turned, dk_sum, dv_sum, inner, s_held, p_held = refs[lower : lower + 7]
        left, d_held, grads, near = refs[lower + 7 : lower + 11]
        exchange.bind(
            list(refs[9 : 9 + many]) + [grads.at[part] for part in range(3)],
            out_refs,
            refs[lower + 11 :],
        )
        seq = pl.program_id(1)
        spot = pl.program_id(0) * seqs + seq
        load = pltpu.make_async_copy(turned_all, left, near.at[0])
        pl.when(spot == 0)(load.start)

        @pl.when(spot == seqs)
        def _():
            load.wait()
            for part in range(3):
                product = mxu(left[...], d_held[part]).astype(BF16)
                grads[part] = product.reshape(ways, share, wide)

        k_turned[...] = jnp.transpose(k_ref[...])
        product = jnp.transpose(mix[...].astype(F32) * grad[...].astype(F32))
        for pair in range(per):
            for half in range(2):
                lower = pair * PAIR + half * HEAD
                inner[pair, half : half + 1, :] = column_sum(product[lower : lower + HEAD, :])
        dk_sum[...] = jnp.zeros_like(dk_sum)
        dv_sum[...] = jnp.zeros_like(dv_sum)

        def body(i, carry):
            exchange.tick(spot * items + i, ticks)
            pair = i // count
            part = i - pair * count
            cols = pl.ds(pl.multiple_of(pair * PAIR, PAIR), PAIR)
            part = pl.ds(pl.multiple_of(part * block, block), block)
            for half in range(2):
                head = pl.ds(pl.multiple_of(pair * PAIR + half * HEAD, HEAD), HEAD)
                query = head_mask(q_ref[part, cols], half)
                cot = head_mask(grad[part, cols], half)
                s_held[half] = mxu(k_ref[:, cols], query, TRANSPOSED)
                p_held[half] = mxu(v_ref[:, cols], cot, TRANSPOSED)
                probs = jnp.exp2(s_held[half] * SCALE2 - tot[0, pair, half : half + 1, part])
                d_scores = (probs * (p_held[half] - inner[pair, half : half + 1, part])).astype(BF16)
                dv_sum[:, cols] += mxu(probs.astype(BF16), cot)
                dk_sum[:, cols] += mxu(d_scores, query)
                dq_turned[head, part] = mxu(k_turned[head, :], d_scores)
            return carry

        lax.fori_loop(0, items, body, 0)
        d_queries = jnp.transpose(dq_turned[...])
        for source, target in ((d_queries, dq), (dk_sum, dk)):
            for pair in range(per):
                v = source[:, pair * PAIR : (pair + 1) * PAIR] * SCALE
                v = v * cos[...] - partner_lanes(v) * sin[...]
                target[:, pair * PAIR : (pair + 1) * PAIR] = v.astype(BF16)
        dv[...] = dv_sum[...].astype(BF16)

        @pl.when(spot < seqs)
        def _():
            here = pl.ds(pl.multiple_of(seq * seq_length, seq_length), seq_length)
            for part, target in enumerate((dq, dk, dv)):
                d_held[part, here, :] = target[...]

        @pl.when(spot == seqs * steps - 1)
        def _():
            exchange.rest(ticks)

    def part_of(which):
        return pl.BlockSpec((seq_length, wide), lambda p, s: (s, which * steps + p))

    table = whole((seq_length, PAIR))
    grads = jax.ShapeDtypeStruct((rows, width), BF16)
    return call(
        kernel,
        "attend_back",
        (steps, seqs),
        [part_of(0), part_of(1), part_of(2), part_of(0), part_of(0)]
        + [pl.BlockSpec((1, per, 2, seq_length), lambda p, s: (s, p, 0, 0))]
        + [table] * 2
        + [pl.BlockSpec(memory_space=pl.ANY)] * (1 + many),
        [part_of(0), part_of(0), part_of(0)] + exchange.out_specs(),
        [grads, grads, grads] + exchange.out_shape(),
        [
            pltpu.VMEM((wide, seq_length), BF16),
            pltpu.VMEM((wide, seq_length), F32),
            pltpu.VMEM((seq_length, wide), F32),
            pltpu.VMEM((seq_length, wide), F32),
            pltpu.VMEM((per, 2, seq_length), F32),
            pltpu.VMEM((2, seq_length, block), F32),
            pltpu.VMEM((2, seq_length, block), F32),
            pltpu.VMEM(turned.shape, BF16),
            pltpu.VMEM((3, rows, wide), BF16),
            pltpu.VMEM((3, ways, share, wide), BF16),
            pltpu.SemaphoreType.DMA((1,)),
        ]
        + exchange.scratch(),
        40 * rows * seq_length * width,
        rows * width * 16,
        rows * seq_length * width // HEAD,
        ident,
    )(qkv, qkv, qkv, mixture, d_mixture, total, *tables, turned, *pieces)


def gelu_pair(v):
    root = math.sqrt(2.0 / math.pi)
    square = v * v
    near = 0.5 + 0.5 * jnp.tanh(v * (root + (root * 0.044715) * square))
    active = v * near
    bend = 2.0 * root + (6.0 * root * 0.044715) * square
    return active, near + (active * (1.0 - near)) * bend


def grouped_rows(ref, ways):
    part = ref.shape[0] // (ways * GROUPS)
    lowers = [(way * GROUPS + group) * part for group in range(GROUPS) for way in range(ways)]
    return jnp.concatenate([ref[lower : lower + part, :] for lower in lowers], axis=0)


def grouped_columns(ref, ways):
    part = ref.shape[1] // (ways * GROUPS)
    lowers = [(way * GROUPS + group) * part for group in range(GROUPS) for way in range(ways)]
    return jnp.concatenate([ref[:, lower : lower + part] for lower in lowers], axis=1)


def halved(arrays):
    return [
        (k, half * v.shape[-1] // 2, (half + 1) * v.shape[-1] // 2)
        for k, v in enumerate(arrays)
        for half in range(2)
    ]


def hidden_units(
    mixture, tokens, cot, starts, lengths, embed, gain, modulation, out_weight, up, up_bias, down,
    times, ident, seqs, block=512,
):
    rows, width = tokens.shape
    ways = lax.axis_size("narrow")
    units = up.shape[1] // GROUPS
    share, part_units = width // ways, units // ways
    seq_length = rows // seqs
    block = min(block, seq_length)
    per_seq = seq_length // block
    steps = rows // block
    turn = steps + ways
    shape_up, shape_down = (ways, share, units), (ways, part_units, width)
    traded = [jax.ShapeDtypeStruct(v, BF16) for v in (shape_up, shape_down) * 2]
    exchange = Exchange(
        [v.shape for v in traded], times, halved(traded), ["whole"] * 2 + ["head"] * 2, range(4)
    )

    def kernel(*refs):
        starts, lengths, mix, tok, emb, gn, w_out, g, mod, b_up = refs[:10]
        emb, gn = row_of(emb, EMBED, width), row_of(gn, GAIN_TWO, width)
        w_ups, w_downs = refs[10 : 10 + ways], refs[10 + ways : 10 + 2 * ways]
        act, d_up, g_bias, d_gate, g_sum = refs[10 + 2 * ways : 15 + 2 * ways]
        outs, left = refs[15 + 2 * ways : 21 + 2 * ways], refs[21 + 2 * ways :]
        n_turned, g_turned, a_held, u_held, down_held, g_up, g_down, near, n_held = left[:9]
        exchange.bind(
            [g_up.at[0], g_down.at[0], g_up.at[1], g_down.at[1]], outs[:4], left[9:]
        )
        step = pl.program_id(0)
        group = step // turn
        at = step - group * turn

        @pl.when(step == 0)
        def _():
            exchange.greet()
            n_turned[width:, :] = jnp.ones((16, rows), BF16)
            d_gate[...] = jnp.zeros_like(d_gate)
            g_sum[...] = jnp.zeros_like(g_sum)

        exchange.tick(step, GROUPS * turn)

        @pl.when(at == 0)
        def _():
            for way in range(ways):
                down_held[way] = w_downs[way][...]

        part = pl.ds(pl.multiple_of(jnp.minimum(at, steps - 1) * block, block), block)

        @pl.when(step < steps)
        def _():
            seq = at // per_seq
            first = (at - seq * per_seq) * block
            start, _ = masked_rows(tok[...], emb[...], starts[seq], lengths[seq], first)
            gate = mod[pl.ds(seq, 1), 2 * width : 3 * width]
            hat, _ = normalized(start + gate * mxu(mix[...], w_out[...]))
            shift = mod[pl.ds(seq, 1), 3 * width : 4 * width]
            scale = mod[pl.ds(seq, 1), 4 * width : 5 * width]
            normed = (hat * (gn[...] * (1.0 + scale)) + shift).astype(BF16)
            n_held[part, :] = normed
            store_shares(n_turned, jnp.transpose(normed), part)
            g_turned[:, part] = jnp.transpose(g[...])
            g_sum[pl.ds(seq, 1), :] += column_sum(g[...].astype(F32))

        @pl.when(at < steps)
        def _():
            seq = at // per_seq
            nrm = n_held[part, :]
            cotangent = g[...].astype(F32)
            d_branch = (mod[pl.ds(seq, 1), 5 * width : 6 * width] * cotangent).astype(BF16)
            for way in range(ways):
                cols = slice(way * part_units, (way + 1) * part_units)
                upper = mxu(nrm, w_ups[way][...]) + b_up[pl.ds(BIAS_UP + group, 1), cols]
                d_active = mxu(d_branch, w_downs[way][...], TRANSPOSED)
                active, slope = gelu_pair(upper)
                active = active.astype(BF16)
                d_upper = (d_active * slope).astype(BF16)
                act[:, cols] = active
                a_held[part, cols] = active
                d_up[:, cols] = d_upper
                u_held[part, cols] = d_upper

        @pl.when(at >= steps)
        def _():
            place = at - steps
            owner = owner_at(exchange.at["narrow"], place)
            cols = pl.ds(pl.multiple_of(owner * part_units, part_units), part_units)
            product = mxu(n_turned[...], u_held[:, cols])
            g_bias[:, cols] = product[width : width + 1]
            g_up[group, :, :, cols] = product[:width].astype(BF16).reshape(
                ways, share, part_units
            )
            own = down_held[owner].astype(F32)
            total = jnp.zeros((part_units, width), F32)
            for seq in range(seqs):
                lower, upper = seq * seq_length, (seq + 1) * seq_length
                product = mxu(g_turned[:, lower:upper], a_held[lower:upper, cols])
                product = jnp.transpose(product)
                total += product * mod[seq : seq + 1, 5 * width : 6 * width]
                d_gate[seq : seq + 1, :] += column_sum(product * own)
            g_down[group, place] = total.astype(BF16)

        @pl.when(step == GROUPS * turn - 1)
        def _():
            copies = [
                pltpu.make_async_copy(source.at[GROUPS - 1], target, near.at[k])
                for k, (source, target) in enumerate(((g_up, outs[4]), (g_down, outs[5])))
            ]
            for copy in copies:
                copy.start()
            exchange.rest(GROUPS * turn)
            for copy in copies:
                copy.wait()

    def early(i):
        return (jnp.minimum(lax.rem(i, turn), steps - 1), 0)

    def once(i):
        return (jnp.minimum(i, steps - 1), 0)

    def fixed(shape):
        return pl.BlockSpec(shape, lambda i: (0,) * len(shape))

    by_rows = pl.BlockSpec(
        (block, units), lambda i: (jnp.minimum(lax.rem(i, turn), steps - 1), i // turn)
    )
    by_group = pl.BlockSpec((1, units), lambda i: (0, i // turn))

    def up_piece(way):
        return pl.BlockSpec((width, part_units), lambda i: (0, way * GROUPS + i // turn))

    def down_piece(way):
        return pl.BlockSpec((part_units, width), lambda i: (way * GROUPS + i // turn, 0))

    assert GROUPS == 3
    anywhere = pl.BlockSpec(memory_space=pl.ANY)
    return call(
        kernel,
        "hidden_units",
        (GROUPS * turn,),
        [smem(), smem()]
        + [pl.BlockSpec((block, width), once)] * 2
        + [whole(embed.shape), whole(gain.shape), whole(out_weight.shape)]
        + [pl.BlockSpec((block, width), early)]
        + [whole(modulation.shape), whole(up_bias.shape)]
        + [up_piece(way) for way in range(ways)]
        + [down_piece(way) for way in range(ways)],
        [by_rows, by_rows, by_group, fixed((seqs, width)), fixed((seqs, width))]
        + exchange.out_specs()
        + [anywhere] * 2,
        [
            jax.ShapeDtypeStruct((rows, units * GROUPS), BF16),
            jax.ShapeDtypeStruct((rows, units * GROUPS), BF16),
            jax.ShapeDtypeStruct((1, units * GROUPS), F32),
            jax.ShapeDtypeStruct((seqs, width), F32),
            jax.ShapeDtypeStruct((seqs, width), F32),
        ]
        + exchange.out_shape()
        + [jax.ShapeDtypeStruct(shape_up, BF16), jax.ShapeDtypeStruct(shape_down, BF16)],
        [
            pltpu.VMEM((width + 16, rows), BF16),
            pltpu.VMEM((width, rows), BF16),
            pltpu.VMEM((rows, units), BF16),
            pltpu.VMEM((rows, units), BF16),
            pltpu.VMEM((ways, part_units, width), BF16),
            pltpu.VMEM((GROUPS,) + shape_up, BF16),
            pltpu.VMEM((GROUPS,) + shape_down, BF16),
            pltpu.SemaphoreType.DMA((2,)),
            pltpu.VMEM((rows, width), BF16),
        ]
        + exchange.scratch(),
        8 * rows * width * units * GROUPS,
        GROUPS * (rows * (width * 4 + units * 4) + 8 * width * units),
        rows * units * GROUPS,
        ident,
    )(
        starts, lengths, mixture, tokens, embed, gain, out_weight, cot, modulation, up_bias,
        *[up] * ways, *[down] * ways,
    )


def middle_back(
    mixture, tokens, cot, starts, lengths, embed, gain, modulation, out_weight, d_upper, up, seqs,
    block=256,
):
    rows, width = tokens.shape
    ways = lax.axis_size("narrow")
    seq_length = rows // seqs
    block = min(block, seq_length)
    per_seq = seq_length // block
    steps = rows // block
    hidden_width = d_upper.shape[1]
    share = width // ways

    def kernel(
        starts, lengths, mix, tok, g, emb, gn, mod, w_out, w_up, d_ups, d_middle_out, d_mix, g_out,
        sums, g_sum,
    ):
        emb, gn = row_of(emb, EMBED, width), row_of(gn, GAIN_TWO, width)
        step = pl.program_id(0)
        seq = step // per_seq
        first = (step - seq * per_seq) * block

        @pl.when(step == 0)
        def _():
            g_sum[...] = jnp.zeros_like(g_sum)

        @pl.when(step == seq * per_seq)
        def _():
            sums[...] = jnp.zeros_like(sums)

        def vector(which):
            return mod[pl.ds(seq, 1), which * width : (which + 1) * width]

        attended = mxu(mix[...], w_out[...])
        start, _ = masked_rows(tok[...], emb[...], starts[seq], lengths[seq], first)
        hat, inverse = normalized(start + vector(2) * attended)
        d_normed = mxu(d_ups[...], grouped_columns(w_up, ways), TRANSPOSED)
        d_middle = g[...].astype(F32) + norm_back(
            d_normed * (gn[...] * (1.0 + vector(4))), hat, inverse
        )
        d_middle_out[...] = d_middle
        d_attended = (vector(2) * d_middle).astype(BF16)
        d_mix[...] = mxu(d_attended, w_out[...], TRANSPOSED).astype(BF16)
        g_sum[...] += mxu(jnp.transpose(mix[...]), d_attended)
        sums[0, 0:1, :] += column_sum(d_normed)
        sums[0, 1:2, :] += column_sum(d_normed * hat)
        sums[0, 2:3, :] += column_sum(d_middle * attended)

        @pl.when(step == steps - 1)
        def _():
            for place in range(ways):
                owner = owner_at(lax.axis_index("narrow"), place)
                spot = pl.ds(pl.multiple_of(owner * share, share), share)
                g_out[place] = g_sum[spot, :].astype(BF16)

    row = pl.BlockSpec((block, width), lambda i: (i, 0))
    return call(
        kernel,
        "middle_back",
        (steps,),
        [smem(), smem(), row, row, row, whole(embed.shape), whole(gain.shape)]
        + [whole(modulation.shape), whole(out_weight.shape), whole(up.shape)]
        + [pl.BlockSpec((block, hidden_width), lambda i: (i, 0))],
        (
            row,
            row,
            pl.BlockSpec((ways, share, width), lambda i: (0, 0, 0)),
            pl.BlockSpec((1, 8, width), lambda i: (i // per_seq, 0, 0)),
        ),
        (
            jax.ShapeDtypeStruct((rows, width), F32),
            jax.ShapeDtypeStruct((rows, width), BF16),
            jax.ShapeDtypeStruct((ways, share, width), BF16),
            jax.ShapeDtypeStruct((seqs, 8, width), F32),
        ),
        [pltpu.VMEM((width, width), F32)],
        rows * width * (2 * hidden_width + 6 * width),
        rows * (width * 12 + hidden_width * 2) + 2 * width * hidden_width,
    )(
        starts, lengths, mixture, tokens, cot, embed, gain, modulation, out_weight, up, d_upper,
    )


class Finale(Steps):
    def __init__(self, ways):
        self.ways = ways
        self.wide = lax.axis_size("wide")

    def scratch(self, columns):
        dma = pltpu.SemaphoreType.DMA
        return [
            pltpu.VMEM((self.ways, 8, columns), F32),
            pltpu.VMEM((self.ways, 8, columns), F32),
            pltpu.VMEM((self.wide, 8, columns), F32),
            dma((self.ways,)),
            dma((self.ways,)),
            dma((self.wide,)),
            dma((self.wide,)),
        ]

    def bind(self, held):
        self.parts, self.narrow_got, self.wide_got, *self.sems = held
        self.locate()

    def others(self):
        targets = []
        for offset in range(1, self.ways):
            targets.append({"narrow": lax.rem(self.at["narrow"] + offset, self.ways)})
        for offset in range(1, self.wide):
            targets.append({"wide": lax.rem(self.at["wide"] + offset, self.wide)})
        return targets

    def greet(self):
        barrier = pltpu.get_barrier_semaphore()
        targets = self.others()
        for target in targets:
            pl.semaphore_signal(
                barrier, inc=1, device_id=target, device_id_type=pl.DeviceIdType.MESH
            )
        pl.semaphore_wait(barrier, len(targets))

    def along_narrow(self, offset):
        target = lax.rem(self.at["narrow"] + offset, self.ways)
        return pltpu.make_async_remote_copy(
            src_ref=self.parts.at[target],
            dst_ref=self.narrow_got.at[self.at["narrow"]],
            send_sem=self.sems[0].at[offset],
            recv_sem=self.sems[1].at[offset],
            device_id={"narrow": target},
            device_id_type=pl.DeviceIdType.MESH,
        )

    def along_wide(self, offset):
        me = self.at["wide"]
        return pltpu.make_async_remote_copy(
            src_ref=self.wide_got.at[me],
            dst_ref=self.wide_got.at[me],
            send_sem=self.sems[2].at[offset],
            recv_sem=self.sems[3].at[offset],
            device_id={"wide": lax.rem(me + offset, self.wide)},
            device_id_type=pl.DeviceIdType.MESH,
        )

    def begin(self):
        for offset in range(1, self.ways):
            self.along_narrow(offset).start()
        me = self.at["narrow"]
        self.narrow_got[pl.ds(me, 1)] = self.parts[pl.ds(me, 1)]

    def spread(self, seqs, row_lanes):
        for offset in range(1, self.ways):
            self.along_narrow(offset).wait()
        me = self.at["wide"]
        for way in range(self.ways):
            self.wide_got[pl.ds(me, 1), way * seqs : (way + 1) * seqs, 0:row_lanes] = (
                self.narrow_got[way : way + 1, 0:seqs, 0:row_lanes]
            )
        total = self.narrow_got[0:1, :, row_lanes:]
        for way in range(1, self.ways):
            total += self.narrow_got[way : way + 1, :, row_lanes:]
        self.wide_got[pl.ds(me, 1), :, row_lanes:] = total
        for offset in range(1, self.wide):
            self.along_wide(offset).start()

    def close(self):
        for offset in range(1, self.wide):
            self.along_wide(offset).wait()


def finish(
    turned, d_parts, tokens, d_middle, mixture, starts, lengths, embed, gain, modulation, weight,
    out_weight, down_bias, active, down, features, rows_two, vectors_two, times, ident, seqs,
    wide=384, block=512, late_block=256,
):
    rows, width = tokens.shape
    ways = lax.axis_size("narrow")
    share = width // ways
    seq_length = rows // seqs
    block, late_block = min(block, seq_length), min(late_block, seq_length)
    per_seq, late_per_seq = seq_length // block, seq_length // late_block
    columns, hidden_width = modulation.shape[1] // ways, active.shape[1]
    time_width = features.shape[1]
    window = 2 * PAIR
    lanes = columns + time_width + window
    early, middle, late = 3, rows // block, rows // late_block
    steps = early + middle + late
    exchange = Exchange([(ways, share, wide)] * 3, times, near=range(3))
    finale = Finale(ways)

    def kernel(*refs):
        (
            starts, lengths, left, q_all, k_all, v_all, tok, d_mid, emb, gn, mod, w_qkv_all,
            tok_late, mix, w_out_all, b_down, feat, two, vec, act, w_down_all,
        ) = refs[:21]
        emb, gn = row_of(emb, EMBED, width), row_of(gn, GAIN_ONE, width)
        b_down = row_of(b_down, BIAS_DOWN, width)
        spot = 21
        g_tok, block_out, g_ada, g_ada_bias, g_vec = refs[spot : spot + 5]
        outs = refs[spot + 5 : spot + 8]
        grads, sums = refs[spot + 8 : spot + 10]
        d_held, w_qkv, w_out, w_down, near = refs[spot + 10 : spot + 15]
        small = spot + 15 + 7
        exchange.bind([grads.at[part] for part in range(3)], outs, refs[small:])
        finale.bind(refs[spot + 15 : small])
        step = pl.program_id(0)
        loads = [
            pltpu.make_async_copy(source, d_held.at[part], near.at[part])
            for part, source in enumerate((q_all, k_all, v_all))
        ]
        loads += [
            pltpu.make_async_copy(source, target, near.at[3 + which])
            for which, (source, target) in enumerate(
                ((w_qkv_all, w_qkv), (w_out_all, w_out), (w_down_all, w_down))
            )
        ]

        @pl.when(step == 0)
        def _():
            for load in loads:
                load.start()
            finale.greet()
            sums[...] = jnp.zeros_like(sums)

        exchange.tick(step, steps)

        for part in range(3):
            pl.when(step == part)(loads[part].wait)
        pl.when(step == early)(loads[3].wait)

        @pl.when(step == early + middle)
        def _():
            loads[4].wait()
            loads[5].wait()

        @pl.when(step < early)
        def _():
            product = mxu(left[...], d_held[step, :, width - wide :]).astype(BF16)
            grads[step] = product.reshape(ways, share, wide)

        @pl.when((step >= early) & (step < early + middle))
        def _():
            at = step - early
            seq = at // per_seq
            first = (at - seq * per_seq) * block
            start, inside = masked_rows(
                tok[...], emb[...], starts[seq], lengths[seq], first
            )
            hat, inverse = normalized(start)
            here = pl.ds(pl.multiple_of(at * block, block), block)
            d_normed = mxu(d_held[0, here, :], w_qkv[:, 0:width], TRANSPOSED)
            d_normed += mxu(d_held[1, here, :], w_qkv[:, width : 2 * width], TRANSPOSED)
            d_normed += mxu(d_held[2, here, :], w_qkv[:, 2 * width :], TRANSPOSED)
            scale = mod[pl.ds(seq, 1), width : 2 * width]
            d_start = d_mid[...] + norm_back(d_normed * (gn[...] * (1.0 + scale)), hat, inverse)
            g_tok[...] = jnp.where(inside, 0.0, d_start)
            sums[seq, 0:1, :] += column_sum(d_normed)
            sums[seq, 1:2, :] += column_sum(d_normed * hat)
            sums[seq, 2:3, :] += column_sum(jnp.where(inside, d_start, 0.0))

        @pl.when(step == early + middle)
        def _():
            parts = finale.parts
            embed_sum = jnp.zeros((1, width), F32)
            gain_sum = jnp.zeros((1, width), F32)
            for seq in range(seqs):
                shift, scale = sums[seq, 0:1, :], sums[seq, 1:2, :]
                gain_sum += scale * (1.0 + mod[seq : seq + 1, width : 2 * width])
                embed_sum += sums[seq, 2:3, :]
                row = jnp.concatenate([shift, scale * gn[...], two[seq : seq + 1, :]], axis=1)
                for way in range(ways):
                    parts[way, seq : seq + 1, 0:columns] = row[
                        :, way * columns : (way + 1) * columns
                    ]
            for way in range(ways):
                parts[way, 0:seqs, columns : columns + time_width] = feat[...]
                lower = PAIR * (share * way // PAIR)
                parts[way, 0:1, columns + time_width :] = embed_sum[:, lower : lower + window]
                parts[way, 1:2, columns + time_width :] = gain_sum[:, lower : lower + window]
                parts[way, 2:8, columns + time_width :] = vec[way, 2:8, :]
            finale.begin()

        @pl.when(step == early + middle + 2)
        def _():
            finale.spread(seqs, columns + time_width)

        @pl.when(step >= early + middle)
        def _():
            at = step - early - middle
            seq = at // late_per_seq
            first = (at - seq * late_per_seq) * late_block
            start, _ = masked_rows(
                tok_late[...], emb[...], starts[seq], lengths[seq], first
            )
            attended = mxu(mix[...], w_out[...])
            branch = mxu(act[...], grouped_rows(w_down, ways)) + b_down[...]
            hidden = start + mod[pl.ds(seq, 1), 2 * width : 3 * width] * attended
            block_out[...] = (
                hidden + mod[pl.ds(seq, 1), 5 * width : 6 * width] * branch
            ).astype(BF16)

        @pl.when(step == steps - 1)
        def _():
            finale.close()
            got = finale.wide_got
            every = got[...].reshape(finale.wide * 8, lanes)
            d_mods, feats = every[:, 0:columns], every[:, columns : columns + time_width]
            g_ada[...] = lax.dot_general(
                jnp.transpose(feats), d_mods, PLAIN, precision=FULL_PRECISION,
                preferred_element_type=F32,
            )
            g_ada_bias[...] = column_sum(d_mods)
            total = got[0, :, columns + time_width :]
            for index in range(1, finale.wide):
                total += got[index, :, columns + time_width :]
            g_vec[...] = total
            exchange.rest(steps)

    row = pl.BlockSpec((block, width), lambda i: (jnp.clip(i - early, 0, middle - 1), 0))

    def late_row(wide):
        return pl.BlockSpec(
            (late_block, wide), lambda i: (jnp.maximum(i - early - middle, 0), 0)
        )

    def fixed(shape):
        return pl.BlockSpec(shape, lambda i: (0,) * len(shape))

    anywhere = pl.BlockSpec(memory_space=pl.ANY)
    return call(
        kernel,
        "finish",
        (steps,),
        [smem(), smem(), whole(turned.shape)]
        + [anywhere] * 3
        + [row, row, whole(embed.shape), whole(gain.shape), whole(modulation.shape), anywhere]
        + [late_row(width), late_row(width), anywhere, whole(down_bias.shape)]
        + [whole(features.shape), whole(rows_two.shape), whole(vectors_two.shape)]
        + [late_row(hidden_width), anywhere],
        [
            row,
            late_row(width),
            fixed((time_width, columns)),
            fixed((1, columns)),
            fixed((8, window)),
        ]
        + exchange.out_specs(),
        [
            jax.ShapeDtypeStruct((rows, width), F32),
            jax.ShapeDtypeStruct((rows, width), BF16),
            jax.ShapeDtypeStruct((time_width, columns), F32),
            jax.ShapeDtypeStruct((1, columns), F32),
            jax.ShapeDtypeStruct((8, window), F32),
        ]
        + exchange.out_shape(),
        [
            pltpu.VMEM((3, ways, share, wide), BF16),
            pltpu.VMEM((seqs, 8, width), F32),
            pltpu.VMEM((3, rows, width), BF16),
            pltpu.VMEM(weight.shape, BF16),
            pltpu.VMEM(out_weight.shape, BF16),
            pltpu.VMEM(down.shape, BF16),
            pltpu.SemaphoreType.DMA((6,)),
        ]
        + finale.scratch(lanes)
        + exchange.scratch(),
        2 * rows * width * (7 * width + hidden_width),
        rows * (width * 24 + 2 * hidden_width),
        0,
        ident,
    )(
        starts, lengths, turned, *d_parts, tokens, d_middle, embed, gain, modulation, weight,        tokens, mixture, out_weight, down_bias, features, rows_two, vectors_two, active, down,
    )


def gather_first(small, ada, weight, ident):
    share, wide = weight.shape
    width = wide // 3
    columns = [(0, 0, small.shape[1]), (1, 0, ada.shape[1])]
    columns += [(2, k * width, (k + 1) * width) for k in range(3)]
    gathering = Gather(
        [small.shape, ada.shape, weight.shape], [0] * 5, [0] * 3, columns, (0, 1)
    )

    def kernel(*refs):
        gathering.bind(refs[0:3], refs[3:6], refs[6:])
        gathering.greet()
        gathering.begin(0)
        gathering.begin(1)
        gathering.begin(2)
        for k in range(5):
            gathering.relay(k)
            if k + 3 < 5:
                gathering.begin(k + 3)
            if k > 0:
                gathering.share(k - 1)
        gathering.share(4)
        for k in range(5):
            gathering.close(k)

    return call(
        kernel,
        "gather_first",
        (),
        gathering.in_specs(),
        gathering.out_specs(),
        gathering.out_shape(),
        gathering.scratch(),
        0,
        8 * share * wide,
        0,
        ident,
    )(small, ada, weight)


def assemble(ups, downs, out, qkv):
    share, units = ups[0].shape
    part, width = downs[0].shape
    ways = units // part
    groups = len(ups)

    def kernel(*refs):
        up_in, down_in = refs[:groups], refs[groups : 2 * groups]
        out_in, qkv_in = refs[2 * groups], refs[2 * groups + 1 : 2 * groups + 7]
        g_up, g_down, g_out, g_qkv = refs[2 * groups + 7 :]
        for group in range(groups):
            for way in range(ways):
                lower = (way * groups + group) * part
                g_up[:, lower : lower + part] = up_in[group][
                    :, way * part : (way + 1) * part
                ].astype(F32)
            g_down[group] = down_in[group][...].astype(F32)
        g_out[...] = out_in[...].astype(F32)
        for which in range(6):
            lower = (which % 3) * width + (which // 3) * (width // 2)
            g_qkv[:, lower : lower + width // 2] = qkv_in[which][...].astype(F32)

    pace = 4
    small, tall = share // pace, part // pace

    def rows(count, columns):
        return pl.BlockSpec((count, columns), lambda i: (i, 0))

    g_up, g_down, g_out, g_qkv = call(
        kernel,
        "assemble",
        (pace,),
        [rows(small, units)] * groups
        + [rows(tall, width)] * groups
        + [rows(small, width)]
        + [rows(small, width // 2)] * 6,
        (
            rows(small, units * groups),
            pl.BlockSpec((groups, tall, width), lambda i: (0, i, 0)),
            rows(small, width),
            rows(small, 3 * width),
        ),
        (
            jax.ShapeDtypeStruct((share, units * groups), F32),
            jax.ShapeDtypeStruct((groups, part, width), F32),
            jax.ShapeDtypeStruct((share, width), F32),
            jax.ShapeDtypeStruct((share, 3 * width), F32),
        ),
        [],
        0,
        12 * share * units * groups,
    )(*ups, *downs, out, *qkv)
    return g_up, g_down.reshape(groups * part, width), g_out, g_qkv


def per_device(
    tokens,
    timestep,
    span_start,
    span_length,
    mask_embed,
    ada_weight,
    ada_bias,
    norm_first,
    query_key_value_weight,
    output_weight,
    norm_second,
    up_projection_weight,
    up_projection_bias,
    down_projection_weight,
    down_projection_bias,
    cotangent,
):
    seqs = timestep.shape[0]
    rows, width = tokens.shape
    seq_length = rows // seqs
    ways = lax.axis_size("narrow")
    me = lax.axis_index("narrow")
    share = width // ways
    unit_share = down_projection_weight.shape[0]
    part = unit_share // GROUPS
    units = ways * part
    time_width, columns = ada_weight.shape

    spot = jnp.arange(32 * columns)
    lane = lax.rem(spot, columns)
    owner = jnp.where(spot < (BIAS_UP + 1) * columns, lane // share, lane // part)
    vectors = [mask_embed, norm_first, norm_second, down_projection_bias]
    vectors += [up_projection_bias[group * part : (group + 1) * part] for group in range(GROUPS)]
    small = jnp.zeros((32 * columns,), BF16)
    for row, v in enumerate(vectors):
        for way in range(ways):
            lower = (row + 1) * columns + way * v.shape[0]
            small += jnp.pad(v, (lower, small.shape[0] - lower - v.shape[0]))
    small = jnp.where(owner == me, small, jnp.zeros_like(small))
    small += jnp.pad(ada_bias, (0, small.shape[0] - columns))
    small = small.reshape(32, columns)
    small, ada, w_qkv = gather_first(small, ada_weight, query_key_value_weight, 0)
    vectors = jnp.sum(small[1:9].astype(F32).reshape(8, ways, columns), axis=1)
    features = time_features(timestep, time_width)
    modulation = jnp.dot(features, ada.astype(F32), precision=FULL_PRECISION) + small[0:1].astype(F32)
    tables = rotary_tables(seq_length)

    qkv, turned_one = project(
        tokens, span_start, span_length, vectors, vectors, modulation, w_qkv, tables, seqs
    )
    thirds = [
        (which, third * size, (third + 1) * size)
        for which, size in ((1, unit_share * ways // 3), (2, width // 3))
        for third in range(3)
    ]
    mixture, total, w_out, w_up, w_down = attend(
        qkv,
        [output_weight, up_projection_weight, down_projection_weight],
        [0, 1, 3, 6, 8, 11, 13],
        [5, 5, 2],
        [(0, 0, width)] + thirds,
        1,
        seqs,
    )
    gain_two, bias_down = [vectors[row : row + 1, :width] for row in (GAIN_TWO, BIAS_DOWN)]
    head_times = paced([8, 9, 10, 11], [1, 5, 2, 2, 2, 1]) + paced([17, 17, 18, 19], [1, 4])
    active, d_upper, g_bias, d_gate_two, g_sum, *swaps = hidden_units(
        mixture, tokens, cotangent, span_start, span_length, vectors, vectors, modulation, w_out,
        w_up, vectors, w_down, head_times, 2, seqs,
    )
    d_gate_two += bias_down * g_sum
    d_middle, d_mixture, g_out, sums_two = middle_back(
        mixture, tokens, cotangent, span_start, span_length, vectors, vectors, modulation, w_out,
        d_upper, w_up, seqs,
    )
    d_q, d_k, d_v, *done = attend_back(
        qkv, mixture, d_mixture, total, tables, turned_one, swaps[2:] + [g_out],
        ["tail"] * 2 + ["whole"] * 3, halved(swaps[2:] + [g_out]),
        [[1, 2, 5, 8, 11, 13], [2, 3, 6, 9, 12, 14], [3, 4, 7, 10, 13, 15], [4, 5, 8, 11, 14, 16]]
        + paced([0, 1, 3, 5], [1, 4, 3, 3, 4, 2])
        + paced([6, 8], [1, 3, 3, 3, 3, 2])
        + paced([12, 12, 13], [1, 3, 2, 2, 3, 1]),
        3, seqs,
    )
    scale_two = modulation[:, 4 * width : 5 * width]
    rows_two = jnp.concatenate(
        [sums_two[:, 2], sums_two[:, 0], sums_two[:, 1] * gain_two, d_gate_two], axis=1
    )
    g_norm_two = jnp.sum(sums_two[:, 1] * (1.0 + scale_two), axis=0)
    g_bias_down = jnp.sum(modulation[:, 5 * width :] * g_sum, axis=0)
    lowers = [PAIR * (share * way // PAIR) for way in range(ways)]
    vectors_two = jnp.stack(
        [
            jnp.stack([v[lower : lower + 2 * PAIR] for lower in lowers])
            for v in (g_norm_two, g_norm_two, g_norm_two, g_bias_down)
        ]
        + [g_bias[0].reshape(GROUPS, ways, part)[group] for group in range(GROUPS)]
        + [jnp.zeros((ways, 2 * PAIR), F32)],
        axis=1,
    )
    grad_tokens, block_out, grad_ada_weight, grad_ada_bias, gathered, *g_qkv = finish(
        turned_one, (d_q, d_k, d_v), tokens, d_middle, mixture, span_start, span_length, vectors,
        vectors, modulation, w_qkv, w_out, vectors, active, w_down, features, rows_two,
        vectors_two,
        FINISH_TIMES, 4, seqs,
    )
    skip = lax.rem(share * me, PAIR)
    own = lax.dynamic_slice_in_dim(gathered[:4], skip, share, 1)
    g_ups, g_downs = (swaps[0], *done[0:4:2]), (swaps[1], *done[1:4:2])
    g_up, g_down, g_out, g_qkv = assemble(g_ups, g_downs, done[4], done[5:] + g_qkv)
    return (
        block_out,
        grad_tokens,
        own[0],
        grad_ada_weight,
        grad_ada_bias[0],
        own[1],
        g_qkv,
        g_out,
        own[2],
        g_up,
        gathered[4 : 4 + GROUPS].reshape(-1),
        g_down,
        own[3],
    )


def solution(mesh):
    rows = P(("wide", "narrow"), None)
    per_seq = P(("wide", "narrow"))
    vector, matrix, columns = P("narrow"), P("narrow", None), P(None, "narrow")
    return jax.shard_map(
        per_device,
        mesh=mesh,
        in_specs=(
            rows, per_seq, per_seq, per_seq, vector, columns, vector, vector,
            matrix, matrix, vector, matrix, vector, matrix, vector, rows,
        ),
        out_specs=(
            rows, rows, vector, columns, vector, vector, matrix, matrix, vector, matrix,
            vector, matrix, vector,
        ),
        check_vma=False,
    )
```

```python
import math

import jax
import jax.numpy as jnp
import numpy as np
from jax import lax
from jax.experimental import pallas as pl
from jax.experimental.pallas import tpu as pltpu
from jax.sharding import PartitionSpec as P

HEAD = 64
PAIR = 2 * HEAD
GROUPS = 3
EMBED, GAIN_ONE, GAIN_TWO, BIAS_DOWN, BIAS_UP = range(5)
FINISH_TIMES = [
    [1, 3, 5, 6, 7, 10, 12], [2, 4, 6, 7, 9, 12, 14], [3, 4, 7, 9, 11, 14, 15],
]
EPSILON = 1e-05
FULL_PRECISION = lax.Precision.HIGHEST
F32 = jnp.float32
BF16 = jnp.bfloat16
SCALE = 1.0 / math.sqrt(HEAD)
SCALE2 = SCALE * math.log2(math.e)
VMEM_BYTES = 60 << 20
PLAIN = (((1,), (0,)), ((), ()))
TRANSPOSED = (((1,), (1,)), ((), ()))


def mxu(left, right, dims=PLAIN):
    return lax.dot_general(left, right, dims, preferred_element_type=F32)


def call(
    kernel, name, grid, in_specs, out_specs, out_shape, scratch, flops, moved, exps=0, ident=None
):
    return pl.pallas_call(
        kernel,
        name=name,
        grid=grid,
        in_specs=in_specs,
        out_specs=out_specs,
        out_shape=out_shape,
        scratch_shapes=scratch,
        compiler_params=pltpu.CompilerParams(
            vmem_limit_bytes=VMEM_BYTES, collective_id=ident, has_side_effects=ident is not None
        ),
        cost_estimate=pl.CostEstimate(flops=flops, bytes_accessed=moved, transcendentals=exps),
    )


def whole(shape):
    return pl.BlockSpec(shape, lambda *_: (0,) * len(shape), pipeline_mode=pl.Buffered(1))


def column_third(which, width):
    return pl.BlockSpec((width, width), lambda *_: (0, which), pipeline_mode=pl.Buffered(1))


def row_of(ref, which, width):
    return ref.at[which : which + 1, 0:width]


def smem():
    return pl.BlockSpec(memory_space=pltpu.SMEM)


def time_features(step_ids, feature_count):
    halfway = feature_count // 2
    spacing = jnp.exp(-math.log(10000.0) * jnp.arange(halfway, dtype=F32) / halfway)
    angles = step_ids.astype(F32)[:, None] * spacing[None, :]
    return jax.nn.silu(jnp.concatenate([jnp.cos(angles), jnp.sin(angles)], axis=-1))


def rotary_tables(seq_length):
    halfway = HEAD // 2
    spacing = np.exp(-math.log(10000.0) * np.arange(halfway, dtype=np.float32) / halfway)
    angles = np.arange(seq_length, dtype=np.float32)[:, None] * spacing.astype(np.float32)
    cosine, sine = np.cos(angles), np.sin(angles)
    signed = np.concatenate([-sine, sine] * 2, axis=-1)
    return np.concatenate([cosine] * 4, axis=-1), signed


def partner_lanes(v):
    lane = lax.broadcasted_iota(jnp.int32, (1, PAIR), 1)
    return jnp.where(lax.rem(lane, HEAD) < HEAD // 2, from_ahead(v), from_behind(v))


def from_ahead(v):
    return pltpu.roll(v, PAIR - HEAD // 2, 1)


def from_behind(v):
    return pltpu.roll(v, HEAD // 2, 1)


def masked_rows(tokens, embed, start, length, first_row):
    rows = tokens.shape[0]
    position = lax.broadcasted_iota(jnp.int32, (rows, 1), 0) + first_row
    inside = (position >= start) & (position < start + length)
    return jnp.where(inside, embed, tokens.astype(F32)), inside


def normalized(rows):
    centre = rows - jnp.mean(rows, axis=-1, keepdims=True)
    spread = jnp.mean(centre * centre, axis=-1, keepdims=True)
    inverse = lax.rsqrt(spread + EPSILON)
    return centre * inverse, inverse


def norm_back(d_out, hat, inverse):
    return inverse * (
        d_out
        - jnp.mean(d_out, axis=-1, keepdims=True)
        - hat * jnp.mean(d_out * hat, axis=-1, keepdims=True)
    )


def column_sum(v):
    return jnp.sum(v, axis=0, keepdims=True)


def store_shares(target, value, cols):
    me, ways = lax.axis_index("narrow"), lax.axis_size("narrow")
    share = value.shape[0] // ways
    for place in range(ways):
        lower = pl.multiple_of(place_of(me, place) * share, share)
        target[pl.ds(lower, share), cols] = value[place * share : (place + 1) * share, :]


def place_of(me, other):
    core = lax.rem(me + other, 2)
    chip = lax.rem(me // 2 + other // 2, 2)
    return 2 * (1 - core) + 1 - chip


def owner_at(me, place):
    core, chip = 1 - place // 2, 1 - lax.rem(place, 2)
    return 2 * lax.rem(me // 2 + chip, 2) + lax.rem(me + core, 2)


def project(tokens, starts, lengths, embed, gain, modulation, weight, tables, seqs, block=512):
    rows, width = tokens.shape
    seq_length = rows // seqs
    block = min(block, seq_length)
    per_seq = seq_length // block
    pairs = width // PAIR

    def kernel(starts, lengths, tok, emb, gn, mod, w_q, w_k, w_v, cos, sin, out, nt):
        emb, gn = row_of(emb, EMBED, width), row_of(gn, GAIN_ONE, width)
        step = pl.program_id(0)
        seq = step // per_seq
        first = (step - seq * per_seq) * block
        start, _ = masked_rows(tok[...], emb[...], starts[seq], lengths[seq], first)
        hat, _ = normalized(start)
        shift = mod[pl.ds(seq, 1), 0:width]
        scale = mod[pl.ds(seq, 1), width : 2 * width]
        normed = (hat * (gn[...] * (1.0 + scale)) + shift).astype(BF16)
        store_shares(nt, jnp.transpose(normed), slice(None))
        for which, w in enumerate((w_q, w_k)):
            turned = mxu(normed, w[...])
            for part in range(pairs):
                v = turned[:, part * PAIR : (part + 1) * PAIR]
                v = v * cos[...] + partner_lanes(v) * sin[...]
                lower = which * width + part * PAIR
                out[:, lower : lower + PAIR] = v.astype(BF16)
        out[:, 2 * width :] = mxu(normed, w_v[...]).astype(BF16)

    table = pl.BlockSpec((block, PAIR), lambda i: (lax.rem(i, per_seq), 0))
    return call(
        kernel,
        "project",
        (rows // block,),
        [
            smem(),
            smem(),
            pl.BlockSpec((block, width), lambda i: (i, 0)),
            whole(embed.shape),
            whole(gain.shape),
            whole(modulation.shape),
            column_third(0, width),
            column_third(1, width),
            column_third(2, width),
            table,
            table,
        ],
        (
            pl.BlockSpec((block, 3 * width), lambda i: (i, 0)),
            pl.BlockSpec((width, block), lambda i: (0, i)),
        ),
        (
            jax.ShapeDtypeStruct((rows, 3 * width), BF16),
            jax.ShapeDtypeStruct((width, rows), BF16),
        ),
        [],
        2 * rows * width * 3 * width,
        rows * width * 10 + 6 * width * width,
    )(starts, lengths, tokens, embed, gain, modulation, weight, weight, weight, *tables)


def flip(index, stride):
    return index + stride * (1 - 2 * lax.rem(index // stride, 2))


def exchange_stages():
    count = lax.axis_size("wide")
    strides = [1 << bit for bit in range(1, count.bit_length() - 1)]
    return [("pair", "narrow", 1), ("chip", "narrow", 2), ("split", "wide", 1)] + [
        ("full", "wide", stride) for stride in strides
    ] + [("join", "wide", 1)]


class Steps:
    def in_specs(self):
        return [pl.BlockSpec(memory_space=pl.ANY)] * self.count

    out_specs = in_specs

    def locate(self):
        self.at = {axis: lax.axis_index(axis) for axis in ("wide", "narrow")}
        self.odd = lax.rem(self.at["wide"], 2)

    def half_of(self, rows, which, lower=0):
        side = self.odd if which == 0 else 1 - self.odd
        return pl.ds(pl.multiple_of(lower + side * (rows // 2), rows // 2), rows // 2)

    def greet(self):
        barrier = pltpu.get_barrier_semaphore()
        for axis, stride in self.partners:
            pl.semaphore_signal(
                barrier,
                inc=1,
                device_id={axis: flip(self.at[axis], stride)},
                device_id_type=pl.DeviceIdType.MESH,
            )
        pl.semaphore_wait(barrier, len(self.partners))

    def push(self, source, target, sent, got, axis, stride):
        return pltpu.make_async_remote_copy(
            src_ref=source,
            dst_ref=target,
            send_sem=sent,
            recv_sem=got,
            device_id={axis: flip(self.at[axis], stride)},
            device_id_type=pl.DeviceIdType.MESH,
        )

    def tick(self, now, last, bunch=6):
        planned = sorted(self.plan(), key=lambda item: item[:3])
        times = sorted({item[0] for item in planned if item[0] < last})
        for lower in sorted({when - when % bunch for when in times}):

            @pl.when((now >= lower) & (now < lower + bunch))
            def _(lower=lower):
                for when in times:
                    if lower <= when < lower + bunch:
                        pl.when(now == when)(lambda when=when: self.take(planned, when))

    def take(self, planned, when):
        if when == 0:
            self.greet()
        for item in planned:
            if item[0] == when:
                item[3]()

    def rest(self, last):
        for item in sorted(self.plan(), key=lambda item: item[:3]):
            if item[0] >= last:
                item[3]()


class Gather(Steps):
    partners = (("narrow", 1), ("narrow", 2), ("wide", 1))

    def __init__(self, shapes, begins, waits, columns=None, sideways=()):
        columns = columns or [(k, 0, shape[1]) for k, shape in enumerate(shapes)]
        self.arrays, self.columns = shapes, columns
        self.shapes = [(shapes[k][0], upper - lower) for k, lower, upper in columns]
        self.begins, self.waits = begins, waits
        self.count = len(columns)
        self.sideways = sideways

    def in_specs(self):
        return [pl.BlockSpec(memory_space=pl.ANY)] * len(self.arrays)

    out_specs = in_specs

    def out_shape(self):
        return [
            jax.ShapeDtypeStruct((rows, 4 * cols) if k in self.sideways else (4 * rows, cols), BF16)
            for k, (rows, cols) in enumerate(self.arrays)
        ]

    def scratch(self):
        dma, held = pltpu.SemaphoreType.DMA, []
        for shape in self.shapes:
            held += [dma((5,)), dma((5,)), dma((2,)), pltpu.VMEM(shape, BF16)]
        return held

    def bind(self, ins, outs, held):
        self.refs = [
            (
                ins[k].at[:, lower:upper],
                outs[k] if k in self.sideways else outs[k].at[:, lower:upper],
            )
            + tuple(held[4 * part : 4 * part + 4])
            for part, (k, lower, upper) in enumerate(self.columns)
        ]
        self.locate()

    def block(self, k, index, which=None):
        rows, cols = self.shapes[k]
        if self.columns[k][0] in self.sideways:
            down = slice(None) if which is None else self.half_of(rows, which)
            return down, pl.ds(pl.multiple_of(index * cols, cols), cols)
        if which is None:
            return pl.ds(pl.multiple_of(index * rows, rows), rows), slice(None)
        return self.half_of(rows, which, index * rows), slice(None)

    def remote(self, k, step):
        source, out, sent, got, _, _ = self.refs[k]
        me, across = self.at["narrow"], flip(self.at["narrow"], 2)
        axis, stride = (("narrow", 1), ("narrow", 2), ("wide", 1), ("narrow", 1), ("narrow", 1))[step]
        if step == 0:
            ends = (source, out.at[self.block(k, me)])
        elif step == 1:
            half = self.half_of(self.shapes[k][0], 0)
            ends = (source.at[half, :], out.at[self.block(k, me, 0)])
        else:
            spot = self.block(k, across, 1 if step == 4 else 0)
            ends = (out.at[spot], out.at[spot])
        return self.push(*ends, sent.at[step], got.at[step], axis, stride)

    def local(self, k, which):
        source, out, _, _, near, kept = self.refs[k]
        if which == 0:
            return pltpu.make_async_copy(source, kept, near.at[0])
        return pltpu.make_async_copy(
            kept, out.at[self.block(k, self.at["narrow"])], near.at[1]
        )

    def begin(self, k):
        self.remote(k, 1).start()
        self.remote(k, 0).start()
        self.local(k, 0).start()

    def relay(self, k):
        self.local(k, 0).wait()
        self.local(k, 1).start()
        self.remote(k, 1).wait()
        self.remote(k, 2).start()
        self.remote(k, 3).start()

    def share(self, k):
        self.remote(k, 2).wait()
        self.remote(k, 4).start()

    def close(self, k):
        self.remote(k, 0).wait()
        self.remote(k, 3).wait()
        self.remote(k, 4).wait()
        self.local(k, 1).wait()

    def plan(self):
        planned = []
        for k in range(self.count):
            when = self.begins[k]
            planned.append((when, 0, k, lambda k=k: self.begin(k)))
            for wait, act in zip(self.waits, (self.relay, self.share, self.close)):
                when += wait
                planned.append((when, 1, k, lambda k=k, act=act: act(k)))
        return planned


class Exchange(Steps):
    def __init__(self, shapes, times, columns=None, spans=None, near=()):
        columns = columns or [(k, 0, shape[-1]) for k, shape in enumerate(shapes)]
        spans = spans or ["whole"] * len(shapes)
        self.stages = exchange_stages()
        self.arrays, self.columns = [shape[-2:] for shape in shapes], columns
        self.shapes = [(self.arrays[k][0], upper - lower) for k, lower, upper in columns]
        self.spans = [spans[k] for k, _, _ in columns]
        self.near = [k in near for k, _, _ in columns]
        self.firsts = [2 if span == "tail" else 0 for span in self.spans]
        self.lasts = [1 if span == "head" else len(self.stages) - 1 for span in self.spans]
        self.times = times
        self.count = len(columns)
        self.partners = sorted({(axis, stride) for _, axis, stride in self.stages})

    def in_specs(self):
        return [pl.BlockSpec(memory_space=pl.ANY)] * len(self.arrays)

    out_specs = in_specs

    def out_shape(self):
        return [jax.ShapeDtypeStruct(shape, BF16) for shape in self.arrays]

    def scratch(self):
        held = []
        dma = pltpu.SemaphoreType.DMA
        for (rows, cols), span, near in zip(self.shapes, self.spans, self.near):
            early, late = span != "tail", span != "head"
            held += [
                pltpu.VMEM((2, rows, cols) if early else (2, 16, PAIR), BF16),
                pltpu.VMEM((2, 16, PAIR) if near else (2 if early else 1, rows, cols), BF16),
                pltpu.VMEM((rows, cols) if early else (16, PAIR), BF16),
                pltpu.VMEM((len(self.stages) - 3, rows // 2, cols) if late else (1, 16, PAIR), BF16),
                pltpu.VMEM((rows // 2, cols) if late else (16, PAIR), BF16),
                dma((len(self.stages),)),
                dma((len(self.stages),)),
                dma((2,)),
            ]
        return held

    def bind(self, ins, outs, held):
        self.refs = []
        for part, (k, lower, upper) in enumerate(self.columns):
            every = (slice(None),) * (1 if self.spans[part] == "tail" else 2)
            source, own = ins[k].at[every + (slice(lower, upper),)], held[8 * part : 8 * part + 8]
            if self.near[part]:
                own = [own[0], source.at[2:4]] + list(own[2:])
            self.refs.append((source, outs[k].at[:, lower:upper], *own))
        self.locate()

    def own(self, k):
        kept = self.refs[k][3]
        return kept.at[0 if self.spans[k] == "tail" else 1]

    def remote(self, k, step):
        source, out, pair, kept, chip, halves, mine, sent, got, _ = self.refs[k]
        kind, axis, stride = self.stages[step]
        rows = self.shapes[k][0]
        if kind == "pair":
            ends = (source.at[0:2], pair)
        elif kind == "chip":
            ends = (kept.at[0], chip)
        elif kind == "split":
            ends = (self.own(k).at[self.half_of(rows, 1), :], halves.at[0])
        elif kind == "full":
            ends = (mine, halves.at[step - 2])
        else:
            ends = (mine, out.at[self.half_of(rows, 0), :])
        return self.push(*ends, sent.at[step], got.at[step], axis, stride)

    def load(self, k):
        source, kept, near = self.refs[k][0], self.refs[k][3], self.refs[k][9]
        if self.spans[k] == "tail":
            return pltpu.make_async_copy(source, kept.at[0], near.at[0])
        return pltpu.make_async_copy(source.at[2:4], kept, near.at[0])

    def store(self, k):
        out, mine, near = self.refs[k][1], self.refs[k][6], self.refs[k][9]
        if self.spans[k] == "head":
            return pltpu.make_async_copy(self.own(k), out, near.at[1])
        half = self.half_of(self.shapes[k][0], 0)
        return pltpu.make_async_copy(mine, out.at[half, :], near.at[1])

    def begin(self, k):
        if not self.near[k]:
            self.load(k).start()
        if self.spans[k] != "tail":
            self.remote(k, 0).start()

    def enter(self, k):
        self.load(k).wait()
        self.remote(k, 2).start()

    def end(self, k, step):
        _, _, pair, kept, chip, halves, mine, _, _, _ = self.refs[k]
        kind = self.stages[step][0]
        self.remote(k, step).wait()
        if kind == "pair":
            if not self.near[k]:
                self.load(k).wait()
            kept[...] = kept[...] + pair[...]
        elif kind == "chip":
            kept[1] = kept[1] + chip[...]
        elif kind == "split":
            half = self.half_of(self.shapes[k][0], 0)
            mine[...] = self.own(k)[half, :] + halves[0]
        elif kind == "full":
            mine[...] = mine[...] + halves[step - 2]
        if step < self.lasts[k]:
            self.remote(k, step + 1).start()
        if step == max(self.lasts[k] - 1, 1):
            self.store(k).start()
        if step == self.lasts[k]:
            self.store(k).wait()

    def plan(self):
        planned = []
        for k, (begin, *ends) in enumerate(self.times):
            first, last = self.firsts[k], self.lasts[k]
            planned.append((begin, 0, k, lambda k=k: self.begin(k)))
            if first:
                planned.append((ends[0], 1, k, lambda k=k: self.enter(k)))
                ends = [0] + ends
            for step in range(first, last + 1):
                when = ends[-1] if step == last else ends[min(step, 4)]
                planned.append((when, 1, k, lambda k=k, step=step: self.end(k, step)))
        return planned


def paced(begins, waits):
    return [[begin + sum(waits[:count]) for count in range(len(waits) + 1)] for begin in begins]


def head_mask(v, half):
    lane = lax.broadcasted_iota(jnp.int32, (1, PAIR), 1)
    keep = (lane < HEAD) if half == 0 else (lane >= HEAD)
    return jnp.where(keep, v, jnp.zeros_like(v))


def attend(qkv, shares, begins, waits, columns, ident, seqs, block=512, per=3):
    rows, width = qkv.shape[0], qkv.shape[1] // 3
    seq_length = rows // seqs
    block = min(block, seq_length)
    pairs = width // PAIR
    count = seq_length // block
    steps = pairs // per
    items = per * count
    wide = per * PAIR

    gathering = Gather([v.shape for v in shares], begins, waits, columns)
    many = len(shares)
    ticks = seqs * steps * items

    def kernel(*refs):
        q_ref, k_ref, v_ref = refs[:3]
        out, total = refs[3 + many : 5 + many]
        v_turned, out_turned, held = refs[5 + 2 * many : 8 + 2 * many]
        gathering.bind(refs[3 : 3 + many], refs[5 + many : 5 + 2 * many], refs[8 + 2 * many :])
        spot = pl.program_id(0) * steps + pl.program_id(1)
        v_turned[...] = jnp.transpose(v_ref[...])

        def place(i):
            pair = i // count
            part = i - pair * count
            return (
                pair,
                pl.ds(pl.multiple_of(pair * PAIR, PAIR), PAIR),
                pl.ds(pl.multiple_of(part * block, block), block),
            )

        def score(i, half):
            _, cols, part = place(i)
            held[half] = mxu(k_ref[:, cols], head_mask(q_ref[part, cols], half), TRANSPOSED)

        def finish(i, half):
            pair, _, part = place(i)
            scores = held[half]
            top = jnp.max(scores, axis=0, keepdims=True)
            exponent = jnp.exp2(scores * SCALE2 - top * SCALE2).astype(BF16)
            head = pl.ds(pl.multiple_of(pair * PAIR + half * HEAD, HEAD), HEAD)
            left = jnp.concatenate([v_turned[head, :], jnp.ones((16, seq_length), BF16)], axis=0)
            mixed = mxu(left, exponent)
            denominator = mixed[HEAD : HEAD + 1]
            out_turned[head, part] = mixed[:HEAD] * (1.0 / denominator)
            total[0, pair, half : half + 1, part] = top * SCALE2 + jnp.log2(denominator)

        score(0, 0)

        def body(i, carry):
            gathering.tick(spot * items + i, ticks)
            score(i, 1)
            finish(i, 0)
            score(jnp.minimum(i + 1, items - 1), 0)
            finish(i, 1)
            return carry

        lax.fori_loop(0, items, body, 0)
        out[...] = jnp.transpose(out_turned[...]).astype(BF16)

        @pl.when(spot == seqs * steps - 1)
        def _():
            gathering.rest(ticks)

    def part_of(which):
        return pl.BlockSpec((seq_length, wide), lambda s, p: (s, which * steps + p))

    return call(
        kernel,
        "attend",
        (seqs, steps),
        [part_of(0), part_of(1), part_of(2)] + gathering.in_specs(),
        [part_of(0), pl.BlockSpec((1, per, 2, seq_length), lambda s, p: (s, p, 0, 0))]
        + gathering.out_specs(),
        [
            jax.ShapeDtypeStruct((rows, width), BF16),
            jax.ShapeDtypeStruct((seqs, pairs, 2, seq_length), F32),
        ]
        + gathering.out_shape(),
        [
            pltpu.VMEM((wide, seq_length), BF16),
            pltpu.VMEM((wide, seq_length), F32),
            pltpu.VMEM((2, seq_length, block), F32),
        ]
        + gathering.scratch(),
        16 * rows * seq_length * width,
        rows * width * 8,
        rows * seq_length * width // HEAD,
        ident,
    )(qkv, qkv, qkv, *shares)


def attend_back(
    qkv, mixture, d_mixture, total, tables, turned, pieces, spans, columns, times, ident, seqs,
    block=512, per=3,
):
    rows, width = mixture.shape
    seq_length = rows // seqs
    block = min(block, seq_length)
    pairs = width // PAIR
    count = seq_length // block
    steps = pairs // per
    items = per * count
    wide = per * PAIR
    ways = lax.axis_size("narrow")
    share = width // ways
    own = [jax.ShapeDtypeStruct((ways, share, wide), BF16)] * 3
    traded = list(pieces) + own
    exchange = Exchange(
        [v.shape for v in traded],
        times,
        list(columns) + [(len(pieces) + part, 0, wide) for part in range(3)],
        list(spans) + ["whole"] * 3,
        [len(pieces) + part for part in range(3)],
    )
    many, outs = len(pieces), len(traded)
    assert steps == 2
    ticks = seqs * steps * items

    def kernel(*refs):
        q_ref, k_ref, v_ref, mix, grad, tot, cos, sin, turned_all = refs[:9]
        lower = 9 + many
        dq, dk, dv = refs[lower : lower + 3]
        out_refs, lower = refs[lower + 3 : lower + 3 + outs], lower + 3 + outs
        k_turned, dq_turned, dk_sum, dv_sum, inner, s_held, p_held = refs[lower : lower + 7]
        left, d_held, grads, near = refs[lower + 7 : lower + 11]
        exchange.bind(
            list(refs[9 : 9 + many]) + [grads.at[part] for part in range(3)],
            out_refs,
            refs[lower + 11 :],
        )
        seq = pl.program_id(1)
        spot = pl.program_id(0) * seqs + seq
        load = pltpu.make_async_copy(turned_all, left, near.at[0])
        pl.when(spot == 0)(load.start)

        @pl.when(spot == seqs)
        def _():
            load.wait()
            for part in range(3):
                product = mxu(left[...], d_held[part]).astype(BF16)
                grads[part] = product.reshape(ways, share, wide)

        k_turned[...] = jnp.transpose(k_ref[...])
        product = jnp.transpose(mix[...].astype(F32) * grad[...].astype(F32))
        for pair in range(per):
            for half in range(2):
                lower = pair * PAIR + half * HEAD
                inner[pair, half : half + 1, :] = column_sum(product[lower : lower + HEAD, :])
        dk_sum[...] = jnp.zeros_like(dk_sum)
        dv_sum[...] = jnp.zeros_like(dv_sum)

        def body(i, carry):
            exchange.tick(spot * items + i, ticks)
            pair = i // count
            part = i - pair * count
            cols = pl.ds(pl.multiple_of(pair * PAIR, PAIR), PAIR)
            part = pl.ds(pl.multiple_of(part * block, block), block)
            for half in range(2):
                head = pl.ds(pl.multiple_of(pair * PAIR + half * HEAD, HEAD), HEAD)
                query = head_mask(q_ref[part, cols], half)
                cot = head_mask(grad[part, cols], half)
                s_held[half] = mxu(k_ref[:, cols], query, TRANSPOSED)
                p_held[half] = mxu(v_ref[:, cols], cot, TRANSPOSED)
                probs = jnp.exp2(s_held[half] * SCALE2 - tot[0, pair, half : half + 1, part])
                d_scores = (probs * (p_held[half] - inner[pair, half : half + 1, part])).astype(BF16)
                dv_sum[:, cols] += mxu(probs.astype(BF16), cot)
                dk_sum[:, cols] += mxu(d_scores, query)
                dq_turned[head, part] = mxu(k_turned[head, :], d_scores)
            return carry

        lax.fori_loop(0, items, body, 0)
        d_queries = jnp.transpose(dq_turned[...])
        for source, target in ((d_queries, dq), (dk_sum, dk)):
            for pair in range(per):
                v = source[:, pair * PAIR : (pair + 1) * PAIR] * SCALE
                v = v * cos[...] - partner_lanes(v) * sin[...]
                target[:, pair * PAIR : (pair + 1) * PAIR] = v.astype(BF16)
        dv[...] = dv_sum[...].astype(BF16)

        @pl.when(spot < seqs)
        def _():
            here = pl.ds(pl.multiple_of(seq * seq_length, seq_length), seq_length)
            for part, target in enumerate((dq, dk, dv)):
                d_held[part, here, :] = target[...]

        @pl.when(spot == seqs * steps - 1)
        def _():
            exchange.rest(ticks)

    def part_of(which):
        return pl.BlockSpec((seq_length, wide), lambda p, s: (s, which * steps + p))

    table = whole((seq_length, PAIR))
    grads = jax.ShapeDtypeStruct((rows, width), BF16)
    return call(
        kernel,
        "attend_back",
        (steps, seqs),
        [part_of(0), part_of(1), part_of(2), part_of(0), part_of(0)]
        + [pl.BlockSpec((1, per, 2, seq_length), lambda p, s: (s, p, 0, 0))]
        + [table] * 2
        + [pl.BlockSpec(memory_space=pl.ANY)] * (1 + many),
        [part_of(0), part_of(0), part_of(0)] + exchange.out_specs(),
        [grads, grads, grads] + exchange.out_shape(),
        [
            pltpu.VMEM((wide, seq_length), BF16),
            pltpu.VMEM((wide, seq_length), F32),
            pltpu.VMEM((seq_length, wide), F32),
            pltpu.VMEM((seq_length, wide), F32),
            pltpu.VMEM((per, 2, seq_length), F32),
            pltpu.VMEM((2, seq_length, block), F32),
            pltpu.VMEM((2, seq_length, block), F32),
            pltpu.VMEM(turned.shape, BF16),
            pltpu.VMEM((3, rows, wide), BF16),
            pltpu.VMEM((3, ways, share, wide), BF16),
            pltpu.SemaphoreType.DMA((1,)),
        ]
        + exchange.scratch(),
        40 * rows * seq_length * width,
        rows * width * 16,
        rows * seq_length * width // HEAD,
        ident,
    )(qkv, qkv, qkv, mixture, d_mixture, total, *tables, turned, *pieces)


def gelu_pair(v):
    root = math.sqrt(2.0 / math.pi)
    square = v * v
    near = 0.5 + 0.5 * jnp.tanh(v * (root + (root * 0.044715) * square))
    active = v * near
    bend = 2.0 * root + (6.0 * root * 0.044715) * square
    return active, near + (active * (1.0 - near)) * bend


def grouped_rows(ref, ways):
    part = ref.shape[0] // (ways * GROUPS)
    lowers = [(way * GROUPS + group) * part for group in range(GROUPS) for way in range(ways)]
    return jnp.concatenate([ref[lower : lower + part, :] for lower in lowers], axis=0)


def grouped_columns(ref, ways):
    part = ref.shape[1] // (ways * GROUPS)
    lowers = [(way * GROUPS + group) * part for group in range(GROUPS) for way in range(ways)]
    return jnp.concatenate([ref[:, lower : lower + part] for lower in lowers], axis=1)


def halved(arrays):
    return [
        (k, half * v.shape[-1] // 2, (half + 1) * v.shape[-1] // 2)
        for k, v in enumerate(arrays)
        for half in range(2)
    ]


def hidden_units(
    mixture, tokens, cot, starts, lengths, embed, gain, modulation, out_weight, up, up_bias, down,
    times, ident, seqs, block=512,
):
    rows, width = tokens.shape
    ways = lax.axis_size("narrow")
    units = up.shape[1] // GROUPS
    share, part_units = width // ways, units // ways
    seq_length = rows // seqs
    block = min(block, seq_length)
    per_seq = seq_length // block
    steps = rows // block
    turn = steps + ways
    shape_up, shape_down = (ways, share, units), (ways, part_units, width)
    traded = [jax.ShapeDtypeStruct(v, BF16) for v in (shape_up, shape_down) * 2]
    exchange = Exchange(
        [v.shape for v in traded], times, halved(traded), ["whole"] * 2 + ["head"] * 2, range(4)
    )

    def kernel(*refs):
        starts, lengths, mix, tok, emb, gn, w_out, g, mod, b_up = refs[:10]
        emb, gn = row_of(emb, EMBED, width), row_of(gn, GAIN_TWO, width)
        w_ups, w_downs = refs[10 : 10 + ways], refs[10 + ways : 10 + 2 * ways]
        act, d_up, g_bias, d_gate, g_sum = refs[10 + 2 * ways : 15 + 2 * ways]
        outs, left = refs[15 + 2 * ways : 21 + 2 * ways], refs[21 + 2 * ways :]
        n_turned, g_turned, a_held, u_held, down_held, g_up, g_down, near, n_held = left[:9]
        exchange.bind(
            [g_up.at[0], g_down.at[0], g_up.at[1], g_down.at[1]], outs[:4], left[9:]
        )
        step = pl.program_id(0)
        group = step // turn
        at = step - group * turn

        @pl.when(step == 0)
        def _():
            exchange.greet()
            n_turned[width:, :] = jnp.ones((16, rows), BF16)
            d_gate[...] = jnp.zeros_like(d_gate)
            g_sum[...] = jnp.zeros_like(g_sum)

        exchange.tick(step, GROUPS * turn)

        @pl.when(at == 0)
        def _():
            for way in range(ways):
                down_held[way] = w_downs[way][...]

        part = pl.ds(pl.multiple_of(jnp.minimum(at, steps - 1) * block, block), block)

        @pl.when(step < steps)
        def _():
            seq = at // per_seq
            first = (at - seq * per_seq) * block
            start, _ = masked_rows(tok[...], emb[...], starts[seq], lengths[seq], first)
            gate = mod[pl.ds(seq, 1), 2 * width : 3 * width]
            hat, _ = normalized(start + gate * mxu(mix[...], w_out[...]))
            shift = mod[pl.ds(seq, 1), 3 * width : 4 * width]
            scale = mod[pl.ds(seq, 1), 4 * width : 5 * width]
            normed = (hat * (gn[...] * (1.0 + scale)) + shift).astype(BF16)
            n_held[part, :] = normed
            store_shares(n_turned, jnp.transpose(normed), part)
            g_turned[:, part] = jnp.transpose(g[...])
            g_sum[pl.ds(seq, 1), :] += column_sum(g[...].astype(F32))

        @pl.when(at < steps)
        def _():
            seq = at // per_seq
            nrm = n_held[part, :]
            cotangent = g[...].astype(F32)
            d_branch = (mod[pl.ds(seq, 1), 5 * width : 6 * width] * cotangent).astype(BF16)
            for way in range(ways):
                cols = slice(way * part_units, (way + 1) * part_units)
                upper = mxu(nrm, w_ups[way][...]) + b_up[pl.ds(BIAS_UP + group, 1), cols]
                d_active = mxu(d_branch, w_downs[way][...], TRANSPOSED)
                active, slope = gelu_pair(upper)
                active = active.astype(BF16)
                d_upper = (d_active * slope).astype(BF16)
                act[:, cols] = active
                a_held[part, cols] = active
                d_up[:, cols] = d_upper
                u_held[part, cols] = d_upper

        @pl.when(at >= steps)
        def _():
            place = at - steps
            owner = owner_at(exchange.at["narrow"], place)
            cols = pl.ds(pl.multiple_of(owner * part_units, part_units), part_units)
            product = mxu(n_turned[...], u_held[:, cols])
            g_bias[:, cols] = product[width : width + 1]
            g_up[group, :, :, cols] = product[:width].astype(BF16).reshape(
                ways, share, part_units
            )
            own = down_held[owner].astype(F32)
            total = jnp.zeros((part_units, width), F32)
            for seq in range(seqs):
                lower, upper = seq * seq_length, (seq + 1) * seq_length
                product = mxu(g_turned[:, lower:upper], a_held[lower:upper, cols])
                product = jnp.transpose(product)
                total += product * mod[seq : seq + 1, 5 * width : 6 * width]
                d_gate[seq : seq + 1, :] += column_sum(product * own)
            g_down[group, place] = total.astype(BF16)

        @pl.when(step == GROUPS * turn - 1)
        def _():
            copies = [
                pltpu.make_async_copy(source.at[GROUPS - 1], target, near.at[k])
                for k, (source, target) in enumerate(((g_up, outs[4]), (g_down, outs[5])))
            ]
            for copy in copies:
                copy.start()
            exchange.rest(GROUPS * turn)
            for copy in copies:
                copy.wait()

    def early(i):
        return (jnp.minimum(lax.rem(i, turn), steps - 1), 0)

    def once(i):
        return (jnp.minimum(i, steps - 1), 0)

    def fixed(shape):
        return pl.BlockSpec(shape, lambda i: (0,) * len(shape))

    by_rows = pl.BlockSpec(
        (block, units), lambda i: (jnp.minimum(lax.rem(i, turn), steps - 1), i // turn)
    )
    by_group = pl.BlockSpec((1, units), lambda i: (0, i // turn))

    def up_piece(way):
        return pl.BlockSpec((width, part_units), lambda i: (0, way * GROUPS + i // turn))

    def down_piece(way):
        return pl.BlockSpec((part_units, width), lambda i: (way * GROUPS + i // turn, 0))

    assert GROUPS == 3
    anywhere = pl.BlockSpec(memory_space=pl.ANY)
    return call(
        kernel,
        "hidden_units",
        (GROUPS * turn,),
        [smem(), smem()]
        + [pl.BlockSpec((block, width), once)] * 2
        + [whole(embed.shape), whole(gain.shape), whole(out_weight.shape)]
        + [pl.BlockSpec((block, width), early)]
        + [whole(modulation.shape), whole(up_bias.shape)]
        + [up_piece(way) for way in range(ways)]
        + [down_piece(way) for way in range(ways)],
        [by_rows, by_rows, by_group, fixed((seqs, width)), fixed((seqs, width))]
        + exchange.out_specs()
        + [anywhere] * 2,
        [
            jax.ShapeDtypeStruct((rows, units * GROUPS), BF16),
            jax.ShapeDtypeStruct((rows, units * GROUPS), BF16),
            jax.ShapeDtypeStruct((1, units * GROUPS), F32),
            jax.ShapeDtypeStruct((seqs, width), F32),
            jax.ShapeDtypeStruct((seqs, width), F32),
        ]
        + exchange.out_shape()
        + [jax.ShapeDtypeStruct(shape_up, BF16), jax.ShapeDtypeStruct(shape_down, BF16)],
        [
            pltpu.VMEM((width + 16, rows), BF16),
            pltpu.VMEM((width, rows), BF16),
            pltpu.VMEM((rows, units), BF16),
            pltpu.VMEM((rows, units), BF16),
            pltpu.VMEM((ways, part_units, width), BF16),
            pltpu.VMEM((GROUPS,) + shape_up, BF16),
            pltpu.VMEM((GROUPS,) + shape_down, BF16),
            pltpu.SemaphoreType.DMA((2,)),
            pltpu.VMEM((rows, width), BF16),
        ]
        + exchange.scratch(),
        8 * rows * width * units * GROUPS,
        GROUPS * (rows * (width * 4 + units * 4) + 8 * width * units),
        rows * units * GROUPS,
        ident,
    )(
        starts, lengths, mixture, tokens, embed, gain, out_weight, cot, modulation, up_bias,
        *[up] * ways, *[down] * ways,
    )


def middle_back(
    mixture, tokens, cot, starts, lengths, embed, gain, modulation, out_weight, d_upper, up, seqs,
    block=256,
):
    rows, width = tokens.shape
    ways = lax.axis_size("narrow")
    seq_length = rows // seqs
    block = min(block, seq_length)
    per_seq = seq_length // block
    steps = rows // block
    hidden_width = d_upper.shape[1]
    share = width // ways

    def kernel(
        starts, lengths, mix, tok, g, emb, gn, mod, w_out, w_up, d_ups, d_middle_out, d_mix, g_out,
        sums, g_sum,
    ):
        emb, gn = row_of(emb, EMBED, width), row_of(gn, GAIN_TWO, width)
        step = pl.program_id(0)
        seq = step // per_seq
        first = (step - seq * per_seq) * block

        @pl.when(step == 0)
        def _():
            g_sum[...] = jnp.zeros_like(g_sum)

        @pl.when(step == seq * per_seq)
        def _():
            sums[...] = jnp.zeros_like(sums)

        def vector(which):
            return mod[pl.ds(seq, 1), which * width : (which + 1) * width]

        attended = mxu(mix[...], w_out[...])
        start, _ = masked_rows(tok[...], emb[...], starts[seq], lengths[seq], first)
        hat, inverse = normalized(start + vector(2) * attended)
        d_normed = mxu(d_ups[...], grouped_columns(w_up, ways), TRANSPOSED)
        d_middle = g[...].astype(F32) + norm_back(
            d_normed * (gn[...] * (1.0 + vector(4))), hat, inverse
        )
        d_middle_out[...] = d_middle
        d_attended = (vector(2) * d_middle).astype(BF16)
        d_mix[...] = mxu(d_attended, w_out[...], TRANSPOSED).astype(BF16)
        g_sum[...] += mxu(jnp.transpose(mix[...]), d_attended)
        sums[0, 0:1, :] += column_sum(d_normed)
        sums[0, 1:2, :] += column_sum(d_normed * hat)
        sums[0, 2:3, :] += column_sum(d_middle * attended)

        @pl.when(step == steps - 1)
        def _():
            for place in range(ways):
                owner = owner_at(lax.axis_index("narrow"), place)
                spot = pl.ds(pl.multiple_of(owner * share, share), share)
                g_out[place] = g_sum[spot, :].astype(BF16)

    row = pl.BlockSpec((block, width), lambda i: (i, 0))
    return call(
        kernel,
        "middle_back",
        (steps,),
        [smem(), smem(), row, row, row, whole(embed.shape), whole(gain.shape)]
        + [whole(modulation.shape), whole(out_weight.shape), whole(up.shape)]
        + [pl.BlockSpec((block, hidden_width), lambda i: (i, 0))],
        (
            row,
            row,
            pl.BlockSpec((ways, share, width), lambda i: (0, 0, 0)),
            pl.BlockSpec((1, 8, width), lambda i: (i // per_seq, 0, 0)),
        ),
        (
            jax.ShapeDtypeStruct((rows, width), F32),
            jax.ShapeDtypeStruct((rows, width), BF16),
            jax.ShapeDtypeStruct((ways, share, width), BF16),
            jax.ShapeDtypeStruct((seqs, 8, width), F32),
        ),
        [pltpu.VMEM((width, width), F32)],
        rows * width * (2 * hidden_width + 6 * width),
        rows * (width * 12 + hidden_width * 2) + 2 * width * hidden_width,
    )(
        starts, lengths, mixture, tokens, cot, embed, gain, modulation, out_weight, up, d_upper,
    )


class Finale(Steps):
    def __init__(self, ways):
        self.ways = ways
        self.wide = lax.axis_size("wide")

    def scratch(self, columns):
        dma = pltpu.SemaphoreType.DMA
        return [
            pltpu.VMEM((self.ways, 8, columns), F32),
            pltpu.VMEM((self.ways, 8, columns), F32),
            pltpu.VMEM((self.wide, 8, columns), F32),
            dma((self.ways,)),
            dma((self.ways,)),
            dma((self.wide,)),
            dma((self.wide,)),
        ]

    def bind(self, held):
        self.parts, self.narrow_got, self.wide_got, *self.sems = held
        self.locate()

    def others(self):
        targets = []
        for offset in range(1, self.ways):
            targets.append({"narrow": lax.rem(self.at["narrow"] + offset, self.ways)})
        for offset in range(1, self.wide):
            targets.append({"wide": lax.rem(self.at["wide"] + offset, self.wide)})
        return targets

    def greet(self):
        barrier = pltpu.get_barrier_semaphore()
        targets = self.others()
        for target in targets:
            pl.semaphore_signal(
                barrier, inc=1, device_id=target, device_id_type=pl.DeviceIdType.MESH
            )
        pl.semaphore_wait(barrier, len(targets))

    def along_narrow(self, offset):
        target = lax.rem(self.at["narrow"] + offset, self.ways)
        return pltpu.make_async_remote_copy(
            src_ref=self.parts.at[target],
            dst_ref=self.narrow_got.at[self.at["narrow"]],
            send_sem=self.sems[0].at[offset],
            recv_sem=self.sems[1].at[offset],
            device_id={"narrow": target},
            device_id_type=pl.DeviceIdType.MESH,
        )

    def along_wide(self, offset):
        me = self.at["wide"]
        return pltpu.make_async_remote_copy(
            src_ref=self.wide_got.at[me],
            dst_ref=self.wide_got.at[me],
            send_sem=self.sems[2].at[offset],
            recv_sem=self.sems[3].at[offset],
            device_id={"wide": lax.rem(me + offset, self.wide)},
            device_id_type=pl.DeviceIdType.MESH,
        )

    def begin(self):
        for offset in range(1, self.ways):
            self.along_narrow(offset).start()
        me = self.at["narrow"]
        self.narrow_got[pl.ds(me, 1)] = self.parts[pl.ds(me, 1)]

    def spread(self, seqs, row_lanes):
        for offset in range(1, self.ways):
            self.along_narrow(offset).wait()
        me = self.at["wide"]
        for way in range(self.ways):
            self.wide_got[pl.ds(me, 1), way * seqs : (way + 1) * seqs, 0:row_lanes] = (
                self.narrow_got[way : way + 1, 0:seqs, 0:row_lanes]
            )
        total = self.narrow_got[0:1, :, row_lanes:]
        for way in range(1, self.ways):
            total += self.narrow_got[way : way + 1, :, row_lanes:]
        self.wide_got[pl.ds(me, 1), :, row_lanes:] = total
        for offset in range(1, self.wide):
            self.along_wide(offset).start()

    def close(self):
        for offset in range(1, self.wide):
            self.along_wide(offset).wait()


def finish(
    turned, d_parts, tokens, d_middle, mixture, starts, lengths, embed, gain, modulation, weight,
    out_weight, down_bias, active, down, features, rows_two, vectors_two, times, ident, seqs,
    wide=384, block=512, late_block=256,
):
    rows, width = tokens.shape
    ways = lax.axis_size("narrow")
    share = width // ways
    seq_length = rows // seqs
    block, late_block = min(block, seq_length), min(late_block, seq_length)
    per_seq, late_per_seq = seq_length // block, seq_length // late_block
    columns, hidden_width = modulation.shape[1] // ways, active.shape[1]
    time_width = features.shape[1]
    window = 2 * PAIR
    lanes = columns + time_width + window
    early, middle, late = 3, rows // block, rows // late_block
    steps = early + middle + late
    exchange = Exchange([(ways, share, wide)] * 3, times, near=range(3))
    finale = Finale(ways)

    def kernel(*refs):
        (
            starts, lengths, left, q_all, k_all, v_all, tok, d_mid, emb, gn, mod, w_qkv_all,
            tok_late, mix, w_out_all, b_down, feat, two, vec, act, w_down_all,
        ) = refs[:21]
        emb, gn = row_of(emb, EMBED, width), row_of(gn, GAIN_ONE, width)
        b_down = row_of(b_down, BIAS_DOWN, width)
        spot = 21
        g_tok, block_out, g_ada, g_ada_bias, g_vec = refs[spot : spot + 5]
        outs = refs[spot + 5 : spot + 8]
        grads, sums = refs[spot + 8 : spot + 10]
        d_held, w_qkv, w_out, w_down, near = refs[spot + 10 : spot + 15]
        small = spot + 15 + 7
        exchange.bind([grads.at[part] for part in range(3)], outs, refs[small:])
        finale.bind(refs[spot + 15 : small])
        step = pl.program_id(0)
        loads = [
            pltpu.make_async_copy(source, d_held.at[part], near.at[part])
            for part, source in enumerate((q_all, k_all, v_all))
        ]
        loads += [
            pltpu.make_async_copy(source, target, near.at[3 + which])
            for which, (source, target) in enumerate(
                ((w_qkv_all, w_qkv), (w_out_all, w_out), (w_down_all, w_down))
            )
        ]

        @pl.when(step == 0)
        def _():
            for load in loads:
                load.start()
            finale.greet()
            sums[...] = jnp.zeros_like(sums)

        exchange.tick(step, steps)

        for part in range(3):
            pl.when(step == part)(loads[part].wait)
        pl.when(step == early)(loads[3].wait)

        @pl.when(step == early + middle)
        def _():
            loads[4].wait()
            loads[5].wait()

        @pl.when(step < early)
        def _():
            product = mxu(left[...], d_held[step, :, width - wide :]).astype(BF16)
            grads[step] = product.reshape(ways, share, wide)

        @pl.when((step >= early) & (step < early + middle))
        def _():
            at = step - early
            seq = at // per_seq
            first = (at - seq * per_seq) * block
            start, inside = masked_rows(
                tok[...], emb[...], starts[seq], lengths[seq], first
            )
            hat, inverse = normalized(start)
            here = pl.ds(pl.multiple_of(at * block, block), block)
            d_normed = mxu(d_held[0, here, :], w_qkv[:, 0:width], TRANSPOSED)
            d_normed += mxu(d_held[1, here, :], w_qkv[:, width : 2 * width], TRANSPOSED)
            d_normed += mxu(d_held[2, here, :], w_qkv[:, 2 * width :], TRANSPOSED)
            scale = mod[pl.ds(seq, 1), width : 2 * width]
            d_start = d_mid[...] + norm_back(d_normed * (gn[...] * (1.0 + scale)), hat, inverse)
            g_tok[...] = jnp.where(inside, 0.0, d_start)
            sums[seq, 0:1, :] += column_sum(d_normed)
            sums[seq, 1:2, :] += column_sum(d_normed * hat)
            sums[seq, 2:3, :] += column_sum(jnp.where(inside, d_start, 0.0))

        @pl.when(step == early + middle)
        def _():
            parts = finale.parts
            embed_sum = jnp.zeros((1, width), F32)
            gain_sum = jnp.zeros((1, width), F32)
            for seq in range(seqs):
                shift, scale = sums[seq, 0:1, :], sums[seq, 1:2, :]
                gain_sum += scale * (1.0 + mod[seq : seq + 1, width : 2 * width])
                embed_sum += sums[seq, 2:3, :]
                row = jnp.concatenate([shift, scale * gn[...], two[seq : seq + 1, :]], axis=1)
                for way in range(ways):
                    parts[way, seq : seq + 1, 0:columns] = row[
                        :, way * columns : (way + 1) * columns
                    ]
            for way in range(ways):
                parts[way, 0:seqs, columns : columns + time_width] = feat[...]
                lower = PAIR * (share * way // PAIR)
                parts[way, 0:1, columns + time_width :] = embed_sum[:, lower : lower + window]
                parts[way, 1:2, columns + time_width :] = gain_sum[:, lower : lower + window]
                parts[way, 2:8, columns + time_width :] = vec[way, 2:8, :]
            finale.begin()

        @pl.when(step == early + middle + 2)
        def _():
            finale.spread(seqs, columns + time_width)

        @pl.when(step >= early + middle)
        def _():
            at = step - early - middle
            seq = at // late_per_seq
            first = (at - seq * late_per_seq) * late_block
            start, _ = masked_rows(
                tok_late[...], emb[...], starts[seq], lengths[seq], first
            )
            attended = mxu(mix[...], w_out[...])
            branch = mxu(act[...], grouped_rows(w_down, ways)) + b_down[...]
            hidden = start + mod[pl.ds(seq, 1), 2 * width : 3 * width] * attended
            block_out[...] = (
                hidden + mod[pl.ds(seq, 1), 5 * width : 6 * width] * branch
            ).astype(BF16)

        @pl.when(step == steps - 1)
        def _():
            finale.close()
            got = finale.wide_got
            every = got[...].reshape(finale.wide * 8, lanes)
            d_mods, feats = every[:, 0:columns], every[:, columns : columns + time_width]
            g_ada[...] = lax.dot_general(
                jnp.transpose(feats), d_mods, PLAIN, precision=FULL_PRECISION,
                preferred_element_type=F32,
            )
            g_ada_bias[...] = column_sum(d_mods)
            total = got[0, :, columns + time_width :]
            for index in range(1, finale.wide):
                total += got[index, :, columns + time_width :]
            g_vec[...] = total
            exchange.rest(steps)

    row = pl.BlockSpec((block, width), lambda i: (jnp.clip(i - early, 0, middle - 1), 0))

    def late_row(wide):
        return pl.BlockSpec(
            (late_block, wide), lambda i: (jnp.maximum(i - early - middle, 0), 0)
        )

    def fixed(shape):
        return pl.BlockSpec(shape, lambda i: (0,) * len(shape))

    anywhere = pl.BlockSpec(memory_space=pl.ANY)
    return call(
        kernel,
        "finish",
        (steps,),
        [smem(), smem(), whole(turned.shape)]
        + [anywhere] * 3
        + [row, row, whole(embed.shape), whole(gain.shape), whole(modulation.shape), anywhere]
        + [late_row(width), late_row(width), anywhere, whole(down_bias.shape)]
        + [whole(features.shape), whole(rows_two.shape), whole(vectors_two.shape)]
        + [late_row(hidden_width), anywhere],
        [
            row,
            late_row(width),
            fixed((time_width, columns)),
            fixed((1, columns)),
            fixed((8, window)),
        ]
        + exchange.out_specs(),
        [
            jax.ShapeDtypeStruct((rows, width), F32),
            jax.ShapeDtypeStruct((rows, width), BF16),
            jax.ShapeDtypeStruct((time_width, columns), F32),
            jax.ShapeDtypeStruct((1, columns), F32),
            jax.ShapeDtypeStruct((8, window), F32),
        ]
        + exchange.out_shape(),
        [
            pltpu.VMEM((3, ways, share, wide), BF16),
            pltpu.VMEM((seqs, 8, width), F32),
            pltpu.VMEM((3, rows, width), BF16),
            pltpu.VMEM(weight.shape, BF16),
            pltpu.VMEM(out_weight.shape, BF16),
            pltpu.VMEM(down.shape, BF16),
            pltpu.SemaphoreType.DMA((6,)),
        ]
        + finale.scratch(lanes)
        + exchange.scratch(),
        2 * rows * width * (7 * width + hidden_width),
        rows * (width * 24 + 2 * hidden_width),
        0,
        ident,
    )(
        starts, lengths, turned, *d_parts, tokens, d_middle, embed, gain, modulation, weight,        tokens, mixture, out_weight, down_bias, features, rows_two, vectors_two, active, down,
    )


def gather_first(small, ada, weight, ident):
    share, wide = weight.shape
    width = wide // 3
    columns = [(0, 0, small.shape[1]), (1, 0, ada.shape[1])]
    columns += [(2, k * width, (k + 1) * width) for k in range(3)]
    gathering = Gather(
        [small.shape, ada.shape, weight.shape], [0] * 5, [0] * 3, columns, (0, 1)
    )

    def kernel(*refs):
        gathering.bind(refs[0:3], refs[3:6], refs[6:])
        gathering.greet()
        gathering.begin(0)
        gathering.begin(1)
        gathering.begin(2)
        for k in range(5):
            gathering.relay(k)
            if k + 3 < 5:
                gathering.begin(k + 3)
            if k > 0:
                gathering.share(k - 1)
        gathering.share(4)
        for k in range(5):
            gathering.close(k)

    return call(
        kernel,
        "gather_first",
        (),
        gathering.in_specs(),
        gathering.out_specs(),
        gathering.out_shape(),
        gathering.scratch(),
        0,
        8 * share * wide,
        0,
        ident,
    )(small, ada, weight)


def assemble(ups, downs, out, qkv):
    share, units = ups[0].shape
    part, width = downs[0].shape
    ways = units // part
    groups = len(ups)

    def kernel(*refs):
        up_in, down_in = refs[:groups], refs[groups : 2 * groups]
        out_in, qkv_in = refs[2 * groups], refs[2 * groups + 1 : 2 * groups + 7]
        g_up, g_down, g_out, g_qkv = refs[2 * groups + 7 :]
        for group in range(groups):
            for way in range(ways):
                lower = (way * groups + group) * part
                g_up[:, lower : lower + part] = up_in[group][
                    :, way * part : (way + 1) * part
                ].astype(F32)
            g_down[group] = down_in[group][...].astype(F32)
        g_out[...] = out_in[...].astype(F32)
        for which in range(6):
            lower = (which % 3) * width + (which // 3) * (width // 2)
            g_qkv[:, lower : lower + width // 2] = qkv_in[which][...].astype(F32)

    pace = 4
    small, tall = share // pace, part // pace

    def rows(count, columns):
        return pl.BlockSpec((count, columns), lambda i: (i, 0))

    g_up, g_down, g_out, g_qkv = call(
        kernel,
        "assemble",
        (pace,),
        [rows(small, units)] * groups
        + [rows(tall, width)] * groups
        + [rows(small, width)]
        + [rows(small, width // 2)] * 6,
        (
            rows(small, units * groups),
            pl.BlockSpec((groups, tall, width), lambda i: (0, i, 0)),
            rows(small, width),
            rows(small, 3 * width),
        ),
        (
            jax.ShapeDtypeStruct((share, units * groups), F32),
            jax.ShapeDtypeStruct((groups, part, width), F32),
            jax.ShapeDtypeStruct((share, width), F32),
            jax.ShapeDtypeStruct((share, 3 * width), F32),
        ),
        [],
        0,
        12 * share * units * groups,
    )(*ups, *downs, out, *qkv)
    return g_up, g_down.reshape(groups * part, width), g_out, g_qkv


def per_device(
    tokens,
    timestep,
    span_start,
    span_length,
    mask_embed,
    ada_weight,
    ada_bias,
    norm_first,
    query_key_value_weight,
    output_weight,
    norm_second,
    up_projection_weight,
    up_projection_bias,
    down_projection_weight,
    down_projection_bias,
    cotangent,
):
    seqs = timestep.shape[0]
    rows, width = tokens.shape
    seq_length = rows // seqs
    ways = lax.axis_size("narrow")
    me = lax.axis_index("narrow")
    share = width // ways
    unit_share = down_projection_weight.shape[0]
    part = unit_share // GROUPS
    units = ways * part
    time_width, columns = ada_weight.shape

    spot = jnp.arange(32 * columns)
    lane = lax.rem(spot, columns)
    owner = jnp.where(spot < (BIAS_UP + 1) * columns, lane // share, lane // part)
    vectors = [mask_embed, norm_first, norm_second, down_projection_bias]
    vectors += [up_projection_bias[group * part : (group + 1) * part] for group in range(GROUPS)]
    small = jnp.zeros((32 * columns,), BF16)
    for row, v in enumerate(vectors):
        for way in range(ways):
            lower = (row + 1) * columns + way * v.shape[0]
            small += jnp.pad(v, (lower, small.shape[0] - lower - v.shape[0]))
    small = jnp.where(owner == me, small, jnp.zeros_like(small))
    small += jnp.pad(ada_bias, (0, small.shape[0] - columns))
    small = small.reshape(32, columns)
    small, ada, w_qkv = gather_first(small, ada_weight, query_key_value_weight, 0)
    vectors = jnp.sum(small[1:9].astype(F32).reshape(8, ways, columns), axis=1)
    features = time_features(timestep, time_width)
    modulation = jnp.dot(features, ada.astype(F32), precision=FULL_PRECISION) + small[0:1].astype(F32)
    tables = rotary_tables(seq_length)

    qkv, turned_one = project(
        tokens, span_start, span_length, vectors, vectors, modulation, w_qkv, tables, seqs
    )
    thirds = [
        (which, third * size, (third + 1) * size)
        for which, size in ((1, unit_share * ways // 3), (2, width // 3))
        for third in range(3)
    ]
    mixture, total, w_out, w_up, w_down = attend(
        qkv,
        [output_weight, up_projection_weight, down_projection_weight],
        [0, 1, 3, 6, 8, 11, 13],
        [5, 5, 2],
        [(0, 0, width)] + thirds,
        1,
        seqs,
    )
    gain_two, bias_down = [vectors[row : row + 1, :width] for row in (GAIN_TWO, BIAS_DOWN)]
    head_times = paced([8, 9, 10, 11], [1, 5, 2, 2, 2, 1]) + paced([17, 17, 18, 19], [1, 4])
    active, d_upper, g_bias, d_gate_two, g_sum, *swaps = hidden_units(
        mixture, tokens, cotangent, span_start, span_length, vectors, vectors, modulation, w_out,
        w_up, vectors, w_down, head_times, 2, seqs,
    )
    d_gate_two += bias_down * g_sum
    d_middle, d_mixture, g_out, sums_two = middle_back(
        mixture, tokens, cotangent, span_start, span_length, vectors, vectors, modulation, w_out,
        d_upper, w_up, seqs,
    )
    d_q, d_k, d_v, *done = attend_back(
        qkv, mixture, d_mixture, total, tables, turned_one, swaps[2:] + [g_out],
        ["tail"] * 2 + ["whole"] * 3, halved(swaps[2:] + [g_out]),
        [[1, 2, 5, 8, 11, 13], [2, 3, 6, 9, 12, 14], [3, 4, 7, 10, 13, 15], [4, 5, 8, 11, 14, 16]]
        + paced([0, 1, 3, 5], [1, 4, 3, 3, 4, 2])
        + paced([6, 8], [1, 3, 3, 3, 3, 2])
        + paced([12, 12, 13], [1, 3, 2, 2, 3, 1]),
        3, seqs,
    )
    scale_two = modulation[:, 4 * width : 5 * width]
    rows_two = jnp.concatenate(
        [sums_two[:, 2], sums_two[:, 0], sums_two[:, 1] * gain_two, d_gate_two], axis=1
    )
    g_norm_two = jnp.sum(sums_two[:, 1] * (1.0 + scale_two), axis=0)
    g_bias_down = jnp.sum(modulation[:, 5 * width :] * g_sum, axis=0)
    lowers = [PAIR * (share * way // PAIR) for way in range(ways)]
    vectors_two = jnp.stack(
        [
            jnp.stack([v[lower : lower + 2 * PAIR] for lower in lowers])
            for v in (g_norm_two, g_norm_two, g_norm_two, g_bias_down)
        ]
        + [g_bias[0].reshape(GROUPS, ways, part)[group] for group in range(GROUPS)]
        + [jnp.zeros((ways, 2 * PAIR), F32)],
        axis=1,
    )
    grad_tokens, block_out, grad_ada_weight, grad_ada_bias, gathered, *g_qkv = finish(
        turned_one, (d_q, d_k, d_v), tokens, d_middle, mixture, span_start, span_length, vectors,
        vectors, modulation, w_qkv, w_out, vectors, active, w_down, features, rows_two,
        vectors_two,
        FINISH_TIMES, 4, seqs,
    )
    skip = lax.rem(share * me, PAIR)
    own = lax.dynamic_slice(gathered, (0, skip), (4, share))
    g_ups, g_downs = (swaps[0], *done[0:4:2]), (swaps[1], *done[1:4:2])
    g_up, g_down, g_out, g_qkv = assemble(g_ups, g_downs, done[4], done[5:] + g_qkv)
    return (
        block_out,
        grad_tokens,
        own[0],
        grad_ada_weight,
        grad_ada_bias.reshape(-1),
        own[1],
        g_qkv,
        g_out,
        own[2],
        g_up,
        gathered[4 : 4 + GROUPS].reshape(-1),
        g_down,
        own[3],
    )


def solution(mesh):
    rows = P(("wide", "narrow"), None)
    per_seq = P(("wide", "narrow"))
    vector, matrix, columns = P("narrow"), P("narrow", None), P(None, "narrow")
    return jax.shard_map(
        per_device,
        mesh=mesh,
        in_specs=(
            rows, per_seq, per_seq, per_seq, vector, columns, vector, vector,
            matrix, matrix, vector, matrix, vector, matrix, vector, rows,
        ),
        out_specs=(
            rows, rows, vector, columns, vector, vector, matrix, matrix, vector, matrix,
            vector, matrix, vector,
        ),
        check_vma=False,
    )
```
